32 devices in a mesh: dp: 4 (over x, core), sp: 8 (over z, y).
Axes of the slice: x: 2, y: 2, z: 4, core: 2. Of those that a mesh axis runs over, the one named last changes fastest.
Arguments:
- inputs: bfloat16 [4, 8, 256, 1152], P('dp', 'sp'), may hold values from -6 to 6
- timesteps: int32 [4], replicated, may hold values from 0 to 999
- segment_ids: int32 [4, 8], P('dp'), may hold values from 0 to 2, never falling along the last dimension, each value on 1 to 4 neighbouring positions
- spatial_attend_in: bfloat16 [1152, 3456], P('dp', 'sp'), may hold values from -0.1875 to 0.1875
- spatial_attend_bias: bfloat16 [2304], P('dp'), may hold values from -3 to 3
- spatial_attend_out: bfloat16 [1152, 1152], P('dp', 'sp'), may hold values from -0.75 to 0.75
- spatial_out_bias: bfloat16 [1152], P('dp'), may hold values from -2 to 2
- spatial_expand: bfloat16 [1152, 4608], P('dp', 'sp'), may hold values from -0.1875 to 0.1875
- spatial_expand_bias: bfloat16 [4608], P('dp'), may hold values from -3 to 3
- spatial_shrink: bfloat16 [4608, 1152], P('dp', 'sp'), may hold values from -0.09375 to 0.09375
- spatial_shrink_bias: bfloat16 [1152], P('dp'), may hold values from -2 to 2
- spatial_modulate: bfloat16 [1152, 6912], P('dp', 'sp'), may hold values from -0.375 to 0.375
- spatial_modulate_bias: bfloat16 [6912], P('dp'), may hold values from -2 to 2
- temporal_attend_in: bfloat16 [1152, 3456], P('dp', 'sp'), may hold values from -0.1875 to 0.1875
- temporal_attend_bias: bfloat16 [2304], P('dp'), may hold values from -3 to 3
- temporal_attend_out: bfloat16 [1152, 1152], P('dp', 'sp'), may hold values from -0.375 to 0.375
- temporal_out_bias: bfloat16 [1152], P('dp'), may hold values from -2 to 2
- temporal_expand: bfloat16 [1152, 4608], P('dp', 'sp'), may hold values from -0.1875 to 0.1875
- temporal_expand_bias: bfloat16 [4608], P('dp'), may hold values from -3 to 3
- temporal_shrink: bfloat16 [4608, 1152], P('dp', 'sp'), may hold values from -0.09375 to 0.09375
- temporal_shrink_bias: bfloat16 [1152], P('dp'), may hold values from -2 to 2
- temporal_modulate: bfloat16 [1152, 6912], P('dp', 'sp'), may hold values from -0.375 to 0.375
- temporal_modulate_bias: bfloat16 [6912], P('dp'), may hold values from -2 to 2
- cotangent: bfloat16 [4, 8, 256, 1152], P('dp', 'sp'), may hold values from -6 to 6
Outputs:
- output: bfloat16 [4, 8, 256, 1152], P('dp', 'sp')
- input_gradient: bfloat16 [4, 8, 256, 1152], P('dp', 'sp')
- spatial_attend_in_gradient: float32 [1152, 3456], P('dp', 'sp')
- spatial_attend_bias_gradient: float32 [2304], P('dp')
- spatial_attend_out_gradient: float32 [1152, 1152], P('dp', 'sp')
- spatial_out_bias_gradient: float32 [1152], P('dp')
- spatial_expand_gradient: float32 [1152, 4608], P('dp', 'sp')
- spatial_expand_bias_gradient: float32 [4608], P('dp')
- spatial_shrink_gradient: float32 [4608, 1152], P('dp', 'sp')
- spatial_shrink_bias_gradient: float32 [1152], P('dp')
- spatial_modulate_gradient: float32 [1152, 6912], P('dp', 'sp')
- spatial_modulate_bias_gradient: float32 [6912], P('dp')
- temporal_attend_in_gradient: float32 [1152, 3456], P('dp', 'sp')
- temporal_attend_bias_gradient: float32 [2304], P('dp')
- temporal_attend_out_gradient: float32 [1152, 1152], P('dp', 'sp')
- temporal_out_bias_gradient: float32 [1152], P('dp')
- temporal_expand_gradient: float32 [1152, 4608], P('dp', 'sp')
- temporal_expand_bias_gradient: float32 [4608], P('dp')
- temporal_shrink_gradient: float32 [4608, 1152], P('dp', 'sp')
- temporal_shrink_bias_gradient: float32 [1152], P('dp')
- temporal_modulate_gradient: float32 [1152, 6912], P('dp', 'sp')
- temporal_modulate_bias_gradient: float32 [6912], P('dp')
The draws below stay inside these ranges and needn't reach their ends.
Inputs may be any that keep to these rules, and one draw needn't show every extreme that they name: `segment_ids`: in each sequence the ids never fall along the frame slots and every id from 0 to 2 appears; each clip covers 1 to 4 slots.
All inputs are finite; a program needn't handle non-finite values.
Results may differ from the reference program's by a relative error of at most 0.024.
Values may be sent and summed in bfloat16 or wider, within the bound.
A program may use at most 512 MiB of HBM per device.

```python
import math
import jax
import jax.numpy as jnp
import numpy as np
from jax import lax

D = 1152
H = 16
HD = 72
MLP = 4608
P_SIZE = 256
F = 8
SEQS = 4


def plant(entries, rng, low, largest):
    longest = entries.shape.index(max(entries.shape))
    spots = []
    for shift in (0, 1):
        where = [jax.random.randint(jax.random.fold_in(rng, axis), (), 0, length) for axis, length in enumerate(entries.shape)]
        where[longest] = (where[longest] + shift) % entries.shape[longest]
        spots.append(tuple(where))
    return entries.at[spots[0]].set(low).at[spots[1]].set(largest)


def level_of(key, dims, shards, least, largest):
    def one(dim, shards_of):
        heights = jax.random.uniform(jax.random.fold_in(jax.random.fold_in(key, 6), dim), (shards_of,), jnp.float32, least / len(shards), largest / len(shards))
        return jnp.repeat(jnp.exp(heights), dims[dim] // shards_of).reshape((-1,) + (1,) * (len(dims) - dim - 1))

    gain = one(*shards[0])
    for cut in shards[1:]:
        gain = gain * one(*cut)
    return gain


def length_profile(number_of, total, most, skew):
    portions = [(1 << 20) // math.isqrt(standing ** skew) + 1 for standing in range(2, number_of + 1)]
    spare, given = total - most - (number_of - 1), [1] * (number_of - 1)
    while spare > 0:
        movable = [i for i in range(number_of - 1) if given[i] < most]
        mass, remaining = sum([portions[i] for i in movable]), spare
        for i in movable:
            addition = min(most - given[i], max(1, remaining * portions[i] // mass), spare)
            given[i] = given[i] + addition
            spare = spare - addition
    return np.array([most] + given)


def ragged_sizes(stream_key, number_of, total, most, skew):
    if number_of == 2:
        one = jax.random.randint(stream_key, (), max(1, total - most), min(most, total - 1) + 1)
        return jnp.stack([one, total - one])
    lengths = jnp.asarray(length_profile(number_of, total, most, skew), jnp.int32)
    twos = (number_of - 1) // 2
    donor, sink = lengths[1:1 + 2 * twos:2], lengths[2:2 + 2 * twos:2]
    margin = jnp.minimum(donor - 1, most - sink)
    moved = jax.random.randint(jax.random.fold_in(stream_key, 1), (twos,), 0, 1 << 20) % (margin + 1)
    lengths = lengths.at[1:1 + 2 * twos:2].set(donor - moved).at[2:2 + 2 * twos:2].set(sink + moved)
    return lengths[jax.random.permutation(jax.random.fold_in(stream_key, 2), number_of)]


def bell_draw(stream_key, dims, spread, bound, split=(), kind=jnp.bfloat16):
    drawn = jax.random.normal(stream_key, dims, jnp.float32) * spread
    if len(split) > 0:
        drawn = level_of(stream_key, dims, split, -0.22, 0.18) * drawn
    return jnp.clip(drawn, min=-bound, max=bound).astype(kind)


def setup_inputs(seed: int = 0) -> dict:
    seeds = jax.random.split(jax.random.key(seed), 25)
    inputs = bell_draw(seeds[0], (SEQS, F, P_SIZE, D), 1.0, 6.0, ((0, 4), (1, 8)))
    timesteps = plant(jax.random.randint(seeds[1], (SEQS,), 0, 1000), jax.random.fold_in(seeds[1], 1), 0, 999).astype(jnp.int32)
    segment_ids = jax.vmap(lambda own: jnp.searchsorted(jnp.cumsum(ragged_sizes(own, F // 4 + 1, F, F // 2, 1)), jnp.arange(F), side="right"))(jax.random.split(seeds[2], SEQS)).reshape((SEQS, F)).astype(jnp.int32)
    spatial_attend_in = bell_draw(seeds[3], (D, 3 * D), D ** -0.5, 0.1875, ((0, 4), (1, 8)))
    spatial_attend_bias = bell_draw(seeds[4], (2 * D,), 0.5, 3.0, ((0, 4),))
    spatial_attend_out = bell_draw(seeds[5], (D, D), (D // 16) ** -0.5, 0.75, ((0, 4), (1, 8)))
    spatial_out_bias = bell_draw(seeds[6], (D,), 0.3, 2.0, ((0, 4),))
    spatial_expand = bell_draw(seeds[7], (D, MLP), D ** -0.5, 0.1875, ((0, 4), (1, 8)))
    spatial_expand_bias = bell_draw(seeds[8], (MLP,), 0.5, 3.0, ((0, 4),))
    spatial_shrink = bell_draw(seeds[9], (MLP, D), MLP ** -0.5, 0.09375, ((0, 4), (1, 8)))
    spatial_shrink_bias = bell_draw(seeds[10], (D,), 0.3, 2.0, ((0, 4),))
    spatial_modulate = bell_draw(seeds[11], (D, 6 * D), (D // 4) ** -0.5, 0.375, ((0, 4), (1, 8)))
    spatial_modulate_bias = bell_draw(seeds[12], (6 * D,), 0.3, 2.0, ((0, 4),))
    temporal_attend_in = bell_draw(seeds[13], (D, 3 * D), D ** -0.5, 0.1875, ((0, 4), (1, 8)))
    temporal_attend_bias = bell_draw(seeds[14], (2 * D,), 0.5, 3.0, ((0, 4),))
    temporal_attend_out = bell_draw(seeds[15], (D, D), (D // 4) ** -0.5, 0.375, ((0, 4), (1, 8)))
    temporal_out_bias = bell_draw(seeds[16], (D,), 0.3, 2.0, ((0, 4),))
    temporal_expand = bell_draw(seeds[17], (D, MLP), D ** -0.5, 0.1875, ((0, 4), (1, 8)))
    temporal_expand_bias = bell_draw(seeds[18], (MLP,), 0.5, 3.0, ((0, 4),))
    temporal_shrink = bell_draw(seeds[19], (MLP, D), MLP ** -0.5, 0.09375, ((0, 4), (1, 8)))
    temporal_shrink_bias = bell_draw(seeds[20], (D,), 0.3, 2.0, ((0, 4),))
    temporal_modulate = bell_draw(seeds[21], (D, 6 * D), (D // 4) ** -0.5, 0.375, ((0, 4), (1, 8)))
    temporal_modulate_bias = bell_draw(seeds[22], (6 * D,), 0.3, 2.0, ((0, 4),))
    cotangent = bell_draw(seeds[23], (SEQS, F, P_SIZE, D), 1.0, 6.0, ((0, 4), (1, 8)))
    return dict(inputs=inputs, timesteps=timesteps, segment_ids=segment_ids, spatial_attend_in=spatial_attend_in, spatial_attend_bias=spatial_attend_bias, spatial_attend_out=spatial_attend_out, spatial_out_bias=spatial_out_bias, spatial_expand=spatial_expand, spatial_expand_bias=spatial_expand_bias, spatial_shrink=spatial_shrink, spatial_shrink_bias=spatial_shrink_bias, spatial_modulate=spatial_modulate, spatial_modulate_bias=spatial_modulate_bias, temporal_attend_in=temporal_attend_in, temporal_attend_bias=temporal_attend_bias, temporal_attend_out=temporal_attend_out, temporal_out_bias=temporal_out_bias, temporal_expand=temporal_expand, temporal_expand_bias=temporal_expand_bias, temporal_shrink=temporal_shrink, temporal_shrink_bias=temporal_shrink_bias, temporal_modulate=temporal_modulate, temporal_modulate_bias=temporal_modulate_bias, cotangent=cotangent)


EPSILON = 1e-06
HIGHEST_PRECISION = lax.Precision.HIGHEST
SPATIAL_FORMS = ('sabhe,sache->sahbc', 'sahbc,sache->sabhe')
TEMPORAL_FORMS = ('sabhe,scbhe->sbhac', 'sbhac,scbhe->sabhe')

@jax.custom_vjp
def low(v):
    return lax.optimization_barrier(v.astype(jnp.bfloat16)).astype(jnp.float32)

@jax.custom_vjp
def low_back(v):
    return v

def low_keep(v):
    return (low(v), None)

def low_pass(kept, grad):
    return (grad,)

def back_keep(v):
    return (v, None)

def back_low(kept, grad):
    return (low(grad),)
low.defvjp(low_keep, low_pass)
low_back.defvjp(back_keep, back_low)

def sinusoid(timesteps):
    half_width = D // 2
    frequencies = jnp.exp(-math.log(10000.0) * jnp.arange(half_width, dtype=jnp.float32) / half_width)
    angles = timesteps.astype(jnp.float32)[:, None] * frequencies[None, :]
    return jnp.concatenate([jnp.cos(angles), jnp.sin(angles)], axis=1)

def layer_norm(tensor):
    centered = tensor - lax.optimization_barrier(jnp.mean(tensor, axis=-1, keepdims=True))
    return centered * lax.rsqrt(lax.optimization_barrier(jnp.mean(centered * centered, axis=-1, keepdims=True)) + EPSILON)

def matmul(left_side, right_side):
    return jnp.matmul(left_side, right_side, precision=HIGHEST_PRECISION)

def block(stream, condition, params, forms, allowed):
    attend_in, attend_bias, attend_out, out_bias, expand, expand_bias, shrink, shrink_bias, modulate_weight, modulate_bias = params
    modulation = matmul(condition, modulate_weight) + modulate_bias
    pieces = [modulation[:, None, None, slot * D:(slot + 1) * D] for slot in range(6)]
    normed = low(layer_norm(stream) * (1.0 + pieces[1]) + pieces[0])
    joined_bias = jnp.concatenate([attend_bias[:D], jnp.zeros((D,), attend_bias.dtype), attend_bias[D:]])
    projected = low(low_back(matmul(normed, attend_in) + joined_bias))
    head_shape = projected.shape[:3] + (H, HD)
    queries = projected[..., :D].reshape(head_shape)
    key_rows = projected[..., D:2 * D].reshape(head_shape)
    values = projected[..., 2 * D:].reshape(head_shape)
    scores = low_back(jnp.einsum(forms[0], queries, key_rows, precision=HIGHEST_PRECISION) * HD ** (-0.5))
    if allowed is not None:
        scores = jnp.where(allowed, scores, -1e+30)
    softmax_probs = jax.nn.softmax(scores, axis=-1)
    mixture = low(low_back(jnp.einsum(forms[1], low(softmax_probs), values, precision=HIGHEST_PRECISION)))
    mixture = mixture.reshape(stream.shape)
    attended = low_back(matmul(mixture, attend_out) + out_bias)
    middle = stream + pieces[2] * attended
    normed_second = low(layer_norm(middle) * (1.0 + pieces[4]) + pieces[3])
    hidden = low_back(matmul(normed_second, expand) + expand_bias)
    activated = low(jax.nn.gelu(hidden, approximate=True))
    branch = low_back(matmul(activated, shrink) + shrink_bias)
    return middle + pieces[5] * branch

def forward(stream, condition, allowed, spatial, temporal):
    spatial_out = block(stream, condition, spatial, SPATIAL_FORMS, None)
    passed = low_back(low(spatial_out))
    temporal_out = block(passed, condition, temporal, TEMPORAL_FORMS, allowed)
    return low(temporal_out)

def reference(inputs, timesteps, segment_ids, spatial_attend_in, spatial_attend_bias, spatial_attend_out, spatial_out_bias, spatial_expand, spatial_expand_bias, spatial_shrink, spatial_shrink_bias, spatial_modulate, spatial_modulate_bias, temporal_attend_in, temporal_attend_bias, temporal_attend_out, temporal_out_bias, temporal_expand, temporal_expand_bias, temporal_shrink, temporal_shrink_bias, temporal_modulate, temporal_modulate_bias, cotangent):
    spatial = tuple((array.astype(jnp.float32) for array in (spatial_attend_in, spatial_attend_bias, spatial_attend_out, spatial_out_bias, spatial_expand, spatial_expand_bias, spatial_shrink, spatial_shrink_bias, spatial_modulate, spatial_modulate_bias)))
    temporal = tuple((array.astype(jnp.float32) for array in (temporal_attend_in, temporal_attend_bias, temporal_attend_out, temporal_out_bias, temporal_expand, temporal_expand_bias, temporal_shrink, temporal_shrink_bias, temporal_modulate, temporal_modulate_bias)))
    condition_all = low(jax.nn.silu(sinusoid(timesteps)))
    group_size = math.gcd(SEQS, max(1, 4096 // (F * P_SIZE)))
    group_count = SEQS // group_size
    grouped = (inputs.reshape(group_count, group_size, F, P_SIZE, D), condition_all.reshape(group_count, group_size, D), segment_ids.reshape(group_count, group_size, F), cotangent.reshape(group_count, group_size, F, P_SIZE, D))

    def one_group(totals, members):
        group_input, group_condition, group_segments, group_cotangent = members
        allowed = (group_segments[:, :, None] == group_segments[:, None, :])[:, None, None, :, :]

        def run(stream, spatial_params, temporal_params):
            return forward(stream, group_condition, allowed, spatial_params, temporal_params)
        result, pullback = jax.vjp(run, group_input.astype(jnp.float32), spatial, temporal)
        back_stream, back_spatial, back_temporal = pullback(group_cotangent.astype(jnp.float32))
        totals = jax.tree.map(jnp.add, totals, (back_spatial, back_temporal))
        return (totals, (result.astype(jnp.bfloat16), back_stream.astype(jnp.bfloat16)))
    zeros = jax.tree.map(jnp.zeros_like, (spatial, temporal))
    (spatial_grads, temporal_grads), (results, back_inputs) = lax.scan(one_group, zeros, grouped)
    output = results.reshape(SEQS, F, P_SIZE, D)
    input_gradient = back_inputs.reshape(SEQS, F, P_SIZE, D)
    return (output, input_gradient, spatial_grads[0], spatial_grads[1], spatial_grads[2], spatial_grads[3], spatial_grads[4], spatial_grads[5], spatial_grads[6], spatial_grads[7], spatial_grads[8], spatial_grads[9], temporal_grads[0], temporal_grads[1], temporal_grads[2], temporal_grads[3], temporal_grads[4], temporal_grads[5], temporal_grads[6], temporal_grads[7], temporal_grads[8], temporal_grads[9])
```

```python
import math

import jax
import jax.numpy as jnp
from jax import lax
from jax.sharding import PartitionSpec as P

D = 1152
H = 16
HD = 72


EPSILON = 1e-06
HIGHEST_PRECISION = lax.Precision.HIGHEST
SPATIAL_FORMS = ("sabhe,sache->sahbc", "sahbc,sache->sabhe", "sahbc,sabhe->sache")
TEMPORAL_FORMS = ("sabhe,scbhe->sbhac", "sbhac,scbhe->sabhe", "sbhac,sabhe->scbhe")


def sinusoid(timesteps):
    half_width = D // 2
    frequencies = jnp.exp(
        -math.log(10000.0) * jnp.arange(half_width, dtype=jnp.float32) / half_width
    )
    angles = timesteps.astype(jnp.float32)[:, None] * frequencies[None, :]
    return jnp.concatenate([jnp.cos(angles), jnp.sin(angles)], axis=1)


def layer_norm(tensor):
    centered = tensor - jnp.mean(tensor, axis=-1, keepdims=True)
    return centered * lax.rsqrt(jnp.mean(centered * centered, axis=-1, keepdims=True) + EPSILON)


def modulate(tensor, shift_part, scale_part):
    return layer_norm(tensor) * (1.0 + scale_part) + shift_part


def matmul(left_side, right_side):
    return jnp.dot(left_side, right_side, preferred_element_type=jnp.float32)


def back_matmul(gradient, matrix):
    return lax.dot_general(
        gradient,
        matrix,
        (((gradient.ndim - 1,), (1,)), ((), ())),
        preferred_element_type=jnp.float32,
    )


def outer_product(left_side, right_side):
    flat_left = left_side.reshape(-1, left_side.shape[-1])
    flat_right = right_side.reshape(-1, right_side.shape[-1])
    return lax.dot_general(
        flat_left, flat_right, (((0,), (0,)), ((), ())), preferred_element_type=jnp.float32
    )


def column_totals(tensor):
    return jnp.sum(tensor.astype(jnp.float32).reshape(-1, tensor.shape[-1]), axis=0)


def per_sequence(tensor):
    return jnp.sum(tensor, axis=(1, 2))


def over_data(core, biases):
    attend_in, attend_out, expand, shrink = core
    attend_bias, out_bias, expand_bias, shrink_bias, modulate_bias = biases
    gathered = (
        lax.all_gather(attend_in, "dp", axis=0, tiled=True),
        lax.all_gather(attend_out, "dp", axis=0, tiled=True),
        lax.all_gather(expand, "dp", axis=0, tiled=True),
        lax.all_gather(shrink, "dp", axis=0, tiled=True),
        lax.all_gather(attend_bias, "dp", axis=0, tiled=True),
        lax.all_gather(out_bias, "dp", axis=0, tiled=True),
        lax.all_gather(expand_bias, "dp", axis=0, tiled=True),
        lax.all_gather(shrink_bias, "dp", axis=0, tiled=True),
        lax.all_gather(modulate_bias, "dp", axis=0, tiled=True),
    )
    return (gathered[:4], gathered[4:])


def over_frames(core):
    attend_in, attend_out, expand, shrink = core
    gathered = (
        lax.all_gather(attend_in, "sp", axis=1, tiled=True),
        lax.all_gather(attend_out, "sp", axis=1, tiled=True),
        lax.all_gather(expand, "sp", axis=1, tiled=True),
        lax.all_gather(shrink, "sp", axis=1, tiled=True),
    )
    return gathered


def collect(core, biases):
    core_rows, biases_full = over_data(core, biases)
    core_full = over_frames(core_rows)
    return (core_full, biases_full)


def own_rows(condition_all, rows):
    return lax.dynamic_slice_in_dim(condition_all, lax.axis_index("dp") * rows, rows, 1)


def modulation_of(condition_all, modulate_weights):
    rows = modulate_weights[0].shape[0]
    own = own_rows(condition_all, rows)
    partial_terms = jnp.stack([matmul(own, weight) for weight in modulate_weights], axis=1)
    summed = lax.psum_scatter(partial_terms, "dp", scatter_dimension=0, tiled=True)
    full = lax.all_gather(summed, "sp", axis=2, tiled=True)
    return [full[:, slot] for slot in range(len(modulate_weights))]


def sum_over_frames(terms):
    attend_in, attend_out, expand, shrink = terms
    return (
        lax.psum_scatter(
            attend_in.astype(jnp.bfloat16), "sp", scatter_dimension=1, tiled=True
        ).astype(jnp.float32),
        lax.psum_scatter(
            attend_out.astype(jnp.bfloat16), "sp", scatter_dimension=1, tiled=True
        ).astype(jnp.float32),
        lax.psum_scatter(expand.astype(jnp.bfloat16), "sp", scatter_dimension=1, tiled=True).astype(
            jnp.float32
        ),
        lax.psum_scatter(shrink.astype(jnp.bfloat16), "sp", scatter_dimension=1, tiled=True).astype(
            jnp.float32
        ),
    )


def sum_over_data(terms):
    attend_in, attend_out, expand, shrink = terms
    return (
        lax.psum_scatter(
            attend_in.astype(jnp.bfloat16), "dp", scatter_dimension=0, tiled=True
        ).astype(jnp.float32),
        lax.psum_scatter(
            attend_out.astype(jnp.bfloat16), "dp", scatter_dimension=0, tiled=True
        ).astype(jnp.float32),
        lax.psum_scatter(expand.astype(jnp.bfloat16), "dp", scatter_dimension=0, tiled=True).astype(
            jnp.float32
        ),
        lax.psum_scatter(shrink.astype(jnp.bfloat16), "dp", scatter_dimension=0, tiled=True).astype(
            jnp.float32
        ),
    )


def modulate_gradients(condition_all, back_modulations, rows):
    joined = jnp.stack(back_modulations, axis=1)
    columns = lax.psum_scatter(joined, "sp", scatter_dimension=2, tiled=True)
    every = lax.all_gather(columns, "dp", axis=0, tiled=True)
    own = own_rows(condition_all, rows).astype(jnp.float32)
    return [
        jnp.dot(own.T, every[:, slot], precision=HIGHEST_PRECISION)
        for slot in range(len(back_modulations))
    ]


def finish(core_terms, bias_terms):
    matrix_grads = sum_over_data(sum_over_frames(core_terms))
    attend_bias, out_bias, expand_bias, shrink_bias, modulate_bias = bias_terms
    totals = lax.psum(
        (attend_bias, out_bias, expand_bias, shrink_bias, modulate_bias), ("dp", "sp")
    )
    data_index = lax.axis_index("dp")
    data_count = lax.axis_size("dp")
    bias_grads = tuple(
        (
            lax.dynamic_slice_in_dim(
                total_bias,
                data_index * (total_bias.shape[0] // data_count),
                total_bias.shape[0] // data_count,
            )
            for total_bias in totals
        )
    )
    return (matrix_grads, bias_grads)


def frames_to_patches(tensor):
    return lax.all_to_all(tensor, "sp", split_axis=2, concat_axis=1, tiled=True)


def patches_to_frames(tensor):
    return lax.all_to_all(tensor, "sp", split_axis=1, concat_axis=2, tiled=True)


def attention_scores(queries, key_rows, forms, allowed):
    scores = jnp.einsum(forms[0], queries, key_rows, preferred_element_type=jnp.float32) * HD ** (
        -0.5
    )
    if allowed is not None:
        scores = jnp.where(allowed, scores, -1e30)
    return scores


def block_forward(stream, modulation, core, biases, forms, allowed):
    attend_in, attend_out, expand, shrink = core
    attend_bias, out_bias, expand_bias, shrink_bias, modulate_bias = biases
    model_width = stream.shape[-1]
    pieces = [
        modulation[:, None, None, slot * model_width : (slot + 1) * model_width]
        for slot in range(6)
    ]
    normed = modulate(stream, pieces[0], pieces[1]).astype(jnp.bfloat16)
    bias_float = attend_bias.astype(jnp.float32)
    joined_bias = jnp.concatenate(
        [bias_float[:model_width], jnp.zeros((model_width,), jnp.float32), bias_float[model_width:]]
    )
    projected = (matmul(normed, attend_in) + joined_bias).astype(jnp.bfloat16)
    head_shape = projected.shape[:3] + (H, HD)
    queries = projected[..., :model_width].reshape(head_shape)
    key_rows = projected[..., model_width : 2 * model_width].reshape(head_shape)
    values = projected[..., 2 * model_width :].reshape(head_shape)
    scores = attention_scores(queries, key_rows, forms, allowed)
    highest = jnp.max(scores, axis=-1, keepdims=True)
    exponent = jnp.exp(scores - highest)
    denominator = jnp.sum(exponent, axis=-1, keepdims=True)
    softmax_probs = exponent / denominator
    logsum = highest + jnp.log(denominator)
    mixture = (
        jnp.einsum(
            forms[1], softmax_probs.astype(jnp.bfloat16), values, preferred_element_type=jnp.float32
        )
        .astype(jnp.bfloat16)
        .reshape(stream.shape)
    )
    attended = matmul(mixture, attend_out) + out_bias.astype(jnp.float32)
    middle = stream + pieces[2] * attended
    normed_second = modulate(middle, pieces[3], pieces[4]).astype(jnp.bfloat16)
    hidden = matmul(normed_second, expand) + expand_bias.astype(jnp.float32)
    activated = jax.nn.gelu(hidden, approximate=True).astype(jnp.bfloat16)
    branch = matmul(activated, shrink) + shrink_bias.astype(jnp.float32)
    result = middle + pieces[5] * branch
    kept = (
        pieces,
        normed,
        queries,
        key_rows,
        values,
        logsum,
        mixture,
        attended,
        middle,
        normed_second,
        hidden,
        activated,
        branch,
    )
    return (result, kept)


def block_backward(incoming, stream, core, forms, allowed, kept):
    attend_in, attend_out, expand, shrink = core
    (
        pieces,
        normed,
        queries,
        key_rows,
        values,
        logsum,
        mixture,
        attended,
        middle,
        normed_second,
        hidden,
        activated,
        branch,
    ) = kept
    model_width = stream.shape[-1]
    sequences = stream.shape[0]
    back_branch = (pieces[5] * incoming).astype(jnp.bfloat16)
    back_gate_second = per_sequence(incoming * branch)
    shrink_term = outer_product(activated, back_branch)
    shrink_bias_term = column_totals(back_branch)
    back_activated = back_matmul(back_branch, shrink)
    _, gelu_pull = jax.vjp(lambda tensor: jax.nn.gelu(tensor, approximate=True), hidden)
    back_hidden = gelu_pull(back_activated)[0].astype(jnp.bfloat16)
    expand_term = outer_product(normed_second, back_hidden)
    expand_bias_term = column_totals(back_hidden)
    back_normed_second = back_matmul(back_hidden, expand)
    _, second_pull = jax.vjp(modulate, middle, pieces[3], pieces[4])
    back_middle, back_shift_second, back_scale_second = second_pull(back_normed_second)
    back_middle = back_middle + incoming
    back_attended = (pieces[2] * back_middle).astype(jnp.bfloat16)
    back_gate_first = per_sequence(back_middle * attended)
    out_term = outer_product(mixture, back_attended)
    out_bias_term = column_totals(back_attended)
    back_mixture = (
        back_matmul(back_attended, attend_out).astype(jnp.bfloat16).reshape(queries.shape)
    )
    scores = attention_scores(queries, key_rows, forms, allowed)
    softmax_probs = jnp.exp(scores - logsum)
    back_probs = jnp.einsum(forms[0], back_mixture, values, preferred_element_type=jnp.float32)
    back_values = jnp.einsum(
        forms[2],
        softmax_probs.astype(jnp.bfloat16),
        back_mixture,
        preferred_element_type=jnp.float32,
    )
    row_delta = jnp.sum(softmax_probs * back_probs, axis=-1, keepdims=True)
    back_scores = (softmax_probs * (back_probs - row_delta)).astype(jnp.bfloat16)
    score_scale = HD ** (-0.5)
    back_queries = (
        jnp.einsum(forms[1], back_scores, key_rows, preferred_element_type=jnp.float32)
        * score_scale
    )
    back_keys = (
        jnp.einsum(forms[2], back_scores, queries, preferred_element_type=jnp.float32) * score_scale
    )
    flat_shape = stream.shape
    back_projected = jnp.concatenate(
        [
            back_queries.reshape(flat_shape),
            back_keys.reshape(flat_shape),
            back_values.reshape(flat_shape),
        ],
        axis=-1,
    ).astype(jnp.bfloat16)
    attend_in_term = outer_product(normed, back_projected)
    projected_totals = column_totals(back_projected)
    attend_bias_term = jnp.concatenate(
        [projected_totals[:model_width], projected_totals[2 * model_width :]]
    )
    back_normed = back_matmul(back_projected, attend_in)
    _, first_pull = jax.vjp(modulate, stream, pieces[0], pieces[1])
    back_stream, back_shift_first, back_scale_first = first_pull(back_normed)
    back_stream = back_stream + back_middle
    back_modulation = jnp.concatenate(
        [
            back_shift_first.reshape(sequences, model_width),
            back_scale_first.reshape(sequences, model_width),
            back_gate_first,
            back_shift_second.reshape(sequences, model_width),
            back_scale_second.reshape(sequences, model_width),
            back_gate_second,
        ],
        axis=1,
    )
    modulate_bias_term = jnp.sum(back_modulation, axis=0)
    core_terms = (attend_in_term, out_term, expand_term, shrink_term)
    bias_terms = (
        attend_bias_term,
        out_bias_term,
        expand_bias_term,
        shrink_bias_term,
        modulate_bias_term,
    )
    return (back_stream, core_terms, back_modulation, bias_terms)


def shards(
    inputs,
    timesteps,
    segment_ids,
    spatial_attend_in,
    spatial_attend_bias,
    spatial_attend_out,
    spatial_out_bias,
    spatial_expand,
    spatial_expand_bias,
    spatial_shrink,
    spatial_shrink_bias,
    spatial_modulate,
    spatial_modulate_bias,
    temporal_attend_in,
    temporal_attend_bias,
    temporal_attend_out,
    temporal_out_bias,
    temporal_expand,
    temporal_expand_bias,
    temporal_shrink,
    temporal_shrink_bias,
    temporal_modulate,
    temporal_modulate_bias,
    cotangent,
):
    condition_all = jax.nn.silu(sinusoid(timesteps)).astype(jnp.bfloat16)
    allowed = (segment_ids[:, :, None] == segment_ids[:, None, :])[:, None, None, :, :]
    spatial_core = (spatial_attend_in, spatial_attend_out, spatial_expand, spatial_shrink)
    spatial_biases = (
        spatial_attend_bias,
        spatial_out_bias,
        spatial_expand_bias,
        spatial_shrink_bias,
        spatial_modulate_bias,
    )
    temporal_core = (temporal_attend_in, temporal_attend_out, temporal_expand, temporal_shrink)
    temporal_biases = (
        temporal_attend_bias,
        temporal_out_bias,
        temporal_expand_bias,
        temporal_shrink_bias,
        temporal_modulate_bias,
    )
    stream = inputs.astype(jnp.float32)
    modulations = modulation_of(condition_all, (spatial_modulate, temporal_modulate))
    core, biases = collect(spatial_core, spatial_biases)
    modulation = modulations[0] + biases[4].astype(jnp.float32)
    spatial_core = core
    spatial_out, spatial_kept = block_forward(stream, modulation, core, biases, SPATIAL_FORMS, None)
    passed = frames_to_patches(spatial_out.astype(jnp.bfloat16)).astype(jnp.float32)
    core, biases = collect(temporal_core, temporal_biases)
    modulation = modulations[1] + biases[4].astype(jnp.float32)
    temporal_out, temporal_kept = block_forward(
        passed, modulation, core, biases, TEMPORAL_FORMS, allowed
    )
    output = patches_to_frames(temporal_out.astype(jnp.bfloat16))
    incoming = frames_to_patches(cotangent).astype(jnp.float32)
    back_passed, core_terms, back_temporal, bias_terms = block_backward(
        incoming, passed, core, TEMPORAL_FORMS, allowed, temporal_kept
    )
    temporal_grads, temporal_bias_grads = finish(core_terms, bias_terms)
    back_spatial = patches_to_frames(back_passed.astype(jnp.bfloat16)).astype(jnp.float32)
    back_inputs, core_terms, back_spatial_modulation, bias_terms = block_backward(
        back_spatial, stream, spatial_core, SPATIAL_FORMS, None, spatial_kept
    )
    spatial_grads, spatial_bias_grads = finish(core_terms, bias_terms)
    modulate_grads = modulate_gradients(
        condition_all, (back_spatial_modulation, back_temporal), spatial_modulate.shape[0]
    )
    return (
        output,
        back_inputs.astype(jnp.bfloat16),
        spatial_grads[0],
        spatial_bias_grads[0],
        spatial_grads[1],
        spatial_bias_grads[1],
        spatial_grads[2],
        spatial_bias_grads[2],
        spatial_grads[3],
        spatial_bias_grads[3],
        modulate_grads[0],
        spatial_bias_grads[4],
        temporal_grads[0],
        temporal_bias_grads[0],
        temporal_grads[1],
        temporal_bias_grads[1],
        temporal_grads[2],
        temporal_bias_grads[2],
        temporal_grads[3],
        temporal_bias_grads[3],
        modulate_grads[1],
        temporal_bias_grads[4],
    )


def solution(mesh):
    placed = (
        P("dp", "sp", None, None),
        P(),
        P("dp", None),
        P("dp", "sp"),
        P("dp"),
        P("dp", "sp"),
        P("dp"),
        P("dp", "sp"),
        P("dp"),
        P("dp", "sp"),
        P("dp"),
        P("dp", "sp"),
        P("dp"),
        P("dp", "sp"),
        P("dp"),
        P("dp", "sp"),
        P("dp"),
        P("dp", "sp"),
        P("dp"),
        P("dp", "sp"),
        P("dp"),
        P("dp", "sp"),
        P("dp"),
        P("dp", "sp", None, None),
    )
    return jax.shard_map(
        shards,
        mesh=mesh,
        in_specs=placed,
        out_specs=(
            P("dp", "sp", None, None),
            P("dp", "sp", None, None),
            P("dp", "sp"),
            P("dp"),
            P("dp", "sp"),
            P("dp"),
            P("dp", "sp"),
            P("dp"),
            P("dp", "sp"),
            P("dp"),
            P("dp", "sp"),
            P("dp"),
            P("dp", "sp"),
            P("dp"),
            P("dp", "sp"),
            P("dp"),
            P("dp", "sp"),
            P("dp"),
            P("dp", "sp"),
            P("dp"),
            P("dp", "sp"),
            P("dp"),
        ),
        check_vma=False,
    )
```

```python
import functools
import math

import jax
import jax.numpy as jnp
from jax import lax
from jax.experimental import pallas as pl
from jax.experimental.pallas import tpu as pltpu
from jax.sharding import PartitionSpec as P

D = 1152
H = 16
HD = 72


EPSILON = 1e-06
HIGHEST_PRECISION = lax.Precision.HIGHEST
SPATIAL_FORMS = ("sabhe,sache->sahbc", "sahbc,sache->sabhe", "sahbc,sabhe->sache")
TEMPORAL_FORMS = ("sabhe,scbhe->sbhac", "sbhac,scbhe->sabhe", "sbhac,sabhe->scbhe")


MESH = pl.DeviceIdType.MESH
CHUNKS = (
    ("p", 0, 144, "zxy"),
    ("p", 144, 144, "zyx"),
    ("s", 0, 48, "xyz"),
    ("s", 48, 48, "yxz"),
    ("s", 96, 48, "zxy"),
)


class Place:
    def __init__(self):
        d, s = lax.axis_index("dp"), lax.axis_index("sp")
        self.x, self.c = d // 2, d % 2
        self.z, self.y = s // 2, s % 2


def dev(x, c, z, y):
    return (x * 2 + c, z * 2 + y)


def guarded(cond, f):
    if cond is None:
        f()
    else:
        pl.when(cond)(f)


def gather_kernel(chunks, p_in, s_in, p_out, s_out, rsem, osem, ssem, lsem):
    me = Place()
    x, c, z, y = me.x, me.c, me.z, me.y

    barrier = pltpu.get_barrier_semaphore()
    peers = [(1 - x, c, z, y), (x, c, z, 1 - y), (x, 1 - c, z, y)]
    for peer in peers:
        pl.semaphore_signal(barrier, inc=1, device_id=dev(*peer), device_id_type=MESH)
    for step in (1, -1):
        @pl.when((z + step >= 0) & (z + step <= 3))
        def _():
            pl.semaphore_signal(barrier, inc=1, device_id=dev(x, c, z + step, y), device_id_type=MESH)
    pl.semaphore_wait(barrier, 3 + jnp.where((z > 0) & (z < 3), 2, 1))

    def dst(ch, bx, bc, bz, by):
        which, r0, n, _ = ch
        d, s = bx * 2 + bc, bz * 2 + by
        if which == "p":
            return p_out.at[s, pl.ds(d * 288 + r0, n), :]
        return s_out.at[d, pl.ds(s * 144 + r0, n), :]

    def src_own(ch):
        which, r0, n, _ = ch
        return (p_in if which == "p" else s_in).at[pl.ds(r0, n), :]

    sends = []

    def blk(bx, bz, by):
        return (bx * 4 + bz) * 2 + by

    def copy_to(k, ch, own, b, target, direction):
        bx, bz, by = b
        src = src_own(ch) if own else dst(ch, bx, c, bz, by)
        if direction == "c":
            sem = osem.at[k, blk(bx, bz, by)]
        else:
            sem = rsem.at[k, blk(bx, bz, by)]
        didx = {"x": 0, "y": 1, "u": 2, "d": 3, "c": 4}[direction]
        return pltpu.make_async_remote_copy(
            src_ref=src, dst_ref=dst(ch, bx, c, bz, by),
            send_sem=ssem.at[k, didx, blk(bx, bz, by)], recv_sem=sem,
            device_id=dev(*target), device_id_type=MESH)

    def place_of(rel):
        rx, ry, dz = rel
        return (1 - x if rx else x, z + dz, 1 - y if ry else y)

    def forward(k, ch, rel):
        rx, ry, dz = rel
        order = ch[3]
        own = rel == (0, 0, 0)
        b = place_of(rel)
        nz = {"x": rx, "y": ry, "z": dz}
        last = max([i for i in range(3) if nz[order[i]]], default=-1)
        for i in range(3):
            dim = order[i]
            if i > last:
                if dim == "x":
                    start(k, ch, own, b, lambda: (1 - x, c, z, y), "x", lambda: None, dz, rel)
                elif dim == "y":
                    start(k, ch, own, b, lambda: (x, c, z, 1 - y), "y", lambda: None, dz, rel)
                else:
                    start(k, ch, own, b, lambda: (x, c, z + 1, y), "u", lambda: z < 3, dz, rel)
                    start(k, ch, own, b, lambda: (x, c, z - 1, y), "d", lambda: z > 0, dz, rel)
            elif i == last and dim == "z":
                if dz < 0:
                    start(k, ch, own, b, lambda: (x, c, z + 1, y), "u", lambda: z < 3, dz, rel)
                else:
                    start(k, ch, own, b, lambda: (x, c, z - 1, y), "d", lambda: z > 0, dz, rel)
        start(k, ch, own, b, lambda: (x, 1 - c, z, y), "c", lambda: None, dz, rel)

    def start(k, ch, own, b, target, direction, cond, dz, rel):
        guarded(cond(), lambda: copy_to(k, ch, own, b, target(), direction).start())
        def again(rel=rel):
            copy_to(k, ch, own, place_of(rel), target(), direction).wait_send()
        sends.append((cond, dz, again))

    def exists(dz):
        return None if dz == 0 else ((z + dz >= 0) & (z + dz <= 3))

    rels = [(0, 0, 0)]
    for h in (0, 1, 2, 3):
        for rx, ry in ((0, 0), (1, 0), (0, 1), (1, 1)):
            for dz in ((0,) if h == 0 else (h, -h)):
                if (rx, ry, dz) != (0, 0, 0):
                    rels.append((rx, ry, dz))
    def hops(r): return (abs(r[2]) + r[0] + r[1])
    rels = [rels[0]] + sorted(rels[1:], key=hops)

    local = []
    for k, ch in enumerate(chunks):
        cp = pltpu.make_async_copy(src_own(ch), dst(ch, x, c, z, y), lsem.at[k])
        cp.start()
        local.append(cp)
    for rel in rels:
        cond = exists(rel[2])
        def body():
            for k, ch in enumerate(chunks):
                rx, ry, dz = rel
                b = place_of(rel)
                if rel != (0, 0, 0):
                    pltpu.make_async_copy(src_own(ch), dst(ch, b[0], c, b[1], b[2]), rsem.at[k, blk(*b)]).wait()
                forward(k, ch, rel)
        guarded(cond, body)
    for cp in local:
        cp.wait()
    for rel in rels:
        def body():
            rx, ry, dz = rel
            b = place_of(rel)
            for k, ch in enumerate(chunks):
                pltpu.make_async_copy(src_own(ch), dst(ch, b[0], 1 - c, b[1], b[2]), osem.at[k, blk(*b)]).wait()
        guarded(exists(rel[2]), body)
    for cond, dz, again in sends:
        ex, co = exists(dz), cond()
        full = co if ex is None else (ex if co is None else (co & ex))
        guarded(full, again)


def gather(p, s, collective_id):
    chunks = CHUNKS
    nk = len(chunks)
    return pl.pallas_call(
        functools.partial(gather_kernel, chunks),
        out_shape=(jax.ShapeDtypeStruct((8, 1152, 1152), jnp.bfloat16), jax.ShapeDtypeStruct((4, 1152, 1152), jnp.bfloat16)),
        in_specs=[pl.BlockSpec(memory_space=pl.ANY)] * 2,
        out_specs=[pl.BlockSpec(memory_space=pl.ANY)] * 2,
        scratch_shapes=[
            pltpu.SemaphoreType.DMA((nk, 16)), pltpu.SemaphoreType.DMA((nk, 16)),
            pltpu.SemaphoreType.DMA((nk, 5, 16)), pltpu.SemaphoreType.DMA((nk,))],
        compiler_params=pltpu.CompilerParams(collective_id=collective_id, has_side_effects=True),
    )(p, s)


RELS = sorted([(rx, ry, dz) for rx in (0, 1) for ry in (0, 1) for dz in range(-3, 4)], key=lambda r: (r[0] + r[1] + abs(r[2]), r != (0, 0, 0)))


def links(rel, order):
    rx, ry, dz = rel
    nz = {"x": rx, "y": ry, "z": dz}
    last = max([i for i in range(3) if nz[order[i]]], default=-1)
    out = []
    for i in range(3):
        dim = order[i]
        if i > last:
            out += ["u", "d"] if dim == "z" else [dim]
        elif i == last and dim == "z":
            out += ["u"] if dz < 0 else ["d"]
    parent = None
    if last >= 0:
        dim = order[last]
        parent = dim if dim != "z" else ("d" if dz < 0 else "u")
    return out, parent


def slots_of(order):
    size, count = {}, 1
    for dim in order:
        size[dim] = count * (5 if dim == "z" else 1)
        count *= 4 if dim == "z" else 2
    base, total = {}, 0
    for dim in order:
        base[dim] = total
        total += size[dim]
    return base, total


def scatter_kernel(chunks, rowbase, p_in, s_in, p_out, s_out, acc, core, got, lsem, csem, dsem, rsem, ssem):
    me = Place()
    x, c, z, y = me.x, me.c, me.z, me.y
    barrier = pltpu.get_barrier_semaphore()
    for peer in [(1 - x, c, z, y), (x, c, z, 1 - y), (x, 1 - c, z, y)]:
        pl.semaphore_signal(barrier, inc=1, device_id=dev(*peer), device_id_type=MESH)
    for step in (1, -1):
        @pl.when((z + step >= 0) & (z + step <= 3))
        def _():
            pl.semaphore_signal(barrier, inc=1, device_id=dev(x, c, z + step, y), device_id_type=MESH)
    pl.semaphore_wait(barrier, 3 + jnp.where((z > 0) & (z < 3), 2, 1))

    def place_of(rel):
        rx, ry, dz = rel
        return (1 - x if rx else x, z + dz, 1 - y if ry else y)

    def blk(bx, bz, by):
        return (bx * 4 + bz) * 2 + by

    def term(ch, bx, bc, bz, by):
        which, r0, n, _ = ch
        d, s = bx * 2 + bc, bz * 2 + by
        if which == "p":
            return p_in.at[s, pl.ds(d * 288 + r0, n), :]
        return s_in.at[d, pl.ds(s * 144 + r0, n), :]

    def held(ref, k, ch, b):
        return ref.at[blk(*b), pl.ds(rowbase[k][0], ch[2]), :]

    def exists(dz):
        return None if dz == 0 else ((z + dz >= 0) & (z + dz <= 3))

    def load(k, ch, b):
        return pltpu.make_async_copy(term(ch, b[0], c, b[1], b[2]), held(acc, k, ch, b), lsem.at[k, blk(*b)])

    def cross(k, ch, b):
        return pltpu.make_async_remote_copy(
            src_ref=term(ch, b[0], 1 - c, b[1], b[2]), dst_ref=held(core, k, ch, b),
            send_sem=dsem.at[k, blk(*b)], recv_sem=csem.at[k, blk(*b)],
            device_id=dev(x, 1 - c, z, y), device_id_type=MESH)

    rels = RELS[::-1]
    for rel in rels:
        def body():
            b = place_of(rel)
            for k, ch in enumerate(chunks):
                load(k, ch, b).start()
                cross(k, ch, b).start()
        guarded(exists(rel[2]), body)

    def slot(k, ch, b, direction, at):
        order = ch[3]
        base, _ = slots_of(order)
        dim = "z" if direction in "ud" else direction
        coord = {"x": (b[0], 2), "y": (b[2], 2), "z": (b[1], 4)}
        index = 0
        for d in order[:order.index(dim)]:
            index = index * coord[d][1] + coord[d][0]
        if dim == "z":
            inner = b[1] if direction == "d" else jnp.where(b[1] == at[1], 4, b[1])
            index = index * 5 + inner
        return base[dim] + index

    def got_at(k, ch, j):
        return got.at[pl.ds(pl.multiple_of(rowbase[k][1] + j * ch[2], 16), ch[2]), :]

    def target_of(direction):
        return {"x": (1 - x, c, z, y), "y": (x, c, z, 1 - y), "u": (x, c, z + 1, y), "d": (x, c, z - 1, y)}[direction]

    back = {"x": "x", "y": "y", "u": "d", "d": "u"}

    def send(k, ch, b, direction):
        tx, tc, tz, ty = target_of(direction)
        j = slot(k, ch, b, back[direction], (tx, tz, ty))
        return pltpu.make_async_remote_copy(
            src_ref=held(acc, k, ch, b), dst_ref=got_at(k, ch, j),
            send_sem=ssem.at[k, blk(*b)], recv_sem=rsem.at[k, j],
            device_id=dev(tx, tc, tz, ty), device_id_type=MESH)

    def add_rows(k, ch, b, j_list, final):
        n = ch[2]
        i = blk(*b)
        @pl.loop(0, n // 16)
        def _(t):
            r = pl.multiple_of(rowbase[k][0] + t * 16, 16)
            v = acc[i, pl.ds(r, 16), :].astype(jnp.float32) + core[i, pl.ds(r, 16), :].astype(jnp.float32)
            for cond, j in j_list:
                q = got[pl.ds(pl.multiple_of(rowbase[k][1] + j * n + t * 16, 16), 16), :].astype(jnp.float32)
                v = v + (q if cond is None else jnp.where(cond, q, 0.0))
            if final is None:
                acc[i, pl.ds(r, 16), :] = v.astype(jnp.bfloat16)
            else:
                final[pl.ds(pl.multiple_of(ch[1] + t * 16, 16), 16), :] = v

    for rel in rels:
        def body():
            b = place_of(rel)
            for k, ch in enumerate(chunks):
                children, parent = links(rel, ch[3])
                load(k, ch, b).wait()
                pltpu.make_async_copy(held(core, k, ch, b), held(core, k, ch, b), csem.at[k, blk(*b)]).wait()
                js = []
                for direction in children:
                    cond = {"u": z < 3, "d": z > 0}.get(direction)
                    j = slot(k, ch, b, direction, (x, z, y))
                    def wait():
                        pltpu.make_async_copy(got_at(k, ch, j), got_at(k, ch, j), rsem.at[k, j]).wait()
                    guarded(cond, wait)
                    js.append((cond, j))
                final = None if parent else (p_out if ch[0] == "p" else s_out)
                add_rows(k, ch, b, js, final)
                if parent:
                    send(k, ch, b, parent).start()
        guarded(exists(rel[2]), body)
    for rel in rels:
        def body():
            b = place_of(rel)
            for k, ch in enumerate(chunks):
                _, parent = links(rel, ch[3])
                if parent:
                    send(k, ch, b, parent).wait_send()
                cross(k, ch, b).wait_send()
        guarded(exists(rel[2]), body)


def scatter(p, s, collective_id):
    chunks = CHUNKS
    nk = len(chunks)
    rowbase, total, most = [], 0, 0
    at = {"p": 0, "s": 288}
    for ch in chunks:
        _, count = slots_of(ch[3])
        rowbase.append((at[ch[0]] + ch[1], total))
        total += count * ch[2]
        most = max(most, count)
    return pl.pallas_call(
        functools.partial(scatter_kernel, chunks, rowbase),
        out_shape=(jax.ShapeDtypeStruct((288, 1152), jnp.float32), jax.ShapeDtypeStruct((144, 1152), jnp.float32)),
        in_specs=[pl.BlockSpec(memory_space=pl.ANY)] * 2,
        out_specs=[pl.BlockSpec(memory_space=pltpu.VMEM)] * 2,
        scratch_shapes=[
            pltpu.VMEM((16, 432, 1152), jnp.bfloat16), pltpu.VMEM((16, 432, 1152), jnp.bfloat16),
            pltpu.VMEM((total, 1152), jnp.bfloat16),
            pltpu.SemaphoreType.DMA((nk, 16)), pltpu.SemaphoreType.DMA((nk, 16)), pltpu.SemaphoreType.DMA((nk, 16)),
            pltpu.SemaphoreType.DMA((nk, most)), pltpu.SemaphoreType.DMA((nk, 16))],
        compiler_params=pltpu.CompilerParams(collective_id=collective_id, has_side_effects=True, vmem_limit_bytes=60 << 20),
    )(p, s)


def sinusoid(timesteps):
    half_width = D // 2
    frequencies = jnp.exp(
        -math.log(10000.0) * jnp.arange(half_width, dtype=jnp.float32) / half_width
    )
    angles = timesteps.astype(jnp.float32)[:, None] * frequencies[None, :]
    return jnp.concatenate([jnp.cos(angles), jnp.sin(angles)], axis=1)


def layer_norm(tensor):
    centered = tensor - jnp.mean(tensor, axis=-1, keepdims=True)
    return centered * lax.rsqrt(jnp.mean(centered * centered, axis=-1, keepdims=True) + EPSILON)


def modulate(tensor, shift_part, scale_part):
    return layer_norm(tensor) * (1.0 + scale_part) + shift_part


def matmul(left_side, right_side):
    return jnp.dot(left_side, right_side, preferred_element_type=jnp.float32)


def back_matmul(gradient, matrix):
    return lax.dot_general(
        gradient,
        matrix,
        (((gradient.ndim - 1,), (1,)), ((), ())),
        preferred_element_type=jnp.float32,
    )


def outer_product(left_side, right_side):
    flat_left = left_side.reshape(-1, left_side.shape[-1])
    flat_right = right_side.reshape(-1, right_side.shape[-1])
    return lax.dot_general(
        flat_left, flat_right, (((0,), (0,)), ((), ())), preferred_element_type=jnp.float32
    )


def column_totals(tensor):
    return jnp.sum(tensor.astype(jnp.float32).reshape(-1, tensor.shape[-1]), axis=0)


def per_sequence(tensor):
    return jnp.sum(tensor, axis=(1, 2))


def over_data(core, biases):
    attend_in, attend_out, expand, shrink = core
    attend_bias, out_bias, expand_bias, shrink_bias, modulate_bias = biases
    gathered = (
        lax.all_gather(attend_in, "dp", axis=0, tiled=True),
        lax.all_gather(attend_out, "dp", axis=0, tiled=True),
        lax.all_gather(expand, "dp", axis=0, tiled=True),
        lax.all_gather(shrink, "dp", axis=0, tiled=True),
        lax.all_gather(attend_bias, "dp", axis=0, tiled=True),
        lax.all_gather(out_bias, "dp", axis=0, tiled=True),
        lax.all_gather(expand_bias, "dp", axis=0, tiled=True),
        lax.all_gather(shrink_bias, "dp", axis=0, tiled=True),
        lax.all_gather(modulate_bias, "dp", axis=0, tiled=True),
    )
    return (gathered[:4], gathered[4:])


def over_frames(core):
    attend_in, attend_out, expand, shrink = core
    gathered = (
        lax.all_gather(attend_in, "sp", axis=1, tiled=True),
        lax.all_gather(attend_out, "sp", axis=1, tiled=True),
        lax.all_gather(expand, "sp", axis=1, tiled=True),
        lax.all_gather(shrink, "sp", axis=1, tiled=True),
    )
    return gathered


def collect(core, biases, fast, collective_id):
    if fast:
        return collect_packed(core, biases, collective_id)
    core_rows, biases_full = over_data(core, biases)
    core_full = over_frames(core_rows)
    return (core_full, biases_full)


def fits(mesh):
    return mesh.shape["dp"] == 4 and mesh.shape["sp"] == 8


def collect_packed(core, biases, collective_id):
    attend_in, attend_out, expand, shrink = core
    packed = jnp.concatenate([attend_in, attend_out, expand], axis=1)
    slabs, across = gather(packed, shrink.T, collective_id)
    rows = slabs.transpose(1, 0, 2)
    full = (
        rows[:, :, :432].reshape(D, 3 * D),
        rows[:, :, 432:576].reshape(D, D),
        rows[:, :, 576:].reshape(D, 4 * D),
        across.transpose(0, 2, 1).reshape(4 * D, D),
    )
    biases_full = tuple(lax.all_gather(bias, "dp", axis=0, tiled=True) for bias in biases)
    return (full, biases_full)


def sum_packed(terms, collective_id):
    attend_in, attend_out, expand, shrink = [term.astype(jnp.bfloat16) for term in terms]
    slabs = jnp.concatenate(
        [attend_in.reshape(D, 8, 432), attend_out.reshape(D, 8, 144), expand.reshape(D, 8, 576)],
        axis=2,
    ).transpose(1, 0, 2)
    across = shrink.reshape(4, D, D).transpose(0, 2, 1)
    packed, turned = scatter(slabs, across, collective_id)
    return (packed[:, :432], packed[:, 432:576], packed[:, 576:], turned.T)


def own_rows(condition_all, rows):
    return lax.dynamic_slice_in_dim(condition_all, lax.axis_index("dp") * rows, rows, 1)


def modulation_of(condition_all, modulate_weights):
    rows = modulate_weights[0].shape[0]
    own = own_rows(condition_all, rows)
    partial_terms = jnp.stack([matmul(own, weight) for weight in modulate_weights], axis=1)
    summed = lax.psum_scatter(partial_terms, "dp", scatter_dimension=0, tiled=True)
    full = lax.all_gather(summed, "sp", axis=2, tiled=True)
    return [full[:, slot] for slot in range(len(modulate_weights))]


def sum_over_frames(terms):
    attend_in, attend_out, expand, shrink = terms
    return (
        lax.psum_scatter(
            attend_in.astype(jnp.bfloat16), "sp", scatter_dimension=1, tiled=True
        ).astype(jnp.float32),
        lax.psum_scatter(
            attend_out.astype(jnp.bfloat16), "sp", scatter_dimension=1, tiled=True
        ).astype(jnp.float32),
        lax.psum_scatter(expand.astype(jnp.bfloat16), "sp", scatter_dimension=1, tiled=True).astype(
            jnp.float32
        ),
        lax.psum_scatter(shrink.astype(jnp.bfloat16), "sp", scatter_dimension=1, tiled=True).astype(
            jnp.float32
        ),
    )


def sum_over_data(terms):
    attend_in, attend_out, expand, shrink = terms
    return (
        lax.psum_scatter(
            attend_in.astype(jnp.bfloat16), "dp", scatter_dimension=0, tiled=True
        ).astype(jnp.float32),
        lax.psum_scatter(
            attend_out.astype(jnp.bfloat16), "dp", scatter_dimension=0, tiled=True
        ).astype(jnp.float32),
        lax.psum_scatter(expand.astype(jnp.bfloat16), "dp", scatter_dimension=0, tiled=True).astype(
            jnp.float32
        ),
        lax.psum_scatter(shrink.astype(jnp.bfloat16), "dp", scatter_dimension=0, tiled=True).astype(
            jnp.float32
        ),
    )


def modulate_gradients(condition_all, back_modulations, rows):
    joined = jnp.stack(back_modulations, axis=1)
    columns = lax.psum_scatter(joined, "sp", scatter_dimension=2, tiled=True)
    every = lax.all_gather(columns, "dp", axis=0, tiled=True)
    own = own_rows(condition_all, rows).astype(jnp.float32)
    return [
        jnp.dot(own.T, every[:, slot], precision=HIGHEST_PRECISION)
        for slot in range(len(back_modulations))
    ]


def finish(core_terms, bias_terms, fast, collective_id):
    if fast:
        matrix_grads = sum_packed(core_terms, collective_id)
    else:
        matrix_grads = sum_over_data(sum_over_frames(core_terms))
    attend_bias, out_bias, expand_bias, shrink_bias, modulate_bias = bias_terms
    totals = lax.psum(
        (attend_bias, out_bias, expand_bias, shrink_bias, modulate_bias), ("dp", "sp")
    )
    data_index = lax.axis_index("dp")
    data_count = lax.axis_size("dp")
    bias_grads = tuple(
        (
            lax.dynamic_slice_in_dim(
                total_bias,
                data_index * (total_bias.shape[0] // data_count),
                total_bias.shape[0] // data_count,
            )
            for total_bias in totals
        )
    )
    return (matrix_grads, bias_grads)


def frames_to_patches(tensor):
    return lax.all_to_all(tensor, "sp", split_axis=2, concat_axis=1, tiled=True)


def patches_to_frames(tensor):
    return lax.all_to_all(tensor, "sp", split_axis=1, concat_axis=2, tiled=True)


def attention_scores(queries, key_rows, forms, allowed):
    scores = jnp.einsum(forms[0], queries, key_rows, preferred_element_type=jnp.float32) * HD ** (
        -0.5
    )
    if allowed is not None:
        scores = jnp.where(allowed, scores, -1e30)
    return scores


def block_forward(stream, modulation, core, biases, forms, allowed):
    attend_in, attend_out, expand, shrink = core
    attend_bias, out_bias, expand_bias, shrink_bias, modulate_bias = biases
    model_width = stream.shape[-1]
    pieces = [
        modulation[:, None, None, slot * model_width : (slot + 1) * model_width]
        for slot in range(6)
    ]
    normed = modulate(stream, pieces[0], pieces[1]).astype(jnp.bfloat16)
    bias_float = attend_bias.astype(jnp.float32)
    joined_bias = jnp.concatenate(
        [bias_float[:model_width], jnp.zeros((model_width,), jnp.float32), bias_float[model_width:]]
    )
    projected = (matmul(normed, attend_in) + joined_bias).astype(jnp.bfloat16)
    head_shape = projected.shape[:3] + (H, HD)
    queries = projected[..., :model_width].reshape(head_shape)
    key_rows = projected[..., model_width : 2 * model_width].reshape(head_shape)
    values = projected[..., 2 * model_width :].reshape(head_shape)
    scores = attention_scores(queries, key_rows, forms, allowed)
    highest = jnp.max(scores, axis=-1, keepdims=True)
    exponent = jnp.exp(scores - highest)
    denominator = jnp.sum(exponent, axis=-1, keepdims=True)
    softmax_probs = exponent / denominator
    logsum = highest + jnp.log(denominator)
    mixture = (
        jnp.einsum(
            forms[1], softmax_probs.astype(jnp.bfloat16), values, preferred_element_type=jnp.float32
        )
        .astype(jnp.bfloat16)
        .reshape(stream.shape)
    )
    attended = matmul(mixture, attend_out) + out_bias.astype(jnp.float32)
    middle = stream + pieces[2] * attended
    normed_second = modulate(middle, pieces[3], pieces[4]).astype(jnp.bfloat16)
    hidden = matmul(normed_second, expand) + expand_bias.astype(jnp.float32)
    activated = jax.nn.gelu(hidden, approximate=True).astype(jnp.bfloat16)
    branch = matmul(activated, shrink) + shrink_bias.astype(jnp.float32)
    result = middle + pieces[5] * branch
    kept = (
        pieces,
        normed,
        queries,
        key_rows,
        values,
        logsum,
        mixture,
        attended,
        middle,
        normed_second,
        hidden,
        activated,
        branch,
    )
    return (result, kept)


def block_backward(incoming, stream, core, forms, allowed, kept):
    attend_in, attend_out, expand, shrink = core
    (
        pieces,
        normed,
        queries,
        key_rows,
        values,
        logsum,
        mixture,
        attended,
        middle,
        normed_second,
        hidden,
        activated,
        branch,
    ) = kept
    model_width = stream.shape[-1]
    sequences = stream.shape[0]
    back_branch = (pieces[5] * incoming).astype(jnp.bfloat16)
    back_gate_second = per_sequence(incoming * branch)
    shrink_term = outer_product(activated, back_branch)
    shrink_bias_term = column_totals(back_branch)
    back_activated = back_matmul(back_branch, shrink)
    _, gelu_pull = jax.vjp(lambda tensor: jax.nn.gelu(tensor, approximate=True), hidden)
    back_hidden = gelu_pull(back_activated)[0].astype(jnp.bfloat16)
    expand_term = outer_product(normed_second, back_hidden)
    expand_bias_term = column_totals(back_hidden)
    back_normed_second = back_matmul(back_hidden, expand)
    _, second_pull = jax.vjp(modulate, middle, pieces[3], pieces[4])
    back_middle, back_shift_second, back_scale_second = second_pull(back_normed_second)
    back_middle = back_middle + incoming
    back_attended = (pieces[2] * back_middle).astype(jnp.bfloat16)
    back_gate_first = per_sequence(back_middle * attended)
    out_term = outer_product(mixture, back_attended)
    out_bias_term = column_totals(back_attended)
    back_mixture = (
        back_matmul(back_attended, attend_out).astype(jnp.bfloat16).reshape(queries.shape)
    )
    scores = attention_scores(queries, key_rows, forms, allowed)
    softmax_probs = jnp.exp(scores - logsum)
    back_probs = jnp.einsum(forms[0], back_mixture, values, preferred_element_type=jnp.float32)
    back_values = jnp.einsum(
        forms[2],
        softmax_probs.astype(jnp.bfloat16),
        back_mixture,
        preferred_element_type=jnp.float32,
    )
    row_delta = jnp.sum(softmax_probs * back_probs, axis=-1, keepdims=True)
    back_scores = (softmax_probs * (back_probs - row_delta)).astype(jnp.bfloat16)
    score_scale = HD ** (-0.5)
    back_queries = (
        jnp.einsum(forms[1], back_scores, key_rows, preferred_element_type=jnp.float32)
        * score_scale
    )
    back_keys = (
        jnp.einsum(forms[2], back_scores, queries, preferred_element_type=jnp.float32) * score_scale
    )
    flat_shape = stream.shape
    back_projected = jnp.concatenate(
        [
            back_queries.reshape(flat_shape),
            back_keys.reshape(flat_shape),
            back_values.reshape(flat_shape),
        ],
        axis=-1,
    ).astype(jnp.bfloat16)
    attend_in_term = outer_product(normed, back_projected)
    projected_totals = column_totals(back_projected)
    attend_bias_term = jnp.concatenate(
        [projected_totals[:model_width], projected_totals[2 * model_width :]]
    )
    back_normed = back_matmul(back_projected, attend_in)
    _, first_pull = jax.vjp(modulate, stream, pieces[0], pieces[1])
    back_stream, back_shift_first, back_scale_first = first_pull(back_normed)
    back_stream = back_stream + back_middle
    back_modulation = jnp.concatenate(
        [
            back_shift_first.reshape(sequences, model_width),
            back_scale_first.reshape(sequences, model_width),
            back_gate_first,
            back_shift_second.reshape(sequences, model_width),
            back_scale_second.reshape(sequences, model_width),
            back_gate_second,
        ],
        axis=1,
    )
    modulate_bias_term = jnp.sum(back_modulation, axis=0)
    core_terms = (attend_in_term, out_term, expand_term, shrink_term)
    bias_terms = (
        attend_bias_term,
        out_bias_term,
        expand_bias_term,
        shrink_bias_term,
        modulate_bias_term,
    )
    return (back_stream, core_terms, back_modulation, bias_terms)


def shards(
    fast,
    inputs,
    timesteps,
    segment_ids,
    spatial_attend_in,
    spatial_attend_bias,
    spatial_attend_out,
    spatial_out_bias,
    spatial_expand,
    spatial_expand_bias,
    spatial_shrink,
    spatial_shrink_bias,
    spatial_modulate,
    spatial_modulate_bias,
    temporal_attend_in,
    temporal_attend_bias,
    temporal_attend_out,
    temporal_out_bias,
    temporal_expand,
    temporal_expand_bias,
    temporal_shrink,
    temporal_shrink_bias,
    temporal_modulate,
    temporal_modulate_bias,
    cotangent,
):
    condition_all = jax.nn.silu(sinusoid(timesteps)).astype(jnp.bfloat16)
    allowed = (segment_ids[:, :, None] == segment_ids[:, None, :])[:, None, None, :, :]
    spatial_core = (spatial_attend_in, spatial_attend_out, spatial_expand, spatial_shrink)
    spatial_biases = (
        spatial_attend_bias,
        spatial_out_bias,
        spatial_expand_bias,
        spatial_shrink_bias,
        spatial_modulate_bias,
    )
    temporal_core = (temporal_attend_in, temporal_attend_out, temporal_expand, temporal_shrink)
    temporal_biases = (
        temporal_attend_bias,
        temporal_out_bias,
        temporal_expand_bias,
        temporal_shrink_bias,
        temporal_modulate_bias,
    )
    stream = inputs.astype(jnp.float32)
    modulations = modulation_of(condition_all, (spatial_modulate, temporal_modulate))
    core, biases = collect(spatial_core, spatial_biases, fast, 0)
    modulation = modulations[0] + biases[4].astype(jnp.float32)
    spatial_core = core
    spatial_out, spatial_kept = block_forward(stream, modulation, core, biases, SPATIAL_FORMS, None)
    passed = frames_to_patches(spatial_out.astype(jnp.bfloat16)).astype(jnp.float32)
    core, biases = collect(temporal_core, temporal_biases, fast, 1)
    modulation = modulations[1] + biases[4].astype(jnp.float32)
    temporal_out, temporal_kept = block_forward(
        passed, modulation, core, biases, TEMPORAL_FORMS, allowed
    )
    output = patches_to_frames(temporal_out.astype(jnp.bfloat16))
    incoming = frames_to_patches(cotangent).astype(jnp.float32)
    back_passed, core_terms, back_temporal, bias_terms = block_backward(
        incoming, passed, core, TEMPORAL_FORMS, allowed, temporal_kept
    )
    temporal_grads, temporal_bias_grads = finish(core_terms, bias_terms, fast, 2)
    back_spatial = patches_to_frames(back_passed.astype(jnp.bfloat16)).astype(jnp.float32)
    back_inputs, core_terms, back_spatial_modulation, bias_terms = block_backward(
        back_spatial, stream, spatial_core, SPATIAL_FORMS, None, spatial_kept
    )
    spatial_grads, spatial_bias_grads = finish(core_terms, bias_terms, fast, 3)
    modulate_grads = modulate_gradients(
        condition_all, (back_spatial_modulation, back_temporal), spatial_modulate.shape[0]
    )
    return (
        output,
        back_inputs.astype(jnp.bfloat16),
        spatial_grads[0],
        spatial_bias_grads[0],
        spatial_grads[1],
        spatial_bias_grads[1],
        spatial_grads[2],
        spatial_bias_grads[2],
        spatial_grads[3],
        spatial_bias_grads[3],
        modulate_grads[0],
        spatial_bias_grads[4],
        temporal_grads[0],
        temporal_bias_grads[0],
        temporal_grads[1],
        temporal_bias_grads[1],
        temporal_grads[2],
        temporal_bias_grads[2],
        temporal_grads[3],
        temporal_bias_grads[3],
        modulate_grads[1],
        temporal_bias_grads[4],
    )


def solution(mesh):
    placed = (
        P("dp", "sp", None, None),
        P(),
        P("dp", None),
        P("dp", "sp"),
        P("dp"),
        P("dp", "sp"),
        P("dp"),
        P("dp", "sp"),
        P("dp"),
        P("dp", "sp"),
        P("dp"),
        P("dp", "sp"),
        P("dp"),
        P("dp", "sp"),
        P("dp"),
        P("dp", "sp"),
        P("dp"),
        P("dp", "sp"),
        P("dp"),
        P("dp", "sp"),
        P("dp"),
        P("dp", "sp"),
        P("dp"),
        P("dp", "sp", None, None),
    )
    return jax.shard_map(
        functools.partial(shards, fits(mesh)),
        mesh=mesh,
        in_specs=placed,
        out_specs=(
            P("dp", "sp", None, None),
            P("dp", "sp", None, None),
            P("dp", "sp"),
            P("dp"),
            P("dp", "sp"),
            P("dp"),
            P("dp", "sp"),
            P("dp"),
            P("dp", "sp"),
            P("dp"),
            P("dp", "sp"),
            P("dp"),
            P("dp", "sp"),
            P("dp"),
            P("dp", "sp"),
            P("dp"),
            P("dp", "sp"),
            P("dp"),
            P("dp", "sp"),
            P("dp"),
            P("dp", "sp"),
            P("dp"),
        ),
        check_vma=False,
    )
```

```python
import functools
import math

import jax
import jax.numpy as jnp
from jax import lax
from jax.experimental import pallas as pl
from jax.experimental.pallas import tpu as pltpu
from jax.sharding import PartitionSpec as P

D = 1152
H = 16
HD = 72


EPSILON = 1e-06
HIGHEST_PRECISION = lax.Precision.HIGHEST
SPATIAL_FORMS = ("sabhe,sache->sahbc", "sahbc,sache->sabhe", "sahbc,sabhe->sache")
TEMPORAL_FORMS = ("sabhe,scbhe->sbhac", "sbhac,scbhe->sabhe", "sbhac,sabhe->scbhe")


MESH = pl.DeviceIdType.MESH
CHUNKS = (
    ("p", 0, 144, "zxy"),
    ("p", 144, 144, "zyx"),
    ("s", 0, 48, "xyz"),
    ("s", 48, 48, "yxz"),
    ("s", 96, 48, "zxy"),
)


class Place:
    def __init__(self):
        d, s = lax.axis_index("dp"), lax.axis_index("sp")
        self.x, self.c = d // 2, d % 2
        self.z, self.y = s // 2, s % 2


def dev(x, c, z, y):
    return (x * 2 + c, z * 2 + y)


def guarded(cond, f):
    if cond is None:
        f()
    else:
        pl.when(cond)(f)


def gather_kernel(chunks, p_in, s_in, p_out, s_out, rsem, osem, ssem, lsem):
    me = Place()
    x, c, z, y = me.x, me.c, me.z, me.y

    barrier = pltpu.get_barrier_semaphore()
    peers = [(1 - x, c, z, y), (x, c, z, 1 - y), (x, 1 - c, z, y)]
    for peer in peers:
        pl.semaphore_signal(barrier, inc=1, device_id=dev(*peer), device_id_type=MESH)
    for step in (1, -1):
        @pl.when((z + step >= 0) & (z + step <= 3))
        def _():
            pl.semaphore_signal(barrier, inc=1, device_id=dev(x, c, z + step, y), device_id_type=MESH)
    pl.semaphore_wait(barrier, 3 + jnp.where((z > 0) & (z < 3), 2, 1))

    def dst(ch, bx, bc, bz, by):
        which, r0, n, _ = ch
        d, s = bx * 2 + bc, bz * 2 + by
        if which == "p":
            return p_out.at[s, pl.ds(d * 288 + r0, n), :]
        return s_out.at[d, pl.ds(s * 144 + r0, n), :]

    def src_own(ch):
        which, r0, n, _ = ch
        return (p_in if which == "p" else s_in).at[pl.ds(r0, n), :]

    sends = []

    def blk(bx, bz, by):
        return (bx * 4 + bz) * 2 + by

    def copy_to(k, ch, own, b, target, direction):
        bx, bz, by = b
        src = src_own(ch) if own else dst(ch, bx, c, bz, by)
        if direction == "c":
            sem = osem.at[k, blk(bx, bz, by)]
        else:
            sem = rsem.at[k, blk(bx, bz, by)]
        didx = {"x": 0, "y": 1, "u": 2, "d": 3, "c": 4}[direction]
        return pltpu.make_async_remote_copy(
            src_ref=src, dst_ref=dst(ch, bx, c, bz, by),
            send_sem=ssem.at[k, didx, blk(bx, bz, by)], recv_sem=sem,
            device_id=dev(*target), device_id_type=MESH)

    def place_of(rel):
        rx, ry, dz = rel
        return (1 - x if rx else x, z + dz, 1 - y if ry else y)

    def forward(k, ch, rel):
        rx, ry, dz = rel
        order = ch[3]
        own = rel == (0, 0, 0)
        b = place_of(rel)
        nz = {"x": rx, "y": ry, "z": dz}
        last = max([i for i in range(3) if nz[order[i]]], default=-1)
        for i in range(3):
            dim = order[i]
            if i > last:
                if dim == "x":
                    start(k, ch, own, b, lambda: (1 - x, c, z, y), "x", lambda: None, dz, rel)
                elif dim == "y":
                    start(k, ch, own, b, lambda: (x, c, z, 1 - y), "y", lambda: None, dz, rel)
                else:
                    start(k, ch, own, b, lambda: (x, c, z + 1, y), "u", lambda: z < 3, dz, rel)
                    start(k, ch, own, b, lambda: (x, c, z - 1, y), "d", lambda: z > 0, dz, rel)
            elif i == last and dim == "z":
                if dz < 0:
                    start(k, ch, own, b, lambda: (x, c, z + 1, y), "u", lambda: z < 3, dz, rel)
                else:
                    start(k, ch, own, b, lambda: (x, c, z - 1, y), "d", lambda: z > 0, dz, rel)
        start(k, ch, own, b, lambda: (x, 1 - c, z, y), "c", lambda: None, dz, rel)

    def start(k, ch, own, b, target, direction, cond, dz, rel):
        guarded(cond(), lambda: copy_to(k, ch, own, b, target(), direction).start())
        def again(rel=rel):
            copy_to(k, ch, own, place_of(rel), target(), direction).wait_send()
        sends.append((cond, dz, again))

    def exists(dz):
        return None if dz == 0 else ((z + dz >= 0) & (z + dz <= 3))

    rels = [(0, 0, 0)]
    for h in (0, 1, 2, 3):
        for rx, ry in ((0, 0), (1, 0), (0, 1), (1, 1)):
            for dz in ((0,) if h == 0 else (h, -h)):
                if (rx, ry, dz) != (0, 0, 0):
                    rels.append((rx, ry, dz))
    def hops(r): return (abs(r[2]) + r[0] + r[1])
    rels = [rels[0]] + sorted(rels[1:], key=hops)

    local = []
    for k, ch in enumerate(chunks):
        cp = pltpu.make_async_copy(src_own(ch), dst(ch, x, c, z, y), lsem.at[k])
        cp.start()
        local.append(cp)
    for rel in rels:
        cond = exists(rel[2])
        def body():
            for k, ch in enumerate(chunks):
                rx, ry, dz = rel
                b = place_of(rel)
                if rel != (0, 0, 0):
                    pltpu.make_async_copy(src_own(ch), dst(ch, b[0], c, b[1], b[2]), rsem.at[k, blk(*b)]).wait()
                forward(k, ch, rel)
        guarded(cond, body)
    for cp in local:
        cp.wait()
    for rel in rels:
        def body():
            rx, ry, dz = rel
            b = place_of(rel)
            for k, ch in enumerate(chunks):
                pltpu.make_async_copy(src_own(ch), dst(ch, b[0], 1 - c, b[1], b[2]), osem.at[k, blk(*b)]).wait()
        guarded(exists(rel[2]), body)
    for cond, dz, again in sends:
        ex, co = exists(dz), cond()
        full = co if ex is None else (ex if co is None else (co & ex))
        guarded(full, again)


def gather(p, s, collective_id):
    chunks = CHUNKS
    nk = len(chunks)
    return pl.pallas_call(
        functools.partial(gather_kernel, chunks),
        out_shape=(jax.ShapeDtypeStruct((8, 1152, 1152), jnp.bfloat16), jax.ShapeDtypeStruct((4, 1152, 1152), jnp.bfloat16)),
        in_specs=[pl.BlockSpec(memory_space=pl.ANY)] * 2,
        out_specs=[pl.BlockSpec(memory_space=pl.ANY)] * 2,
        scratch_shapes=[
            pltpu.SemaphoreType.DMA((nk, 16)), pltpu.SemaphoreType.DMA((nk, 16)),
            pltpu.SemaphoreType.DMA((nk, 5, 16)), pltpu.SemaphoreType.DMA((nk,))],
        compiler_params=pltpu.CompilerParams(collective_id=collective_id, has_side_effects=True),
    )(p, s)


RELS = sorted([(rx, ry, dz) for rx in (0, 1) for ry in (0, 1) for dz in range(-3, 4)], key=lambda r: (r[0] + r[1] + abs(r[2]), r != (0, 0, 0)))


def links(rel, order):
    rx, ry, dz = rel
    nz = {"x": rx, "y": ry, "z": dz}
    last = max([i for i in range(3) if nz[order[i]]], default=-1)
    out = []
    for i in range(3):
        dim = order[i]
        if i > last:
            out += ["u", "d"] if dim == "z" else [dim]
        elif i == last and dim == "z":
            out += ["u"] if dz < 0 else ["d"]
    parent = None
    if last >= 0:
        dim = order[last]
        parent = dim if dim != "z" else ("d" if dz < 0 else "u")
    return out, parent


def slots_of(order):
    size, count = {}, 1
    for dim in order:
        size[dim] = count * (5 if dim == "z" else 1)
        count *= 4 if dim == "z" else 2
    base, total = {}, 0
    for dim in order:
        base[dim] = total
        total += size[dim]
    return base, total


def scatter_kernel(chunks, rowbase, p_in, s_in, p_out, s_out, acc, core, got, lsem, csem, dsem, rsem, ssem):
    me = Place()
    x, c, z, y = me.x, me.c, me.z, me.y
    barrier = pltpu.get_barrier_semaphore()
    for peer in [(1 - x, c, z, y), (x, c, z, 1 - y), (x, 1 - c, z, y)]:
        pl.semaphore_signal(barrier, inc=1, device_id=dev(*peer), device_id_type=MESH)
    for step in (1, -1):
        @pl.when((z + step >= 0) & (z + step <= 3))
        def _():
            pl.semaphore_signal(barrier, inc=1, device_id=dev(x, c, z + step, y), device_id_type=MESH)
    pl.semaphore_wait(barrier, 3 + jnp.where((z > 0) & (z < 3), 2, 1))

    def place_of(rel):
        rx, ry, dz = rel
        return (1 - x if rx else x, z + dz, 1 - y if ry else y)

    def blk(bx, bz, by):
        return (bx * 4 + bz) * 2 + by

    def term(ch, bx, bc, bz, by):
        which, r0, n, _ = ch
        d, s = bx * 2 + bc, bz * 2 + by
        if which == "p":
            return p_in.at[s, pl.ds(d * 288 + r0, n), :]
        return s_in.at[d, pl.ds(s * 144 + r0, n), :]

    def held(ref, k, ch, b):
        return ref.at[blk(*b), pl.ds(rowbase[k][0], ch[2]), :]

    def exists(dz):
        return None if dz == 0 else ((z + dz >= 0) & (z + dz <= 3))

    def load(k, ch, b):
        return pltpu.make_async_copy(term(ch, b[0], c, b[1], b[2]), held(acc, k, ch, b), lsem.at[k, blk(*b)])

    def cross(k, ch, b):
        return pltpu.make_async_remote_copy(
            src_ref=term(ch, b[0], 1 - c, b[1], b[2]), dst_ref=held(core, k, ch, b),
            send_sem=dsem.at[k, blk(*b)], recv_sem=csem.at[k, blk(*b)],
            device_id=dev(x, 1 - c, z, y), device_id_type=MESH)

    rels = RELS[::-1]
    for rel in rels:
        def body():
            b = place_of(rel)
            for k, ch in enumerate(chunks):
                load(k, ch, b).start()
                cross(k, ch, b).start()
        guarded(exists(rel[2]), body)

    def slot(k, ch, b, direction, at):
        order = ch[3]
        base, _ = slots_of(order)
        dim = "z" if direction in "ud" else direction
        coord = {"x": (b[0], 2), "y": (b[2], 2), "z": (b[1], 4)}
        index = 0
        for d in order[:order.index(dim)]:
            index = index * coord[d][1] + coord[d][0]
        if dim == "z":
            inner = b[1] if direction == "d" else jnp.where(b[1] == at[1], 4, b[1])
            index = index * 5 + inner
        return base[dim] + index

    def got_at(k, ch, j):
        return got.at[pl.ds(pl.multiple_of(rowbase[k][1] + j * ch[2], 16), ch[2]), :]

    def target_of(direction):
        return {"x": (1 - x, c, z, y), "y": (x, c, z, 1 - y), "u": (x, c, z + 1, y), "d": (x, c, z - 1, y)}[direction]

    back = {"x": "x", "y": "y", "u": "d", "d": "u"}

    def send(k, ch, b, direction):
        tx, tc, tz, ty = target_of(direction)
        j = slot(k, ch, b, back[direction], (tx, tz, ty))
        return pltpu.make_async_remote_copy(
            src_ref=held(acc, k, ch, b), dst_ref=got_at(k, ch, j),
            send_sem=ssem.at[k, blk(*b)], recv_sem=rsem.at[k, j],
            device_id=dev(tx, tc, tz, ty), device_id_type=MESH)

    def add_rows(k, ch, b, j_list, final):
        n = ch[2]
        i = blk(*b)
        @pl.loop(0, n // 16)
        def _(t):
            r = pl.multiple_of(rowbase[k][0] + t * 16, 16)
            v = acc[i, pl.ds(r, 16), :].astype(jnp.float32) + core[i, pl.ds(r, 16), :].astype(jnp.float32)
            for cond, j in j_list:
                q = got[pl.ds(pl.multiple_of(rowbase[k][1] + j * n + t * 16, 16), 16), :].astype(jnp.float32)
                v = v + (q if cond is None else jnp.where(cond, q, 0.0))
            if final is None:
                acc[i, pl.ds(r, 16), :] = v.astype(jnp.bfloat16)
            else:
                final[pl.ds(pl.multiple_of(ch[1] + t * 16, 16), 16), :] = v

    for rel in rels:
        def body():
            b = place_of(rel)
            for k, ch in enumerate(chunks):
                children, parent = links(rel, ch[3])
                load(k, ch, b).wait()
                pltpu.make_async_copy(held(core, k, ch, b), held(core, k, ch, b), csem.at[k, blk(*b)]).wait()
                js = []
                for direction in children:
                    cond = {"u": z < 3, "d": z > 0}.get(direction)
                    j = slot(k, ch, b, direction, (x, z, y))
                    def wait():
                        pltpu.make_async_copy(got_at(k, ch, j), got_at(k, ch, j), rsem.at[k, j]).wait()
                    guarded(cond, wait)
                    js.append((cond, j))
                final = None if parent else (p_out if ch[0] == "p" else s_out)
                add_rows(k, ch, b, js, final)
                if parent:
                    send(k, ch, b, parent).start()
        guarded(exists(rel[2]), body)
    for rel in rels:
        def body():
            b = place_of(rel)
            for k, ch in enumerate(chunks):
                _, parent = links(rel, ch[3])
                if parent:
                    send(k, ch, b, parent).wait_send()
                cross(k, ch, b).wait_send()
        guarded(exists(rel[2]), body)


def scatter(p, s, collective_id):
    chunks = CHUNKS
    nk = len(chunks)
    rowbase, total, most = [], 0, 0
    at = {"p": 0, "s": 288}
    for ch in chunks:
        _, count = slots_of(ch[3])
        rowbase.append((at[ch[0]] + ch[1], total))
        total += count * ch[2]
        most = max(most, count)
    return pl.pallas_call(
        functools.partial(scatter_kernel, chunks, rowbase),
        out_shape=(jax.ShapeDtypeStruct((288, 1152), jnp.float32), jax.ShapeDtypeStruct((144, 1152), jnp.float32)),
        in_specs=[pl.BlockSpec(memory_space=pl.ANY)] * 2,
        out_specs=[pl.BlockSpec(memory_space=pltpu.VMEM)] * 2,
        scratch_shapes=[
            pltpu.VMEM((16, 432, 1152), jnp.bfloat16), pltpu.VMEM((16, 432, 1152), jnp.bfloat16),
            pltpu.VMEM((total, 1152), jnp.bfloat16),
            pltpu.SemaphoreType.DMA((nk, 16)), pltpu.SemaphoreType.DMA((nk, 16)), pltpu.SemaphoreType.DMA((nk, 16)),
            pltpu.SemaphoreType.DMA((nk, most)), pltpu.SemaphoreType.DMA((nk, 16))],
        compiler_params=pltpu.CompilerParams(collective_id=collective_id, has_side_effects=True, vmem_limit_bytes=60 << 20),
    )(p, s)


TOKENS = 256
WIDTH = 1152
SCALE = HD ** (-0.5)
NEGATIVE = -1e30


def dot(a, b):
    return lax.dot_general(a, b, (((1,), (0,)), ((), ())), preferred_element_type=jnp.float32)


def dot_nt(a, b):
    return lax.dot_general(a, b, (((1,), (1,)), ((), ())), preferred_element_type=jnp.float32)


def dot_tn(a, b):
    return lax.dot_general(a, b, (((0,), (0,)), ((), ())), preferred_element_type=jnp.float32)


def by_rows(body, step=32):
    @pl.loop(0, TOKENS // step)
    def _(i):
        body(pl.ds(pl.multiple_of(i * step, step), step))


def statistics(v):
    centered = v - jnp.mean(v, axis=1, keepdims=True)
    scale = lax.rsqrt(jnp.mean(centered * centered, axis=1, keepdims=True) + EPSILON)
    return centered * scale, scale


def fold(v):
    return jnp.sum(v.reshape(v.shape[0] // 8, 8, v.shape[1]), axis=0)


def gelu_both(h):
    c, a = math.sqrt(2.0 / math.pi), 0.044715
    square = h * h
    t = jnp.tanh(c * h * (1.0 + a * square))
    half = 0.5 * (1.0 + t)
    return h * half, half + 0.5 * h * (1.0 - t * t) * (c * (1.0 + 3.0 * a * square))


WIN_IN, WIN_OUT, WIN_EXP = slice(0, 512), slice(384, 640), slice(512, 1152)


def forward_pass(e, y):
    mod = e.mod
    shift1, scale1, gate1 = [lambda i=i: mod[i : i + 1, :] for i in range(3)]
    shift2, scale2, gate2 = [lambda i=i: mod[i : i + 1, :] for i in range(3, 6)]

    e.bslab[...] = jnp.zeros(e.bslab.shape, jnp.float32)
    for s in range(8):
        for row, first in ((0, 0), (1, 2 * WIDTH)):
            lo, hi = max(432 * s, first), min(432 * (s + 1), first + WIDTH)
            if lo < hi:
                e.bslab[s, 0:1, lo - 432 * s : hi - 432 * s] = e.bias[
                    row : row + 1, lo - first : hi - first
                ]

    def first(r):
        n, _ = statistics(e.x[r, :].astype(jnp.float32))
        e.normed[r, :] = (n * (1.0 + scale1()) + shift1()).astype(jnp.bfloat16)

    by_rows(first)

    @pl.loop(0, 8)
    def _(s):
        e.wait_p(s)
        v = dot(e.normed[...], e.pv[s, :, WIN_IN]) + e.bslab[s, 0:1, :]
        for j in range(6):
            e.heads[6 * s + j] = v[:, HD * j : HD * (j + 1)].astype(jnp.bfloat16)

    @pl.loop(0, H)
    def _(h):
        scores = dot_nt(e.heads[h], e.heads[H + h]) * SCALE
        if e.mask is not None:
            scores = scores + e.mask[...]
        exponent = jnp.exp(scores - jnp.max(scores, axis=1, keepdims=True))
        probs = exponent / jnp.sum(exponent, axis=1, keepdims=True)
        e.mh[h] = dot(probs.astype(jnp.bfloat16), e.heads[2 * H + h]).astype(jnp.bfloat16)

    for h in range(H):
        e.mixture[:, HD * h : HD * (h + 1)] = e.mh[h]
    for s in range(8):
        v = dot(e.mixture[...], e.pv[s, :, WIN_OUT])
        e.attended[:, 144 * s : 144 * (s + 1)] = v[:, 48:192]

    def second(r):
        attended = e.attended[r, :] + e.bias[2:3, :]
        e.attended[r, :] = attended
        middle = e.x[r, :].astype(jnp.float32) + gate1() * attended
        e.middle[r, :] = middle
        n, _ = statistics(middle)
        e.normed2[r, :] = (n * (1.0 + scale2()) + shift2()).astype(jnp.bfloat16)

    by_rows(second)
    e.branch[...] = jnp.zeros(e.branch.shape, jnp.float32)

    @pl.loop(0, 4)
    def _(d):
        for half in range(2):
            v = dot(e.normed2[...], e.pv[2 * d + half, :, WIN_EXP])
            e.tmp[:, 576 * half : 576 * (half + 1)] = v[:, 64:640]

        def activate(r):
            value, slope = gelu_both(e.tmp[r, :] + e.bias[pl.ds(4 + d, 1), :])
            e.act[d, r, :] = value.astype(jnp.bfloat16)
            if e.slope is not None:
                e.slope[d, r, :] = slope

        by_rows(activate)
        e.wait_s(d)
        e.branch[...] += dot_nt(e.act[d], e.sv[d])

    def third(r):
        branch = e.branch[r, :] + e.bias[3:4, :]
        e.branch[r, :] = branch
        if y is not None:
            y[r, :] = (e.middle[r, :] + gate2() * branch).astype(jnp.bfloat16)

    by_rows(third)


def backward_pass(e):
    mod = e.mod
    gate1, scale1 = lambda: mod[2:3, :], lambda: mod[1:2, :]
    gate2, scale2 = lambda: mod[5:6, :], lambda: mod[4:5, :]
    e.sums[...] = jnp.zeros(e.sums.shape, jnp.float32)
    e.bout[...] = jnp.zeros(e.bout.shape, jnp.bfloat16)
    for s in range(8):
        e.bexp[s, :, 0:128] = jnp.zeros((TOKENS, 128), jnp.bfloat16)
        e.bin[s, :, 384:512] = jnp.zeros((TOKENS, 128), jnp.bfloat16)

    def first(r):
        g = e.g[r, :].astype(jnp.float32)
        back = (gate2() * g).astype(jnp.bfloat16)
        e.bb[r, :] = back
        e.sums[5] += fold(g * e.branch[r, :])
        e.sums[7] += fold(back.astype(jnp.float32))

    by_rows(first)

    @pl.loop(0, 4)
    def _(d):
        e.tmp[...] = dot(e.bb[...], e.sv[d])

        def hidden(r):
            back = (e.tmp[r, :] * e.slope[d, r, :]).astype(jnp.bfloat16)
            for half in range(2):
                e.bexp[2 * d + half, r, 64:640] = back[:, 576 * half : 576 * (half + 1)]
            e.sums[8 + d] += fold(back.astype(jnp.float32))

        by_rows(hidden)

    e.tmp[...] = jnp.zeros(e.tmp.shape, jnp.float32)

    @pl.loop(0, 8)
    def _(s):
        e.tmp[...] += dot_nt(e.bexp[s], e.pv[s, :, WIN_EXP])

    def second(r):
        n, scale = statistics(e.middle[r, :])
        back_normed = e.tmp[r, :]
        e.sums[3] += fold(back_normed)
        e.sums[4] += fold(back_normed * n)
        u = back_normed * (1.0 + scale2())
        inner = jnp.mean(u, axis=1, keepdims=True) + n * jnp.mean(u * n, axis=1, keepdims=True)
        back_middle = e.g[r, :].astype(jnp.float32) + scale * (u - inner)
        e.middle[r, :] = back_middle
        e.sums[2] += fold(back_middle * e.attended[r, :])
        back = (gate1() * back_middle).astype(jnp.bfloat16)
        e.sums[6] += fold(back.astype(jnp.float32))
        for s in range(8):
            e.bout[s, r, 48:192] = back[:, 144 * s : 144 * (s + 1)]

    by_rows(second)
    e.tmp[...] = jnp.zeros(e.tmp.shape, jnp.float32)

    @pl.loop(0, 8)
    def _(s):
        e.tmp[...] += dot_nt(e.bout[s], e.pv[s, :, WIN_OUT])

    for h in range(H):
        e.mh[h] = e.tmp[:, HD * h : HD * (h + 1)].astype(jnp.bfloat16)

    @pl.loop(0, H)
    def _(h):
        q, k, v, back = e.heads[h], e.heads[H + h], e.heads[2 * H + h], e.mh[h]
        scores = dot_nt(q, k) * SCALE
        if e.mask is not None:
            scores = scores + e.mask[...]
        exponent = jnp.exp(scores - jnp.max(scores, axis=1, keepdims=True))
        probs = exponent / jnp.sum(exponent, axis=1, keepdims=True)
        back_probs = dot_nt(back, v)
        e.heads[2 * H + h] = dot_tn(probs.astype(jnp.bfloat16), back).astype(jnp.bfloat16)
        delta = jnp.sum(probs * back_probs, axis=1, keepdims=True)
        back_scores = (probs * (back_probs - delta)).astype(jnp.bfloat16)
        e.heads[h] = (dot(back_scores, k) * SCALE).astype(jnp.bfloat16)
        e.heads[H + h] = (dot_tn(back_scores, q) * SCALE).astype(jnp.bfloat16)

    e.tmp[...] = jnp.zeros(e.tmp.shape, jnp.float32)
    ones = jnp.ones((8, TOKENS), jnp.bfloat16)

    @pl.loop(0, 8)
    def _(s):
        for j in range(6):
            e.bin[s, :, HD * j : HD * (j + 1)] = e.heads[6 * s + j]
        e.bslab[s] = dot(ones, e.bin[s])
        e.tmp[...] += dot_nt(e.bin[s], e.pv[s, :, WIN_IN])

    def third(r):
        n, scale = statistics(e.x[r, :].astype(jnp.float32))
        back_normed = e.tmp[r, :]
        e.sums[0] += fold(back_normed)
        e.sums[1] += fold(back_normed * n)
        u = back_normed * (1.0 + scale1())
        inner = jnp.mean(u, axis=1, keepdims=True) + n * jnp.mean(u * n, axis=1, keepdims=True)
        e.back_x[r, :] = (e.middle[r, :] + scale * (u - inner)).astype(jnp.bfloat16)

    by_rows(third)

    for s in range(8):
        for row, first_column in ((0, 0), (1, 2 * WIDTH)):
            lo, hi = max(432 * s, first_column), min(432 * (s + 1), first_column + WIDTH)
            if lo < hi:
                e.bias_grad[row : row + 1, lo - first_column : hi - first_column] = e.bslab[
                    s, 0:1, lo - 432 * s : hi - 432 * s
                ]
    for row, slot in ((2, 6), (3, 7), (4, 8), (5, 9), (6, 10), (7, 11)):
        e.bias_grad[row : row + 1, :] = jnp.sum(e.sums[slot], axis=0, keepdims=True)
    for slot in range(6):
        e.mod_grad[slot : slot + 1, :] = jnp.sum(e.sums[slot], axis=0, keepdims=True)
    e.mod_grad[6:8, :] = jnp.zeros((2, WIDTH), jnp.float32)


class Refs:
    pass


WEIGHT_SCRATCH = (
    ("pv", (8, WIDTH, WIDTH), jnp.bfloat16),
    ("sv", (4, WIDTH, WIDTH), jnp.bfloat16),
)
FORWARD_SCRATCH = (
    ("bslab", (8, 8, 512), jnp.float32),
    ("heads", (3 * H, TOKENS, HD), jnp.bfloat16),
    ("mh", (H, TOKENS, HD), jnp.bfloat16),
    ("attended", (TOKENS, WIDTH), jnp.float32),
    ("middle", (TOKENS, WIDTH), jnp.float32),
    ("branch", (TOKENS, WIDTH), jnp.float32),
    ("tmp", (TOKENS, WIDTH), jnp.float32),
)
OPERANDS = (
    ("normed", (TOKENS, WIDTH), jnp.bfloat16),
    ("mixture", (TOKENS, WIDTH), jnp.bfloat16),
    ("normed2", (TOKENS, WIDTH), jnp.bfloat16),
    ("act", (4, TOKENS, WIDTH), jnp.bfloat16),
)
BACK_OPERANDS = (
    ("bb", (TOKENS, WIDTH), jnp.bfloat16),
    ("bin", (8, TOKENS, 512), jnp.bfloat16),
    ("bout", (8, TOKENS, 256), jnp.bfloat16),
    ("bexp", (8, TOKENS, 640), jnp.bfloat16),
)
BACKWARD_SCRATCH = (
    ("slope", (4, TOKENS, WIDTH), jnp.float32),
    ("sums", (12, 8, WIDTH), jnp.float32),
)


def load_weights(e, p_hbm, s_hbm, psem, ssem):
    def p_copy(s):
        return pltpu.make_async_copy(p_hbm.at[s], e.pv.at[s], psem.at[s])

    def s_copy(d):
        return pltpu.make_async_copy(s_hbm.at[d], e.sv.at[d], ssem.at[d])

    @pl.loop(0, 8)
    def _(s):
        p_copy(s).start()

    @pl.loop(0, 4)
    def _(d):
        s_copy(d).start()

    e.wait_p = lambda s: p_copy(s).wait()
    e.wait_s = lambda d: s_copy(d).wait()


def block_kernel(names, *refs):
    e = Refs()
    e.mask, e.slope, e.y = None, None, None
    for name, ref in zip(names, refs):
        setattr(e, name, ref)
    load_weights(e, e.p, e.s, e.psem, e.ssem)
    forward_pass(e, e.y)
    if "g" in names:
        backward_pass(e)


def block_call(x, mod, bias, p, s, mask=None, g=None, give_y=True):
    inputs = [("x", x), ("mod", mod), ("bias", bias), ("p", p), ("s", s)]
    if mask is not None:
        inputs.append(("mask", mask))
    if g is not None:
        inputs.append(("g", g))
    outs, scratch = [], list(WEIGHT_SCRATCH + FORWARD_SCRATCH)
    if give_y:
        outs.append(("y", (TOKENS, WIDTH), jnp.bfloat16))
    if g is None:
        scratch += OPERANDS
    else:
        outs += [
            ("back_x", (TOKENS, WIDTH), jnp.bfloat16),
            ("bias_grad", (8, WIDTH), jnp.float32),
            ("mod_grad", (8, WIDTH), jnp.float32),
        ]
        outs += OPERANDS + BACK_OPERANDS
        scratch += BACKWARD_SCRATCH
    names = [name for name, *_ in inputs + outs + scratch] + ["psem", "ssem"]
    any_spec, vmem = pl.BlockSpec(memory_space=pl.ANY), pl.BlockSpec(memory_space=pltpu.VMEM)
    results = pl.pallas_call(
        functools.partial(block_kernel, names),
        out_shape=[jax.ShapeDtypeStruct(shape, kind) for _, shape, kind in outs],
        in_specs=[any_spec if name in ("p", "s") else vmem for name, _ in inputs],
        out_specs=[vmem] * len(outs),
        scratch_shapes=[pltpu.VMEM(shape, kind) for _, shape, kind in scratch]
        + [pltpu.SemaphoreType.DMA((8,)), pltpu.SemaphoreType.DMA((4,))],
        compiler_params=pltpu.CompilerParams(vmem_limit_bytes=63 << 20),
        name="block_both" if g is not None else "block_forward",
    )(*[value for _, value in inputs])
    return dict(zip([name for name, *_ in outs], results))


def gradient_p_kernel(normed, mixture, normed2, b_in, b_out, b_exp, out, n_t, m_t, n2_t):
    @pl.when(pl.program_id(0) == 0)
    def _():
        n_t[...] = normed[...].T
        m_t[...] = mixture[...].T
        n2_t[...] = normed2[...].T

    @pl.loop(0, 4)
    def _(i):
        r = pl.ds(pl.multiple_of(i * 288, 16), 288)
        first = dot(n_t[r, :], b_in[0])
        second = dot(m_t[r, :], b_out[0])
        third = dot(n2_t[r, :], b_exp[0])
        out[0, r, 0:384] = first[:, 0:384].astype(jnp.bfloat16)
        out[0, r, 384:512] = (first[:, 384:] + second[:, :128]).astype(jnp.bfloat16)
        out[0, r, 512:640] = (second[:, 128:] + third[:, :128]).astype(jnp.bfloat16)
        out[0, r, 640:] = third[:, 128:].astype(jnp.bfloat16)


def gradient_s_kernel(back, act, out, back_t):
    @pl.when(pl.program_id(0) == 0)
    def _():
        back_t[...] = back[...].T

    @pl.loop(0, 4)
    def _(i):
        r = pl.ds(pl.multiple_of(i * 288, 16), 288)
        out[0, r, :] = dot(back_t[r, :], act[0]).astype(jnp.bfloat16)


def gradient_slabs(o):
    whole = pl.BlockSpec((TOKENS, WIDTH), lambda i: (0, 0))
    piece = lambda n: pl.BlockSpec((1, TOKENS, n), lambda i: (i, 0, 0))
    slab = pl.BlockSpec((1, WIDTH, WIDTH), lambda i: (i, 0, 0))
    turned = pltpu.VMEM((WIDTH, TOKENS), jnp.bfloat16)
    p = pl.pallas_call(
        gradient_p_kernel,
        grid=(8,),
        out_shape=jax.ShapeDtypeStruct((8, WIDTH, WIDTH), jnp.bfloat16),
        in_specs=[whole] * 3 + [piece(512), piece(256), piece(640)],
        out_specs=slab,
        scratch_shapes=[turned] * 3,
        compiler_params=pltpu.CompilerParams(vmem_limit_bytes=48 << 20),
    )(o["normed"], o["mixture"], o["normed2"], o["bin"], o["bout"], o["bexp"])
    s = pl.pallas_call(
        gradient_s_kernel,
        grid=(4,),
        out_shape=jax.ShapeDtypeStruct((4, WIDTH, WIDTH), jnp.bfloat16),
        in_specs=[whole, piece(WIDTH)],
        out_specs=slab,
        scratch_shapes=[turned],
        compiler_params=pltpu.CompilerParams(vmem_limit_bytes=48 << 20),
    )(o["bb"], o["act"])
    return p, s


def sinusoid(timesteps):
    half_width = D // 2
    frequencies = jnp.exp(
        -math.log(10000.0) * jnp.arange(half_width, dtype=jnp.float32) / half_width
    )
    angles = timesteps.astype(jnp.float32)[:, None] * frequencies[None, :]
    return jnp.concatenate([jnp.cos(angles), jnp.sin(angles)], axis=1)


def layer_norm(tensor):
    centered = tensor - jnp.mean(tensor, axis=-1, keepdims=True)
    return centered * lax.rsqrt(jnp.mean(centered * centered, axis=-1, keepdims=True) + EPSILON)


def modulate(tensor, shift_part, scale_part):
    return layer_norm(tensor) * (1.0 + scale_part) + shift_part


def matmul(left_side, right_side):
    return jnp.dot(left_side, right_side, preferred_element_type=jnp.float32)


def back_matmul(gradient, matrix):
    return lax.dot_general(
        gradient,
        matrix,
        (((gradient.ndim - 1,), (1,)), ((), ())),
        preferred_element_type=jnp.float32,
    )


def outer_product(left_side, right_side):
    flat_left = left_side.reshape(-1, left_side.shape[-1])
    flat_right = right_side.reshape(-1, right_side.shape[-1])
    return lax.dot_general(
        flat_left, flat_right, (((0,), (0,)), ((), ())), preferred_element_type=jnp.float32
    )


def column_totals(tensor):
    return jnp.sum(tensor.astype(jnp.float32).reshape(-1, tensor.shape[-1]), axis=0)


def per_sequence(tensor):
    return jnp.sum(tensor, axis=(1, 2))


def over_data(core, biases):
    attend_in, attend_out, expand, shrink = core
    attend_bias, out_bias, expand_bias, shrink_bias, modulate_bias = biases
    gathered = (
        lax.all_gather(attend_in, "dp", axis=0, tiled=True),
        lax.all_gather(attend_out, "dp", axis=0, tiled=True),
        lax.all_gather(expand, "dp", axis=0, tiled=True),
        lax.all_gather(shrink, "dp", axis=0, tiled=True),
        lax.all_gather(attend_bias, "dp", axis=0, tiled=True),
        lax.all_gather(out_bias, "dp", axis=0, tiled=True),
        lax.all_gather(expand_bias, "dp", axis=0, tiled=True),
        lax.all_gather(shrink_bias, "dp", axis=0, tiled=True),
        lax.all_gather(modulate_bias, "dp", axis=0, tiled=True),
    )
    return (gathered[:4], gathered[4:])


def over_frames(core):
    attend_in, attend_out, expand, shrink = core
    gathered = (
        lax.all_gather(attend_in, "sp", axis=1, tiled=True),
        lax.all_gather(attend_out, "sp", axis=1, tiled=True),
        lax.all_gather(expand, "sp", axis=1, tiled=True),
        lax.all_gather(shrink, "sp", axis=1, tiled=True),
    )
    return gathered


def collect(core, biases, fast, collective_id):
    if fast:
        return collect_packed(core, biases, collective_id)
    core_rows, biases_full = over_data(core, biases)
    core_full = over_frames(core_rows)
    return (core_full, biases_full)


def fits(mesh):
    return mesh.shape["dp"] == 4 and mesh.shape["sp"] == 8


def collect_packed(core, biases, collective_id):
    attend_in, attend_out, expand, shrink = core
    packed = jnp.concatenate([attend_in, attend_out, expand], axis=1)
    slabs, across = gather(packed, shrink.T, collective_id)
    rows = slabs.transpose(1, 0, 2)
    full = (
        rows[:, :, :432].reshape(D, 3 * D),
        rows[:, :, 432:576].reshape(D, D),
        rows[:, :, 576:].reshape(D, 4 * D),
        across.transpose(0, 2, 1).reshape(4 * D, D),
    )
    biases_full = tuple(lax.all_gather(bias, "dp", axis=0, tiled=True) for bias in biases)
    return (full, biases_full)


def sum_packed(terms, collective_id):
    attend_in, attend_out, expand, shrink = [term.astype(jnp.bfloat16) for term in terms]
    slabs = jnp.concatenate(
        [attend_in.reshape(D, 8, 432), attend_out.reshape(D, 8, 144), expand.reshape(D, 8, 576)],
        axis=2,
    ).transpose(1, 0, 2)
    across = shrink.reshape(4, D, D).transpose(0, 2, 1)
    packed, turned = scatter(slabs, across, collective_id)
    return (packed[:, :432], packed[:, 432:576], packed[:, 576:], turned.T)


def own_rows(condition_all, rows):
    return lax.dynamic_slice_in_dim(condition_all, lax.axis_index("dp") * rows, rows, 1)


def modulation_of(condition_all, modulate_weights):
    rows = modulate_weights[0].shape[0]
    own = own_rows(condition_all, rows)
    partial_terms = jnp.stack([matmul(own, weight) for weight in modulate_weights], axis=1)
    summed = lax.psum_scatter(partial_terms, "dp", scatter_dimension=0, tiled=True)
    full = lax.all_gather(summed, "sp", axis=2, tiled=True)
    return [full[:, slot] for slot in range(len(modulate_weights))]


def sum_over_frames(terms):
    attend_in, attend_out, expand, shrink = terms
    return (
        lax.psum_scatter(
            attend_in.astype(jnp.bfloat16), "sp", scatter_dimension=1, tiled=True
        ).astype(jnp.float32),
        lax.psum_scatter(
            attend_out.astype(jnp.bfloat16), "sp", scatter_dimension=1, tiled=True
        ).astype(jnp.float32),
        lax.psum_scatter(expand.astype(jnp.bfloat16), "sp", scatter_dimension=1, tiled=True).astype(
            jnp.float32
        ),
        lax.psum_scatter(shrink.astype(jnp.bfloat16), "sp", scatter_dimension=1, tiled=True).astype(
            jnp.float32
        ),
    )


def sum_over_data(terms):
    attend_in, attend_out, expand, shrink = terms
    return (
        lax.psum_scatter(
            attend_in.astype(jnp.bfloat16), "dp", scatter_dimension=0, tiled=True
        ).astype(jnp.float32),
        lax.psum_scatter(
            attend_out.astype(jnp.bfloat16), "dp", scatter_dimension=0, tiled=True
        ).astype(jnp.float32),
        lax.psum_scatter(expand.astype(jnp.bfloat16), "dp", scatter_dimension=0, tiled=True).astype(
            jnp.float32
        ),
        lax.psum_scatter(shrink.astype(jnp.bfloat16), "dp", scatter_dimension=0, tiled=True).astype(
            jnp.float32
        ),
    )


def modulate_gradients(condition_all, back_modulations, rows):
    joined = jnp.stack(back_modulations, axis=1)
    columns = lax.psum_scatter(joined, "sp", scatter_dimension=2, tiled=True)
    every = lax.all_gather(columns, "dp", axis=0, tiled=True)
    own = own_rows(condition_all, rows).astype(jnp.float32)
    return [
        jnp.dot(own.T, every[:, slot], precision=HIGHEST_PRECISION)
        for slot in range(len(back_modulations))
    ]


def finish(core_terms, bias_terms, fast, collective_id):
    if fast:
        matrix_grads = sum_packed(core_terms, collective_id)
    else:
        matrix_grads = sum_over_data(sum_over_frames(core_terms))
    attend_bias, out_bias, expand_bias, shrink_bias, modulate_bias = bias_terms
    totals = lax.psum(
        (attend_bias, out_bias, expand_bias, shrink_bias, modulate_bias), ("dp", "sp")
    )
    data_index = lax.axis_index("dp")
    data_count = lax.axis_size("dp")
    bias_grads = tuple(
        (
            lax.dynamic_slice_in_dim(
                total_bias,
                data_index * (total_bias.shape[0] // data_count),
                total_bias.shape[0] // data_count,
            )
            for total_bias in totals
        )
    )
    return (matrix_grads, bias_grads)


def frames_to_patches(tensor):
    return lax.all_to_all(tensor, "sp", split_axis=2, concat_axis=1, tiled=True)


def patches_to_frames(tensor):
    return lax.all_to_all(tensor, "sp", split_axis=1, concat_axis=2, tiled=True)


def attention_scores(queries, key_rows, forms, allowed):
    scores = jnp.einsum(forms[0], queries, key_rows, preferred_element_type=jnp.float32) * HD ** (
        -0.5
    )
    if allowed is not None:
        scores = jnp.where(allowed, scores, -1e30)
    return scores


def block_forward(stream, modulation, core, biases, forms, allowed):
    attend_in, attend_out, expand, shrink = core
    attend_bias, out_bias, expand_bias, shrink_bias, modulate_bias = biases
    model_width = stream.shape[-1]
    pieces = [
        modulation[:, None, None, slot * model_width : (slot + 1) * model_width]
        for slot in range(6)
    ]
    normed = modulate(stream, pieces[0], pieces[1]).astype(jnp.bfloat16)
    bias_float = attend_bias.astype(jnp.float32)
    joined_bias = jnp.concatenate(
        [bias_float[:model_width], jnp.zeros((model_width,), jnp.float32), bias_float[model_width:]]
    )
    projected = (matmul(normed, attend_in) + joined_bias).astype(jnp.bfloat16)
    head_shape = projected.shape[:3] + (H, HD)
    queries = projected[..., :model_width].reshape(head_shape)
    key_rows = projected[..., model_width : 2 * model_width].reshape(head_shape)
    values = projected[..., 2 * model_width :].reshape(head_shape)
    scores = attention_scores(queries, key_rows, forms, allowed)
    highest = jnp.max(scores, axis=-1, keepdims=True)
    exponent = jnp.exp(scores - highest)
    denominator = jnp.sum(exponent, axis=-1, keepdims=True)
    softmax_probs = exponent / denominator
    logsum = highest + jnp.log(denominator)
    mixture = (
        jnp.einsum(
            forms[1], softmax_probs.astype(jnp.bfloat16), values, preferred_element_type=jnp.float32
        )
        .astype(jnp.bfloat16)
        .reshape(stream.shape)
    )
    attended = matmul(mixture, attend_out) + out_bias.astype(jnp.float32)
    middle = stream + pieces[2] * attended
    normed_second = modulate(middle, pieces[3], pieces[4]).astype(jnp.bfloat16)
    hidden = matmul(normed_second, expand) + expand_bias.astype(jnp.float32)
    activated = jax.nn.gelu(hidden, approximate=True).astype(jnp.bfloat16)
    branch = matmul(activated, shrink) + shrink_bias.astype(jnp.float32)
    result = middle + pieces[5] * branch
    kept = (
        pieces,
        normed,
        queries,
        key_rows,
        values,
        logsum,
        mixture,
        attended,
        middle,
        normed_second,
        hidden,
        activated,
        branch,
    )
    return (result, kept)


def block_backward(incoming, stream, core, forms, allowed, kept):
    attend_in, attend_out, expand, shrink = core
    (
        pieces,
        normed,
        queries,
        key_rows,
        values,
        logsum,
        mixture,
        attended,
        middle,
        normed_second,
        hidden,
        activated,
        branch,
    ) = kept
    model_width = stream.shape[-1]
    sequences = stream.shape[0]
    back_branch = (pieces[5] * incoming).astype(jnp.bfloat16)
    back_gate_second = per_sequence(incoming * branch)
    shrink_term = outer_product(activated, back_branch)
    shrink_bias_term = column_totals(back_branch)
    back_activated = back_matmul(back_branch, shrink)
    _, gelu_pull = jax.vjp(lambda tensor: jax.nn.gelu(tensor, approximate=True), hidden)
    back_hidden = gelu_pull(back_activated)[0].astype(jnp.bfloat16)
    expand_term = outer_product(normed_second, back_hidden)
    expand_bias_term = column_totals(back_hidden)
    back_normed_second = back_matmul(back_hidden, expand)
    _, second_pull = jax.vjp(modulate, middle, pieces[3], pieces[4])
    back_middle, back_shift_second, back_scale_second = second_pull(back_normed_second)
    back_middle = back_middle + incoming
    back_attended = (pieces[2] * back_middle).astype(jnp.bfloat16)
    back_gate_first = per_sequence(back_middle * attended)
    out_term = outer_product(mixture, back_attended)
    out_bias_term = column_totals(back_attended)
    back_mixture = (
        back_matmul(back_attended, attend_out).astype(jnp.bfloat16).reshape(queries.shape)
    )
    scores = attention_scores(queries, key_rows, forms, allowed)
    softmax_probs = jnp.exp(scores - logsum)
    back_probs = jnp.einsum(forms[0], back_mixture, values, preferred_element_type=jnp.float32)
    back_values = jnp.einsum(
        forms[2],
        softmax_probs.astype(jnp.bfloat16),
        back_mixture,
        preferred_element_type=jnp.float32,
    )
    row_delta = jnp.sum(softmax_probs * back_probs, axis=-1, keepdims=True)
    back_scores = (softmax_probs * (back_probs - row_delta)).astype(jnp.bfloat16)
    score_scale = HD ** (-0.5)
    back_queries = (
        jnp.einsum(forms[1], back_scores, key_rows, preferred_element_type=jnp.float32)
        * score_scale
    )
    back_keys = (
        jnp.einsum(forms[2], back_scores, queries, preferred_element_type=jnp.float32) * score_scale
    )
    flat_shape = stream.shape
    back_projected = jnp.concatenate(
        [
            back_queries.reshape(flat_shape),
            back_keys.reshape(flat_shape),
            back_values.reshape(flat_shape),
        ],
        axis=-1,
    ).astype(jnp.bfloat16)
    attend_in_term = outer_product(normed, back_projected)
    projected_totals = column_totals(back_projected)
    attend_bias_term = jnp.concatenate(
        [projected_totals[:model_width], projected_totals[2 * model_width :]]
    )
    back_normed = back_matmul(back_projected, attend_in)
    _, first_pull = jax.vjp(modulate, stream, pieces[0], pieces[1])
    back_stream, back_shift_first, back_scale_first = first_pull(back_normed)
    back_stream = back_stream + back_middle
    back_modulation = jnp.concatenate(
        [
            back_shift_first.reshape(sequences, model_width),
            back_scale_first.reshape(sequences, model_width),
            back_gate_first,
            back_shift_second.reshape(sequences, model_width),
            back_scale_second.reshape(sequences, model_width),
            back_gate_second,
        ],
        axis=1,
    )
    modulate_bias_term = jnp.sum(back_modulation, axis=0)
    core_terms = (attend_in_term, out_term, expand_term, shrink_term)
    bias_terms = (
        attend_bias_term,
        out_bias_term,
        expand_bias_term,
        shrink_bias_term,
        modulate_bias_term,
    )
    return (back_stream, core_terms, back_modulation, bias_terms)


def shards(
    fast,
    inputs,
    timesteps,
    segment_ids,
    spatial_attend_in,
    spatial_attend_bias,
    spatial_attend_out,
    spatial_out_bias,
    spatial_expand,
    spatial_expand_bias,
    spatial_shrink,
    spatial_shrink_bias,
    spatial_modulate,
    spatial_modulate_bias,
    temporal_attend_in,
    temporal_attend_bias,
    temporal_attend_out,
    temporal_out_bias,
    temporal_expand,
    temporal_expand_bias,
    temporal_shrink,
    temporal_shrink_bias,
    temporal_modulate,
    temporal_modulate_bias,
    cotangent,
):
    condition_all = jax.nn.silu(sinusoid(timesteps)).astype(jnp.bfloat16)
    allowed = (segment_ids[:, :, None] == segment_ids[:, None, :])[:, None, None, :, :]
    spatial_core = (spatial_attend_in, spatial_attend_out, spatial_expand, spatial_shrink)
    spatial_biases = (
        spatial_attend_bias,
        spatial_out_bias,
        spatial_expand_bias,
        spatial_shrink_bias,
        spatial_modulate_bias,
    )
    temporal_core = (temporal_attend_in, temporal_attend_out, temporal_expand, temporal_shrink)
    temporal_biases = (
        temporal_attend_bias,
        temporal_out_bias,
        temporal_expand_bias,
        temporal_shrink_bias,
        temporal_modulate_bias,
    )
    stream = inputs.astype(jnp.float32)
    modulations = modulation_of(condition_all, (spatial_modulate, temporal_modulate))
    core, biases = collect(spatial_core, spatial_biases, fast, 0)
    modulation = modulations[0] + biases[4].astype(jnp.float32)
    spatial_core = core
    spatial_out, spatial_kept = block_forward(stream, modulation, core, biases, SPATIAL_FORMS, None)
    passed = frames_to_patches(spatial_out.astype(jnp.bfloat16)).astype(jnp.float32)
    core, biases = collect(temporal_core, temporal_biases, fast, 1)
    modulation = modulations[1] + biases[4].astype(jnp.float32)
    temporal_out, temporal_kept = block_forward(
        passed, modulation, core, biases, TEMPORAL_FORMS, allowed
    )
    output = patches_to_frames(temporal_out.astype(jnp.bfloat16))
    incoming = frames_to_patches(cotangent).astype(jnp.float32)
    back_passed, core_terms, back_temporal, bias_terms = block_backward(
        incoming, passed, core, TEMPORAL_FORMS, allowed, temporal_kept
    )
    temporal_grads, temporal_bias_grads = finish(core_terms, bias_terms, fast, 2)
    back_spatial = patches_to_frames(back_passed.astype(jnp.bfloat16)).astype(jnp.float32)
    back_inputs, core_terms, back_spatial_modulation, bias_terms = block_backward(
        back_spatial, stream, spatial_core, SPATIAL_FORMS, None, spatial_kept
    )
    spatial_grads, spatial_bias_grads = finish(core_terms, bias_terms, fast, 3)
    modulate_grads = modulate_gradients(
        condition_all, (back_spatial_modulation, back_temporal), spatial_modulate.shape[0]
    )
    return (
        output,
        back_inputs.astype(jnp.bfloat16),
        spatial_grads[0],
        spatial_bias_grads[0],
        spatial_grads[1],
        spatial_bias_grads[1],
        spatial_grads[2],
        spatial_bias_grads[2],
        spatial_grads[3],
        spatial_bias_grads[3],
        modulate_grads[0],
        spatial_bias_grads[4],
        temporal_grads[0],
        temporal_bias_grads[0],
        temporal_grads[1],
        temporal_bias_grads[1],
        temporal_grads[2],
        temporal_bias_grads[2],
        temporal_grads[3],
        temporal_bias_grads[3],
        modulate_grads[1],
        temporal_bias_grads[4],
    )


def fast_shards(
    inputs,
    timesteps,
    segment_ids,
    spatial_attend_in,
    spatial_attend_bias,
    spatial_attend_out,
    spatial_out_bias,
    spatial_expand,
    spatial_expand_bias,
    spatial_shrink,
    spatial_shrink_bias,
    spatial_modulate,
    spatial_modulate_bias,
    temporal_attend_in,
    temporal_attend_bias,
    temporal_attend_out,
    temporal_out_bias,
    temporal_expand,
    temporal_expand_bias,
    temporal_shrink,
    temporal_shrink_bias,
    temporal_modulate,
    temporal_modulate_bias,
    cotangent,
):
    condition_all = jax.nn.silu(sinusoid(timesteps)).astype(jnp.bfloat16)
    modulations = modulation_of(condition_all, (spatial_modulate, temporal_modulate))
    spatial_p, spatial_s = gather(
        jnp.concatenate([spatial_attend_in, spatial_attend_out, spatial_expand], axis=1),
        spatial_shrink.T,
        0,
    )
    temporal_p, temporal_s = gather(
        jnp.concatenate([temporal_attend_in, temporal_attend_out, temporal_expand], axis=1),
        temporal_shrink.T,
        1,
    )

    def small(modulation, biases):
        attend, out, expand, shrink, modulate = [
            lax.all_gather(bias, "dp", axis=0, tiled=True).astype(jnp.float32) for bias in biases
        ]
        rows = jnp.concatenate([attend, out, shrink, expand]).reshape(8, D)
        mod = (modulation[0] + modulate).reshape(6, D)
        return jnp.concatenate([mod, jnp.zeros((2, D), jnp.float32)]), rows

    spatial_mod, spatial_bias = small(
        modulations[0],
        (
            spatial_attend_bias,
            spatial_out_bias,
            spatial_expand_bias,
            spatial_shrink_bias,
            spatial_modulate_bias,
        ),
    )
    temporal_mod, temporal_bias = small(
        modulations[1],
        (
            temporal_attend_bias,
            temporal_out_bias,
            temporal_expand_bias,
            temporal_shrink_bias,
            temporal_modulate_bias,
        ),
    )
    x = inputs.reshape(TOKENS, WIDTH)
    frames = 8
    clip = jnp.repeat(segment_ids[0], TOKENS // frames)
    spot = jnp.arange(TOKENS) % (TOKENS // frames)
    same = (clip[:, None] == clip[None, :]) & (spot[:, None] == spot[None, :])
    mask = jnp.where(same, 0.0, NEGATIVE).astype(jnp.float32)

    first = block_call(x, spatial_mod, spatial_bias, spatial_p, spatial_s)
    passed = frames_to_patches(first["y"].reshape(inputs.shape)).reshape(TOKENS, WIDTH)
    incoming = frames_to_patches(cotangent).reshape(TOKENS, WIDTH)
    t = block_call(
        passed, temporal_mod, temporal_bias, temporal_p, temporal_s, mask=mask, g=incoming
    )
    patches = (1, frames, TOKENS // frames, WIDTH)
    output = patches_to_frames(t["y"].reshape(patches))
    back_spatial = patches_to_frames(t["back_x"].reshape(patches)).reshape(TOKENS, WIDTH)
    temporal_grads = scatter(*gradient_slabs(t), 2)
    b = block_call(
        x, spatial_mod, spatial_bias, spatial_p, spatial_s, g=back_spatial, give_y=False
    )
    spatial_grads = scatter(*gradient_slabs(b), 3)

    modulate_grads = modulate_gradients(
        condition_all,
        (b["mod_grad"][:6].reshape(1, 6 * D), t["mod_grad"][:6].reshape(1, 6 * D)),
        spatial_modulate.shape[0],
    )
    totals = lax.psum(
        jnp.stack([b["bias_grad"], b["mod_grad"], t["bias_grad"], t["mod_grad"]]), ("dp", "sp")
    )
    index = lax.axis_index("dp")

    def bias_grads(rows, mod):
        flat = rows.reshape(8 * D)
        pieces = (flat[: 2 * D], flat[2 * D : 3 * D], flat[4 * D :], flat[3 * D : 4 * D], mod[:6].reshape(6 * D))
        return [
            lax.dynamic_slice_in_dim(piece, index * (piece.shape[0] // 4), piece.shape[0] // 4)
            for piece in pieces
        ]

    def outputs(grads, bias, modulate_grad):
        packed, turned = grads
        return (
            packed[:, :432],
            bias[0],
            packed[:, 432:576],
            bias[1],
            packed[:, 576:],
            bias[2],
            turned.T,
            bias[3],
            modulate_grad,
            bias[4],
        )

    return (
        (output, b["back_x"].reshape(inputs.shape))
        + outputs(spatial_grads, bias_grads(totals[0], totals[1]), modulate_grads[0])
        + outputs(temporal_grads, bias_grads(totals[2], totals[3]), modulate_grads[1])
    )


def solution(mesh):
    placed = (
        P("dp", "sp", None, None),
        P(),
        P("dp", None),
        P("dp", "sp"),
        P("dp"),
        P("dp", "sp"),
        P("dp"),
        P("dp", "sp"),
        P("dp"),
        P("dp", "sp"),
        P("dp"),
        P("dp", "sp"),
        P("dp"),
        P("dp", "sp"),
        P("dp"),
        P("dp", "sp"),
        P("dp"),
        P("dp", "sp"),
        P("dp"),
        P("dp", "sp"),
        P("dp"),
        P("dp", "sp"),
        P("dp"),
        P("dp", "sp", None, None),
    )
    return jax.shard_map(
        fast_shards if fits(mesh) else functools.partial(shards, False),
        mesh=mesh,
        in_specs=placed,
        out_specs=(
            P("dp", "sp", None, None),
            P("dp", "sp", None, None),
            P("dp", "sp"),
            P("dp"),
            P("dp", "sp"),
            P("dp"),
            P("dp", "sp"),
            P("dp"),
            P("dp", "sp"),
            P("dp"),
            P("dp", "sp"),
            P("dp"),
            P("dp", "sp"),
            P("dp"),
            P("dp", "sp"),
            P("dp"),
            P("dp", "sp"),
            P("dp"),
            P("dp", "sp"),
            P("dp"),
            P("dp", "sp"),
            P("dp"),
        ),
        check_vma=False,
    )
```

```python
import functools
import math

import jax
import jax.numpy as jnp
from jax import lax
from jax.experimental import pallas as pl
from jax.experimental.pallas import tpu as pltpu
from jax.sharding import PartitionSpec as P

D = 1152
H = 16
HD = 72


EPSILON = 1e-06
HIGHEST_PRECISION = lax.Precision.HIGHEST
SPATIAL_FORMS = ("sabhe,sache->sahbc", "sahbc,sache->sabhe", "sahbc,sabhe->sache")
TEMPORAL_FORMS = ("sabhe,scbhe->sbhac", "sbhac,scbhe->sabhe", "sbhac,sabhe->scbhe")


MESH = pl.DeviceIdType.MESH
TOKENS = 256
WIDTH = 1152
CHUNKS = (
    ("p", 0, 144, "zxy"),
    ("p", 144, 144, "zyx"),
    ("s", 0, 48, "xyz"),
    ("s", 48, 48, "yxz"),
    ("s", 96, 48, "zxy"),
)
RELS = sorted(
    [(rx, ry, dz) for rx in (0, 1) for ry in (0, 1) for dz in range(-3, 4)],
    key=lambda r: (r[0] + r[1] + abs(r[2]), r != (0, 0, 0)),
)


class Place:
    def __init__(self):
        self.d, self.s = lax.axis_index("dp"), lax.axis_index("sp")
        self.x, self.c = self.d // 2, self.d % 2
        self.z, self.y = self.s // 2, self.s % 2

    def at(self, rel):
        rx, ry, dz = rel
        return (1 - self.x if rx else self.x, self.z + dz, 1 - self.y if ry else self.y)

    def exists(self, dz):
        return None if dz == 0 else ((self.z + dz >= 0) & (self.z + dz <= 3))

    def neighbour(self, direction):
        x, c, z, y = self.x, self.c, self.z, self.y
        return {
            "x": lambda: dev(1 - x, c, z, y),
            "y": lambda: dev(x, c, z, 1 - y),
            "u": lambda: dev(x, c, z + 1, y),
            "d": lambda: dev(x, c, z - 1, y),
            "c": lambda: dev(x, 1 - c, z, y),
        }[direction]()

    def has(self, direction):
        return {"u": lambda: self.z < 3, "d": lambda: self.z > 0}.get(direction, lambda: None)()


def dev(x, c, z, y):
    return (x * 2 + c, z * 2 + y)


def blk(b):
    return (b[0] * 4 + b[1]) * 2 + b[2]


def both(a, b):
    return b if a is None else (a if b is None else (a & b))


def guarded(cond, f):
    if cond is None:
        f()
    else:
        pl.when(cond)(f)


def greet(me):
    barrier = pltpu.get_barrier_semaphore()
    for k in range(1, 4):
        pl.semaphore_signal(
            barrier, inc=1, device_id=((me.d + k) % 4, me.s), device_id_type=MESH
        )
    for k in range(1, 8):
        pl.semaphore_signal(
            barrier, inc=1, device_id=(me.d, (me.s + k) % 8), device_id_type=MESH
        )
    pl.semaphore_wait(barrier, 10)


def links(rel, order):
    nz = {"x": rel[0], "y": rel[1], "z": rel[2]}
    last = max([i for i in range(3) if nz[order[i]]], default=-1)
    out = []
    for i, dim in enumerate(order):
        if i > last:
            out += ["u", "d"] if dim == "z" else [dim]
        elif i == last and dim == "z":
            out += ["u"] if rel[2] < 0 else ["d"]
    parent = None
    if last >= 0:
        parent = order[last] if order[last] != "z" else ("d" if rel[2] < 0 else "u")
    return out, parent


class Gather:
    SEMS = (
        ((len(CHUNKS), 16), (len(CHUNKS), 16), (len(CHUNKS), 5, 16), (len(CHUNKS),))
    )

    def __init__(self, me, p_in, s_in, p_out, s_out, arrived, crossed, sent, local):
        self.me, self.ins, self.outs = me, {"p": p_in, "s": s_in}, {"p": p_out, "s": s_out}
        self.arrived, self.crossed, self.sent, self.local = arrived, crossed, sent, local

    def own(self, ch):
        return self.ins[ch[0]].at[pl.ds(ch[1], ch[2]), :]

    def place(self, ch, b, core):
        d, s = b[0] * 2 + core, b[1] * 2 + b[2]
        if ch[0] == "p":
            return self.outs["p"].at[s, pl.ds(d * 288 + ch[1], ch[2]), :]
        return self.outs["s"].at[d, pl.ds(s * 144 + ch[1], ch[2]), :]

    def copy(self, k, rel, direction):
        me, ch = self.me, CHUNKS[k]
        b = me.at(rel)
        there = self.place(ch, b, me.c)
        return pltpu.make_async_remote_copy(
            src_ref=self.own(ch) if rel == (0, 0, 0) else there,
            dst_ref=there,
            send_sem=self.sent.at[k, "xyudc".index(direction), blk(b)],
            recv_sem=(self.crossed if direction == "c" else self.arrived).at[k, blk(b)],
            device_id=me.neighbour(direction),
            device_id_type=MESH,
        )

    def ends(self, k, rel):
        return links(rel, CHUNKS[k][3])[0] + ["c"]

    def event(self, k, rel):
        me, ch = self.me, CHUNKS[k]

        def body():
            if rel == (0, 0, 0):
                pltpu.make_async_copy(
                    self.own(ch), self.place(ch, me.at(rel), me.c), self.local.at[k]
                ).start()
            else:
                self.wait_in(k, rel, me.c, self.arrived)
            for direction in self.ends(k, rel):
                guarded(me.has(direction), lambda: self.copy(k, rel, direction).start())

        guarded(me.exists(rel[2]), body)

    def wait_in(self, k, rel, core, sems):
        b, ch = self.me.at(rel), CHUNKS[k]
        pltpu.make_async_copy(self.own(ch), self.place(ch, b, core), sems.at[k, blk(b)]).wait()

    def events(self):
        return [
            functools.partial(self.event, k, rel) for rel in RELS for k in range(len(CHUNKS))
        ]

    def finish(self):
        me = self.me
        for k, ch in enumerate(CHUNKS):
            pltpu.make_async_copy(
                self.own(ch), self.place(ch, me.at((0, 0, 0)), me.c), self.local.at[k]
            ).wait()
        for rel in RELS:

            def body():
                for k in range(len(CHUNKS)):
                    self.wait_in(k, rel, 1 - me.c, self.crossed)
                    for direction in self.ends(k, rel):
                        guarded(
                            me.has(direction), lambda: self.copy(k, rel, direction).wait_send()
                        )

            guarded(me.exists(rel[2]), body)


def slots_of(order):
    base, total, count = {}, 0, 1
    for dim in order:
        base[dim] = total
        total += count * (5 if dim == "z" else 1)
        count *= 4 if dim == "z" else 2
    return base, total


ROW_OF = [(ch[1] if ch[0] == "p" else 288 + ch[1]) for ch in CHUNKS]
SLOTS = [slots_of(ch[3])[1] for ch in CHUNKS]
SLOT_ROW = [sum(n * ch[2] for n, ch in zip(SLOTS[:k], CHUNKS)) for k in range(len(CHUNKS))]
SLOT_ROWS = sum(n * ch[2] for n, ch in zip(SLOTS, CHUNKS))


class Scatter:
    SEMS = (
        (len(CHUNKS), 16),
        (len(CHUNKS), 16),
        (len(CHUNKS), 16),
        (len(CHUNKS), max(SLOTS)),
        (len(CHUNKS), 16),
    )

    def __init__(self, me, p_in, s_in, p_out, s_out, acc, core, got, *sems):
        self.me, self.ins, self.outs = me, {"p": p_in, "s": s_in}, {"p": p_out, "s": s_out}
        self.acc, self.core, self.got = acc, core, got
        self.loaded, self.crossed, self.cross_sent, self.arrived, self.sent = sems

    def term(self, ch, b, core):
        d, s = b[0] * 2 + core, b[1] * 2 + b[2]
        if ch[0] == "p":
            return self.ins["p"].at[s, pl.ds(d * 288 + ch[1], ch[2]), :]
        return self.ins["s"].at[d, pl.ds(s * 144 + ch[1], ch[2]), :]

    def held(self, ref, k, b):
        return ref.at[blk(b), pl.ds(ROW_OF[k], CHUNKS[k][2]), :]

    def load(self, k, b):
        return pltpu.make_async_copy(
            self.term(CHUNKS[k], b, self.me.c), self.held(self.acc, k, b), self.loaded.at[k, blk(b)]
        )

    def cross(self, k, b):
        return pltpu.make_async_remote_copy(
            src_ref=self.term(CHUNKS[k], b, 1 - self.me.c),
            dst_ref=self.held(self.core, k, b),
            send_sem=self.cross_sent.at[k, blk(b)],
            recv_sem=self.crossed.at[k, blk(b)],
            device_id=self.me.neighbour("c"),
            device_id_type=MESH,
        )

    def slot(self, k, b, direction, z):
        order = CHUNKS[k][3]
        base, _ = slots_of(order)
        dim = "z" if direction in "ud" else direction
        coord = {"x": (b[0], 2), "y": (b[2], 2), "z": (b[1], 4)}
        index = 0
        for d in order[: order.index(dim)]:
            index = index * coord[d][1] + coord[d][0]
        if dim == "z":
            inner = b[1] if direction == "d" else jnp.where(b[1] == z, 4, b[1])
            index = index * 5 + inner
        return base[dim] + index

    def got_at(self, k, j):
        n = CHUNKS[k][2]
        return self.got.at[pl.ds(pl.multiple_of(SLOT_ROW[k] + j * n, 16), n), :]

    def send(self, k, b, direction):
        z = self.me.z + {"u": 1, "d": -1}.get(direction, 0)
        j = self.slot(k, b, {"x": "x", "y": "y", "u": "d", "d": "u"}[direction], z)
        return pltpu.make_async_remote_copy(
            src_ref=self.held(self.acc, k, b),
            dst_ref=self.got_at(k, j),
            send_sem=self.sent.at[k, blk(b)],
            recv_sem=self.arrived.at[k, j],
            device_id=self.me.neighbour(direction),
            device_id_type=MESH,
        )

    def add(self, k, b, messages, final):
        ch, i = CHUNKS[k], blk(b)

        @pl.loop(0, ch[2] // 16)
        def _(t):
            r = pl.ds(pl.multiple_of(ROW_OF[k] + t * 16, 16), 16)
            v = self.acc[i, r, :].astype(jnp.float32) + self.core[i, r, :].astype(jnp.float32)
            for cond, j in messages:
                at = pl.ds(pl.multiple_of(SLOT_ROW[k] + j * ch[2] + t * 16, 16), 16)
                q = self.got[at, :].astype(jnp.float32)
                v = v + (q if cond is None else jnp.where(cond, q, 0.0))
            if final is None:
                self.acc[i, r, :] = v.astype(jnp.bfloat16)
            else:
                final[pl.ds(pl.multiple_of(ch[1] + t * 16, 16), 16), :] = v

    def begin(self):
        for rel in RELS[::-1]:

            def body():
                b = self.me.at(rel)
                for k in range(len(CHUNKS)):
                    self.load(k, b).start()
                    self.cross(k, b).start()

            guarded(self.me.exists(rel[2]), body)

    def event(self, k, rel):
        me, ch = self.me, CHUNKS[k]

        def body():
            b = me.at(rel)
            children, parent = links(rel, ch[3])
            self.load(k, b).wait()
            held = self.held(self.core, k, b)
            pltpu.make_async_copy(held, held, self.crossed.at[k, blk(b)]).wait()
            messages = []
            for direction in children:
                cond, j = me.has(direction), self.slot(k, b, direction, me.z)

                def wait():
                    at = self.got_at(k, j)
                    pltpu.make_async_copy(at, at, self.arrived.at[k, j]).wait()

                guarded(cond, wait)
                messages.append((cond, j))
            self.add(k, b, messages, None if parent else self.outs[ch[0]])
            if parent:
                self.send(k, b, parent).start()

        guarded(me.exists(rel[2]), body)

    def events(self):
        return [
            functools.partial(self.event, k, rel) for rel in RELS[::-1] for k in range(len(CHUNKS))
        ]

    def finish(self):
        for rel in RELS:

            def body():
                b = self.me.at(rel)
                for k, ch in enumerate(CHUNKS):
                    _, parent = links(rel, ch[3])
                    if parent:
                        self.send(k, b, parent).wait_send()
                    self.cross(k, b).wait_send()

            guarded(self.me.exists(rel[2]), body)


class Exchange:
    def __init__(self, me, source, target, sent, arrived, local):
        self.me, self.source, self.target = me, source, target
        self.sent, self.arrived, self.local = sent, arrived, local

    def rows(self, ref, s):
        return ref.at[pl.ds(pl.multiple_of(s * 32, 32), 32), :]

    def copy(self, k):
        me = self.me
        other = (me.s + k) % 8
        return pltpu.make_async_remote_copy(
            src_ref=self.rows(self.source, other),
            dst_ref=self.rows(self.target, me.s),
            send_sem=self.sent.at[k],
            recv_sem=self.arrived.at[k],
            device_id=(me.d, other),
            device_id_type=MESH,
        )

    def stay(self):
        return pltpu.make_async_copy(
            self.rows(self.source, self.me.s), self.rows(self.target, self.me.s), self.local
        )

    def start(self):
        self.stay().start()
        for k in range(1, 8):
            self.copy(k).start()

    def finish(self):
        self.stay().wait()
        for k in range(1, 8):
            at = self.rows(self.target, (self.me.s - k + 8) % 8)
            pltpu.make_async_copy(at, at, self.arrived.at[k]).wait()
            self.copy(k).wait_send()


class Spread:
    def __init__(self, me, axis, source, target, sent, arrived, each):
        self.me, self.axis, self.source, self.target = me, axis, source, target
        self.sent, self.arrived, self.each = sent, arrived, each
        self.n = 4 if axis == "dp" else 8
        self.i = me.d if axis == "dp" else me.s

    def copy(self, k):
        other = (self.i + k) % self.n
        return pltpu.make_async_remote_copy(
            src_ref=self.source.at[other] if self.each else self.source,
            dst_ref=self.target.at[self.i],
            send_sem=self.sent.at[k],
            recv_sem=self.arrived.at[k],
            device_id=(other, self.me.s) if self.axis == "dp" else (self.me.d, other),
            device_id_type=MESH,
        )

    def start(self):
        for k in range(1, self.n):
            self.copy(k).start()
        self.target[self.i] = self.source[self.i] if self.each else self.source[...]

    def finish(self):
        for k in range(1, self.n):
            at = self.target.at[(self.i - k + self.n) % self.n]
            pltpu.make_async_copy(at, at, self.arrived.at[k]).wait()
            self.copy(k).wait_send()


def pieces(start, length, width=WIDTH):
    out, done = [], 0
    while done < length:
        row, column = divmod(start + done, width)
        n = min(width - column, length - done)
        out.append((row, column, n, done))
        done += n
    return out


def interleave(events, stages):
    cuts = sorted((int(share * len(events)), i) for i, (share, _) in enumerate(stages))
    done = 0
    for cut, i in cuts:
        for event in events[done:cut]:
            event()
        done = max(done, cut)
        stages[i][1]()
    for event in events[done:]:
        event()


def dma_sems(*shapes):
    return [pltpu.SemaphoreType.DMA(shape) for shape in shapes]


ANY_SPEC = pl.BlockSpec(memory_space=pl.ANY)
VMEM_SPEC = pl.BlockSpec(memory_space=pltpu.VMEM)
SLABS = (
    jax.ShapeDtypeStruct((8, WIDTH, WIDTH), jnp.bfloat16),
    jax.ShapeDtypeStruct((4, WIDTH, WIDTH), jnp.bfloat16),
)
STREAM = jax.ShapeDtypeStruct((TOKENS, WIDTH), jnp.bfloat16)


def first_gather_kernel(
    p_in, s_in, pack, cond, weight0, weight1, cot, p_out, s_out, mod_out, bias_out, incoming,
    packs, part, parts, whole, wholes, *sems,
):
    me = Place()
    gather = Gather(me, p_in, s_in, p_out, s_out, *sems[:4])
    exchange = Exchange(me, cot, incoming, *sems[4:7])
    biases = Spread(me, "dp", pack, packs, *sems[7:9], False)
    terms = Spread(me, "dp", part, parts, *sems[9:11], True)
    columns = Spread(me, "sp", whole, wholes, *sems[11:13], False)
    greet(me)

    def begin():
        biases.start()
        for i, weight in enumerate((weight0, weight1)):
            product = jnp.dot(cond[...], weight[...], preferred_element_type=jnp.float32)
            for q in range(4):
                part[q, i : i + 1, :] = product[q : q + 1, :]
        terms.start()
        exchange.start()

    def middle():
        terms.finish()
        whole[...] = jnp.sum(parts[...], axis=0)
        columns.start()

    def end():
        columns.finish()
        biases.finish()
        exchange.finish()
        for i in range(2):
            mod_out[i] = jnp.zeros((8, WIDTH), jnp.float32)
            for s in range(8):
                for row, column, n, at in pieces(864 * s, 864):
                    mod_out[i, row : row + 1, column : column + n] = wholes[
                        s, i : i + 1, at : at + n
                    ]
            for k in range(4):
                for first, n_all in ((0, WIDTH), (WIDTH, 576)):
                    source = 4 * i + 2 + first // WIDTH
                    for row, column, n, at in pieces(1728 * k + first, n_all):
                        mod_out[i, row : row + 1, column : column + n] += packs[
                            k, source : source + 1, at : at + n
                        ]
                top = 4 * i
                bias_out[i, k // 2 : k // 2 + 1, 576 * (k % 2) : 576 * (k % 2 + 1)] = packs[
                    k, top : top + 1, 0:576
                ]
                for row, at in ((2, 576), (3, 864)):
                    bias_out[i, row : row + 1, 288 * k : 288 * (k + 1)] = packs[
                        k, top : top + 1, at : at + 288
                    ]
                bias_out[i, 4 + k : 5 + k, :] = packs[k, top + 1 : top + 2, :]

    events = gather.events()
    own = len(CHUNKS)
    interleave(events, [(own / len(events), begin), (0.3, middle), (0.8, end)])
    gather.finish()


def first_gather(p, s, pack, cond, weights, cotangent):
    return pl.pallas_call(
        first_gather_kernel,
        out_shape=SLABS
        + (
            jax.ShapeDtypeStruct((2, 8, WIDTH), jnp.float32),
            jax.ShapeDtypeStruct((2, 8, WIDTH), jnp.float32),
            STREAM,
        ),
        in_specs=[ANY_SPEC] * 2 + [VMEM_SPEC] * 4 + [ANY_SPEC],
        out_specs=(ANY_SPEC, ANY_SPEC, VMEM_SPEC, VMEM_SPEC, ANY_SPEC),
        scratch_shapes=[
            pltpu.VMEM((4, 8, WIDTH), jnp.float32),
            pltpu.VMEM((4, 8, 864), jnp.float32),
            pltpu.VMEM((4, 8, 864), jnp.float32),
            pltpu.VMEM((8, 864), jnp.float32),
            pltpu.VMEM((8, 8, 864), jnp.float32),
        ]
        + dma_sems(*Gather.SEMS, (8,), (8,), (), (4,), (4,), (4,), (4,), (8,), (8,)),
        compiler_params=pltpu.CompilerParams(collective_id=0, has_side_effects=True),
        name="first_gather",
    )(p, s, pack, cond, *weights, cotangent)


def second_gather_kernel(p_in, s_in, y, p_out, s_out, passed, *sems):
    me = Place()
    gather = Gather(me, p_in, s_in, p_out, s_out, *sems[:4])
    exchange = Exchange(me, y, passed, *sems[4:7])
    greet(me)
    events = gather.events()
    interleave(events, [(0.2, exchange.start), (0.8, exchange.finish)])
    gather.finish()


def second_gather(p, s, y):
    return pl.pallas_call(
        second_gather_kernel,
        out_shape=SLABS + (STREAM,),
        in_specs=[ANY_SPEC] * 3,
        out_specs=(ANY_SPEC,) * 3,
        scratch_shapes=dma_sems(*Gather.SEMS, (8,), (8,), ()),
        compiler_params=pltpu.CompilerParams(collective_id=1, has_side_effects=True),
        name="second_gather",
    )(p, s, y)


def scatter_kernel(streams, *refs):
    p_in, s_in, bias_grad, mod_grad, cond = refs[:5]
    sources = refs[5 : 5 + streams]
    refs = refs[5 + streams :]
    p_out, s_out, weight_grad, totals = refs[:4]
    targets = refs[4 : 4 + streams]
    refs = refs[4 + streams :]
    acc, core, got, small, small_in, row_sum, row_in, total = refs[:8]
    sems = refs[8:]
    me = Place()
    scatter = Scatter(me, p_in, s_in, p_out, s_out, acc, core, got, *sems[:5])
    over_frames = Spread(me, "sp", small, small_in, *sems[5:7], True)
    over_data = Spread(me, "dp", row_sum, row_in, *sems[7:9], False)
    over_all = Spread(me, "sp", total, totals, *sems[9:11], False)
    exchanges = [
        Exchange(me, source, target, *sems[11 + 3 * i : 14 + 3 * i])
        for i, (source, target) in enumerate(zip(sources, targets))
    ]
    greet(me)
    for exchange in exchanges:
        exchange.start()
    scatter.begin()

    def begin():
        small[...] = jnp.zeros(small.shape, jnp.float32)
        for s in range(8):
            small[s, 0:1, :] = bias_grad[s : s + 1, :]
            for row, column, n, at in pieces(864 * s, 864):
                small[s, 1:2, at : at + n] = mod_grad[row : row + 1, column : column + n]
        over_frames.start()

    def second():
        over_frames.finish()
        row_sum[...] = jnp.sum(small_in[...], axis=0)
        over_data.start()

    def third():
        over_data.finish()
        total[...] = jnp.sum(row_in[...], axis=0)
        over_all.start()
        for t in range(9):
            r = slice(32 * t, 32 * (t + 1))
            v = cond[r, 0:1] * row_in[0, 1:2, 0:864]
            for q in range(1, 4):
                v = v + cond[r, q : q + 1] * row_in[q, 1:2, 0:864]
            weight_grad[r, :] = v

    def fourth():
        over_all.finish()
        for exchange in exchanges:
            exchange.finish()

    interleave(
        scatter.events(), [(0.05, begin), (0.3, second), (0.5, third), (0.8, fourth)]
    )
    scatter.finish()


def scatter_call(slabs, bias_grad, mod_grad, cond, streams, collective_id):
    n = len(streams)
    block = pltpu.VMEM((16, 432, WIDTH), jnp.bfloat16)
    rows = jax.ShapeDtypeStruct
    return pl.pallas_call(
        functools.partial(scatter_kernel, n),
        out_shape=[
            rows((288, WIDTH), jnp.float32),
            rows((144, WIDTH), jnp.float32),
            rows((288, 864), jnp.float32),
            rows((8, 8, WIDTH), jnp.float32),
        ]
        + [STREAM] * n,
        in_specs=[ANY_SPEC] * 2 + [VMEM_SPEC] * 3 + [ANY_SPEC] * n,
        out_specs=[VMEM_SPEC] * 4 + [ANY_SPEC] * n,
        scratch_shapes=[block, block, pltpu.VMEM((SLOT_ROWS, WIDTH), jnp.bfloat16)]
        + [
            pltpu.VMEM(shape, jnp.float32)
            for shape in ((8, 8, WIDTH), (8, 8, WIDTH), (8, WIDTH), (4, 8, WIDTH), (8, WIDTH))
        ]
        + dma_sems(*Scatter.SEMS, (8,), (8,), (4,), (4,), (8,), (8,), *([(8,), (8,), ()] * n)),
        compiler_params=pltpu.CompilerParams(
            collective_id=collective_id, has_side_effects=True, vmem_limit_bytes=60 << 20
        ),
        name="first_scatter" if n else "second_scatter",
    )(*slabs, bias_grad, mod_grad, cond, *streams)


def unpack_kernel(*refs):
    ins, outs = refs[:6], refs[6:]
    d = lax.axis_index("dp")
    for i in range(2):
        packed, turned, totals = ins[3 * i : 3 * i + 3]
        a_in, a_bias, a_out, o_bias, expand, e_bias, shrink, s_bias, m_bias = outs[
            9 * i : 9 * i + 9
        ]
        a_in[...] = packed[:, 0:432]
        a_out[...] = packed[:, 432:576]
        expand[...] = packed[:, 576:1152]
        shrink[...] = turned[...].T
        for k in range(4):

            @pl.when(d == k)
            def _():
                half = 576 * (k % 2)
                a_bias[...] = totals[k // 2, 0:1, half : half + 576]
                o_bias[...] = totals[2, 0:1, 288 * k : 288 * (k + 1)]
                s_bias[...] = totals[3, 0:1, 288 * k : 288 * (k + 1)]
                e_bias[...] = totals[4 + k, 0:1, :]
                for s in (2 * k, 2 * k + 1):
                    to = 864 * (s % 2)
                    m_bias[:, to : to + 864] = totals[s, 1:2, 0:864]


def unpack(*grads):
    shapes = [(288, 432), (1, 576), (288, 144), (1, 288), (288, 576), (1, 1152), (1152, 144)]
    shapes += [(1, 288), (1, 1728)]
    outs = pl.pallas_call(
        unpack_kernel,
        out_shape=[jax.ShapeDtypeStruct(shape, jnp.float32) for shape in shapes * 2],
        in_specs=[VMEM_SPEC] * 6,
        out_specs=[VMEM_SPEC] * 18,
        compiler_params=pltpu.CompilerParams(vmem_limit_bytes=32 << 20),
        name="unpack",
    )(*grads)
    return [out.reshape(-1) if out.shape[0] == 1 else out for out in outs]


SCALE = HD ** (-0.5)
NEGATIVE = -1e30


def dot(a, b):
    return lax.dot_general(a, b, (((1,), (0,)), ((), ())), preferred_element_type=jnp.float32)


def dot_nt(a, b):
    return lax.dot_general(a, b, (((1,), (1,)), ((), ())), preferred_element_type=jnp.float32)


def dot_tn(a, b):
    return lax.dot_general(a, b, (((0,), (0,)), ((), ())), preferred_element_type=jnp.float32)


def by_rows(body, step=32):
    @pl.loop(0, TOKENS // step)
    def _(i):
        body(pl.ds(pl.multiple_of(i * step, step), step))


def statistics(v):
    centered = v - jnp.mean(v, axis=1, keepdims=True)
    scale = lax.rsqrt(jnp.mean(centered * centered, axis=1, keepdims=True) + EPSILON)
    return centered * scale, scale


def fold(v):
    return jnp.sum(v.reshape(v.shape[0] // 8, 8, v.shape[1]), axis=0)


def gelu_both(h):
    c, a = math.sqrt(2.0 / math.pi), 0.044715
    square = h * h
    t = jnp.tanh(c * h * (1.0 + a * square))
    half = 0.5 * (1.0 + t)
    return h * half, half + 0.5 * h * (1.0 - t * t) * (c * (1.0 + 3.0 * a * square))


WIN_IN, WIN_OUT, WIN_EXP = slice(0, 512), slice(384, 640), slice(512, 1152)


def forward_pass(e, y):
    mod = e.mod
    shift1, scale1, gate1 = [lambda i=i: mod[i : i + 1, :] for i in range(3)]
    shift2, scale2, gate2 = [lambda i=i: mod[i : i + 1, :] for i in range(3, 6)]

    e.bslab[...] = jnp.zeros(e.bslab.shape, jnp.float32)
    for s in range(8):
        for row, first in ((0, 0), (1, 2 * WIDTH)):
            lo, hi = max(432 * s, first), min(432 * (s + 1), first + WIDTH)
            if lo < hi:
                e.bslab[s, 0:1, lo - 432 * s : hi - 432 * s] = e.bias[
                    row : row + 1, lo - first : hi - first
                ]

    def first(r):
        n, _ = statistics(e.x[r, :].astype(jnp.float32))
        e.normed[r, :] = (n * (1.0 + scale1()) + shift1()).astype(jnp.bfloat16)

    by_rows(first)

    @pl.loop(0, 8)
    def _(s):
        e.wait_p(s)
        v = dot(e.normed[...], e.pv[s, :, WIN_IN]) + e.bslab[s, 0:1, :]
        for j in range(6):
            e.heads[6 * s + j] = v[:, HD * j : HD * (j + 1)].astype(jnp.bfloat16)

    @pl.loop(0, H)
    def _(h):
        scores = dot_nt(e.heads[h], e.heads[H + h]) * SCALE
        if e.mask is not None:
            scores = scores + e.mask[...]
        exponent = jnp.exp(scores - jnp.max(scores, axis=1, keepdims=True))
        probs = exponent / jnp.sum(exponent, axis=1, keepdims=True)
        e.mh[h] = dot(probs.astype(jnp.bfloat16), e.heads[2 * H + h]).astype(jnp.bfloat16)

    for h in range(H):
        e.mixture[:, HD * h : HD * (h + 1)] = e.mh[h]
    for s in range(8):
        v = dot(e.mixture[...], e.pv[s, :, WIN_OUT])
        e.attended[:, 144 * s : 144 * (s + 1)] = v[:, 48:192]

    def second(r):
        attended = e.attended[r, :] + e.bias[2:3, :]
        e.attended[r, :] = attended
        middle = e.x[r, :].astype(jnp.float32) + gate1() * attended
        e.middle[r, :] = middle
        n, _ = statistics(middle)
        e.normed2[r, :] = (n * (1.0 + scale2()) + shift2()).astype(jnp.bfloat16)

    by_rows(second)
    e.branch[...] = jnp.zeros(e.branch.shape, jnp.float32)

    @pl.loop(0, 4)
    def _(d):
        for half in range(2):
            v = dot(e.normed2[...], e.pv[2 * d + half, :, WIN_EXP])
            e.tmp[:, 576 * half : 576 * (half + 1)] = v[:, 64:640]

        def activate(r):
            value, slope = gelu_both(e.tmp[r, :] + e.bias[pl.ds(4 + d, 1), :])
            e.act[d, r, :] = value.astype(jnp.bfloat16)
            if e.slope is not None:
                e.slope[d, r, :] = slope

        by_rows(activate)
        e.wait_s(d)
        e.branch[...] += dot_nt(e.act[d], e.sv[d])

    def third(r):
        branch = e.branch[r, :] + e.bias[3:4, :]
        e.branch[r, :] = branch
        if y is not None:
            y[r, :] = (e.middle[r, :] + gate2() * branch).astype(jnp.bfloat16)

    by_rows(third)


def backward_pass(e):
    mod = e.mod
    gate1, scale1 = lambda: mod[2:3, :], lambda: mod[1:2, :]
    gate2, scale2 = lambda: mod[5:6, :], lambda: mod[4:5, :]
    e.sums[...] = jnp.zeros(e.sums.shape, jnp.float32)
    e.bout[...] = jnp.zeros(e.bout.shape, jnp.bfloat16)
    for s in range(8):
        e.bexp[s, :, 0:128] = jnp.zeros((TOKENS, 128), jnp.bfloat16)
        e.bin[s, :, 384:512] = jnp.zeros((TOKENS, 128), jnp.bfloat16)

    def first(r):
        g = e.g[r, :].astype(jnp.float32)
        back = (gate2() * g).astype(jnp.bfloat16)
        e.bb[r, :] = back
        e.sums[5] += fold(g * e.branch[r, :])
        e.sums[7] += fold(back.astype(jnp.float32))

    by_rows(first)

    @pl.loop(0, 4)
    def _(d):
        e.tmp[...] = dot(e.bb[...], e.sv[d])

        def hidden(r):
            back = (e.tmp[r, :] * e.slope[d, r, :]).astype(jnp.bfloat16)
            for half in range(2):
                e.bexp[2 * d + half, r, 64:640] = back[:, 576 * half : 576 * (half + 1)]
            e.sums[8 + d] += fold(back.astype(jnp.float32))

        by_rows(hidden)

    e.tmp[...] = jnp.zeros(e.tmp.shape, jnp.float32)

    @pl.loop(0, 8)
    def _(s):
        e.tmp[...] += dot_nt(e.bexp[s], e.pv[s, :, WIN_EXP])

    def second(r):
        n, scale = statistics(e.middle[r, :])
        back_normed = e.tmp[r, :]
        e.sums[3] += fold(back_normed)
        e.sums[4] += fold(back_normed * n)
        u = back_normed * (1.0 + scale2())
        inner = jnp.mean(u, axis=1, keepdims=True) + n * jnp.mean(u * n, axis=1, keepdims=True)
        back_middle = e.g[r, :].astype(jnp.float32) + scale * (u - inner)
        e.middle[r, :] = back_middle
        e.sums[2] += fold(back_middle * e.attended[r, :])
        back = (gate1() * back_middle).astype(jnp.bfloat16)
        e.sums[6] += fold(back.astype(jnp.float32))
        for s in range(8):
            e.bout[s, r, 48:192] = back[:, 144 * s : 144 * (s + 1)]

    by_rows(second)
    e.tmp[...] = jnp.zeros(e.tmp.shape, jnp.float32)

    @pl.loop(0, 8)
    def _(s):
        e.tmp[...] += dot_nt(e.bout[s], e.pv[s, :, WIN_OUT])

    for h in range(H):
        e.mh[h] = e.tmp[:, HD * h : HD * (h + 1)].astype(jnp.bfloat16)

    @pl.loop(0, H)
    def _(h):
        q, k, v, back = e.heads[h], e.heads[H + h], e.heads[2 * H + h], e.mh[h]
        scores = dot_nt(q, k) * SCALE
        if e.mask is not None:
            scores = scores + e.mask[...]
        exponent = jnp.exp(scores - jnp.max(scores, axis=1, keepdims=True))
        probs = exponent / jnp.sum(exponent, axis=1, keepdims=True)
        back_probs = dot_nt(back, v)
        e.heads[2 * H + h] = dot_tn(probs.astype(jnp.bfloat16), back).astype(jnp.bfloat16)
        delta = jnp.sum(probs * back_probs, axis=1, keepdims=True)
        back_scores = (probs * (back_probs - delta)).astype(jnp.bfloat16)
        e.heads[h] = (dot(back_scores, k) * SCALE).astype(jnp.bfloat16)
        e.heads[H + h] = (dot_tn(back_scores, q) * SCALE).astype(jnp.bfloat16)

    e.tmp[...] = jnp.zeros(e.tmp.shape, jnp.float32)
    ones = jnp.ones((8, TOKENS), jnp.bfloat16)

    @pl.loop(0, 8)
    def _(s):
        for j in range(6):
            e.bin[s, :, HD * j : HD * (j + 1)] = e.heads[6 * s + j]
        e.bslab[s] = dot(ones, e.bin[s])
        e.tmp[...] += dot_nt(e.bin[s], e.pv[s, :, WIN_IN])

    def third(r):
        n, scale = statistics(e.x[r, :].astype(jnp.float32))
        back_normed = e.tmp[r, :]
        e.sums[0] += fold(back_normed)
        e.sums[1] += fold(back_normed * n)
        u = back_normed * (1.0 + scale1())
        inner = jnp.mean(u, axis=1, keepdims=True) + n * jnp.mean(u * n, axis=1, keepdims=True)
        e.back_x[r, :] = (e.middle[r, :] + scale * (u - inner)).astype(jnp.bfloat16)

    by_rows(third)

    for s in range(8):
        for row, first_column in ((0, 0), (1, 2 * WIDTH)):
            lo, hi = max(432 * s, first_column), min(432 * (s + 1), first_column + WIDTH)
            if lo < hi:
                e.bias_grad[row : row + 1, lo - first_column : hi - first_column] = e.bslab[
                    s, 0:1, lo - 432 * s : hi - 432 * s
                ]
    for row, slot in ((2, 6), (3, 7), (4, 8), (5, 9), (6, 10), (7, 11)):
        e.bias_grad[row : row + 1, :] = jnp.sum(e.sums[slot], axis=0, keepdims=True)
    for slot in range(6):
        e.mod_grad[slot : slot + 1, :] = jnp.sum(e.sums[slot], axis=0, keepdims=True)
    e.mod_grad[6:8, :] = jnp.zeros((2, WIDTH), jnp.float32)


class Refs:
    pass


WEIGHT_SCRATCH = (
    ("pv", (8, WIDTH, WIDTH), jnp.bfloat16),
    ("sv", (4, WIDTH, WIDTH), jnp.bfloat16),
)
FORWARD_SCRATCH = (
    ("bslab", (8, 8, 512), jnp.float32),
    ("heads", (3 * H, TOKENS, HD), jnp.bfloat16),
    ("mh", (H, TOKENS, HD), jnp.bfloat16),
    ("attended", (TOKENS, WIDTH), jnp.float32),
    ("middle", (TOKENS, WIDTH), jnp.float32),
    ("branch", (TOKENS, WIDTH), jnp.float32),
    ("tmp", (TOKENS, WIDTH), jnp.float32),
)
OPERANDS = (
    ("normed", (TOKENS, WIDTH), jnp.bfloat16),
    ("mixture", (TOKENS, WIDTH), jnp.bfloat16),
    ("normed2", (TOKENS, WIDTH), jnp.bfloat16),
    ("act", (4, TOKENS, WIDTH), jnp.bfloat16),
)
BACK_OPERANDS = (
    ("bb", (TOKENS, WIDTH), jnp.bfloat16),
    ("bin", (8, TOKENS, 512), jnp.bfloat16),
    ("bout", (8, TOKENS, 256), jnp.bfloat16),
    ("bexp", (8, TOKENS, 640), jnp.bfloat16),
)
BACKWARD_SCRATCH = (
    ("slope", (4, TOKENS, WIDTH), jnp.float32),
    ("sums", (12, 8, WIDTH), jnp.float32),
)


def load_weights(e, p_hbm, s_hbm, psem, ssem):
    def p_copy(s):
        return pltpu.make_async_copy(p_hbm.at[s], e.pv.at[s], psem.at[s])

    def s_copy(d):
        return pltpu.make_async_copy(s_hbm.at[d], e.sv.at[d], ssem.at[d])

    @pl.loop(0, 8)
    def _(s):
        p_copy(s).start()

    @pl.loop(0, 4)
    def _(d):
        s_copy(d).start()

    e.wait_p = lambda s: p_copy(s).wait()
    e.wait_s = lambda d: s_copy(d).wait()


def block_kernel(names, block, *refs):
    e = Refs()
    e.mask, e.slope, e.y = None, None, None
    for name, ref in zip(names, refs):
        setattr(e, name, ref)
    e.mod, e.bias = e.mods.at[block], e.biases.at[block]
    load_weights(e, e.p, e.s, e.psem, e.ssem)
    if "segments" in names:
        fill_mask(e)
    forward_pass(e, e.y)
    if "g" in names:
        backward_pass(e)


def fill_mask(e):
    frames = e.segments.shape[1]
    each = TOKENS // frames

    def clips(axis):
        frame = lax.broadcasted_iota(jnp.int32, (TOKENS, TOKENS), axis) // each
        clip = jnp.zeros((TOKENS, TOKENS), jnp.int32)
        for f in range(frames):
            clip = jnp.where(frame == f, e.segments[0, f], clip)
        return clip

    def spots(axis):
        return lax.broadcasted_iota(jnp.int32, (TOKENS, TOKENS), axis) % each

    same = (clips(0) == clips(1)) & (spots(0) == spots(1))
    e.mask[...] = jnp.where(same, 0.0, NEGATIVE)


def block_call(x, mods, biases, block, p, s, segments=None, g=None, give_y=True):
    inputs = [("x", x), ("mods", mods), ("biases", biases), ("p", p), ("s", s)]
    if segments is not None:
        inputs.append(("segments", segments))
    if g is not None:
        inputs.append(("g", g))
    outs, scratch = [], list(WEIGHT_SCRATCH + FORWARD_SCRATCH)
    if segments is not None:
        scratch.append(("mask", (TOKENS, TOKENS), jnp.float32))
    if give_y:
        outs.append(("y", (TOKENS, WIDTH), jnp.bfloat16))
    if g is None:
        scratch += OPERANDS
    else:
        outs += [
            ("back_x", (TOKENS, WIDTH), jnp.bfloat16),
            ("bias_grad", (8, WIDTH), jnp.float32),
            ("mod_grad", (8, WIDTH), jnp.float32),
        ]
        outs += OPERANDS + BACK_OPERANDS
        scratch += BACKWARD_SCRATCH
    names = [name for name, *_ in inputs + outs + scratch] + ["psem", "ssem"]
    smem = pl.BlockSpec(memory_space=pltpu.SMEM)
    spec = lambda name: {"p": ANY_SPEC, "s": ANY_SPEC, "segments": smem}.get(name, VMEM_SPEC)
    results = pl.pallas_call(
        functools.partial(block_kernel, names, block),
        out_shape=[jax.ShapeDtypeStruct(shape, kind) for _, shape, kind in outs],
        in_specs=[spec(name) for name, _ in inputs],
        out_specs=[VMEM_SPEC] * len(outs),
        scratch_shapes=[pltpu.VMEM(shape, kind) for _, shape, kind in scratch]
        + [pltpu.SemaphoreType.DMA((8,)), pltpu.SemaphoreType.DMA((4,))],
        compiler_params=pltpu.CompilerParams(vmem_limit_bytes=63 << 20),
        name="block_both" if g is not None else "block_forward",
    )(*[value for _, value in inputs])
    return dict(zip([name for name, *_ in outs], results))


def gradient_p_kernel(normed, mixture, normed2, b_in, b_out, b_exp, out, n_t, m_t, n2_t):
    @pl.when(pl.program_id(0) == 0)
    def _():
        n_t[...] = normed[...].T
        m_t[...] = mixture[...].T
        n2_t[...] = normed2[...].T

    @pl.loop(0, 4)
    def _(i):
        r = pl.ds(pl.multiple_of(i * 288, 16), 288)
        first = dot(n_t[r, :], b_in[0])
        second = dot(m_t[r, :], b_out[0])
        third = dot(n2_t[r, :], b_exp[0])
        out[0, r, 0:384] = first[:, 0:384].astype(jnp.bfloat16)
        out[0, r, 384:512] = (first[:, 384:] + second[:, :128]).astype(jnp.bfloat16)
        out[0, r, 512:640] = (second[:, 128:] + third[:, :128]).astype(jnp.bfloat16)
        out[0, r, 640:] = third[:, 128:].astype(jnp.bfloat16)


def gradient_s_kernel(back, act, out, back_t):
    @pl.when(pl.program_id(0) == 0)
    def _():
        back_t[...] = back[...].T

    @pl.loop(0, 4)
    def _(i):
        r = pl.ds(pl.multiple_of(i * 288, 16), 288)
        out[0, r, :] = dot(back_t[r, :], act[0]).astype(jnp.bfloat16)


def gradient_slabs(o):
    whole = pl.BlockSpec((TOKENS, WIDTH), lambda i: (0, 0))
    piece = lambda n: pl.BlockSpec((1, TOKENS, n), lambda i: (i, 0, 0))
    slab = pl.BlockSpec((1, WIDTH, WIDTH), lambda i: (i, 0, 0))
    turned = pltpu.VMEM((WIDTH, TOKENS), jnp.bfloat16)
    p = pl.pallas_call(
        gradient_p_kernel,
        grid=(8,),
        out_shape=jax.ShapeDtypeStruct((8, WIDTH, WIDTH), jnp.bfloat16),
        in_specs=[whole] * 3 + [piece(512), piece(256), piece(640)],
        out_specs=slab,
        scratch_shapes=[turned] * 3,
        compiler_params=pltpu.CompilerParams(vmem_limit_bytes=48 << 20),
    )(o["normed"], o["mixture"], o["normed2"], o["bin"], o["bout"], o["bexp"])
    s = pl.pallas_call(
        gradient_s_kernel,
        grid=(4,),
        out_shape=jax.ShapeDtypeStruct((4, WIDTH, WIDTH), jnp.bfloat16),
        in_specs=[whole, piece(WIDTH)],
        out_specs=slab,
        scratch_shapes=[turned],
        compiler_params=pltpu.CompilerParams(vmem_limit_bytes=48 << 20),
    )(o["bb"], o["act"])
    return p, s


def sinusoid(timesteps):
    half_width = D // 2
    frequencies = jnp.exp(
        -math.log(10000.0) * jnp.arange(half_width, dtype=jnp.float32) / half_width
    )
    angles = timesteps.astype(jnp.float32)[:, None] * frequencies[None, :]
    return jnp.concatenate([jnp.cos(angles), jnp.sin(angles)], axis=1)


def layer_norm(tensor):
    centered = tensor - jnp.mean(tensor, axis=-1, keepdims=True)
    return centered * lax.rsqrt(jnp.mean(centered * centered, axis=-1, keepdims=True) + EPSILON)


def modulate(tensor, shift_part, scale_part):
    return layer_norm(tensor) * (1.0 + scale_part) + shift_part


def matmul(left_side, right_side):
    return jnp.dot(left_side, right_side, preferred_element_type=jnp.float32)


def back_matmul(gradient, matrix):
    return lax.dot_general(
        gradient,
        matrix,
        (((gradient.ndim - 1,), (1,)), ((), ())),
        preferred_element_type=jnp.float32,
    )


def outer_product(left_side, right_side):
    flat_left = left_side.reshape(-1, left_side.shape[-1])
    flat_right = right_side.reshape(-1, right_side.shape[-1])
    return lax.dot_general(
        flat_left, flat_right, (((0,), (0,)), ((), ())), preferred_element_type=jnp.float32
    )


def column_totals(tensor):
    return jnp.sum(tensor.astype(jnp.float32).reshape(-1, tensor.shape[-1]), axis=0)


def per_sequence(tensor):
    return jnp.sum(tensor, axis=(1, 2))


def over_data(core, biases):
    attend_in, attend_out, expand, shrink = core
    attend_bias, out_bias, expand_bias, shrink_bias, modulate_bias = biases
    gathered = (
        lax.all_gather(attend_in, "dp", axis=0, tiled=True),
        lax.all_gather(attend_out, "dp", axis=0, tiled=True),
        lax.all_gather(expand, "dp", axis=0, tiled=True),
        lax.all_gather(shrink, "dp", axis=0, tiled=True),
        lax.all_gather(attend_bias, "dp", axis=0, tiled=True),
        lax.all_gather(out_bias, "dp", axis=0, tiled=True),
        lax.all_gather(expand_bias, "dp", axis=0, tiled=True),
        lax.all_gather(shrink_bias, "dp", axis=0, tiled=True),
        lax.all_gather(modulate_bias, "dp", axis=0, tiled=True),
    )
    return (gathered[:4], gathered[4:])


def over_frames(core):
    attend_in, attend_out, expand, shrink = core
    gathered = (
        lax.all_gather(attend_in, "sp", axis=1, tiled=True),
        lax.all_gather(attend_out, "sp", axis=1, tiled=True),
        lax.all_gather(expand, "sp", axis=1, tiled=True),
        lax.all_gather(shrink, "sp", axis=1, tiled=True),
    )
    return gathered


def collect(core, biases):
    core_rows, biases_full = over_data(core, biases)
    core_full = over_frames(core_rows)
    return (core_full, biases_full)


def own_rows(condition_all, rows):
    return lax.dynamic_slice_in_dim(condition_all, lax.axis_index("dp") * rows, rows, 1)


def modulation_of(condition_all, modulate_weights):
    rows = modulate_weights[0].shape[0]
    own = own_rows(condition_all, rows)
    partial_terms = jnp.stack([matmul(own, weight) for weight in modulate_weights], axis=1)
    summed = lax.psum_scatter(partial_terms, "dp", scatter_dimension=0, tiled=True)
    full = lax.all_gather(summed, "sp", axis=2, tiled=True)
    return [full[:, slot] for slot in range(len(modulate_weights))]


def sum_over_frames(terms):
    attend_in, attend_out, expand, shrink = terms
    return (
        lax.psum_scatter(
            attend_in.astype(jnp.bfloat16), "sp", scatter_dimension=1, tiled=True
        ).astype(jnp.float32),
        lax.psum_scatter(
            attend_out.astype(jnp.bfloat16), "sp", scatter_dimension=1, tiled=True
        ).astype(jnp.float32),
        lax.psum_scatter(expand.astype(jnp.bfloat16), "sp", scatter_dimension=1, tiled=True).astype(
            jnp.float32
        ),
        lax.psum_scatter(shrink.astype(jnp.bfloat16), "sp", scatter_dimension=1, tiled=True).astype(
            jnp.float32
        ),
    )


def sum_over_data(terms):
    attend_in, attend_out, expand, shrink = terms
    return (
        lax.psum_scatter(
            attend_in.astype(jnp.bfloat16), "dp", scatter_dimension=0, tiled=True
        ).astype(jnp.float32),
        lax.psum_scatter(
            attend_out.astype(jnp.bfloat16), "dp", scatter_dimension=0, tiled=True
        ).astype(jnp.float32),
        lax.psum_scatter(expand.astype(jnp.bfloat16), "dp", scatter_dimension=0, tiled=True).astype(
            jnp.float32
        ),
        lax.psum_scatter(shrink.astype(jnp.bfloat16), "dp", scatter_dimension=0, tiled=True).astype(
            jnp.float32
        ),
    )


def modulate_gradients(condition_all, back_modulations, rows):
    joined = jnp.stack(back_modulations, axis=1)
    columns = lax.psum_scatter(joined, "sp", scatter_dimension=2, tiled=True)
    every = lax.all_gather(columns, "dp", axis=0, tiled=True)
    own = own_rows(condition_all, rows).astype(jnp.float32)
    return [
        jnp.dot(own.T, every[:, slot], precision=HIGHEST_PRECISION)
        for slot in range(len(back_modulations))
    ]


def finish(core_terms, bias_terms):
    matrix_grads = sum_over_data(sum_over_frames(core_terms))
    attend_bias, out_bias, expand_bias, shrink_bias, modulate_bias = bias_terms
    totals = lax.psum(
        (attend_bias, out_bias, expand_bias, shrink_bias, modulate_bias), ("dp", "sp")
    )
    data_index = lax.axis_index("dp")
    data_count = lax.axis_size("dp")
    bias_grads = tuple(
        (
            lax.dynamic_slice_in_dim(
                total_bias,
                data_index * (total_bias.shape[0] // data_count),
                total_bias.shape[0] // data_count,
            )
            for total_bias in totals
        )
    )
    return (matrix_grads, bias_grads)


def frames_to_patches(tensor):
    return lax.all_to_all(tensor, "sp", split_axis=2, concat_axis=1, tiled=True)


def patches_to_frames(tensor):
    return lax.all_to_all(tensor, "sp", split_axis=1, concat_axis=2, tiled=True)


def attention_scores(queries, key_rows, forms, allowed):
    scores = jnp.einsum(forms[0], queries, key_rows, preferred_element_type=jnp.float32) * HD ** (
        -0.5
    )
    if allowed is not None:
        scores = jnp.where(allowed, scores, -1e30)
    return scores


def block_forward(stream, modulation, core, biases, forms, allowed):
    attend_in, attend_out, expand, shrink = core
    attend_bias, out_bias, expand_bias, shrink_bias, modulate_bias = biases
    model_width = stream.shape[-1]
    pieces = [
        modulation[:, None, None, slot * model_width : (slot + 1) * model_width]
        for slot in range(6)
    ]
    normed = modulate(stream, pieces[0], pieces[1]).astype(jnp.bfloat16)
    bias_float = attend_bias.astype(jnp.float32)
    joined_bias = jnp.concatenate(
        [bias_float[:model_width], jnp.zeros((model_width,), jnp.float32), bias_float[model_width:]]
    )
    projected = (matmul(normed, attend_in) + joined_bias).astype(jnp.bfloat16)
    head_shape = projected.shape[:3] + (H, HD)
    queries = projected[..., :model_width].reshape(head_shape)
    key_rows = projected[..., model_width : 2 * model_width].reshape(head_shape)
    values = projected[..., 2 * model_width :].reshape(head_shape)
    scores = attention_scores(queries, key_rows, forms, allowed)
    highest = jnp.max(scores, axis=-1, keepdims=True)
    exponent = jnp.exp(scores - highest)
    denominator = jnp.sum(exponent, axis=-1, keepdims=True)
    softmax_probs = exponent / denominator
    logsum = highest + jnp.log(denominator)
    mixture = (
        jnp.einsum(
            forms[1], softmax_probs.astype(jnp.bfloat16), values, preferred_element_type=jnp.float32
        )
        .astype(jnp.bfloat16)
        .reshape(stream.shape)
    )
    attended = matmul(mixture, attend_out) + out_bias.astype(jnp.float32)
    middle = stream + pieces[2] * attended
    normed_second = modulate(middle, pieces[3], pieces[4]).astype(jnp.bfloat16)
    hidden = matmul(normed_second, expand) + expand_bias.astype(jnp.float32)
    activated = jax.nn.gelu(hidden, approximate=True).astype(jnp.bfloat16)
    branch = matmul(activated, shrink) + shrink_bias.astype(jnp.float32)
    result = middle + pieces[5] * branch
    kept = (
        pieces,
        normed,
        queries,
        key_rows,
        values,
        logsum,
        mixture,
        attended,
        middle,
        normed_second,
        hidden,
        activated,
        branch,
    )
    return (result, kept)


def block_backward(incoming, stream, core, forms, allowed, kept):
    attend_in, attend_out, expand, shrink = core
    (
        pieces,
        normed,
        queries,
        key_rows,
        values,
        logsum,
        mixture,
        attended,
        middle,
        normed_second,
        hidden,
        activated,
        branch,
    ) = kept
    model_width = stream.shape[-1]
    sequences = stream.shape[0]
    back_branch = (pieces[5] * incoming).astype(jnp.bfloat16)
    back_gate_second = per_sequence(incoming * branch)
    shrink_term = outer_product(activated, back_branch)
    shrink_bias_term = column_totals(back_branch)
    back_activated = back_matmul(back_branch, shrink)
    _, gelu_pull = jax.vjp(lambda tensor: jax.nn.gelu(tensor, approximate=True), hidden)
    back_hidden = gelu_pull(back_activated)[0].astype(jnp.bfloat16)
    expand_term = outer_product(normed_second, back_hidden)
    expand_bias_term = column_totals(back_hidden)
    back_normed_second = back_matmul(back_hidden, expand)
    _, second_pull = jax.vjp(modulate, middle, pieces[3], pieces[4])
    back_middle, back_shift_second, back_scale_second = second_pull(back_normed_second)
    back_middle = back_middle + incoming
    back_attended = (pieces[2] * back_middle).astype(jnp.bfloat16)
    back_gate_first = per_sequence(back_middle * attended)
    out_term = outer_product(mixture, back_attended)
    out_bias_term = column_totals(back_attended)
    back_mixture = (
        back_matmul(back_attended, attend_out).astype(jnp.bfloat16).reshape(queries.shape)
    )
    scores = attention_scores(queries, key_rows, forms, allowed)
    softmax_probs = jnp.exp(scores - logsum)
    back_probs = jnp.einsum(forms[0], back_mixture, values, preferred_element_type=jnp.float32)
    back_values = jnp.einsum(
        forms[2],
        softmax_probs.astype(jnp.bfloat16),
        back_mixture,
        preferred_element_type=jnp.float32,
    )
    row_delta = jnp.sum(softmax_probs * back_probs, axis=-1, keepdims=True)
    back_scores = (softmax_probs * (back_probs - row_delta)).astype(jnp.bfloat16)
    score_scale = HD ** (-0.5)
    back_queries = (
        jnp.einsum(forms[1], back_scores, key_rows, preferred_element_type=jnp.float32)
        * score_scale
    )
    back_keys = (
        jnp.einsum(forms[2], back_scores, queries, preferred_element_type=jnp.float32) * score_scale
    )
    flat_shape = stream.shape
    back_projected = jnp.concatenate(
        [
            back_queries.reshape(flat_shape),
            back_keys.reshape(flat_shape),
            back_values.reshape(flat_shape),
        ],
        axis=-1,
    ).astype(jnp.bfloat16)
    attend_in_term = outer_product(normed, back_projected)
    projected_totals = column_totals(back_projected)
    attend_bias_term = jnp.concatenate(
        [projected_totals[:model_width], projected_totals[2 * model_width :]]
    )
    back_normed = back_matmul(back_projected, attend_in)
    _, first_pull = jax.vjp(modulate, stream, pieces[0], pieces[1])
    back_stream, back_shift_first, back_scale_first = first_pull(back_normed)
    back_stream = back_stream + back_middle
    back_modulation = jnp.concatenate(
        [
            back_shift_first.reshape(sequences, model_width),
            back_scale_first.reshape(sequences, model_width),
            back_gate_first,
            back_shift_second.reshape(sequences, model_width),
            back_scale_second.reshape(sequences, model_width),
            back_gate_second,
        ],
        axis=1,
    )
    modulate_bias_term = jnp.sum(back_modulation, axis=0)
    core_terms = (attend_in_term, out_term, expand_term, shrink_term)
    bias_terms = (
        attend_bias_term,
        out_bias_term,
        expand_bias_term,
        shrink_bias_term,
        modulate_bias_term,
    )
    return (back_stream, core_terms, back_modulation, bias_terms)


def shards(
    inputs,
    timesteps,
    segment_ids,
    spatial_attend_in,
    spatial_attend_bias,
    spatial_attend_out,
    spatial_out_bias,
    spatial_expand,
    spatial_expand_bias,
    spatial_shrink,
    spatial_shrink_bias,
    spatial_modulate,
    spatial_modulate_bias,
    temporal_attend_in,
    temporal_attend_bias,
    temporal_attend_out,
    temporal_out_bias,
    temporal_expand,
    temporal_expand_bias,
    temporal_shrink,
    temporal_shrink_bias,
    temporal_modulate,
    temporal_modulate_bias,
    cotangent,
):
    condition_all = jax.nn.silu(sinusoid(timesteps)).astype(jnp.bfloat16)
    allowed = (segment_ids[:, :, None] == segment_ids[:, None, :])[:, None, None, :, :]
    spatial_core = (spatial_attend_in, spatial_attend_out, spatial_expand, spatial_shrink)
    spatial_biases = (
        spatial_attend_bias,
        spatial_out_bias,
        spatial_expand_bias,
        spatial_shrink_bias,
        spatial_modulate_bias,
    )
    temporal_core = (temporal_attend_in, temporal_attend_out, temporal_expand, temporal_shrink)
    temporal_biases = (
        temporal_attend_bias,
        temporal_out_bias,
        temporal_expand_bias,
        temporal_shrink_bias,
        temporal_modulate_bias,
    )
    stream = inputs.astype(jnp.float32)
    modulations = modulation_of(condition_all, (spatial_modulate, temporal_modulate))
    core, biases = collect(spatial_core, spatial_biases)
    modulation = modulations[0] + biases[4].astype(jnp.float32)
    spatial_core = core
    spatial_out, spatial_kept = block_forward(stream, modulation, core, biases, SPATIAL_FORMS, None)
    passed = frames_to_patches(spatial_out.astype(jnp.bfloat16)).astype(jnp.float32)
    core, biases = collect(temporal_core, temporal_biases)
    modulation = modulations[1] + biases[4].astype(jnp.float32)
    temporal_out, temporal_kept = block_forward(
        passed, modulation, core, biases, TEMPORAL_FORMS, allowed
    )
    output = patches_to_frames(temporal_out.astype(jnp.bfloat16))
    incoming = frames_to_patches(cotangent).astype(jnp.float32)
    back_passed, core_terms, back_temporal, bias_terms = block_backward(
        incoming, passed, core, TEMPORAL_FORMS, allowed, temporal_kept
    )
    temporal_grads, temporal_bias_grads = finish(core_terms, bias_terms)
    back_spatial = patches_to_frames(back_passed.astype(jnp.bfloat16)).astype(jnp.float32)
    back_inputs, core_terms, back_spatial_modulation, bias_terms = block_backward(
        back_spatial, stream, spatial_core, SPATIAL_FORMS, None, spatial_kept
    )
    spatial_grads, spatial_bias_grads = finish(core_terms, bias_terms)
    modulate_grads = modulate_gradients(
        condition_all, (back_spatial_modulation, back_temporal), spatial_modulate.shape[0]
    )
    return (
        output,
        back_inputs.astype(jnp.bfloat16),
        spatial_grads[0],
        spatial_bias_grads[0],
        spatial_grads[1],
        spatial_bias_grads[1],
        spatial_grads[2],
        spatial_bias_grads[2],
        spatial_grads[3],
        spatial_bias_grads[3],
        modulate_grads[0],
        spatial_bias_grads[4],
        temporal_grads[0],
        temporal_bias_grads[0],
        temporal_grads[1],
        temporal_bias_grads[1],
        temporal_grads[2],
        temporal_bias_grads[2],
        temporal_grads[3],
        temporal_bias_grads[3],
        modulate_grads[1],
        temporal_bias_grads[4],
    )


def fits(mesh):
    return mesh.shape["dp"] == 4 and mesh.shape["sp"] == 8


def condition_rows(timesteps, rows):
    half = D // 2
    index = lax.axis_index("dp") * rows + jnp.arange(rows, dtype=jnp.int32)
    place = (index % half).astype(jnp.float32)
    frequencies = jnp.exp(-math.log(10000.0) * place / half)
    angles = timesteps.astype(jnp.float32)[:, None] * frequencies[None, :]
    wave = jnp.where((index < half)[None, :], jnp.cos(angles), jnp.sin(angles))
    return jax.nn.silu(wave).astype(jnp.bfloat16)


def fast_shards(
    inputs,
    timesteps,
    segment_ids,
    spatial_attend_in,
    spatial_attend_bias,
    spatial_attend_out,
    spatial_out_bias,
    spatial_expand,
    spatial_expand_bias,
    spatial_shrink,
    spatial_shrink_bias,
    spatial_modulate,
    spatial_modulate_bias,
    temporal_attend_in,
    temporal_attend_bias,
    temporal_attend_out,
    temporal_out_bias,
    temporal_expand,
    temporal_expand_bias,
    temporal_shrink,
    temporal_shrink_bias,
    temporal_modulate,
    temporal_modulate_bias,
    cotangent,
):
    def small(attend, out, expand, shrink, modulate):
        rest = jnp.zeros((2 * D - modulate.shape[0],), jnp.bfloat16)
        return [attend, out, shrink, expand, modulate, rest]

    pack = (
        jnp.concatenate(
            small(
                spatial_attend_bias,
                spatial_out_bias,
                spatial_expand_bias,
                spatial_shrink_bias,
                spatial_modulate_bias,
            )
            + small(
                temporal_attend_bias,
                temporal_out_bias,
                temporal_expand_bias,
                temporal_shrink_bias,
                temporal_modulate_bias,
            )
        )
        .astype(jnp.float32)
        .reshape(8, D)
    )
    cond = jnp.pad(condition_rows(timesteps, spatial_modulate.shape[0]), ((0, 4), (0, 0)))
    cond_columns = cond.astype(jnp.float32).T
    x = inputs.reshape(TOKENS, WIDTH)
    spatial_p, spatial_s, mods, biases, incoming = first_gather(
        jnp.concatenate([spatial_attend_in, spatial_attend_out, spatial_expand], axis=1),
        spatial_shrink.T,
        pack,
        cond,
        (spatial_modulate, temporal_modulate),
        cotangent.reshape(TOKENS, WIDTH),
    )
    first = block_call(x, mods, biases, 0, spatial_p, spatial_s)
    temporal_p, temporal_s, passed = second_gather(
        jnp.concatenate([temporal_attend_in, temporal_attend_out, temporal_expand], axis=1),
        temporal_shrink.T,
        first["y"],
    )
    t = block_call(
        passed, mods, biases, 1, temporal_p, temporal_s, segments=segment_ids, g=incoming
    )
    packed_t, turned_t, modulate_t, totals_t, output, back_spatial = scatter_call(
        gradient_slabs(t), t["bias_grad"], t["mod_grad"], cond_columns, (t["y"], t["back_x"]), 2
    )
    b = block_call(x, mods, biases, 0, spatial_p, spatial_s, g=back_spatial, give_y=False)
    packed_s, turned_s, modulate_s, totals_s = scatter_call(
        gradient_slabs(b), b["bias_grad"], b["mod_grad"], cond_columns, (), 3
    )
    outs = unpack(packed_s, turned_s, totals_s, packed_t, turned_t, totals_t)
    return (
        output.reshape(inputs.shape),
        b["back_x"].reshape(inputs.shape),
        *outs[:8],
        modulate_s,
        outs[8],
        *outs[9:17],
        modulate_t,
        outs[17],
    )


def solution(mesh):
    placed = (
        P("dp", "sp", None, None),
        P(),
        P("dp", None),
        P("dp", "sp"),
        P("dp"),
        P("dp", "sp"),
        P("dp"),
        P("dp", "sp"),
        P("dp"),
        P("dp", "sp"),
        P("dp"),
        P("dp", "sp"),
        P("dp"),
        P("dp", "sp"),
        P("dp"),
        P("dp", "sp"),
        P("dp"),
        P("dp", "sp"),
        P("dp"),
        P("dp", "sp"),
        P("dp"),
        P("dp", "sp"),
        P("dp"),
        P("dp", "sp", None, None),
    )
    return jax.shard_map(
        fast_shards if fits(mesh) else shards,
        mesh=mesh,
        in_specs=placed,
        out_specs=(
            P("dp", "sp", None, None),
            P("dp", "sp", None, None),
            P("dp", "sp"),
            P("dp"),
            P("dp", "sp"),
            P("dp"),
            P("dp", "sp"),
            P("dp"),
            P("dp", "sp"),
            P("dp"),
            P("dp", "sp"),
            P("dp"),
            P("dp", "sp"),
            P("dp"),
            P("dp", "sp"),
            P("dp"),
            P("dp", "sp"),
            P("dp"),
            P("dp", "sp"),
            P("dp"),
            P("dp", "sp"),
            P("dp"),
        ),
        check_vma=False,
    )
```

```python
import functools
import math

import jax
import jax.numpy as jnp
from jax import lax
from jax.experimental import pallas as pl
from jax.experimental.pallas import tpu as pltpu
from jax.sharding import PartitionSpec as P

D = 1152
H = 16
HD = 72


EPSILON = 1e-06
HIGHEST_PRECISION = lax.Precision.HIGHEST
SPATIAL_FORMS = ("sabhe,sache->sahbc", "sahbc,sache->sabhe", "sahbc,sabhe->sache")
TEMPORAL_FORMS = ("sabhe,scbhe->sbhac", "sbhac,scbhe->sabhe", "sbhac,sabhe->scbhe")


MESH = pl.DeviceIdType.MESH
TOKENS = 256
WIDTH = 1152
CHUNKS = (
    ("p", 0, 144, "zxy"),
    ("p", 144, 144, "zyx"),
    ("s", 0, 48, "xyz"),
    ("s", 48, 48, "yxz"),
    ("s", 96, 48, "zxy"),
)
RELS = sorted(
    [(rx, ry, dz) for rx in (0, 1) for ry in (0, 1) for dz in range(-3, 4)],
    key=lambda r: (r[0] + r[1] + abs(r[2]), r != (0, 0, 0)),
)


class Place:
    def __init__(self):
        self.d, self.s = lax.axis_index("dp"), lax.axis_index("sp")
        self.x, self.c = self.d // 2, self.d % 2
        self.z, self.y = self.s // 2, self.s % 2

    def at(self, rel):
        rx, ry, dz = rel
        return (1 - self.x if rx else self.x, self.z + dz, 1 - self.y if ry else self.y)

    def exists(self, dz):
        return None if dz == 0 else ((self.z + dz >= 0) & (self.z + dz <= 3))

    def neighbour(self, direction):
        x, c, z, y = self.x, self.c, self.z, self.y
        return {
            "x": lambda: dev(1 - x, c, z, y),
            "y": lambda: dev(x, c, z, 1 - y),
            "u": lambda: dev(x, c, z + 1, y),
            "d": lambda: dev(x, c, z - 1, y),
            "c": lambda: dev(x, 1 - c, z, y),
        }[direction]()

    def has(self, direction):
        return {"u": lambda: self.z < 3, "d": lambda: self.z > 0}.get(direction, lambda: None)()


def dev(x, c, z, y):
    return (x * 2 + c, z * 2 + y)


def blk(b):
    return (b[0] * 4 + b[1]) * 2 + b[2]


def both(a, b):
    return b if a is None else (a if b is None else (a & b))


def guarded(cond, f):
    if cond is None:
        f()
    else:
        pl.when(cond)(f)


def greet(me):
    barrier = pltpu.get_barrier_semaphore()
    for k in range(1, 4):
        pl.semaphore_signal(
            barrier, inc=1, device_id=((me.d + k) % 4, me.s), device_id_type=MESH
        )
    for k in range(1, 8):
        pl.semaphore_signal(
            barrier, inc=1, device_id=(me.d, (me.s + k) % 8), device_id_type=MESH
        )
    pl.semaphore_wait(barrier, 10)


def links(rel, order):
    nz = {"x": rel[0], "y": rel[1], "z": rel[2]}
    last = max([i for i in range(3) if nz[order[i]]], default=-1)
    out = []
    for i, dim in enumerate(order):
        if i > last:
            out += ["u", "d"] if dim == "z" else [dim]
        elif i == last and dim == "z":
            out += ["u"] if rel[2] < 0 else ["d"]
    parent = None
    if last >= 0:
        parent = order[last] if order[last] != "z" else ("d" if rel[2] < 0 else "u")
    return out, parent


class Gather:
    SEMS = (
        ((len(CHUNKS), 16), (len(CHUNKS), 16), (len(CHUNKS), 5, 16), (len(CHUNKS),))
    )

    def __init__(self, me, p_in, s_in, p_out, s_out, arrived, crossed, sent, local):
        self.me, self.ins, self.outs = me, {"p": p_in, "s": s_in}, {"p": p_out, "s": s_out}
        self.arrived, self.crossed, self.sent, self.local = arrived, crossed, sent, local

    def own(self, ch):
        return self.ins[ch[0]].at[pl.ds(ch[1], ch[2]), :]

    def place(self, ch, b, core):
        d, s = b[0] * 2 + core, b[1] * 2 + b[2]
        if ch[0] == "p":
            return self.outs["p"].at[s, pl.ds(d * 288 + ch[1], ch[2]), :]
        return self.outs["s"].at[d, pl.ds(s * 144 + ch[1], ch[2]), :]

    def copy(self, k, rel, direction):
        me, ch = self.me, CHUNKS[k]
        b = me.at(rel)
        there = self.place(ch, b, me.c)
        return pltpu.make_async_remote_copy(
            src_ref=self.own(ch) if rel == (0, 0, 0) else there,
            dst_ref=there,
            send_sem=self.sent.at[k, "xyudc".index(direction), blk(b)],
            recv_sem=(self.crossed if direction == "c" else self.arrived).at[k, blk(b)],
            device_id=me.neighbour(direction),
            device_id_type=MESH,
        )

    def ends(self, k, rel):
        return links(rel, CHUNKS[k][3])[0] + ["c"]

    def event(self, k, rel):
        me, ch = self.me, CHUNKS[k]

        def body():
            if rel == (0, 0, 0):
                pltpu.make_async_copy(
                    self.own(ch), self.place(ch, me.at(rel), me.c), self.local.at[k]
                ).start()
            else:
                self.wait_in(k, rel, me.c, self.arrived)
            for direction in self.ends(k, rel):
                guarded(me.has(direction), lambda: self.copy(k, rel, direction).start())

        guarded(me.exists(rel[2]), body)

    def wait_in(self, k, rel, core, sems):
        b, ch = self.me.at(rel), CHUNKS[k]
        pltpu.make_async_copy(self.own(ch), self.place(ch, b, core), sems.at[k, blk(b)]).wait()

    def events(self):
        return [
            functools.partial(self.event, k, rel) for rel in RELS for k in range(len(CHUNKS))
        ]

    def finish(self):
        me = self.me
        for k, ch in enumerate(CHUNKS):
            pltpu.make_async_copy(
                self.own(ch), self.place(ch, me.at((0, 0, 0)), me.c), self.local.at[k]
            ).wait()
        for rel in RELS:

            def body():
                for k in range(len(CHUNKS)):
                    self.wait_in(k, rel, 1 - me.c, self.crossed)
                    for direction in self.ends(k, rel):
                        guarded(
                            me.has(direction), lambda: self.copy(k, rel, direction).wait_send()
                        )

            guarded(me.exists(rel[2]), body)


def slots_of(order):
    base, total, count = {}, 0, 1
    for dim in order:
        base[dim] = total
        total += count * (5 if dim == "z" else 1)
        count *= 4 if dim == "z" else 2
    return base, total


ROW_OF = [(ch[1] if ch[0] == "p" else 288 + ch[1]) for ch in CHUNKS]
SLOTS = [slots_of(ch[3])[1] for ch in CHUNKS]
SLOT_ROW = [sum(n * ch[2] for n, ch in zip(SLOTS[:k], CHUNKS)) for k in range(len(CHUNKS))]
SLOT_ROWS = sum(n * ch[2] for n, ch in zip(SLOTS, CHUNKS))


class Scatter:
    SEMS = (
        (len(CHUNKS), 16),
        (len(CHUNKS), 16),
        (len(CHUNKS), 16),
        (len(CHUNKS), max(SLOTS)),
        (len(CHUNKS), 16),
    )

    def __init__(self, me, p_in, s_in, p_out, s_out, acc, core, got, *sems):
        self.me, self.ins, self.outs = me, {"p": p_in, "s": s_in}, {"p": p_out, "s": s_out}
        self.acc, self.core, self.got = acc, core, got
        self.loaded, self.crossed, self.cross_sent, self.arrived, self.sent = sems

    def term(self, ch, b, core):
        d, s = b[0] * 2 + core, b[1] * 2 + b[2]
        if ch[0] == "p":
            return self.ins["p"].at[s, pl.ds(d * 288 + ch[1], ch[2]), :]
        return self.ins["s"].at[d, pl.ds(s * 144 + ch[1], ch[2]), :]

    def held(self, ref, k, b):
        return ref.at[blk(b), pl.ds(ROW_OF[k], CHUNKS[k][2]), :]

    def load(self, k, b):
        return pltpu.make_async_copy(
            self.term(CHUNKS[k], b, self.me.c), self.held(self.acc, k, b), self.loaded.at[k, blk(b)]
        )

    def cross(self, k, b):
        return pltpu.make_async_remote_copy(
            src_ref=self.term(CHUNKS[k], b, 1 - self.me.c),
            dst_ref=self.held(self.core, k, b),
            send_sem=self.cross_sent.at[k, blk(b)],
            recv_sem=self.crossed.at[k, blk(b)],
            device_id=self.me.neighbour("c"),
            device_id_type=MESH,
        )

    def slot(self, k, b, direction, z):
        order = CHUNKS[k][3]
        base, _ = slots_of(order)
        dim = "z" if direction in "ud" else direction
        coord = {"x": (b[0], 2), "y": (b[2], 2), "z": (b[1], 4)}
        index = 0
        for d in order[: order.index(dim)]:
            index = index * coord[d][1] + coord[d][0]
        if dim == "z":
            inner = b[1] if direction == "d" else jnp.where(b[1] == z, 4, b[1])
            index = index * 5 + inner
        return base[dim] + index

    def got_at(self, k, j):
        n = CHUNKS[k][2]
        return self.got.at[pl.ds(pl.multiple_of(SLOT_ROW[k] + j * n, 16), n), :]

    def send(self, k, b, direction):
        z = self.me.z + {"u": 1, "d": -1}.get(direction, 0)
        j = self.slot(k, b, {"x": "x", "y": "y", "u": "d", "d": "u"}[direction], z)
        return pltpu.make_async_remote_copy(
            src_ref=self.held(self.acc, k, b),
            dst_ref=self.got_at(k, j),
            send_sem=self.sent.at[k, blk(b)],
            recv_sem=self.arrived.at[k, j],
            device_id=self.me.neighbour(direction),
            device_id_type=MESH,
        )

    def add(self, k, b, messages, final):
        ch, i = CHUNKS[k], blk(b)

        @pl.loop(0, ch[2] // 16)
        def _(t):
            r = pl.ds(pl.multiple_of(ROW_OF[k] + t * 16, 16), 16)
            v = self.acc[i, r, :].astype(jnp.float32) + self.core[i, r, :].astype(jnp.float32)
            for cond, j in messages:
                at = pl.ds(pl.multiple_of(SLOT_ROW[k] + j * ch[2] + t * 16, 16), 16)
                q = self.got[at, :].astype(jnp.float32)
                v = v + (q if cond is None else jnp.where(cond, q, 0.0))
            if final is None:
                self.acc[i, r, :] = v.astype(jnp.bfloat16)
            else:
                final[pl.ds(pl.multiple_of(ch[1] + t * 16, 16), 16), :] = v

    def begin(self):
        for rel in RELS[::-1]:

            def body():
                b = self.me.at(rel)
                for k in range(len(CHUNKS)):
                    self.load(k, b).start()
                    self.cross(k, b).start()

            guarded(self.me.exists(rel[2]), body)

    def event(self, k, rel):
        me, ch = self.me, CHUNKS[k]

        def body():
            b = me.at(rel)
            children, parent = links(rel, ch[3])
            self.load(k, b).wait()
            held = self.held(self.core, k, b)
            pltpu.make_async_copy(held, held, self.crossed.at[k, blk(b)]).wait()
            messages = []
            for direction in children:
                cond, j = me.has(direction), self.slot(k, b, direction, me.z)

                def wait():
                    at = self.got_at(k, j)
                    pltpu.make_async_copy(at, at, self.arrived.at[k, j]).wait()

                guarded(cond, wait)
                messages.append((cond, j))
            self.add(k, b, messages, None if parent else self.outs[ch[0]])
            if parent:
                self.send(k, b, parent).start()

        guarded(me.exists(rel[2]), body)

    def events(self):
        return [
            functools.partial(self.event, k, rel) for rel in RELS[::-1] for k in range(len(CHUNKS))
        ]

    def finish(self):
        for rel in RELS:

            def body():
                b = self.me.at(rel)
                for k, ch in enumerate(CHUNKS):
                    _, parent = links(rel, ch[3])
                    if parent:
                        self.send(k, b, parent).wait_send()
                    self.cross(k, b).wait_send()

            guarded(self.me.exists(rel[2]), body)


class Exchange:
    def __init__(self, me, source, target, sent, arrived, local):
        self.me, self.source, self.target = me, source, target
        self.sent, self.arrived, self.local = sent, arrived, local

    def rows(self, ref, s):
        return ref.at[pl.ds(pl.multiple_of(s * 32, 32), 32), :]

    def copy(self, k):
        me = self.me
        other = (me.s + k) % 8
        return pltpu.make_async_remote_copy(
            src_ref=self.rows(self.source, other),
            dst_ref=self.rows(self.target, me.s),
            send_sem=self.sent.at[k],
            recv_sem=self.arrived.at[k],
            device_id=(me.d, other),
            device_id_type=MESH,
        )

    def stay(self):
        return pltpu.make_async_copy(
            self.rows(self.source, self.me.s), self.rows(self.target, self.me.s), self.local
        )

    def start(self):
        self.stay().start()
        for k in range(1, 8):
            self.copy(k).start()

    def finish(self):
        self.stay().wait()
        for k in range(1, 8):
            at = self.rows(self.target, (self.me.s - k + 8) % 8)
            pltpu.make_async_copy(at, at, self.arrived.at[k]).wait()
            self.copy(k).wait_send()


class Spread:
    def __init__(self, me, axis, source, target, sent, arrived, each):
        self.me, self.axis, self.source, self.target = me, axis, source, target
        self.sent, self.arrived, self.each = sent, arrived, each
        self.n = 4 if axis == "dp" else 8
        self.i = me.d if axis == "dp" else me.s

    def copy(self, k):
        other = (self.i + k) % self.n
        return pltpu.make_async_remote_copy(
            src_ref=self.source.at[other] if self.each else self.source,
            dst_ref=self.target.at[self.i],
            send_sem=self.sent.at[k],
            recv_sem=self.arrived.at[k],
            device_id=(other, self.me.s) if self.axis == "dp" else (self.me.d, other),
            device_id_type=MESH,
        )

    def start(self):
        for k in range(1, self.n):
            self.copy(k).start()
        self.target[self.i] = self.source[self.i] if self.each else self.source[...]

    def finish(self):
        for k in range(1, self.n):
            at = self.target.at[(self.i - k + self.n) % self.n]
            pltpu.make_async_copy(at, at, self.arrived.at[k]).wait()
            self.copy(k).wait_send()


def pieces(start, length, width=WIDTH):
    out, done = [], 0
    while done < length:
        row, column = divmod(start + done, width)
        n = min(width - column, length - done)
        out.append((row, column, n, done))
        done += n
    return out


def interleave(events, stages):
    cuts = sorted((int(share * len(events)), i) for i, (share, _) in enumerate(stages))
    done = 0
    for cut, i in cuts:
        for event in events[done:cut]:
            event()
        done = max(done, cut)
        stages[i][1]()
    for event in events[done:]:
        event()


def dma_sems(*shapes):
    return [pltpu.SemaphoreType.DMA(shape) for shape in shapes]


ANY_SPEC = pl.BlockSpec(memory_space=pl.ANY)
VMEM_SPEC = pl.BlockSpec(memory_space=pltpu.VMEM)
SLABS = (
    jax.ShapeDtypeStruct((8, WIDTH, WIDTH), jnp.bfloat16),
    jax.ShapeDtypeStruct((4, WIDTH, WIDTH), jnp.bfloat16),
)
STREAM = jax.ShapeDtypeStruct((TOKENS, WIDTH), jnp.bfloat16)


def first_gather_kernel(
    p_in, s_in, pack, cond, weight0, weight1, cot, p_out, s_out, mod_out, bias_out, incoming,
    packs, part, parts, whole, wholes, *sems,
):
    me = Place()
    gather = Gather(me, p_in, s_in, p_out, s_out, *sems[:4])
    exchange = Exchange(me, cot, incoming, *sems[4:7])
    biases = Spread(me, "dp", pack, packs, *sems[7:9], False)
    terms = Spread(me, "dp", part, parts, *sems[9:11], True)
    columns = Spread(me, "sp", whole, wholes, *sems[11:13], False)
    greet(me)

    def begin():
        biases.start()
        for i, weight in enumerate((weight0, weight1)):
            product = jnp.dot(cond[...], weight[...], preferred_element_type=jnp.float32)
            for q in range(4):
                part[q, i : i + 1, :] = product[q : q + 1, :]
        terms.start()
        exchange.start()

    def middle():
        terms.finish()
        whole[...] = jnp.sum(parts[...], axis=0)
        columns.start()

    def end():
        columns.finish()
        biases.finish()
        exchange.finish()
        for i in range(2):
            mod_out[i] = jnp.zeros((8, WIDTH), jnp.float32)
            for s in range(8):
                for row, column, n, at in pieces(864 * s, 864):
                    mod_out[i, row : row + 1, column : column + n] = wholes[
                        s, i : i + 1, at : at + n
                    ]
            for k in range(4):
                for first, n_all in ((0, WIDTH), (WIDTH, 576)):
                    source = 4 * i + 2 + first // WIDTH
                    for row, column, n, at in pieces(1728 * k + first, n_all):
                        mod_out[i, row : row + 1, column : column + n] += packs[
                            k, source : source + 1, at : at + n
                        ]
                top = 4 * i
                bias_out[i, k // 2 : k // 2 + 1, 576 * (k % 2) : 576 * (k % 2 + 1)] = packs[
                    k, top : top + 1, 0:576
                ]
                for row, at in ((2, 576), (3, 864)):
                    bias_out[i, row : row + 1, 288 * k : 288 * (k + 1)] = packs[
                        k, top : top + 1, at : at + 288
                    ]
                bias_out[i, 4 + k : 5 + k, :] = packs[k, top + 1 : top + 2, :]

    events = gather.events()
    own = len(CHUNKS)
    interleave(events, [(own / len(events), begin), (0.3, middle), (0.8, end)])
    gather.finish()


def first_gather(p, s, pack, cond, weights, cotangent):
    return pl.pallas_call(
        first_gather_kernel,
        out_shape=SLABS
        + (
            jax.ShapeDtypeStruct((2, 8, WIDTH), jnp.float32),
            jax.ShapeDtypeStruct((2, 8, WIDTH), jnp.float32),
            STREAM,
        ),
        in_specs=[ANY_SPEC] * 2 + [VMEM_SPEC] * 4 + [ANY_SPEC],
        out_specs=(ANY_SPEC, ANY_SPEC, VMEM_SPEC, VMEM_SPEC, ANY_SPEC),
        scratch_shapes=[
            pltpu.VMEM((4, 8, WIDTH), jnp.float32),
            pltpu.VMEM((4, 8, 864), jnp.float32),
            pltpu.VMEM((4, 8, 864), jnp.float32),
            pltpu.VMEM((8, 864), jnp.float32),
            pltpu.VMEM((8, 8, 864), jnp.float32),
        ]
        + dma_sems(*Gather.SEMS, (8,), (8,), (), (4,), (4,), (4,), (4,), (8,), (8,)),
        compiler_params=pltpu.CompilerParams(collective_id=0, has_side_effects=True),
        name="first_gather",
    )(p, s, pack, cond, *weights, cotangent)


def scatter_kernel(streams, *refs):
    p_in, s_in, bias_grad, mod_grad, cond = refs[:5]
    sources = refs[5 : 5 + streams]
    refs = refs[5 + streams :]
    p_out, s_out, weight_grad, totals = refs[:4]
    targets = refs[4 : 4 + streams]
    refs = refs[4 + streams :]
    acc, core, got, small, small_in, row_sum, row_in, total = refs[:8]
    sems = refs[8:]
    me = Place()
    scatter = Scatter(me, p_in, s_in, p_out, s_out, acc, core, got, *sems[:5])
    over_frames = Spread(me, "sp", small, small_in, *sems[5:7], True)
    over_data = Spread(me, "dp", row_sum, row_in, *sems[7:9], False)
    over_all = Spread(me, "sp", total, totals, *sems[9:11], False)
    exchanges = [
        Exchange(me, source, target, *sems[11 + 3 * i : 14 + 3 * i])
        for i, (source, target) in enumerate(zip(sources, targets))
    ]
    greet(me)
    for exchange in exchanges:
        exchange.start()
    scatter.begin()

    def begin():
        small[...] = jnp.zeros(small.shape, jnp.float32)
        for s in range(8):
            small[s, 0:1, :] = bias_grad[s : s + 1, :]
            for row, column, n, at in pieces(864 * s, 864):
                small[s, 1:2, at : at + n] = mod_grad[row : row + 1, column : column + n]
        over_frames.start()

    def second():
        over_frames.finish()
        row_sum[...] = jnp.sum(small_in[...], axis=0)
        over_data.start()

    def third():
        over_data.finish()
        total[...] = jnp.sum(row_in[...], axis=0)
        over_all.start()
        for t in range(9):
            r = slice(32 * t, 32 * (t + 1))
            v = cond[r, 0:1] * row_in[0, 1:2, 0:864]
            for q in range(1, 4):
                v = v + cond[r, q : q + 1] * row_in[q, 1:2, 0:864]
            weight_grad[r, :] = v

    def fourth():
        over_all.finish()
        for exchange in exchanges:
            exchange.finish()

    interleave(
        scatter.events(), [(0.05, begin), (0.3, second), (0.5, third), (0.8, fourth)]
    )
    scatter.finish()


def scatter_call(slabs, bias_grad, mod_grad, cond, streams, collective_id):
    n = len(streams)
    block = pltpu.VMEM((16, 432, WIDTH), jnp.bfloat16)
    rows = jax.ShapeDtypeStruct
    return pl.pallas_call(
        functools.partial(scatter_kernel, n),
        out_shape=[
            rows((288, WIDTH), jnp.float32),
            rows((144, WIDTH), jnp.float32),
            rows((288, 864), jnp.float32),
            rows((8, 8, WIDTH), jnp.float32),
        ]
        + [STREAM] * n,
        in_specs=[ANY_SPEC] * 2 + [VMEM_SPEC] * 3 + [ANY_SPEC] * n,
        out_specs=[VMEM_SPEC] * 4 + [ANY_SPEC] * n,
        scratch_shapes=[block, block, pltpu.VMEM((SLOT_ROWS, WIDTH), jnp.bfloat16)]
        + [
            pltpu.VMEM(shape, jnp.float32)
            for shape in ((8, 8, WIDTH), (8, 8, WIDTH), (8, WIDTH), (4, 8, WIDTH), (8, WIDTH))
        ]
        + dma_sems(*Scatter.SEMS, (8,), (8,), (4,), (4,), (8,), (8,), *([(8,), (8,), ()] * n)),
        compiler_params=pltpu.CompilerParams(
            collective_id=collective_id, has_side_effects=True, vmem_limit_bytes=60 << 20
        ),
        name="first_scatter" if n else "second_scatter",
    )(*slabs, bias_grad, mod_grad, cond, *streams)


def unpack_kernel(*refs):
    ins, outs = refs[:6], refs[6:]
    d = lax.axis_index("dp")
    for i in range(2):
        packed, turned, totals = ins[3 * i : 3 * i + 3]
        a_in, a_bias, a_out, o_bias, expand, e_bias, shrink, s_bias, m_bias = outs[
            9 * i : 9 * i + 9
        ]
        a_in[...] = packed[:, 0:432]
        a_out[...] = packed[:, 432:576]
        expand[...] = packed[:, 576:1152]
        shrink[...] = turned[...].T
        for k in range(4):

            @pl.when(d == k)
            def _():
                half = 576 * (k % 2)
                a_bias[...] = totals[k // 2, 0:1, half : half + 576]
                o_bias[...] = totals[2, 0:1, 288 * k : 288 * (k + 1)]
                s_bias[...] = totals[3, 0:1, 288 * k : 288 * (k + 1)]
                e_bias[...] = totals[4 + k, 0:1, :]
                for s in (2 * k, 2 * k + 1):
                    to = 864 * (s % 2)
                    m_bias[:, to : to + 864] = totals[s, 1:2, 0:864]


def unpack(*grads):
    shapes = [(288, 432), (1, 576), (288, 144), (1, 288), (288, 576), (1, 1152), (1152, 144)]
    shapes += [(1, 288), (1, 1728)]
    outs = pl.pallas_call(
        unpack_kernel,
        out_shape=[jax.ShapeDtypeStruct(shape, jnp.float32) for shape in shapes * 2],
        in_specs=[VMEM_SPEC] * 6,
        out_specs=[VMEM_SPEC] * 18,
        compiler_params=pltpu.CompilerParams(vmem_limit_bytes=32 << 20),
        name="unpack",
    )(*grads)
    return [out.reshape(-1) if out.shape[0] == 1 else out for out in outs]


SCALE = HD ** (-0.5)
NEGATIVE = -1e30


def dot(a, b):
    return lax.dot_general(a, b, (((1,), (0,)), ((), ())), preferred_element_type=jnp.float32)


def dot_nt(a, b):
    return lax.dot_general(a, b, (((1,), (1,)), ((), ())), preferred_element_type=jnp.float32)


def dot_tn(a, b):
    return lax.dot_general(a, b, (((0,), (0,)), ((), ())), preferred_element_type=jnp.float32)


def by_rows(body, step=32):
    @pl.loop(0, TOKENS // step)
    def _(i):
        body(pl.ds(pl.multiple_of(i * step, step), step))


def statistics(v):
    centered = v - jnp.mean(v, axis=1, keepdims=True)
    scale = lax.rsqrt(jnp.mean(centered * centered, axis=1, keepdims=True) + EPSILON)
    return centered * scale, scale


def fold(v):
    return jnp.sum(v.reshape(v.shape[0] // 8, 8, v.shape[1]), axis=0)


def gelu_both(h):
    c, a = math.sqrt(2.0 / math.pi), 0.044715
    square = h * h
    t = jnp.tanh(c * h * (1.0 + a * square))
    half = 0.5 * (1.0 + t)
    return h * half, half + 0.5 * h * (1.0 - t * t) * (c * (1.0 + 3.0 * a * square))


WIN_IN, WIN_OUT, WIN_EXP = slice(0, 512), slice(384, 640), slice(512, 1152)


def forward_stages(e, y):
    mod = e.mod
    shift1, scale1, gate1 = [lambda i=i: mod[i : i + 1, :] for i in range(3)]
    shift2, scale2, gate2 = [lambda i=i: mod[i : i + 1, :] for i in range(3, 6)]

    def normalize():
        e.bslab[...] = jnp.zeros(e.bslab.shape, jnp.float32)
        for s in range(8):
            for row, first in ((0, 0), (1, 2 * WIDTH)):
                lo, hi = max(432 * s, first), min(432 * (s + 1), first + WIDTH)
                if lo < hi:
                    e.bslab[s, 0:1, lo - 432 * s : hi - 432 * s] = e.bias[
                        row : row + 1, lo - first : hi - first
                    ]

        def rows(r):
            n, _ = statistics(e.x[r, :].astype(jnp.float32))
            e.normed[r, :] = (n * (1.0 + scale1()) + shift1()).astype(jnp.bfloat16)

        by_rows(rows)

    def project(first):
        @pl.loop(first, first + 4)
        def _(s):
            e.wait_p(s)
            v = dot(e.normed[...], e.pv[s, :, WIN_IN]) + e.bslab[s, 0:1, :]
            for j in range(6):
                e.heads[6 * s + j] = v[:, HD * j : HD * (j + 1)].astype(jnp.bfloat16)

    def attend(first):
        @pl.loop(first, first + 4)
        def _(h):
            probs = attention_probs(e, h)
            e.mh[h] = dot(probs.astype(jnp.bfloat16), e.heads[2 * H + h]).astype(jnp.bfloat16)

    def join():
        for h in range(H):
            e.mixture[:, HD * h : HD * (h + 1)] = e.mh[h]
        for s in range(8):
            v = dot(e.mixture[...], e.pv[s, :, WIN_OUT])
            e.attended[:, 144 * s : 144 * (s + 1)] = v[:, 48:192]

    def middle():
        def rows(r):
            attended = e.attended[r, :] + e.bias[2:3, :]
            e.attended[r, :] = attended
            middle = e.x[r, :].astype(jnp.float32) + gate1() * attended
            e.middle[r, :] = middle
            n, _ = statistics(middle)
            e.normed2[r, :] = (n * (1.0 + scale2()) + shift2()).astype(jnp.bfloat16)

        by_rows(rows)
        e.branch[...] = jnp.zeros(e.branch.shape, jnp.float32)

    def expand(d):
        for half in range(2):
            v = dot(e.normed2[...], e.pv[2 * d + half, :, WIN_EXP])
            e.tmp[:, 576 * half : 576 * (half + 1)] = v[:, 64:640]

        def rows(r):
            value, slope = gelu_both(e.tmp[r, :] + e.bias[pl.ds(4 + d, 1), :])
            e.act[d, r, :] = value.astype(jnp.bfloat16)
            if e.slope is not None:
                e.slope[d, r, :] = slope

        by_rows(rows)

    def shrink(d):
        e.wait_s(d)
        e.branch[...] += dot_nt(e.act[d], e.sv[d])

    def mlp(first, count):
        @pl.loop(first, first + count)
        def _(d):
            expand(d)
            shrink(d)

    def close():
        def rows(r):
            branch = e.branch[r, :] + e.bias[3:4, :]
            e.branch[r, :] = branch
            if y is not None:
                y[r, :] = (e.middle[r, :] + gate2() * branch).astype(jnp.bfloat16)

        by_rows(rows)

    part = functools.partial
    return (
        [normalize, part(project, 0), part(project, 4)]
        + [part(attend, h) for h in range(0, H, 4)]
        + [join, middle]
        + [part(mlp, d, 1) for d in range(4)]
        + [close]
    )


def attention_probs(e, h):
    scores = dot_nt(e.heads[h], e.heads[H + h]) * SCALE
    if e.mask is not None:
        scores = scores + e.mask[...]
    exponent = jnp.exp(scores - jnp.max(scores, axis=1, keepdims=True))
    return exponent / jnp.sum(exponent, axis=1, keepdims=True)


def forward_pass(e, y):
    for stage in forward_stages(e, y):
        stage()


def backward_pass(e):
    mod = e.mod
    gate1, scale1 = lambda: mod[2:3, :], lambda: mod[1:2, :]
    gate2, scale2 = lambda: mod[5:6, :], lambda: mod[4:5, :]
    e.sums[...] = jnp.zeros(e.sums.shape, jnp.float32)
    e.bout[...] = jnp.zeros(e.bout.shape, jnp.bfloat16)
    for s in range(8):
        e.bexp[s, :, 0:128] = jnp.zeros((TOKENS, 128), jnp.bfloat16)
        e.bin[s, :, 384:512] = jnp.zeros((TOKENS, 128), jnp.bfloat16)

    def first(r):
        g = e.g[r, :].astype(jnp.float32)
        back = (gate2() * g).astype(jnp.bfloat16)
        e.bb[r, :] = back
        e.sums[5] += fold(g * e.branch[r, :])
        e.sums[7] += fold(back.astype(jnp.float32))

    by_rows(first)

    @pl.loop(0, 4)
    def _(d):
        e.tmp[...] = dot(e.bb[...], e.sv[d])

        def hidden(r):
            back = (e.tmp[r, :] * e.slope[d, r, :]).astype(jnp.bfloat16)
            for half in range(2):
                e.bexp[2 * d + half, r, 64:640] = back[:, 576 * half : 576 * (half + 1)]
            e.sums[8 + d] += fold(back.astype(jnp.float32))

        by_rows(hidden)

    e.tmp[...] = jnp.zeros(e.tmp.shape, jnp.float32)

    @pl.loop(0, 8)
    def _(s):
        e.tmp[...] += dot_nt(e.bexp[s], e.pv[s, :, WIN_EXP])

    def second(r):
        n, scale = statistics(e.middle[r, :])
        back_normed = e.tmp[r, :]
        e.sums[3] += fold(back_normed)
        e.sums[4] += fold(back_normed * n)
        u = back_normed * (1.0 + scale2())
        inner = jnp.mean(u, axis=1, keepdims=True) + n * jnp.mean(u * n, axis=1, keepdims=True)
        back_middle = e.g[r, :].astype(jnp.float32) + scale * (u - inner)
        e.middle[r, :] = back_middle
        e.sums[2] += fold(back_middle * e.attended[r, :])
        back = (gate1() * back_middle).astype(jnp.bfloat16)
        e.sums[6] += fold(back.astype(jnp.float32))
        for s in range(8):
            e.bout[s, r, 48:192] = back[:, 144 * s : 144 * (s + 1)]

    by_rows(second)
    e.tmp[...] = jnp.zeros(e.tmp.shape, jnp.float32)

    @pl.loop(0, 8)
    def _(s):
        e.tmp[...] += dot_nt(e.bout[s], e.pv[s, :, WIN_OUT])

    for h in range(H):
        e.mh[h] = e.tmp[:, HD * h : HD * (h + 1)].astype(jnp.bfloat16)

    @pl.loop(0, H)
    def _(h):
        q, k, v, back = e.heads[h], e.heads[H + h], e.heads[2 * H + h], e.mh[h]
        probs = attention_probs(e, h)
        back_probs = dot_nt(back, v)
        e.heads[2 * H + h] = dot_tn(probs.astype(jnp.bfloat16), back).astype(jnp.bfloat16)
        delta = jnp.sum(probs * back_probs, axis=1, keepdims=True)
        back_scores = (probs * (back_probs - delta)).astype(jnp.bfloat16)
        e.heads[h] = (dot(back_scores, k) * SCALE).astype(jnp.bfloat16)
        e.heads[H + h] = (dot_tn(back_scores, q) * SCALE).astype(jnp.bfloat16)

    e.tmp[...] = jnp.zeros(e.tmp.shape, jnp.float32)
    ones = jnp.ones((8, TOKENS), jnp.bfloat16)

    @pl.loop(0, 8)
    def _(s):
        for j in range(6):
            e.bin[s, :, HD * j : HD * (j + 1)] = e.heads[6 * s + j]
        e.bslab[s] = dot(ones, e.bin[s])
        e.tmp[...] += dot_nt(e.bin[s], e.pv[s, :, WIN_IN])

    def third(r):
        n, scale = statistics(e.x[r, :].astype(jnp.float32))
        back_normed = e.tmp[r, :]
        e.sums[0] += fold(back_normed)
        e.sums[1] += fold(back_normed * n)
        u = back_normed * (1.0 + scale1())
        inner = jnp.mean(u, axis=1, keepdims=True) + n * jnp.mean(u * n, axis=1, keepdims=True)
        e.back_x[r, :] = (e.middle[r, :] + scale * (u - inner)).astype(jnp.bfloat16)

    by_rows(third)

    for s in range(8):
        for row, first_column in ((0, 0), (1, 2 * WIDTH)):
            lo, hi = max(432 * s, first_column), min(432 * (s + 1), first_column + WIDTH)
            if lo < hi:
                e.bias_grad[row : row + 1, lo - first_column : hi - first_column] = e.bslab[
                    s, 0:1, lo - 432 * s : hi - 432 * s
                ]
    for row, slot in ((2, 6), (3, 7), (4, 8), (5, 9), (6, 10), (7, 11)):
        e.bias_grad[row : row + 1, :] = jnp.sum(e.sums[slot], axis=0, keepdims=True)
    for slot in range(6):
        e.mod_grad[slot : slot + 1, :] = jnp.sum(e.sums[slot], axis=0, keepdims=True)
    e.mod_grad[6:8, :] = jnp.zeros((2, WIDTH), jnp.float32)


class Refs:
    pass


WEIGHT_SCRATCH = (
    ("pv", (8, WIDTH, WIDTH), jnp.bfloat16),
    ("sv", (4, WIDTH, WIDTH), jnp.bfloat16),
)
FORWARD_SCRATCH = (
    ("bslab", (8, 8, 512), jnp.float32),
    ("heads", (3 * H, TOKENS, HD), jnp.bfloat16),
    ("mh", (H, TOKENS, HD), jnp.bfloat16),
    ("attended", (TOKENS, WIDTH), jnp.float32),
    ("middle", (TOKENS, WIDTH), jnp.float32),
    ("branch", (TOKENS, WIDTH), jnp.float32),
    ("tmp", (TOKENS, WIDTH), jnp.float32),
)
OPERANDS = (
    ("normed", (TOKENS, WIDTH), jnp.bfloat16),
    ("mixture", (TOKENS, WIDTH), jnp.bfloat16),
    ("normed2", (TOKENS, WIDTH), jnp.bfloat16),
    ("act", (4, TOKENS, WIDTH), jnp.bfloat16),
)
BACK_OPERANDS = (
    ("bb", (TOKENS, WIDTH), jnp.bfloat16),
    ("bin", (8, TOKENS, 512), jnp.bfloat16),
    ("bout", (8, TOKENS, 256), jnp.bfloat16),
    ("bexp", (8, TOKENS, 640), jnp.bfloat16),
)
BACKWARD_SCRATCH = (
    ("slope", (4, TOKENS, WIDTH), jnp.float32),
    ("sums", (12, 8, WIDTH), jnp.float32),
)


def load_weights(e, p_hbm, s_hbm, psem, ssem):
    def p_copy(s):
        return pltpu.make_async_copy(p_hbm.at[s], e.pv.at[s], psem.at[s])

    def s_copy(d):
        return pltpu.make_async_copy(s_hbm.at[d], e.sv.at[d], ssem.at[d])

    @pl.loop(0, 8)
    def _(s):
        p_copy(s).start()

    @pl.loop(0, 4)
    def _(d):
        s_copy(d).start()

    e.wait_p = lambda s: p_copy(s).wait()
    e.wait_s = lambda d: s_copy(d).wait()


def block_kernel(names, block, *refs):
    e = Refs()
    e.mask, e.slope, e.y = None, None, None
    for name, ref in zip(names, refs):
        setattr(e, name, ref)
    e.mod, e.bias = e.mods.at[block], e.biases.at[block]
    load_weights(e, e.p, e.s, e.psem, e.ssem)
    if "segments" in names:
        fill_mask(e)
    forward_pass(e, e.y)
    if "g" in names:
        backward_pass(e)


def fill_mask(e):
    frames = e.segments.shape[1]
    each = TOKENS // frames

    def clips(axis):
        frame = lax.broadcasted_iota(jnp.int32, (TOKENS, TOKENS), axis) // each
        clip = jnp.zeros((TOKENS, TOKENS), jnp.int32)
        for f in range(frames):
            clip = jnp.where(frame == f, e.segments[0, f], clip)
        return clip

    def spots(axis):
        return lax.broadcasted_iota(jnp.int32, (TOKENS, TOKENS), axis) % each

    same = (clips(0) == clips(1)) & (spots(0) == spots(1))
    e.mask[...] = jnp.where(same, 0.0, NEGATIVE)


def block_call(x, mods, biases, block, p, s, segments=None, g=None, give_y=True):
    inputs = [("x", x), ("mods", mods), ("biases", biases), ("p", p), ("s", s)]
    if segments is not None:
        inputs.append(("segments", segments))
    if g is not None:
        inputs.append(("g", g))
    outs, scratch = [], list(WEIGHT_SCRATCH + FORWARD_SCRATCH)
    if segments is not None:
        scratch.append(("mask", (TOKENS, TOKENS), jnp.float32))
    if give_y:
        outs.append(("y", (TOKENS, WIDTH), jnp.bfloat16))
    if g is None:
        scratch += OPERANDS
    else:
        outs += [
            ("back_x", (TOKENS, WIDTH), jnp.bfloat16),
            ("bias_grad", (8, WIDTH), jnp.float32),
            ("mod_grad", (8, WIDTH), jnp.float32),
        ]
        outs += OPERANDS + BACK_OPERANDS
        scratch += BACKWARD_SCRATCH
    names = [name for name, *_ in inputs + outs + scratch] + ["psem", "ssem"]
    smem = pl.BlockSpec(memory_space=pltpu.SMEM)
    spec = lambda name: {"p": ANY_SPEC, "s": ANY_SPEC, "segments": smem}.get(name, VMEM_SPEC)
    results = pl.pallas_call(
        functools.partial(block_kernel, names, block),
        out_shape=[jax.ShapeDtypeStruct(shape, kind) for _, shape, kind in outs],
        in_specs=[spec(name) for name, _ in inputs],
        out_specs=[VMEM_SPEC] * len(outs),
        scratch_shapes=[pltpu.VMEM(shape, kind) for _, shape, kind in scratch]
        + [pltpu.SemaphoreType.DMA((8,)), pltpu.SemaphoreType.DMA((4,))],
        compiler_params=pltpu.CompilerParams(vmem_limit_bytes=63 << 20),
        name="block_both" if g is not None else "block_forward",
    )(*[value for _, value in inputs])
    return dict(zip([name for name, *_ in outs], results))


SECOND_SCRATCH = WEIGHT_SCRATCH + FORWARD_SCRATCH + OPERANDS + (
    ("y", (TOKENS, WIDTH), jnp.bfloat16),
)


def second_gather_kernel(p_in, s_in, x, mods, biases, p, s, p_out, s_out, passed, *refs):
    e = Refs()
    e.mask, e.slope, e.x = None, None, x
    for (name, *_), ref in zip(SECOND_SCRATCH, refs):
        setattr(e, name, ref)
    e.mod, e.bias = mods.at[0], biases.at[0]
    sems = refs[len(SECOND_SCRATCH) :]
    me = Place()
    gather = Gather(me, p_in, s_in, p_out, s_out, *sems[:4])
    exchange = Exchange(me, e.y, passed, *sems[4:7])
    greet(me)
    events = gather.events()
    own = len(CHUNKS) / len(events)
    stages = forward_stages(e, e.y)
    first, last = own, 0.6
    timed = [(own, lambda: load_weights(e, p, s, *sems[7:9]))]
    timed += [
        (first + (last - first) * i / len(stages), stage) for i, stage in enumerate(stages)
    ]
    interleave(events, timed + [(last, exchange.start), (0.95, exchange.finish)])
    gather.finish()


def second_gather(p_own, s_own, x, mods, biases, p, s):
    return pl.pallas_call(
        second_gather_kernel,
        out_shape=SLABS + (STREAM,),
        in_specs=[ANY_SPEC] * 2 + [VMEM_SPEC] * 3 + [ANY_SPEC] * 2,
        out_specs=(ANY_SPEC,) * 3,
        scratch_shapes=[pltpu.VMEM(shape, kind) for _, shape, kind in SECOND_SCRATCH]
        + dma_sems(*Gather.SEMS, (8,), (8,), (), (8,), (4,)),
        compiler_params=pltpu.CompilerParams(
            collective_id=1, has_side_effects=True, vmem_limit_bytes=60 << 20
        ),
        name="second_gather",
    )(p_own, s_own, x, mods, biases, p, s)


def gradient_p_kernel(normed, mixture, normed2, b_in, b_out, b_exp, out, n_t, m_t, n2_t):
    @pl.when(pl.program_id(0) == 0)
    def _():
        n_t[...] = normed[...].T
        m_t[...] = mixture[...].T
        n2_t[...] = normed2[...].T

    @pl.loop(0, 4)
    def _(i):
        r = pl.ds(pl.multiple_of(i * 288, 16), 288)
        first = dot(n_t[r, :], b_in[0])
        second = dot(m_t[r, :], b_out[0])
        third = dot(n2_t[r, :], b_exp[0])
        out[0, r, 0:384] = first[:, 0:384].astype(jnp.bfloat16)
        out[0, r, 384:512] = (first[:, 384:] + second[:, :128]).astype(jnp.bfloat16)
        out[0, r, 512:640] = (second[:, 128:] + third[:, :128]).astype(jnp.bfloat16)
        out[0, r, 640:] = third[:, 128:].astype(jnp.bfloat16)


def gradient_s_kernel(back, act, out, back_t):
    @pl.when(pl.program_id(0) == 0)
    def _():
        back_t[...] = back[...].T

    @pl.loop(0, 4)
    def _(i):
        r = pl.ds(pl.multiple_of(i * 288, 16), 288)
        out[0, r, :] = dot(back_t[r, :], act[0]).astype(jnp.bfloat16)


def gradient_slabs(o):
    whole = pl.BlockSpec((TOKENS, WIDTH), lambda i: (0, 0))
    piece = lambda n: pl.BlockSpec((1, TOKENS, n), lambda i: (i, 0, 0))
    slab = pl.BlockSpec((1, WIDTH, WIDTH), lambda i: (i, 0, 0))
    turned = pltpu.VMEM((WIDTH, TOKENS), jnp.bfloat16)
    p = pl.pallas_call(
        gradient_p_kernel,
        grid=(8,),
        out_shape=jax.ShapeDtypeStruct((8, WIDTH, WIDTH), jnp.bfloat16),
        in_specs=[whole] * 3 + [piece(512), piece(256), piece(640)],
        out_specs=slab,
        scratch_shapes=[turned] * 3,
        compiler_params=pltpu.CompilerParams(vmem_limit_bytes=48 << 20),
    )(o["normed"], o["mixture"], o["normed2"], o["bin"], o["bout"], o["bexp"])
    s = pl.pallas_call(
        gradient_s_kernel,
        grid=(4,),
        out_shape=jax.ShapeDtypeStruct((4, WIDTH, WIDTH), jnp.bfloat16),
        in_specs=[whole, piece(WIDTH)],
        out_specs=slab,
        scratch_shapes=[turned],
        compiler_params=pltpu.CompilerParams(vmem_limit_bytes=48 << 20),
    )(o["bb"], o["act"])
    return p, s


def sinusoid(timesteps):
    half_width = D // 2
    frequencies = jnp.exp(
        -math.log(10000.0) * jnp.arange(half_width, dtype=jnp.float32) / half_width
    )
    angles = timesteps.astype(jnp.float32)[:, None] * frequencies[None, :]
    return jnp.concatenate([jnp.cos(angles), jnp.sin(angles)], axis=1)


def layer_norm(tensor):
    centered = tensor - jnp.mean(tensor, axis=-1, keepdims=True)
    return centered * lax.rsqrt(jnp.mean(centered * centered, axis=-1, keepdims=True) + EPSILON)


def modulate(tensor, shift_part, scale_part):
    return layer_norm(tensor) * (1.0 + scale_part) + shift_part


def matmul(left_side, right_side):
    return jnp.dot(left_side, right_side, preferred_element_type=jnp.float32)


def back_matmul(gradient, matrix):
    return lax.dot_general(
        gradient,
        matrix,
        (((gradient.ndim - 1,), (1,)), ((), ())),
        preferred_element_type=jnp.float32,
    )


def outer_product(left_side, right_side):
    flat_left = left_side.reshape(-1, left_side.shape[-1])
    flat_right = right_side.reshape(-1, right_side.shape[-1])
    return lax.dot_general(
        flat_left, flat_right, (((0,), (0,)), ((), ())), preferred_element_type=jnp.float32
    )


def column_totals(tensor):
    return jnp.sum(tensor.astype(jnp.float32).reshape(-1, tensor.shape[-1]), axis=0)


def per_sequence(tensor):
    return jnp.sum(tensor, axis=(1, 2))


def over_data(core, biases):
    attend_in, attend_out, expand, shrink = core
    attend_bias, out_bias, expand_bias, shrink_bias, modulate_bias = biases
    gathered = (
        lax.all_gather(attend_in, "dp", axis=0, tiled=True),
        lax.all_gather(attend_out, "dp", axis=0, tiled=True),
        lax.all_gather(expand, "dp", axis=0, tiled=True),
        lax.all_gather(shrink, "dp", axis=0, tiled=True),
        lax.all_gather(attend_bias, "dp", axis=0, tiled=True),
        lax.all_gather(out_bias, "dp", axis=0, tiled=True),
        lax.all_gather(expand_bias, "dp", axis=0, tiled=True),
        lax.all_gather(shrink_bias, "dp", axis=0, tiled=True),
        lax.all_gather(modulate_bias, "dp", axis=0, tiled=True),
    )
    return (gathered[:4], gathered[4:])


def over_frames(core):
    attend_in, attend_out, expand, shrink = core
    gathered = (
        lax.all_gather(attend_in, "sp", axis=1, tiled=True),
        lax.all_gather(attend_out, "sp", axis=1, tiled=True),
        lax.all_gather(expand, "sp", axis=1, tiled=True),
        lax.all_gather(shrink, "sp", axis=1, tiled=True),
    )
    return gathered


def collect(core, biases):
    core_rows, biases_full = over_data(core, biases)
    core_full = over_frames(core_rows)
    return (core_full, biases_full)


def own_rows(condition_all, rows):
    return lax.dynamic_slice_in_dim(condition_all, lax.axis_index("dp") * rows, rows, 1)


def modulation_of(condition_all, modulate_weights):
    rows = modulate_weights[0].shape[0]
    own = own_rows(condition_all, rows)
    partial_terms = jnp.stack([matmul(own, weight) for weight in modulate_weights], axis=1)
    summed = lax.psum_scatter(partial_terms, "dp", scatter_dimension=0, tiled=True)
    full = lax.all_gather(summed, "sp", axis=2, tiled=True)
    return [full[:, slot] for slot in range(len(modulate_weights))]


def sum_over_frames(terms):
    attend_in, attend_out, expand, shrink = terms
    return (
        lax.psum_scatter(
            attend_in.astype(jnp.bfloat16), "sp", scatter_dimension=1, tiled=True
        ).astype(jnp.float32),
        lax.psum_scatter(
            attend_out.astype(jnp.bfloat16), "sp", scatter_dimension=1, tiled=True
        ).astype(jnp.float32),
        lax.psum_scatter(expand.astype(jnp.bfloat16), "sp", scatter_dimension=1, tiled=True).astype(
            jnp.float32
        ),
        lax.psum_scatter(shrink.astype(jnp.bfloat16), "sp", scatter_dimension=1, tiled=True).astype(
            jnp.float32
        ),
    )


def sum_over_data(terms):
    attend_in, attend_out, expand, shrink = terms
    return (
        lax.psum_scatter(
            attend_in.astype(jnp.bfloat16), "dp", scatter_dimension=0, tiled=True
        ).astype(jnp.float32),
        lax.psum_scatter(
            attend_out.astype(jnp.bfloat16), "dp", scatter_dimension=0, tiled=True
        ).astype(jnp.float32),
        lax.psum_scatter(expand.astype(jnp.bfloat16), "dp", scatter_dimension=0, tiled=True).astype(
            jnp.float32
        ),
        lax.psum_scatter(shrink.astype(jnp.bfloat16), "dp", scatter_dimension=0, tiled=True).astype(
            jnp.float32
        ),
    )


def modulate_gradients(condition_all, back_modulations, rows):
    joined = jnp.stack(back_modulations, axis=1)
    columns = lax.psum_scatter(joined, "sp", scatter_dimension=2, tiled=True)
    every = lax.all_gather(columns, "dp", axis=0, tiled=True)
    own = own_rows(condition_all, rows).astype(jnp.float32)
    return [
        jnp.dot(own.T, every[:, slot], precision=HIGHEST_PRECISION)
        for slot in range(len(back_modulations))
    ]


def finish(core_terms, bias_terms):
    matrix_grads = sum_over_data(sum_over_frames(core_terms))
    attend_bias, out_bias, expand_bias, shrink_bias, modulate_bias = bias_terms
    totals = lax.psum(
        (attend_bias, out_bias, expand_bias, shrink_bias, modulate_bias), ("dp", "sp")
    )
    data_index = lax.axis_index("dp")
    data_count = lax.axis_size("dp")
    bias_grads = tuple(
        (
            lax.dynamic_slice_in_dim(
                total_bias,
                data_index * (total_bias.shape[0] // data_count),
                total_bias.shape[0] // data_count,
            )
            for total_bias in totals
        )
    )
    return (matrix_grads, bias_grads)


def frames_to_patches(tensor):
    return lax.all_to_all(tensor, "sp", split_axis=2, concat_axis=1, tiled=True)


def patches_to_frames(tensor):
    return lax.all_to_all(tensor, "sp", split_axis=1, concat_axis=2, tiled=True)


def attention_scores(queries, key_rows, forms, allowed):
    scores = jnp.einsum(forms[0], queries, key_rows, preferred_element_type=jnp.float32) * HD ** (
        -0.5
    )
    if allowed is not None:
        scores = jnp.where(allowed, scores, -1e30)
    return scores


def block_forward(stream, modulation, core, biases, forms, allowed):
    attend_in, attend_out, expand, shrink = core
    attend_bias, out_bias, expand_bias, shrink_bias, modulate_bias = biases
    model_width = stream.shape[-1]
    pieces = [
        modulation[:, None, None, slot * model_width : (slot + 1) * model_width]
        for slot in range(6)
    ]
    normed = modulate(stream, pieces[0], pieces[1]).astype(jnp.bfloat16)
    bias_float = attend_bias.astype(jnp.float32)
    joined_bias = jnp.concatenate(
        [bias_float[:model_width], jnp.zeros((model_width,), jnp.float32), bias_float[model_width:]]
    )
    projected = (matmul(normed, attend_in) + joined_bias).astype(jnp.bfloat16)
    head_shape = projected.shape[:3] + (H, HD)
    queries = projected[..., :model_width].reshape(head_shape)
    key_rows = projected[..., model_width : 2 * model_width].reshape(head_shape)
    values = projected[..., 2 * model_width :].reshape(head_shape)
    scores = attention_scores(queries, key_rows, forms, allowed)
    highest = jnp.max(scores, axis=-1, keepdims=True)
    exponent = jnp.exp(scores - highest)
    denominator = jnp.sum(exponent, axis=-1, keepdims=True)
    softmax_probs = exponent / denominator
    logsum = highest + jnp.log(denominator)
    mixture = (
        jnp.einsum(
            forms[1], softmax_probs.astype(jnp.bfloat16), values, preferred_element_type=jnp.float32
        )
        .astype(jnp.bfloat16)
        .reshape(stream.shape)
    )
    attended = matmul(mixture, attend_out) + out_bias.astype(jnp.float32)
    middle = stream + pieces[2] * attended
    normed_second = modulate(middle, pieces[3], pieces[4]).astype(jnp.bfloat16)
    hidden = matmul(normed_second, expand) + expand_bias.astype(jnp.float32)
    activated = jax.nn.gelu(hidden, approximate=True).astype(jnp.bfloat16)
    branch = matmul(activated, shrink) + shrink_bias.astype(jnp.float32)
    result = middle + pieces[5] * branch
    kept = (
        pieces,
        normed,
        queries,
        key_rows,
        values,
        logsum,
        mixture,
        attended,
        middle,
        normed_second,
        hidden,
        activated,
        branch,
    )
    return (result, kept)


def block_backward(incoming, stream, core, forms, allowed, kept):
    attend_in, attend_out, expand, shrink = core
    (
        pieces,
        normed,
        queries,
        key_rows,
        values,
        logsum,
        mixture,
        attended,
        middle,
        normed_second,
        hidden,
        activated,
        branch,
    ) = kept
    model_width = stream.shape[-1]
    sequences = stream.shape[0]
    back_branch = (pieces[5] * incoming).astype(jnp.bfloat16)
    back_gate_second = per_sequence(incoming * branch)
    shrink_term = outer_product(activated, back_branch)
    shrink_bias_term = column_totals(back_branch)
    back_activated = back_matmul(back_branch, shrink)
    _, gelu_pull = jax.vjp(lambda tensor: jax.nn.gelu(tensor, approximate=True), hidden)
    back_hidden = gelu_pull(back_activated)[0].astype(jnp.bfloat16)
    expand_term = outer_product(normed_second, back_hidden)
    expand_bias_term = column_totals(back_hidden)
    back_normed_second = back_matmul(back_hidden, expand)
    _, second_pull = jax.vjp(modulate, middle, pieces[3], pieces[4])
    back_middle, back_shift_second, back_scale_second = second_pull(back_normed_second)
    back_middle = back_middle + incoming
    back_attended = (pieces[2] * back_middle).astype(jnp.bfloat16)
    back_gate_first = per_sequence(back_middle * attended)
    out_term = outer_product(mixture, back_attended)
    out_bias_term = column_totals(back_attended)
    back_mixture = (
        back_matmul(back_attended, attend_out).astype(jnp.bfloat16).reshape(queries.shape)
    )
    scores = attention_scores(queries, key_rows, forms, allowed)
    softmax_probs = jnp.exp(scores - logsum)
    back_probs = jnp.einsum(forms[0], back_mixture, values, preferred_element_type=jnp.float32)
    back_values = jnp.einsum(
        forms[2],
        softmax_probs.astype(jnp.bfloat16),
        back_mixture,
        preferred_element_type=jnp.float32,
    )
    row_delta = jnp.sum(softmax_probs * back_probs, axis=-1, keepdims=True)
    back_scores = (softmax_probs * (back_probs - row_delta)).astype(jnp.bfloat16)
    score_scale = HD ** (-0.5)
    back_queries = (
        jnp.einsum(forms[1], back_scores, key_rows, preferred_element_type=jnp.float32)
        * score_scale
    )
    back_keys = (
        jnp.einsum(forms[2], back_scores, queries, preferred_element_type=jnp.float32) * score_scale
    )
    flat_shape = stream.shape
    back_projected = jnp.concatenate(
        [
            back_queries.reshape(flat_shape),
            back_keys.reshape(flat_shape),
            back_values.reshape(flat_shape),
        ],
        axis=-1,
    ).astype(jnp.bfloat16)
    attend_in_term = outer_product(normed, back_projected)
    projected_totals = column_totals(back_projected)
    attend_bias_term = jnp.concatenate(
        [projected_totals[:model_width], projected_totals[2 * model_width :]]
    )
    back_normed = back_matmul(back_projected, attend_in)
    _, first_pull = jax.vjp(modulate, stream, pieces[0], pieces[1])
    back_stream, back_shift_first, back_scale_first = first_pull(back_normed)
    back_stream = back_stream + back_middle
    back_modulation = jnp.concatenate(
        [
            back_shift_first.reshape(sequences, model_width),
            back_scale_first.reshape(sequences, model_width),
            back_gate_first,
            back_shift_second.reshape(sequences, model_width),
            back_scale_second.reshape(sequences, model_width),
            back_gate_second,
        ],
        axis=1,
    )
    modulate_bias_term = jnp.sum(back_modulation, axis=0)
    core_terms = (attend_in_term, out_term, expand_term, shrink_term)
    bias_terms = (
        attend_bias_term,
        out_bias_term,
        expand_bias_term,
        shrink_bias_term,
        modulate_bias_term,
    )
    return (back_stream, core_terms, back_modulation, bias_terms)


def shards(
    inputs,
    timesteps,
    segment_ids,
    spatial_attend_in,
    spatial_attend_bias,
    spatial_attend_out,
    spatial_out_bias,
    spatial_expand,
    spatial_expand_bias,
    spatial_shrink,
    spatial_shrink_bias,
    spatial_modulate,
    spatial_modulate_bias,
    temporal_attend_in,
    temporal_attend_bias,
    temporal_attend_out,
    temporal_out_bias,
    temporal_expand,
    temporal_expand_bias,
    temporal_shrink,
    temporal_shrink_bias,
    temporal_modulate,
    temporal_modulate_bias,
    cotangent,
):
    condition_all = jax.nn.silu(sinusoid(timesteps)).astype(jnp.bfloat16)
    allowed = (segment_ids[:, :, None] == segment_ids[:, None, :])[:, None, None, :, :]
    spatial_core = (spatial_attend_in, spatial_attend_out, spatial_expand, spatial_shrink)
    spatial_biases = (
        spatial_attend_bias,
        spatial_out_bias,
        spatial_expand_bias,
        spatial_shrink_bias,
        spatial_modulate_bias,
    )
    temporal_core = (temporal_attend_in, temporal_attend_out, temporal_expand, temporal_shrink)
    temporal_biases = (
        temporal_attend_bias,
        temporal_out_bias,
        temporal_expand_bias,
        temporal_shrink_bias,
        temporal_modulate_bias,
    )
    stream = inputs.astype(jnp.float32)
    modulations = modulation_of(condition_all, (spatial_modulate, temporal_modulate))
    core, biases = collect(spatial_core, spatial_biases)
    modulation = modulations[0] + biases[4].astype(jnp.float32)
    spatial_core = core
    spatial_out, spatial_kept = block_forward(stream, modulation, core, biases, SPATIAL_FORMS, None)
    passed = frames_to_patches(spatial_out.astype(jnp.bfloat16)).astype(jnp.float32)
    core, biases = collect(temporal_core, temporal_biases)
    modulation = modulations[1] + biases[4].astype(jnp.float32)
    temporal_out, temporal_kept = block_forward(
        passed, modulation, core, biases, TEMPORAL_FORMS, allowed
    )
    output = patches_to_frames(temporal_out.astype(jnp.bfloat16))
    incoming = frames_to_patches(cotangent).astype(jnp.float32)
    back_passed, core_terms, back_temporal, bias_terms = block_backward(
        incoming, passed, core, TEMPORAL_FORMS, allowed, temporal_kept
    )
    temporal_grads, temporal_bias_grads = finish(core_terms, bias_terms)
    back_spatial = patches_to_frames(back_passed.astype(jnp.bfloat16)).astype(jnp.float32)
    back_inputs, core_terms, back_spatial_modulation, bias_terms = block_backward(
        back_spatial, stream, spatial_core, SPATIAL_FORMS, None, spatial_kept
    )
    spatial_grads, spatial_bias_grads = finish(core_terms, bias_terms)
    modulate_grads = modulate_gradients(
        condition_all, (back_spatial_modulation, back_temporal), spatial_modulate.shape[0]
    )
    return (
        output,
        back_inputs.astype(jnp.bfloat16),
        spatial_grads[0],
        spatial_bias_grads[0],
        spatial_grads[1],
        spatial_bias_grads[1],
        spatial_grads[2],
        spatial_bias_grads[2],
        spatial_grads[3],
        spatial_bias_grads[3],
        modulate_grads[0],
        spatial_bias_grads[4],
        temporal_grads[0],
        temporal_bias_grads[0],
        temporal_grads[1],
        temporal_bias_grads[1],
        temporal_grads[2],
        temporal_bias_grads[2],
        temporal_grads[3],
        temporal_bias_grads[3],
        modulate_grads[1],
        temporal_bias_grads[4],
    )


def fits(mesh):
    return mesh.shape["dp"] == 4 and mesh.shape["sp"] == 8


def condition_rows(timesteps, rows):
    half = D // 2
    index = lax.axis_index("dp") * rows + jnp.arange(rows, dtype=jnp.int32)
    place = (index % half).astype(jnp.float32)
    frequencies = jnp.exp(-math.log(10000.0) * place / half)
    angles = timesteps.astype(jnp.float32)[:, None] * frequencies[None, :]
    wave = jnp.where((index < half)[None, :], jnp.cos(angles), jnp.sin(angles))
    return jax.nn.silu(wave).astype(jnp.bfloat16)


def fast_shards(
    inputs,
    timesteps,
    segment_ids,
    spatial_attend_in,
    spatial_attend_bias,
    spatial_attend_out,
    spatial_out_bias,
    spatial_expand,
    spatial_expand_bias,
    spatial_shrink,
    spatial_shrink_bias,
    spatial_modulate,
    spatial_modulate_bias,
    temporal_attend_in,
    temporal_attend_bias,
    temporal_attend_out,
    temporal_out_bias,
    temporal_expand,
    temporal_expand_bias,
    temporal_shrink,
    temporal_shrink_bias,
    temporal_modulate,
    temporal_modulate_bias,
    cotangent,
):
    def small(attend, out, expand, shrink, modulate):
        rest = jnp.zeros((2 * D - modulate.shape[0],), jnp.bfloat16)
        return [attend, out, shrink, expand, modulate, rest]

    pack = (
        jnp.concatenate(
            small(
                spatial_attend_bias,
                spatial_out_bias,
                spatial_expand_bias,
                spatial_shrink_bias,
                spatial_modulate_bias,
            )
            + small(
                temporal_attend_bias,
                temporal_out_bias,
                temporal_expand_bias,
                temporal_shrink_bias,
                temporal_modulate_bias,
            )
        )
        .astype(jnp.float32)
        .reshape(8, D)
    )
    cond = jnp.pad(condition_rows(timesteps, spatial_modulate.shape[0]), ((0, 4), (0, 0)))
    cond_columns = cond.astype(jnp.float32).T
    x = inputs.reshape(TOKENS, WIDTH)
    spatial_p, spatial_s, mods, biases, incoming = first_gather(
        jnp.concatenate([spatial_attend_in, spatial_attend_out, spatial_expand], axis=1),
        spatial_shrink.T,
        pack,
        cond,
        (spatial_modulate, temporal_modulate),
        cotangent.reshape(TOKENS, WIDTH),
    )
    temporal_p, temporal_s, passed = second_gather(
        jnp.concatenate([temporal_attend_in, temporal_attend_out, temporal_expand], axis=1),
        temporal_shrink.T,
        x,
        mods,
        biases,
        spatial_p,
        spatial_s,
    )
    t = block_call(
        passed, mods, biases, 1, temporal_p, temporal_s, segments=segment_ids, g=incoming
    )
    packed_t, turned_t, modulate_t, totals_t, output, back_spatial = scatter_call(
        gradient_slabs(t), t["bias_grad"], t["mod_grad"], cond_columns, (t["y"], t["back_x"]), 2
    )
    b = block_call(x, mods, biases, 0, spatial_p, spatial_s, g=back_spatial, give_y=False)
    packed_s, turned_s, modulate_s, totals_s = scatter_call(
        gradient_slabs(b), b["bias_grad"], b["mod_grad"], cond_columns, (), 3
    )
    outs = unpack(packed_s, turned_s, totals_s, packed_t, turned_t, totals_t)
    return (
        output.reshape(inputs.shape),
        b["back_x"].reshape(inputs.shape),
        *outs[:8],
        modulate_s,
        outs[8],
        *outs[9:17],
        modulate_t,
        outs[17],
    )


def solution(mesh):
    placed = (
        P("dp", "sp", None, None),
        P(),
        P("dp", None),
        P("dp", "sp"),
        P("dp"),
        P("dp", "sp"),
        P("dp"),
        P("dp", "sp"),
        P("dp"),
        P("dp", "sp"),
        P("dp"),
        P("dp", "sp"),
        P("dp"),
        P("dp", "sp"),
        P("dp"),
        P("dp", "sp"),
        P("dp"),
        P("dp", "sp"),
        P("dp"),
        P("dp", "sp"),
        P("dp"),
        P("dp", "sp"),
        P("dp"),
        P("dp", "sp", None, None),
    )
    return jax.shard_map(
        fast_shards if fits(mesh) else shards,
        mesh=mesh,
        in_specs=placed,
        out_specs=(
            P("dp", "sp", None, None),
            P("dp", "sp", None, None),
            P("dp", "sp"),
            P("dp"),
            P("dp", "sp"),
            P("dp"),
            P("dp", "sp"),
            P("dp"),
            P("dp", "sp"),
            P("dp"),
            P("dp", "sp"),
            P("dp"),
            P("dp", "sp"),
            P("dp"),
            P("dp", "sp"),
            P("dp"),
            P("dp", "sp"),
            P("dp"),
            P("dp", "sp"),
            P("dp"),
            P("dp", "sp"),
            P("dp"),
        ),
        check_vma=False,
    )
```

```python
import functools
import math

import jax
import jax.numpy as jnp
from jax import lax
from jax.experimental import pallas as pl
from jax.experimental.pallas import tpu as pltpu
from jax.sharding import PartitionSpec as P

D = 1152
H = 16
HD = 72


EPSILON = 1e-06
HIGHEST_PRECISION = lax.Precision.HIGHEST
SPATIAL_FORMS = ("sabhe,sache->sahbc", "sahbc,sache->sabhe", "sahbc,sabhe->sache")
TEMPORAL_FORMS = ("sabhe,scbhe->sbhac", "sbhac,scbhe->sabhe", "sbhac,sabhe->scbhe")


MESH = pl.DeviceIdType.MESH
TOKENS = 256
WIDTH = 1152
P_CHUNKS = (("p", 0, 144, "zxy"), ("p", 144, 144, "zyx"))
CHUNKS = P_CHUNKS + (("s", 0, 48, "xyz"), ("s", 48, 48, "yxz"), ("s", 96, 48, "zxy"))
CHUNKS_ONE = P_CHUNKS + (("s", 0, 80, "yxz"), ("s", 80, 32, "zxy"), ("s", 112, 32, "zyx"))
CHUNKS_TWO = P_CHUNKS + (("s", 0, 64, "yxz"), ("s", 64, 64, "zyx"), ("s", 128, 16, "zxy"))
RELS = sorted(
    [(rx, ry, dz) for rx in (0, 1) for ry in (0, 1) for dz in range(-3, 4)],
    key=lambda r: (r[0] + r[1] + abs(r[2]), r != (0, 0, 0)),
)


class Place:
    def __init__(self):
        self.d, self.s = lax.axis_index("dp"), lax.axis_index("sp")
        self.x, self.c = self.d // 2, self.d % 2
        self.z, self.y = self.s // 2, self.s % 2

    def at(self, rel):
        rx, ry, dz = rel
        return (1 - self.x if rx else self.x, self.z + dz, 1 - self.y if ry else self.y)

    def exists(self, dz):
        return None if dz == 0 else ((self.z + dz >= 0) & (self.z + dz <= 3))

    def neighbour(self, direction):
        x, c, z, y = self.x, self.c, self.z, self.y
        return {
            "x": lambda: dev(1 - x, c, z, y),
            "y": lambda: dev(x, c, z, 1 - y),
            "u": lambda: dev(x, c, z + 1, y),
            "d": lambda: dev(x, c, z - 1, y),
            "c": lambda: dev(x, 1 - c, z, y),
        }[direction]()

    def has(self, direction):
        return {"u": lambda: self.z < 3, "d": lambda: self.z > 0}.get(direction, lambda: None)()


def dev(x, c, z, y):
    return (x * 2 + c, z * 2 + y)


def blk(b):
    return (b[0] * 4 + b[1]) * 2 + b[2]


def both(a, b):
    return b if a is None else (a if b is None else (a & b))


def guarded(cond, f):
    if cond is None:
        f()
    else:
        pl.when(cond)(f)


def greet(me):
    barrier = pltpu.get_barrier_semaphore()
    for k in range(1, 4):
        pl.semaphore_signal(
            barrier, inc=1, device_id=((me.d + k) % 4, me.s), device_id_type=MESH
        )
    for k in range(1, 8):
        pl.semaphore_signal(
            barrier, inc=1, device_id=(me.d, (me.s + k) % 8), device_id_type=MESH
        )
    pl.semaphore_wait(barrier, 10)


def links(rel, order):
    nz = {"x": rel[0], "y": rel[1], "z": rel[2]}
    last = max([i for i in range(3) if nz[order[i]]], default=-1)
    out = []
    for i, dim in enumerate(order):
        if i > last:
            out += ["u", "d"] if dim == "z" else [dim]
        elif i == last and dim == "z":
            out += ["u"] if rel[2] < 0 else ["d"]
    parent = None
    if last >= 0:
        parent = order[last] if order[last] != "z" else ("d" if rel[2] < 0 else "u")
    return out, parent


class Gather:
    SEMS = ((5, 16), (5, 16), (5, 5, 16), (5,))

    def __init__(self, me, chunks, p_in, s_in, p_out, s_out, arrived, crossed, sent, local):
        self.chunks = chunks
        self.me, self.ins, self.outs = me, {"p": p_in, "s": s_in}, {"p": p_out, "s": s_out}
        self.arrived, self.crossed, self.sent, self.local = arrived, crossed, sent, local

    def own(self, ch):
        return self.ins[ch[0]].at[pl.ds(ch[1], ch[2]), :]

    def place(self, ch, b, core):
        d, s = b[0] * 2 + core, b[1] * 2 + b[2]
        if ch[0] == "p":
            return self.outs["p"].at[s, pl.ds(d * 288 + ch[1], ch[2]), :]
        return self.outs["s"].at[d, pl.ds(s * 144 + ch[1], ch[2]), :]

    def copy(self, k, rel, direction):
        me, ch = self.me, self.chunks[k]
        b = me.at(rel)
        there = self.place(ch, b, me.c)
        return pltpu.make_async_remote_copy(
            src_ref=self.own(ch) if rel == (0, 0, 0) else there,
            dst_ref=there,
            send_sem=self.sent.at[k, "xyudc".index(direction), blk(b)],
            recv_sem=(self.crossed if direction == "c" else self.arrived).at[k, blk(b)],
            device_id=me.neighbour(direction),
            device_id_type=MESH,
        )

    def ends(self, k, rel):
        return links(rel, self.chunks[k][3])[0] + ["c"]

    def event(self, k, rel):
        me, ch = self.me, self.chunks[k]

        def body():
            if rel == (0, 0, 0):
                pltpu.make_async_copy(
                    self.own(ch), self.place(ch, me.at(rel), me.c), self.local.at[k]
                ).start()
            else:
                self.wait_in(k, rel, me.c, self.arrived)
            for direction in self.ends(k, rel):
                guarded(me.has(direction), lambda: self.copy(k, rel, direction).start())

        guarded(me.exists(rel[2]), body)

    def wait_in(self, k, rel, core, sems):
        b, ch = self.me.at(rel), self.chunks[k]
        pltpu.make_async_copy(self.own(ch), self.place(ch, b, core), sems.at[k, blk(b)]).wait()

    def events(self):
        return [
            functools.partial(self.event, k, rel) for rel in RELS for k in range(len(self.chunks))
        ]

    def finish(self):
        me = self.me
        for k, ch in enumerate(self.chunks):
            pltpu.make_async_copy(
                self.own(ch), self.place(ch, me.at((0, 0, 0)), me.c), self.local.at[k]
            ).wait()
        for rel in RELS:

            def body():
                for k in range(len(self.chunks)):
                    self.wait_in(k, rel, 1 - me.c, self.crossed)
                    for direction in self.ends(k, rel):
                        guarded(
                            me.has(direction), lambda: self.copy(k, rel, direction).wait_send()
                        )

            guarded(me.exists(rel[2]), body)


def slots_of(order):
    base, total, count = {}, 0, 1
    for dim in order:
        base[dim] = total
        total += count * (5 if dim == "z" else 1)
        count *= 4 if dim == "z" else 2
    return base, total


BLOCK = 432
CROSS_RING = 5
OPERAND_SCRATCH = (
    ("normed_t", (WIDTH, TOKENS), jnp.bfloat16),
    ("mixture_t", (WIDTH, TOKENS), jnp.bfloat16),
    ("normed2_t", (WIDTH, TOKENS), jnp.bfloat16),
    ("bb_t", (WIDTH, TOKENS), jnp.bfloat16),
    ("bin", (8, TOKENS, 512), jnp.bfloat16),
    ("bout", (8, TOKENS, 256), jnp.bfloat16),
    ("bexp", (8, TOKENS, 640), jnp.bfloat16),
    ("act", (4, TOKENS, WIDTH), jnp.bfloat16),
)
OPERAND_NAMES = ("normed", "mixture", "normed2", "bb", "bin", "bout", "bexp", "act")


class Scatter:
    def __init__(self, me, chunks, o, p_out, s_out, own, cross, core, got, *sems):
        self.me, self.chunks, self.o = me, chunks, o
        self.outs = {"p": p_out, "s": s_out}
        self.own, self.cross, self.core, self.got = own, cross, core, got
        self.crossed, self.cross_sent, self.arrived, self.sent = sems
        self.rels = RELS[::-1]
        self.rows, self.slot_row, total = [], [], 0
        for ch in chunks:
            self.rows.append(ch[1] if ch[0] == "p" else 288 + ch[1])
            self.slot_row.append(total)
            total += slots_of(ch[3])[1] * ch[2]

    @staticmethod
    def scratch(chunks):
        rows = sum(slots_of(ch[3])[1] * ch[2] for ch in chunks)
        most = max(slots_of(ch[3])[1] for ch in chunks)
        n = len(chunks)
        buffers = [
            pltpu.VMEM((BLOCK, WIDTH), jnp.bfloat16),
            pltpu.VMEM((CROSS_RING, BLOCK, WIDTH), jnp.bfloat16),
            pltpu.VMEM((16, BLOCK, WIDTH), jnp.bfloat16),
            pltpu.VMEM((rows, WIDTH), jnp.bfloat16),
        ]
        return buffers, [(16,), (16,), (n, most), (n, 16)]

    def compute(self, b, core, target):
        o, d, s = self.o, b[0] * 2 + core, b[1] * 2 + b[2]

        @pl.loop(0, 2)
        def _(i):
            at = pl.ds(pl.multiple_of(d * 288 + i * 144, 16), 144)
            to = pl.ds(pl.multiple_of(i * 144, 16), 144)
            first = dot(o.normed_t[at, :], o.bin[s])
            second = dot(o.mixture_t[at, :], o.bout[s])
            third = dot(o.normed2_t[at, :], o.bexp[s])
            target[to, 0:384] = first[:, 0:384].astype(jnp.bfloat16)
            target[to, 384:512] = (first[:, 384:] + second[:, :128]).astype(jnp.bfloat16)
            target[to, 512:640] = (second[:, 128:] + third[:, :128]).astype(jnp.bfloat16)
            target[to, 640:] = third[:, 128:].astype(jnp.bfloat16)

        at = pl.ds(pl.multiple_of(s * 144, 16), 144)
        target[288:432, :] = dot(o.bb_t[at, :], o.act[d]).astype(jnp.bfloat16)

    def cross_copy(self, i):
        b = self.me.at(self.rels[i])
        return pltpu.make_async_remote_copy(
            src_ref=self.cross.at[i % CROSS_RING],
            dst_ref=self.core.at[blk(b)],
            send_sem=self.cross_sent.at[blk(b)],
            recv_sem=self.crossed.at[blk(b)],
            device_id=self.me.neighbour("c"),
            device_id_type=MESH,
        )

    def slot(self, k, b, direction, z):
        order = self.chunks[k][3]
        base, _ = slots_of(order)
        dim = "z" if direction in "ud" else direction
        coord = {"x": (b[0], 2), "y": (b[2], 2), "z": (b[1], 4)}
        index = 0
        for d in order[: order.index(dim)]:
            index = index * coord[d][1] + coord[d][0]
        if dim == "z":
            inner = b[1] if direction == "d" else jnp.where(b[1] == z, 4, b[1])
            index = index * 5 + inner
        return base[dim] + index

    def got_at(self, k, j):
        n = self.chunks[k][2]
        return self.got.at[pl.ds(pl.multiple_of(self.slot_row[k] + j * n, 16), n), :]

    def send(self, k, i):
        rel = self.rels[i]
        b, direction = self.me.at(rel), links(rel, self.chunks[k][3])[1]
        z = self.me.z + {"u": 1, "d": -1}.get(direction, 0)
        j = self.slot(k, b, {"x": "x", "y": "y", "u": "d", "d": "u"}[direction], z)
        return pltpu.make_async_remote_copy(
            src_ref=self.core.at[blk(b), pl.ds(self.rows[k], self.chunks[k][2]), :],
            dst_ref=self.got_at(k, j),
            send_sem=self.sent.at[k, blk(b)],
            recv_sem=self.arrived.at[k, j],
            device_id=self.me.neighbour(direction),
            device_id_type=MESH,
        )

    def add(self, k, b, messages, final):
        ch, n = self.chunks[k], blk(b)

        @pl.loop(0, ch[2] // 16)
        def _(t):
            r = pl.ds(pl.multiple_of(self.rows[k] + t * 16, 16), 16)
            v = self.own[r, :].astype(jnp.float32) + self.core[n, r, :].astype(jnp.float32)
            for cond, j in messages:
                at = pl.ds(pl.multiple_of(self.slot_row[k] + j * ch[2] + t * 16, 16), 16)
                q = self.got[at, :].astype(jnp.float32)
                v = v + (q if cond is None else jnp.where(cond, q, 0.0))
            if final is None:
                self.core[n, r, :] = v.astype(jnp.bfloat16)
            else:
                final[pl.ds(pl.multiple_of(ch[1] + t * 16, 16), 16), :] = v

    def guarded(self, i, body):
        guarded(self.me.exists(self.rels[i][2]), body)

    def free_cross(self, i):
        self.guarded(i, lambda: self.cross_copy(i).wait_send())

    def free_own(self, i):
        def body():
            for k, ch in enumerate(self.chunks):
                if links(self.rels[i], ch[3])[1]:
                    self.send(k, i).wait_send()

        self.guarded(i, body)

    def cross_event(self, i):
        if i >= CROSS_RING:
            self.free_cross(i - CROSS_RING)

        def body():
            self.compute(self.me.at(self.rels[i]), 1 - self.me.c, self.cross.at[i % CROSS_RING])
            self.cross_copy(i).start()

        self.guarded(i, body)

    def own_event(self, i):
        me, rel = self.me, self.rels[i]
        def body():
            b = me.at(rel)
            self.compute(b, me.c, self.own)
            held = self.core.at[blk(b)]
            pltpu.make_async_copy(held, held, self.crossed.at[blk(b)]).wait()
            for k, ch in enumerate(self.chunks):
                children, parent = links(rel, ch[3])
                messages = []
                for direction in children:
                    cond, j = me.has(direction), self.slot(k, b, direction, me.z)

                    def wait():
                        at = self.got_at(k, j)
                        pltpu.make_async_copy(at, at, self.arrived.at[k, j]).wait()

                    guarded(cond, wait)
                    messages.append((cond, j))
                self.add(k, b, messages, None if parent else self.outs[ch[0]])
                if parent:
                    self.send(k, i).start()

        self.guarded(i, body)

    def events(self, lag=2):
        n, out = len(self.rels), []
        for i in range(n + lag):
            if i < n:
                out.append(functools.partial(self.cross_event, i))
            if i >= lag:
                out.append(functools.partial(self.own_event, i - lag))
        return out

    def finish(self):
        n = len(self.rels)
        for i in range(n - CROSS_RING, n):
            self.free_cross(i)
        for i in range(n):
            self.free_own(i)


class Exchange:
    def __init__(self, me, source, target, sent, arrived, local):
        self.me, self.source, self.target = me, source, target
        self.sent, self.arrived, self.local = sent, arrived, local

    def rows(self, ref, s):
        return ref.at[pl.ds(pl.multiple_of(s * 32, 32), 32), :]

    def copy(self, k):
        me = self.me
        other = (me.s + k) % 8
        return pltpu.make_async_remote_copy(
            src_ref=self.rows(self.source, other),
            dst_ref=self.rows(self.target, me.s),
            send_sem=self.sent.at[k],
            recv_sem=self.arrived.at[k],
            device_id=(me.d, other),
            device_id_type=MESH,
        )

    def stay(self):
        return pltpu.make_async_copy(
            self.rows(self.source, self.me.s), self.rows(self.target, self.me.s), self.local
        )

    def start(self):
        self.stay().start()
        for k in range(1, 8):
            self.copy(k).start()

    def finish(self):
        self.stay().wait()
        for k in range(1, 8):
            at = self.rows(self.target, (self.me.s - k + 8) % 8)
            pltpu.make_async_copy(at, at, self.arrived.at[k]).wait()
            self.copy(k).wait_send()


class Spread:
    def __init__(self, me, axis, source, target, sent, arrived, each):
        self.me, self.axis, self.source, self.target = me, axis, source, target
        self.sent, self.arrived, self.each = sent, arrived, each
        self.n = 4 if axis == "dp" else 8
        self.i = me.d if axis == "dp" else me.s

    def copy(self, k):
        other = (self.i + k) % self.n
        return pltpu.make_async_remote_copy(
            src_ref=self.source.at[other] if self.each else self.source,
            dst_ref=self.target.at[self.i],
            send_sem=self.sent.at[k],
            recv_sem=self.arrived.at[k],
            device_id=(other, self.me.s) if self.axis == "dp" else (self.me.d, other),
            device_id_type=MESH,
        )

    def start(self):
        for k in range(1, self.n):
            self.copy(k).start()
        self.target[self.i] = self.source[self.i] if self.each else self.source[...]

    def finish(self):
        for k in range(1, self.n):
            at = self.target.at[(self.i - k + self.n) % self.n]
            pltpu.make_async_copy(at, at, self.arrived.at[k]).wait()
            self.copy(k).wait_send()


def pieces(start, length, width=WIDTH):
    out, done = [], 0
    while done < length:
        row, column = divmod(start + done, width)
        n = min(width - column, length - done)
        out.append((row, column, n, done))
        done += n
    return out


def interleave(events, stages):
    cuts = sorted((int(share * len(events)), i) for i, (share, _) in enumerate(stages))
    done = 0
    for cut, i in cuts:
        for event in events[done:cut]:
            event()
        done = max(done, cut)
        stages[i][1]()
    for event in events[done:]:
        event()


def dma_sems(*shapes):
    return [pltpu.SemaphoreType.DMA(shape) for shape in shapes]


ANY_SPEC = pl.BlockSpec(memory_space=pl.ANY)
VMEM_SPEC = pl.BlockSpec(memory_space=pltpu.VMEM)
SLABS = (
    jax.ShapeDtypeStruct((8, WIDTH, WIDTH), jnp.bfloat16),
    jax.ShapeDtypeStruct((4, WIDTH, WIDTH), jnp.bfloat16),
)
STREAM = jax.ShapeDtypeStruct((TOKENS, WIDTH), jnp.bfloat16)


def first_gather_kernel(
    p_in, s_in, pack, cond, weight0, weight1, cot, p_out, s_out, mod_out, bias_out, incoming,
    packs, part, parts, whole, wholes, *sems,
):
    me = Place()
    gather = Gather(me, CHUNKS_ONE, p_in, s_in, p_out, s_out, *sems[:4])
    exchange = Exchange(me, cot, incoming, *sems[4:7])
    biases = Spread(me, "dp", pack, packs, *sems[7:9], False)
    terms = Spread(me, "dp", part, parts, *sems[9:11], True)
    columns = Spread(me, "sp", whole, wholes, *sems[11:13], False)
    greet(me)

    def begin():
        biases.start()
        for i, weight in enumerate((weight0, weight1)):
            product = jnp.dot(cond[...], weight[...], preferred_element_type=jnp.float32)
            for q in range(4):
                part[q, i : i + 1, :] = product[q : q + 1, :]
        terms.start()
        exchange.start()

    def middle():
        terms.finish()
        whole[...] = jnp.sum(parts[...], axis=0)
        columns.start()

    def end():
        columns.finish()
        biases.finish()
        exchange.finish()
        for i in range(2):
            mod_out[i] = jnp.zeros((8, WIDTH), jnp.float32)
            for s in range(8):
                for row, column, n, at in pieces(864 * s, 864):
                    mod_out[i, row : row + 1, column : column + n] = wholes[
                        s, i : i + 1, at : at + n
                    ]
            for k in range(4):
                for first, n_all in ((0, WIDTH), (WIDTH, 576)):
                    source = 6 * i + 4 + first // WIDTH
                    for row, column, n, at in pieces(1728 * k + first, n_all):
                        mod_out[i, row : row + 1, column : column + n] += packs[
                            k, source : source + 1, at : at + n
                        ]
                top = 6 * i
                bias_out[i, k // 2 : k // 2 + 1, 576 * (k % 2) : 576 * (k % 2 + 1)] = packs[
                    k, top : top + 1, 0:576
                ]
                for row in (2, 3):
                    bias_out[i, row : row + 1, 288 * k : 288 * (k + 1)] = packs[
                        k, top + row - 1 : top + row, 0:288
                    ]
                bias_out[i, 4 + k : 5 + k, :] = packs[k, top + 3 : top + 4, :]

    events = gather.events()
    own = len(CHUNKS_ONE)
    interleave(events, [(own / len(events), begin), (0.3, middle), (0.8, end)])
    gather.finish()


def first_gather(p, s, pack, cond, weights, cotangent):
    return pl.pallas_call(
        first_gather_kernel,
        out_shape=SLABS
        + (
            jax.ShapeDtypeStruct((2, 8, WIDTH), jnp.float32),
            jax.ShapeDtypeStruct((2, 8, WIDTH), jnp.float32),
            STREAM,
        ),
        in_specs=[ANY_SPEC] * 2 + [VMEM_SPEC] * 4 + [ANY_SPEC],
        out_specs=(ANY_SPEC, ANY_SPEC, VMEM_SPEC, VMEM_SPEC, ANY_SPEC),
        scratch_shapes=[
            pltpu.VMEM((4, 16, WIDTH), jnp.float32),
            pltpu.VMEM((4, 8, 864), jnp.float32),
            pltpu.VMEM((4, 8, 864), jnp.float32),
            pltpu.VMEM((8, 864), jnp.float32),
            pltpu.VMEM((8, 8, 864), jnp.float32),
        ]
        + dma_sems(*Gather.SEMS, (8,), (8,), (), (4,), (4,), (4,), (4,), (8,), (8,)),
        compiler_params=pltpu.CompilerParams(collective_id=0, has_side_effects=True),
        name="first_gather",
    )(p, s, pack, cond, *weights, cotangent)


def scatter_kernel(streams, chunks, *refs):
    operands = dict(zip(OPERAND_NAMES, refs))
    bias_grad, mod_grad, cond = refs[8:11]
    sources = refs[11 : 11 + streams]
    refs = refs[11 + streams :]
    p_out, s_out, weight_grad, totals = refs[:4]
    targets = refs[4 : 4 + streams]
    refs = refs[4 + streams :]
    o = Refs()
    for (name, *_), ref in zip(OPERAND_SCRATCH, refs):
        setattr(o, name, ref)
    refs = refs[len(OPERAND_SCRATCH) :]
    small, small_in, row_sum, row_in, total = refs[:5]
    buffers, sems = refs[5:9], refs[9:]
    me = Place()
    scatter = Scatter(me, chunks, o, p_out, s_out, *buffers, *sems[:4])
    over_frames = Spread(me, "sp", small, small_in, *sems[4:6], True)
    over_data = Spread(me, "dp", row_sum, row_in, *sems[6:8], False)
    over_all = Spread(me, "sp", total, totals, *sems[8:10], False)
    loaded = sems[10]
    exchanges = [
        Exchange(me, source, target, *sems[11 + 3 * i : 14 + 3 * i])
        for i, (source, target) in enumerate(zip(sources, targets))
    ]
    staged = [buffers[1].at[i, 0:TOKENS, :] for i in range(4)]
    places = staged + [o.bin, o.bout, o.bexp, o.act]
    loads = [
        pltpu.make_async_copy(operands[name], place, loaded.at[i])
        for i, (name, place) in enumerate(zip(OPERAND_NAMES, places))
    ]
    for load in loads:
        load.start()
    greet(me)
    for exchange in exchanges:
        exchange.start()
    for load, source, target in zip(
        loads, staged, (o.normed_t, o.mixture_t, o.normed2_t, o.bb_t)
    ):
        load.wait()
        target[...] = source[...].T
    for load in loads[4:]:
        load.wait()

    def begin():
        small[...] = jnp.zeros(small.shape, jnp.float32)
        for s in range(8):
            small[s, 0:1, :] = bias_grad[s : s + 1, :]
            for row, column, n, at in pieces(864 * s, 864):
                small[s, 1:2, at : at + n] = mod_grad[row : row + 1, column : column + n]
        over_frames.start()

    def second():
        over_frames.finish()
        row_sum[...] = jnp.sum(small_in[...], axis=0)
        over_data.start()

    def third():
        over_data.finish()
        total[...] = jnp.sum(row_in[...], axis=0)
        over_all.start()
        for t in range(9):
            r = slice(32 * t, 32 * (t + 1))
            v = cond[r, 0:1] * row_in[0, 1:2, 0:864]
            for q in range(1, 4):
                v = v + cond[r, q : q + 1] * row_in[q, 1:2, 0:864]
            weight_grad[r, :] = v

    def fourth():
        over_all.finish()
        for exchange in exchanges:
            exchange.finish()

    interleave(
        scatter.events(), [(0.1, begin), (0.35, second), (0.55, third), (0.8, fourth)]
    )
    scatter.finish()


def scatter_call(chunks, o, cond, streams, collective_id):
    n = len(streams)
    rows = jax.ShapeDtypeStruct
    buffers, sems = Scatter.scratch(chunks)
    return pl.pallas_call(
        functools.partial(scatter_kernel, n, chunks),
        out_shape=[
            rows((288, WIDTH), jnp.float32),
            rows((144, WIDTH), jnp.float32),
            rows((288, 864), jnp.float32),
            rows((8, 8, WIDTH), jnp.float32),
        ]
        + [STREAM] * n,
        in_specs=[ANY_SPEC] * 8 + [VMEM_SPEC] * 3 + [ANY_SPEC] * n,
        out_specs=[VMEM_SPEC] * 4 + [ANY_SPEC] * n,
        scratch_shapes=[pltpu.VMEM(shape, kind) for _, shape, kind in OPERAND_SCRATCH]
        + [
            pltpu.VMEM(shape, jnp.float32)
            for shape in ((8, 8, WIDTH), (8, 8, WIDTH), (8, WIDTH), (4, 8, WIDTH), (8, WIDTH))
        ]
        + buffers
        + dma_sems(*sems, (8,), (8,), (4,), (4,), (8,), (8,), (8,), *([(8,), (8,), ()] * n)),
        compiler_params=pltpu.CompilerParams(
            collective_id=collective_id, has_side_effects=True, vmem_limit_bytes=63 << 20
        ),
        name="first_scatter" if n else "second_scatter",
    )(*[o[name] for name in OPERAND_NAMES], o["bias_grad"], o["mod_grad"], cond, *streams)


def unpack_kernel(*refs):
    ins, outs = refs[:6], refs[6:]
    d = lax.axis_index("dp")
    for i in range(2):
        packed, turned, totals = ins[3 * i : 3 * i + 3]
        a_in, a_bias, a_out, o_bias, expand, e_bias, shrink, s_bias, m_bias = outs[
            9 * i : 9 * i + 9
        ]
        a_in[...] = packed[:, 0:432]
        a_out[...] = packed[:, 432:576]
        expand[...] = packed[:, 576:1152]
        shrink[...] = turned[...].T
        for k in range(4):

            @pl.when(d == k)
            def _():
                half = 576 * (k % 2)
                a_bias[...] = totals[k // 2, 0:1, half : half + 576]
                o_bias[...] = totals[2, 0:1, 288 * k : 288 * (k + 1)]
                s_bias[...] = totals[3, 0:1, 288 * k : 288 * (k + 1)]
                e_bias[...] = totals[4 + k, 0:1, :]
                for s in (2 * k, 2 * k + 1):
                    to = 864 * (s % 2)
                    m_bias[:, to : to + 864] = totals[s, 1:2, 0:864]


def unpack(*grads):
    shapes = [(288, 432), (1, 576), (288, 144), (1, 288), (288, 576), (1, 1152), (1152, 144)]
    shapes += [(1, 288), (1, 1728)]
    outs = pl.pallas_call(
        unpack_kernel,
        out_shape=[jax.ShapeDtypeStruct(shape, jnp.float32) for shape in shapes * 2],
        in_specs=[VMEM_SPEC] * 6,
        out_specs=[VMEM_SPEC] * 18,
        compiler_params=pltpu.CompilerParams(vmem_limit_bytes=32 << 20),
        name="unpack",
    )(*grads)
    return [out.reshape(-1) if out.shape[0] == 1 else out for out in outs]


SCALE = HD ** (-0.5)
NEGATIVE = -1e30


def dot(a, b):
    return lax.dot_general(a, b, (((1,), (0,)), ((), ())), preferred_element_type=jnp.float32)


def dot_nt(a, b):
    return lax.dot_general(a, b, (((1,), (1,)), ((), ())), preferred_element_type=jnp.float32)


def dot_tn(a, b):
    return lax.dot_general(a, b, (((0,), (0,)), ((), ())), preferred_element_type=jnp.float32)


def by_rows(body, step=32):
    @pl.loop(0, TOKENS // step)
    def _(i):
        body(pl.ds(pl.multiple_of(i * step, step), step))


def statistics(v):
    centered = v - jnp.mean(v, axis=1, keepdims=True)
    scale = lax.rsqrt(jnp.mean(centered * centered, axis=1, keepdims=True) + EPSILON)
    return centered * scale, scale


def fold(v):
    return jnp.sum(v.reshape(v.shape[0] // 8, 8, v.shape[1]), axis=0)


def gelu_both(h):
    c, a = math.sqrt(2.0 / math.pi), 0.044715
    square = h * h
    t = jnp.tanh(c * h * (1.0 + a * square))
    half = 0.5 * (1.0 + t)
    return h * half, half + 0.5 * h * (1.0 - t * t) * (c * (1.0 + 3.0 * a * square))


WIN_IN, WIN_OUT, WIN_EXP = slice(0, 512), slice(384, 640), slice(512, 1152)


def forward_stages(e, y):
    mod = e.mod
    shift1, scale1, gate1 = [lambda i=i: mod[i : i + 1, :] for i in range(3)]
    shift2, scale2, gate2 = [lambda i=i: mod[i : i + 1, :] for i in range(3, 6)]

    def normalize():
        e.bslab[...] = jnp.zeros(e.bslab.shape, jnp.float32)
        for s in range(8):
            for row, first in ((0, 0), (1, 2 * WIDTH)):
                lo, hi = max(432 * s, first), min(432 * (s + 1), first + WIDTH)
                if lo < hi:
                    e.bslab[s, 0:1, lo - 432 * s : hi - 432 * s] = e.bias[
                        row : row + 1, lo - first : hi - first
                    ]

        def rows(r):
            n, _ = statistics(e.x[r, :].astype(jnp.float32))
            e.normed[r, :] = (n * (1.0 + scale1()) + shift1()).astype(jnp.bfloat16)

        by_rows(rows)

    def project(first):
        @pl.loop(first, first + 4)
        def _(s):
            e.wait_p(s)
            v = dot(e.normed[...], e.pv[s, :, WIN_IN]) + e.bslab[s, 0:1, :]
            for j in range(6):
                e.heads[6 * s + j] = v[:, HD * j : HD * (j + 1)].astype(jnp.bfloat16)

    def attend(first):
        @pl.loop(first, first + 4)
        def _(h):
            probs = attention_probs(e, h)
            e.mh[h] = dot(probs.astype(jnp.bfloat16), e.heads[2 * H + h]).astype(jnp.bfloat16)

    def join():
        for h in range(H):
            e.mixture[:, HD * h : HD * (h + 1)] = e.mh[h]
        for s in range(8):
            v = dot(e.mixture[...], e.pv[s, :, WIN_OUT])
            e.attended[:, 144 * s : 144 * (s + 1)] = v[:, 48:192]

    def middle():
        def rows(r):
            attended = e.attended[r, :] + e.bias[2:3, :]
            e.attended[r, :] = attended
            middle = e.x[r, :].astype(jnp.float32) + gate1() * attended
            e.middle[r, :] = middle
            n, _ = statistics(middle)
            e.normed2[r, :] = (n * (1.0 + scale2()) + shift2()).astype(jnp.bfloat16)

        by_rows(rows)
        e.branch[...] = jnp.zeros(e.branch.shape, jnp.float32)

    def expand(d):
        for half in range(2):
            v = dot(e.normed2[...], e.pv[2 * d + half, :, WIN_EXP])
            e.tmp[:, 576 * half : 576 * (half + 1)] = v[:, 64:640]

        def rows(r):
            value, slope = gelu_both(e.tmp[r, :] + e.bias[pl.ds(4 + d, 1), :])
            e.act[d, r, :] = value.astype(jnp.bfloat16)
            if e.slope is not None:
                e.slope[d, r, :] = slope

        by_rows(rows)

    def shrink(d):
        e.wait_s(d)
        e.branch[...] += dot_nt(e.act[d], e.sv[d])

    def mlp(first, count):
        @pl.loop(first, first + count)
        def _(d):
            expand(d)
            shrink(d)

    def close():
        def rows(r):
            branch = e.branch[r, :] + e.bias[3:4, :]
            e.branch[r, :] = branch
            if y is not None:
                y[r, :] = (e.middle[r, :] + gate2() * branch).astype(jnp.bfloat16)

        by_rows(rows)

    part = functools.partial
    return (
        [normalize, part(project, 0), part(project, 4)]
        + [part(attend, h) for h in range(0, H, 4)]
        + [join, middle]
        + [part(mlp, d, 1) for d in range(4)]
        + [close]
    )


def attention_probs(e, h):
    scores = dot_nt(e.heads[h], e.heads[H + h]) * SCALE
    if e.mask is not None:
        scores = scores + e.mask[...]
    exponent = jnp.exp(scores - jnp.max(scores, axis=1, keepdims=True))
    return exponent / jnp.sum(exponent, axis=1, keepdims=True)


def forward_pass(e, y):
    for stage in forward_stages(e, y):
        stage()


def backward_pass(e):
    mod = e.mod
    gate1, scale1 = lambda: mod[2:3, :], lambda: mod[1:2, :]
    gate2, scale2 = lambda: mod[5:6, :], lambda: mod[4:5, :]
    e.sums[...] = jnp.zeros(e.sums.shape, jnp.float32)
    e.bout[...] = jnp.zeros(e.bout.shape, jnp.bfloat16)
    for s in range(8):
        e.bexp[s, :, 0:128] = jnp.zeros((TOKENS, 128), jnp.bfloat16)
        e.bin[s, :, 384:512] = jnp.zeros((TOKENS, 128), jnp.bfloat16)

    e.wait_kept("branch")

    def first(r):
        g = e.g[r, :].astype(jnp.float32)
        back = (gate2() * g).astype(jnp.bfloat16)
        e.bb[r, :] = back
        e.sums[5] += fold(g * e.branch[r, :])
        e.sums[7] += fold(back.astype(jnp.float32))

    by_rows(first)
    e.wait_kept("slope")

    @pl.loop(0, 4)
    def _(d):
        e.rewait_s(d)
        e.tmp[...] = dot(e.bb[...], e.sv[d])

        def hidden(r):
            back = (e.tmp[r, :] * e.slope[d, r, :]).astype(jnp.bfloat16)
            for half in range(2):
                e.bexp[2 * d + half, r, 64:640] = back[:, 576 * half : 576 * (half + 1)]
            e.sums[8 + d] += fold(back.astype(jnp.float32))

        by_rows(hidden)

    e.tmp[...] = jnp.zeros(e.tmp.shape, jnp.float32)

    @pl.loop(0, 8)
    def _(s):
        e.rewait_p(s)
        e.tmp[...] += dot_nt(e.bexp[s], e.pv[s, :, WIN_EXP])

    e.wait_kept("middle")
    e.wait_kept("attended")
    e.wait_kept("heads")

    def second(r):
        n, scale = statistics(e.middle[r, :])
        back_normed = e.tmp[r, :]
        e.sums[3] += fold(back_normed)
        e.sums[4] += fold(back_normed * n)
        u = back_normed * (1.0 + scale2())
        inner = jnp.mean(u, axis=1, keepdims=True) + n * jnp.mean(u * n, axis=1, keepdims=True)
        back_middle = e.g[r, :].astype(jnp.float32) + scale * (u - inner)
        e.middle[r, :] = back_middle
        e.sums[2] += fold(back_middle * e.attended[r, :])
        back = (gate1() * back_middle).astype(jnp.bfloat16)
        e.sums[6] += fold(back.astype(jnp.float32))
        for s in range(8):
            e.bout[s, r, 48:192] = back[:, 144 * s : 144 * (s + 1)]

    by_rows(second)
    e.tmp[...] = jnp.zeros(e.tmp.shape, jnp.float32)

    @pl.loop(0, 8)
    def _(s):
        e.tmp[...] += dot_nt(e.bout[s], e.pv[s, :, WIN_OUT])

    for h in range(H):
        e.mh[h] = e.tmp[:, HD * h : HD * (h + 1)].astype(jnp.bfloat16)

    @pl.loop(0, H)
    def _(h):
        q, k, v, back = e.heads[h], e.heads[H + h], e.heads[2 * H + h], e.mh[h]
        probs = attention_probs(e, h)
        back_probs = dot_nt(back, v)
        e.heads[2 * H + h] = dot_tn(probs.astype(jnp.bfloat16), back).astype(jnp.bfloat16)
        delta = jnp.sum(probs * back_probs, axis=1, keepdims=True)
        back_scores = (probs * (back_probs - delta)).astype(jnp.bfloat16)
        e.heads[h] = (dot(back_scores, k) * SCALE).astype(jnp.bfloat16)
        e.heads[H + h] = (dot_tn(back_scores, q) * SCALE).astype(jnp.bfloat16)

    e.tmp[...] = jnp.zeros(e.tmp.shape, jnp.float32)
    ones = jnp.ones((8, TOKENS), jnp.bfloat16)

    @pl.loop(0, 8)
    def _(s):
        for j in range(6):
            e.bin[s, :, HD * j : HD * (j + 1)] = e.heads[6 * s + j]
        e.bslab[s] = dot(ones, e.bin[s])
        e.tmp[...] += dot_nt(e.bin[s], e.pv[s, :, WIN_IN])

    def third(r):
        n, scale = statistics(e.x[r, :].astype(jnp.float32))
        back_normed = e.tmp[r, :]
        e.sums[0] += fold(back_normed)
        e.sums[1] += fold(back_normed * n)
        u = back_normed * (1.0 + scale1())
        inner = jnp.mean(u, axis=1, keepdims=True) + n * jnp.mean(u * n, axis=1, keepdims=True)
        e.back_x[r, :] = (e.middle[r, :] + scale * (u - inner)).astype(jnp.bfloat16)

    by_rows(third)

    for s in range(8):
        for row, first_column in ((0, 0), (1, 2 * WIDTH)):
            lo, hi = max(432 * s, first_column), min(432 * (s + 1), first_column + WIDTH)
            if lo < hi:
                e.bias_grad[row : row + 1, lo - first_column : hi - first_column] = e.bslab[
                    s, 0:1, lo - 432 * s : hi - 432 * s
                ]
    for row, slot in ((2, 6), (3, 7), (4, 8), (5, 9), (6, 10), (7, 11)):
        e.bias_grad[row : row + 1, :] = jnp.sum(e.sums[slot], axis=0, keepdims=True)
    for slot in range(6):
        e.mod_grad[slot : slot + 1, :] = jnp.sum(e.sums[slot], axis=0, keepdims=True)
    e.mod_grad[6:8, :] = jnp.zeros((2, WIDTH), jnp.float32)


class Refs:
    pass


WEIGHT_SCRATCH = (
    ("pv", (8, WIDTH, WIDTH), jnp.bfloat16),
    ("sv", (4, WIDTH, WIDTH), jnp.bfloat16),
)
FORWARD_SCRATCH = (
    ("bslab", (8, 8, 512), jnp.float32),
    ("heads", (3 * H, TOKENS, HD), jnp.bfloat16),
    ("mh", (H, TOKENS, HD), jnp.bfloat16),
    ("attended", (TOKENS, WIDTH), jnp.float32),
    ("middle", (TOKENS, WIDTH), jnp.float32),
    ("branch", (TOKENS, WIDTH), jnp.float32),
    ("tmp", (TOKENS, WIDTH), jnp.float32),
)
OPERANDS = (
    ("normed", (TOKENS, WIDTH), jnp.bfloat16),
    ("mixture", (TOKENS, WIDTH), jnp.bfloat16),
    ("normed2", (TOKENS, WIDTH), jnp.bfloat16),
    ("act", (4, TOKENS, WIDTH), jnp.bfloat16),
)
BACK_OPERANDS = (
    ("bb", (TOKENS, WIDTH), jnp.bfloat16),
    ("bin", (8, TOKENS, 512), jnp.bfloat16),
    ("bout", (8, TOKENS, 256), jnp.bfloat16),
    ("bexp", (8, TOKENS, 640), jnp.bfloat16),
)
SLOPE = (("slope", (4, TOKENS, WIDTH), jnp.float32),)
SUMS = (("sums", (12, 8, WIDTH), jnp.float32),)
BACK_OUTS = (
    ("back_x", (TOKENS, WIDTH), jnp.bfloat16),
    ("bias_grad", (8, WIDTH), jnp.float32),
    ("mod_grad", (8, WIDTH), jnp.float32),
)


def load_weights(e, p_hbm, s_hbm, psem, ssem, between=None, s_first=False):
    def p_copy(s):
        return pltpu.make_async_copy(p_hbm.at[s], e.pv.at[s], psem.at[s])

    def s_copy(d):
        return pltpu.make_async_copy(s_hbm.at[d], e.sv.at[d], ssem.at[d])

    def start(copy, n):
        @pl.loop(0, n)
        def _(i):
            copy(i).start()

    if s_first:
        start(s_copy, 4)
        between()
    start(p_copy, 8)
    if not s_first:
        start(s_copy, 4)
    e.wait_p = lambda s: p_copy(s).wait()
    e.wait_s = lambda d: s_copy(d).wait()
    e.rewait_p, e.rewait_s = (e.wait_p, e.wait_s) if s_first else (lambda s: None, lambda d: None)
    e.wait_kept = lambda name: None


def block_kernel(names, block, *refs):
    e = Refs()
    e.mask, e.slope, e.y = None, None, None
    for name, ref in zip(names, refs):
        setattr(e, name, ref)
    e.mod, e.bias = e.mods.at[block], e.biases.at[block]
    load_weights(e, e.p, e.s, e.psem, e.ssem)
    if "segments" in names:
        fill_mask(e)
    forward_pass(e, e.y)
    if "g" in names:
        backward_pass(e)


def fill_mask(e):
    frames = e.segments.shape[1]
    each = TOKENS // frames

    def clips(axis):
        frame = lax.broadcasted_iota(jnp.int32, (TOKENS, TOKENS), axis) // each
        clip = jnp.zeros((TOKENS, TOKENS), jnp.int32)
        for f in range(frames):
            clip = jnp.where(frame == f, e.segments[0, f], clip)
        return clip

    def spots(axis):
        return lax.broadcasted_iota(jnp.int32, (TOKENS, TOKENS), axis) % each

    same = (clips(0) == clips(1)) & (spots(0) == spots(1))
    e.mask[...] = jnp.where(same, 0.0, NEGATIVE)


def block_call(x, mods, biases, block, p, s, segments=None, g=None, give_y=True):
    inputs = [("x", x), ("mods", mods), ("biases", biases), ("p", p), ("s", s)]
    if segments is not None:
        inputs.append(("segments", segments))
    if g is not None:
        inputs.append(("g", g))
    outs, scratch = [], list(WEIGHT_SCRATCH + FORWARD_SCRATCH)
    if segments is not None:
        scratch.append(("mask", (TOKENS, TOKENS), jnp.float32))
    if give_y:
        outs.append(("y", (TOKENS, WIDTH), jnp.bfloat16))
    if g is None:
        scratch += OPERANDS
    else:
        outs += BACK_OUTS + OPERANDS + BACK_OPERANDS
        scratch += SLOPE + SUMS
    names = [name for name, *_ in inputs + outs + scratch] + ["psem", "ssem"]
    smem = pl.BlockSpec(memory_space=pltpu.SMEM)
    spec = lambda name: {"p": ANY_SPEC, "s": ANY_SPEC, "segments": smem}.get(name, VMEM_SPEC)
    results = pl.pallas_call(
        functools.partial(block_kernel, names, block),
        out_shape=[jax.ShapeDtypeStruct(shape, kind) for _, shape, kind in outs],
        in_specs=[spec(name) for name, _ in inputs],
        out_specs=[VMEM_SPEC] * len(outs),
        scratch_shapes=[pltpu.VMEM(shape, kind) for _, shape, kind in scratch]
        + [pltpu.SemaphoreType.DMA((8,)), pltpu.SemaphoreType.DMA((4,))],
        compiler_params=pltpu.CompilerParams(vmem_limit_bytes=63 << 20),
        name="block_both" if g is not None else "block_forward",
    )(*[value for _, value in inputs])
    return dict(zip([name for name, *_ in outs], results))


SECOND_SCRATCH = WEIGHT_SCRATCH + FORWARD_SCRATCH + OPERANDS + SLOPE + (
    ("y", (TOKENS, WIDTH), jnp.bfloat16),
)
KEPT = ("branch", "slope", "middle", "attended", "heads")
SAVED = KEPT + tuple(name for name, *_ in OPERANDS)
SHAPES = {name: (shape, kind) for name, shape, kind in SECOND_SCRATCH}


def second_gather_kernel(p_in, s_in, x, mods, biases, p, s, p_out, s_out, passed, *refs):
    saved, refs = dict(zip(SAVED, refs)), refs[len(SAVED) :]
    e = Refs()
    e.mask, e.x = None, x
    for (name, *_), ref in zip(SECOND_SCRATCH, refs):
        setattr(e, name, ref)
    e.mod, e.bias = mods.at[0], biases.at[0]
    sems = refs[len(SECOND_SCRATCH) :]
    me = Place()
    gather = Gather(me, CHUNKS_ONE, p_in, s_in, p_out, s_out, *sems[:4])
    exchange = Exchange(me, e.y, passed, *sems[4:7])
    greet(me)
    events = gather.events()
    own = len(CHUNKS_ONE) / len(events)
    stages = forward_stages(e, e.y)
    first, last = own, 0.6
    timed = [(own, lambda: load_weights(e, p, s, *sems[7:9]))]
    timed += [
        (first + (last - first) * i / len(stages), stage) for i, stage in enumerate(stages)
    ]
    keeps = [
        pltpu.make_async_copy(getattr(e, name), saved[name], sems[9].at[i])
        for i, name in enumerate(SAVED)
    ]

    def leave():
        exchange.start()
        for keep in keeps:
            keep.start()

    def left():
        exchange.finish()
        for keep in keeps:
            keep.wait()

    interleave(events, timed + [(last, leave), (0.95, left)])
    gather.finish()


def second_gather(p_own, s_own, x, mods, biases, p, s):
    results = pl.pallas_call(
        second_gather_kernel,
        out_shape=SLABS
        + (STREAM,)
        + tuple(jax.ShapeDtypeStruct(*SHAPES[name]) for name in SAVED),
        in_specs=[ANY_SPEC] * 2 + [VMEM_SPEC] * 3 + [ANY_SPEC] * 2,
        out_specs=(ANY_SPEC,) * (3 + len(SAVED)),
        scratch_shapes=[pltpu.VMEM(shape, kind) for _, shape, kind in SECOND_SCRATCH]
        + dma_sems(*Gather.SEMS, (8,), (8,), (), (8,), (4,), (len(SAVED),)),
        compiler_params=pltpu.CompilerParams(
            collective_id=1, has_side_effects=True, vmem_limit_bytes=60 << 20
        ),
        name="second_gather",
    )(p_own, s_own, x, mods, biases, p, s)
    return results[:3], dict(zip(SAVED, results[3:]))


def backward_kernel(names, *refs):
    e = Refs()
    e.mask = None
    for name, ref in zip(names, refs):
        setattr(e, name, ref)
    e.mod, e.bias = e.mods.at[0], e.biases.at[0]
    keeps = {
        name: pltpu.make_async_copy(getattr(e, name + "_kept"), getattr(e, name), e.ksem.at[i])
        for i, name in enumerate(KEPT)
    }
    keeps["branch"].start()
    load_weights(e, e.p, e.s, e.psem, e.ssem, between=keeps["slope"].start, s_first=True)
    for name in KEPT[2:]:
        keeps[name].start()
    e.wait_kept = lambda name: keeps[name].wait()
    backward_pass(e)


def backward_call(x, mods, biases, p, s, g, saved):
    inputs = [("x", x), ("mods", mods), ("biases", biases), ("p", p), ("s", s), ("g", g)]
    inputs += [(name + "_kept", saved[name]) for name in KEPT]
    outs = list(BACK_OUTS + BACK_OPERANDS)
    wanted = KEPT + ("bslab", "mh", "tmp")
    scratch = [item for item in SECOND_SCRATCH if item[0] in wanted]
    scratch = list(WEIGHT_SCRATCH) + scratch + list(SUMS)
    names = [name for name, *_ in inputs + outs + scratch] + ["psem", "ssem", "ksem"]
    spec = lambda name: ANY_SPEC if name in ("p", "s") or "_kept" in name else VMEM_SPEC
    results = pl.pallas_call(
        functools.partial(backward_kernel, names),
        out_shape=[jax.ShapeDtypeStruct(shape, kind) for _, shape, kind in outs],
        in_specs=[spec(name) for name, _ in inputs],
        out_specs=[VMEM_SPEC] * len(outs),
        scratch_shapes=[pltpu.VMEM(shape, kind) for _, shape, kind in scratch]
        + dma_sems((8,), (4,), (len(KEPT),)),
        compiler_params=pltpu.CompilerParams(vmem_limit_bytes=63 << 20),
        name="block_backward",
    )(*[value for _, value in inputs])
    return saved | dict(zip([name for name, *_ in outs], results))


def sinusoid(timesteps):
    half_width = D // 2
    frequencies = jnp.exp(
        -math.log(10000.0) * jnp.arange(half_width, dtype=jnp.float32) / half_width
    )
    angles = timesteps.astype(jnp.float32)[:, None] * frequencies[None, :]
    return jnp.concatenate([jnp.cos(angles), jnp.sin(angles)], axis=1)


def layer_norm(tensor):
    centered = tensor - jnp.mean(tensor, axis=-1, keepdims=True)
    return centered * lax.rsqrt(jnp.mean(centered * centered, axis=-1, keepdims=True) + EPSILON)


def modulate(tensor, shift_part, scale_part):
    return layer_norm(tensor) * (1.0 + scale_part) + shift_part


def matmul(left_side, right_side):
    return jnp.dot(left_side, right_side, preferred_element_type=jnp.float32)


def back_matmul(gradient, matrix):
    return lax.dot_general(
        gradient,
        matrix,
        (((gradient.ndim - 1,), (1,)), ((), ())),
        preferred_element_type=jnp.float32,
    )


def outer_product(left_side, right_side):
    flat_left = left_side.reshape(-1, left_side.shape[-1])
    flat_right = right_side.reshape(-1, right_side.shape[-1])
    return lax.dot_general(
        flat_left, flat_right, (((0,), (0,)), ((), ())), preferred_element_type=jnp.float32
    )


def column_totals(tensor):
    return jnp.sum(tensor.astype(jnp.float32).reshape(-1, tensor.shape[-1]), axis=0)


def per_sequence(tensor):
    return jnp.sum(tensor, axis=(1, 2))


def over_data(core, biases):
    attend_in, attend_out, expand, shrink = core
    attend_bias, out_bias, expand_bias, shrink_bias, modulate_bias = biases
    gathered = (
        lax.all_gather(attend_in, "dp", axis=0, tiled=True),
        lax.all_gather(attend_out, "dp", axis=0, tiled=True),
        lax.all_gather(expand, "dp", axis=0, tiled=True),
        lax.all_gather(shrink, "dp", axis=0, tiled=True),
        lax.all_gather(attend_bias, "dp", axis=0, tiled=True),
        lax.all_gather(out_bias, "dp", axis=0, tiled=True),
        lax.all_gather(expand_bias, "dp", axis=0, tiled=True),
        lax.all_gather(shrink_bias, "dp", axis=0, tiled=True),
        lax.all_gather(modulate_bias, "dp", axis=0, tiled=True),
    )
    return (gathered[:4], gathered[4:])


def over_frames(core):
    attend_in, attend_out, expand, shrink = core
    gathered = (
        lax.all_gather(attend_in, "sp", axis=1, tiled=True),
        lax.all_gather(attend_out, "sp", axis=1, tiled=True),
        lax.all_gather(expand, "sp", axis=1, tiled=True),
        lax.all_gather(shrink, "sp", axis=1, tiled=True),
    )
    return gathered


def collect(core, biases):
    core_rows, biases_full = over_data(core, biases)
    core_full = over_frames(core_rows)
    return (core_full, biases_full)


def own_rows(condition_all, rows):
    return lax.dynamic_slice_in_dim(condition_all, lax.axis_index("dp") * rows, rows, 1)


def modulation_of(condition_all, modulate_weights):
    rows = modulate_weights[0].shape[0]
    own = own_rows(condition_all, rows)
    partial_terms = jnp.stack([matmul(own, weight) for weight in modulate_weights], axis=1)
    summed = lax.psum_scatter(partial_terms, "dp", scatter_dimension=0, tiled=True)
    full = lax.all_gather(summed, "sp", axis=2, tiled=True)
    return [full[:, slot] for slot in range(len(modulate_weights))]


def sum_over_frames(terms):
    attend_in, attend_out, expand, shrink = terms
    return (
        lax.psum_scatter(
            attend_in.astype(jnp.bfloat16), "sp", scatter_dimension=1, tiled=True
        ).astype(jnp.float32),
        lax.psum_scatter(
            attend_out.astype(jnp.bfloat16), "sp", scatter_dimension=1, tiled=True
        ).astype(jnp.float32),
        lax.psum_scatter(expand.astype(jnp.bfloat16), "sp", scatter_dimension=1, tiled=True).astype(
            jnp.float32
        ),
        lax.psum_scatter(shrink.astype(jnp.bfloat16), "sp", scatter_dimension=1, tiled=True).astype(
            jnp.float32
        ),
    )


def sum_over_data(terms):
    attend_in, attend_out, expand, shrink = terms
    return (
        lax.psum_scatter(
            attend_in.astype(jnp.bfloat16), "dp", scatter_dimension=0, tiled=True
        ).astype(jnp.float32),
        lax.psum_scatter(
            attend_out.astype(jnp.bfloat16), "dp", scatter_dimension=0, tiled=True
        ).astype(jnp.float32),
        lax.psum_scatter(expand.astype(jnp.bfloat16), "dp", scatter_dimension=0, tiled=True).astype(
            jnp.float32
        ),
        lax.psum_scatter(shrink.astype(jnp.bfloat16), "dp", scatter_dimension=0, tiled=True).astype(
            jnp.float32
        ),
    )


def modulate_gradients(condition_all, back_modulations, rows):
    joined = jnp.stack(back_modulations, axis=1)
    columns = lax.psum_scatter(joined, "sp", scatter_dimension=2, tiled=True)
    every = lax.all_gather(columns, "dp", axis=0, tiled=True)
    own = own_rows(condition_all, rows).astype(jnp.float32)
    return [
        jnp.dot(own.T, every[:, slot], precision=HIGHEST_PRECISION)
        for slot in range(len(back_modulations))
    ]


def finish(core_terms, bias_terms):
    matrix_grads = sum_over_data(sum_over_frames(core_terms))
    attend_bias, out_bias, expand_bias, shrink_bias, modulate_bias = bias_terms
    totals = lax.psum(
        (attend_bias, out_bias, expand_bias, shrink_bias, modulate_bias), ("dp", "sp")
    )
    data_index = lax.axis_index("dp")
    data_count = lax.axis_size("dp")
    bias_grads = tuple(
        (
            lax.dynamic_slice_in_dim(
                total_bias,
                data_index * (total_bias.shape[0] // data_count),
                total_bias.shape[0] // data_count,
            )
            for total_bias in totals
        )
    )
    return (matrix_grads, bias_grads)


def frames_to_patches(tensor):
    return lax.all_to_all(tensor, "sp", split_axis=2, concat_axis=1, tiled=True)


def patches_to_frames(tensor):
    return lax.all_to_all(tensor, "sp", split_axis=1, concat_axis=2, tiled=True)


def attention_scores(queries, key_rows, forms, allowed):
    scores = jnp.einsum(forms[0], queries, key_rows, preferred_element_type=jnp.float32) * HD ** (
        -0.5
    )
    if allowed is not None:
        scores = jnp.where(allowed, scores, -1e30)
    return scores


def block_forward(stream, modulation, core, biases, forms, allowed):
    attend_in, attend_out, expand, shrink = core
    attend_bias, out_bias, expand_bias, shrink_bias, modulate_bias = biases
    model_width = stream.shape[-1]
    pieces = [
        modulation[:, None, None, slot * model_width : (slot + 1) * model_width]
        for slot in range(6)
    ]
    normed = modulate(stream, pieces[0], pieces[1]).astype(jnp.bfloat16)
    bias_float = attend_bias.astype(jnp.float32)
    joined_bias = jnp.concatenate(
        [bias_float[:model_width], jnp.zeros((model_width,), jnp.float32), bias_float[model_width:]]
    )
    projected = (matmul(normed, attend_in) + joined_bias).astype(jnp.bfloat16)
    head_shape = projected.shape[:3] + (H, HD)
    queries = projected[..., :model_width].reshape(head_shape)
    key_rows = projected[..., model_width : 2 * model_width].reshape(head_shape)
    values = projected[..., 2 * model_width :].reshape(head_shape)
    scores = attention_scores(queries, key_rows, forms, allowed)
    highest = jnp.max(scores, axis=-1, keepdims=True)
    exponent = jnp.exp(scores - highest)
    denominator = jnp.sum(exponent, axis=-1, keepdims=True)
    softmax_probs = exponent / denominator
    logsum = highest + jnp.log(denominator)
    mixture = (
        jnp.einsum(
            forms[1], softmax_probs.astype(jnp.bfloat16), values, preferred_element_type=jnp.float32
        )
        .astype(jnp.bfloat16)
        .reshape(stream.shape)
    )
    attended = matmul(mixture, attend_out) + out_bias.astype(jnp.float32)
    middle = stream + pieces[2] * attended
    normed_second = modulate(middle, pieces[3], pieces[4]).astype(jnp.bfloat16)
    hidden = matmul(normed_second, expand) + expand_bias.astype(jnp.float32)
    activated = jax.nn.gelu(hidden, approximate=True).astype(jnp.bfloat16)
    branch = matmul(activated, shrink) + shrink_bias.astype(jnp.float32)
    result = middle + pieces[5] * branch
    kept = (
        pieces,
        normed,
        queries,
        key_rows,
        values,
        logsum,
        mixture,
        attended,
        middle,
        normed_second,
        hidden,
        activated,
        branch,
    )
    return (result, kept)


def block_backward(incoming, stream, core, forms, allowed, kept):
    attend_in, attend_out, expand, shrink = core
    (
        pieces,
        normed,
        queries,
        key_rows,
        values,
        logsum,
        mixture,
        attended,
        middle,
        normed_second,
        hidden,
        activated,
        branch,
    ) = kept
    model_width = stream.shape[-1]
    sequences = stream.shape[0]
    back_branch = (pieces[5] * incoming).astype(jnp.bfloat16)
    back_gate_second = per_sequence(incoming * branch)
    shrink_term = outer_product(activated, back_branch)
    shrink_bias_term = column_totals(back_branch)
    back_activated = back_matmul(back_branch, shrink)
    _, gelu_pull = jax.vjp(lambda tensor: jax.nn.gelu(tensor, approximate=True), hidden)
    back_hidden = gelu_pull(back_activated)[0].astype(jnp.bfloat16)
    expand_term = outer_product(normed_second, back_hidden)
    expand_bias_term = column_totals(back_hidden)
    back_normed_second = back_matmul(back_hidden, expand)
    _, second_pull = jax.vjp(modulate, middle, pieces[3], pieces[4])
    back_middle, back_shift_second, back_scale_second = second_pull(back_normed_second)
    back_middle = back_middle + incoming
    back_attended = (pieces[2] * back_middle).astype(jnp.bfloat16)
    back_gate_first = per_sequence(back_middle * attended)
    out_term = outer_product(mixture, back_attended)
    out_bias_term = column_totals(back_attended)
    back_mixture = (
        back_matmul(back_attended, attend_out).astype(jnp.bfloat16).reshape(queries.shape)
    )
    scores = attention_scores(queries, key_rows, forms, allowed)
    softmax_probs = jnp.exp(scores - logsum)
    back_probs = jnp.einsum(forms[0], back_mixture, values, preferred_element_type=jnp.float32)
    back_values = jnp.einsum(
        forms[2],
        softmax_probs.astype(jnp.bfloat16),
        back_mixture,
        preferred_element_type=jnp.float32,
    )
    row_delta = jnp.sum(softmax_probs * back_probs, axis=-1, keepdims=True)
    back_scores = (softmax_probs * (back_probs - row_delta)).astype(jnp.bfloat16)
    score_scale = HD ** (-0.5)
    back_queries = (
        jnp.einsum(forms[1], back_scores, key_rows, preferred_element_type=jnp.float32)
        * score_scale
    )
    back_keys = (
        jnp.einsum(forms[2], back_scores, queries, preferred_element_type=jnp.float32) * score_scale
    )
    flat_shape = stream.shape
    back_projected = jnp.concatenate(
        [
            back_queries.reshape(flat_shape),
            back_keys.reshape(flat_shape),
            back_values.reshape(flat_shape),
        ],
        axis=-1,
    ).astype(jnp.bfloat16)
    attend_in_term = outer_product(normed, back_projected)
    projected_totals = column_totals(back_projected)
    attend_bias_term = jnp.concatenate(
        [projected_totals[:model_width], projected_totals[2 * model_width :]]
    )
    back_normed = back_matmul(back_projected, attend_in)
    _, first_pull = jax.vjp(modulate, stream, pieces[0], pieces[1])
    back_stream, back_shift_first, back_scale_first = first_pull(back_normed)
    back_stream = back_stream + back_middle
    back_modulation = jnp.concatenate(
        [
            back_shift_first.reshape(sequences, model_width),
            back_scale_first.reshape(sequences, model_width),
            back_gate_first,
            back_shift_second.reshape(sequences, model_width),
            back_scale_second.reshape(sequences, model_width),
            back_gate_second,
        ],
        axis=1,
    )
    modulate_bias_term = jnp.sum(back_modulation, axis=0)
    core_terms = (attend_in_term, out_term, expand_term, shrink_term)
    bias_terms = (
        attend_bias_term,
        out_bias_term,
        expand_bias_term,
        shrink_bias_term,
        modulate_bias_term,
    )
    return (back_stream, core_terms, back_modulation, bias_terms)


def shards(
    inputs,
    timesteps,
    segment_ids,
    spatial_attend_in,
    spatial_attend_bias,
    spatial_attend_out,
    spatial_out_bias,
    spatial_expand,
    spatial_expand_bias,
    spatial_shrink,
    spatial_shrink_bias,
    spatial_modulate,
    spatial_modulate_bias,
    temporal_attend_in,
    temporal_attend_bias,
    temporal_attend_out,
    temporal_out_bias,
    temporal_expand,
    temporal_expand_bias,
    temporal_shrink,
    temporal_shrink_bias,
    temporal_modulate,
    temporal_modulate_bias,
    cotangent,
):
    condition_all = jax.nn.silu(sinusoid(timesteps)).astype(jnp.bfloat16)
    allowed = (segment_ids[:, :, None] == segment_ids[:, None, :])[:, None, None, :, :]
    spatial_core = (spatial_attend_in, spatial_attend_out, spatial_expand, spatial_shrink)
    spatial_biases = (
        spatial_attend_bias,
        spatial_out_bias,
        spatial_expand_bias,
        spatial_shrink_bias,
        spatial_modulate_bias,
    )
    temporal_core = (temporal_attend_in, temporal_attend_out, temporal_expand, temporal_shrink)
    temporal_biases = (
        temporal_attend_bias,
        temporal_out_bias,
        temporal_expand_bias,
        temporal_shrink_bias,
        temporal_modulate_bias,
    )
    stream = inputs.astype(jnp.float32)
    modulations = modulation_of(condition_all, (spatial_modulate, temporal_modulate))
    core, biases = collect(spatial_core, spatial_biases)
    modulation = modulations[0] + biases[4].astype(jnp.float32)
    spatial_core = core
    spatial_out, spatial_kept = block_forward(stream, modulation, core, biases, SPATIAL_FORMS, None)
    passed = frames_to_patches(spatial_out.astype(jnp.bfloat16)).astype(jnp.float32)
    core, biases = collect(temporal_core, temporal_biases)
    modulation = modulations[1] + biases[4].astype(jnp.float32)
    temporal_out, temporal_kept = block_forward(
        passed, modulation, core, biases, TEMPORAL_FORMS, allowed
    )
    output = patches_to_frames(temporal_out.astype(jnp.bfloat16))
    incoming = frames_to_patches(cotangent).astype(jnp.float32)
    back_passed, core_terms, back_temporal, bias_terms = block_backward(
        incoming, passed, core, TEMPORAL_FORMS, allowed, temporal_kept
    )
    temporal_grads, temporal_bias_grads = finish(core_terms, bias_terms)
    back_spatial = patches_to_frames(back_passed.astype(jnp.bfloat16)).astype(jnp.float32)
    back_inputs, core_terms, back_spatial_modulation, bias_terms = block_backward(
        back_spatial, stream, spatial_core, SPATIAL_FORMS, None, spatial_kept
    )
    spatial_grads, spatial_bias_grads = finish(core_terms, bias_terms)
    modulate_grads = modulate_gradients(
        condition_all, (back_spatial_modulation, back_temporal), spatial_modulate.shape[0]
    )
    return (
        output,
        back_inputs.astype(jnp.bfloat16),
        spatial_grads[0],
        spatial_bias_grads[0],
        spatial_grads[1],
        spatial_bias_grads[1],
        spatial_grads[2],
        spatial_bias_grads[2],
        spatial_grads[3],
        spatial_bias_grads[3],
        modulate_grads[0],
        spatial_bias_grads[4],
        temporal_grads[0],
        temporal_bias_grads[0],
        temporal_grads[1],
        temporal_bias_grads[1],
        temporal_grads[2],
        temporal_bias_grads[2],
        temporal_grads[3],
        temporal_bias_grads[3],
        modulate_grads[1],
        temporal_bias_grads[4],
    )


def fits(mesh):
    return mesh.shape["dp"] == 4 and mesh.shape["sp"] == 8


def condition_rows(timesteps, rows):
    half = D // 2
    index = lax.axis_index("dp") * rows + jnp.arange(rows, dtype=jnp.int32)
    place = (index % half).astype(jnp.float32)
    frequencies = jnp.exp(-math.log(10000.0) * place / half)
    angles = timesteps.astype(jnp.float32)[:, None] * frequencies[None, :]
    wave = jnp.where((index < half)[None, :], jnp.cos(angles), jnp.sin(angles))
    return jax.nn.silu(wave).astype(jnp.bfloat16)


def fast_shards(
    inputs,
    timesteps,
    segment_ids,
    spatial_attend_in,
    spatial_attend_bias,
    spatial_attend_out,
    spatial_out_bias,
    spatial_expand,
    spatial_expand_bias,
    spatial_shrink,
    spatial_shrink_bias,
    spatial_modulate,
    spatial_modulate_bias,
    temporal_attend_in,
    temporal_attend_bias,
    temporal_attend_out,
    temporal_out_bias,
    temporal_expand,
    temporal_expand_bias,
    temporal_shrink,
    temporal_shrink_bias,
    temporal_modulate,
    temporal_modulate_bias,
    cotangent,
):
    def small(attend, out, expand, shrink, modulate):
        rows = [attend, out, shrink, expand, modulate[:D], modulate[D:]]
        return [jnp.pad(row.astype(jnp.float32)[None], ((0, 0), (0, D - row.shape[0]))) for row in rows]

    pack = jnp.concatenate(
        small(
            spatial_attend_bias,
            spatial_out_bias,
            spatial_expand_bias,
            spatial_shrink_bias,
            spatial_modulate_bias,
        )
        + small(
            temporal_attend_bias,
            temporal_out_bias,
            temporal_expand_bias,
            temporal_shrink_bias,
            temporal_modulate_bias,
        )
        + [jnp.zeros((4, D), jnp.float32)]
    )
    cond = jnp.pad(condition_rows(timesteps, spatial_modulate.shape[0]), ((0, 4), (0, 0)))
    cond_columns = cond.astype(jnp.float32).T
    x = inputs.reshape(TOKENS, WIDTH)
    spatial_p, spatial_s, mods, biases, incoming = first_gather(
        jnp.concatenate([spatial_attend_in, spatial_attend_out, spatial_expand], axis=1),
        spatial_shrink.T,
        pack,
        cond,
        (spatial_modulate, temporal_modulate),
        cotangent.reshape(TOKENS, WIDTH),
    )
    (temporal_p, temporal_s, passed), saved = second_gather(
        jnp.concatenate([temporal_attend_in, temporal_attend_out, temporal_expand], axis=1),
        temporal_shrink.T,
        x,
        mods,
        biases,
        spatial_p,
        spatial_s,
    )
    t = block_call(
        passed, mods, biases, 1, temporal_p, temporal_s, segments=segment_ids, g=incoming
    )
    packed_t, turned_t, modulate_t, totals_t, output, back_spatial = scatter_call(
        CHUNKS_TWO, t, cond_columns, (t["y"], t["back_x"]), 2
    )
    b = backward_call(x, mods, biases, spatial_p, spatial_s, back_spatial, saved)
    packed_s, turned_s, modulate_s, totals_s = scatter_call(CHUNKS, b, cond_columns, (), 3)
    outs = unpack(packed_s, turned_s, totals_s, packed_t, turned_t, totals_t)
    return (
        output.reshape(inputs.shape),
        b["back_x"].reshape(inputs.shape),
        *outs[:8],
        modulate_s,
        outs[8],
        *outs[9:17],
        modulate_t,
        outs[17],
    )


def solution(mesh):
    placed = (
        P("dp", "sp", None, None),
        P(),
        P("dp", None),
        P("dp", "sp"),
        P("dp"),
        P("dp", "sp"),
        P("dp"),
        P("dp", "sp"),
        P("dp"),
        P("dp", "sp"),
        P("dp"),
        P("dp", "sp"),
        P("dp"),
        P("dp", "sp"),
        P("dp"),
        P("dp", "sp"),
        P("dp"),
        P("dp", "sp"),
        P("dp"),
        P("dp", "sp"),
        P("dp"),
        P("dp", "sp"),
        P("dp"),
        P("dp", "sp", None, None),
    )
    return jax.shard_map(
        fast_shards if fits(mesh) else shards,
        mesh=mesh,
        in_specs=placed,
        out_specs=(
            P("dp", "sp", None, None),
            P("dp", "sp", None, None),
            P("dp", "sp"),
            P("dp"),
            P("dp", "sp"),
            P("dp"),
            P("dp", "sp"),
            P("dp"),
            P("dp", "sp"),
            P("dp"),
            P("dp", "sp"),
            P("dp"),
            P("dp", "sp"),
            P("dp"),
            P("dp", "sp"),
            P("dp"),
            P("dp", "sp"),
            P("dp"),
            P("dp", "sp"),
            P("dp"),
            P("dp", "sp"),
            P("dp"),
        ),
        check_vma=False,
    )
```

```python
import functools
import math

import jax
import jax.numpy as jnp
from jax import lax
from jax.experimental import pallas as pl
from jax.experimental.pallas import tpu as pltpu
from jax.sharding import PartitionSpec as P

D = 1152
H = 16
HD = 72


EPSILON = 1e-06
HIGHEST_PRECISION = lax.Precision.HIGHEST
SPATIAL_FORMS = ("sabhe,sache->sahbc", "sahbc,sache->sabhe", "sahbc,sabhe->sache")
TEMPORAL_FORMS = ("sabhe,scbhe->sbhac", "sbhac,scbhe->sabhe", "sbhac,sabhe->scbhe")


MESH = pl.DeviceIdType.MESH
TOKENS = 256
WIDTH = 1152
CHUNKS_ONE = (
    ("p", 0, 144, "zxy"),
    ("p", 144, 144, "zyx"),
    ("s", 0, 80, "yxz"),
    ("s", 80, 32, "zxy"),
    ("s", 112, 32, "zyx"),
)
S_CHUNKS = (("s", 0, 48, "zxy"), ("s", 48, 64, "zyx"), ("s", 112, 32, "yxz"))
P_CHUNKS = (
    ("p", 0, 112, "zxy"),
    ("p", 112, 112, "zyx"),
    ("p", 224, 32, "xyz"),
    ("p", 256, 32, "yxz"),
)
RELS = sorted(
    [(rx, ry, dz) for rx in (0, 1) for ry in (0, 1) for dz in range(-3, 4)],
    key=lambda r: (r[0] + r[1] + abs(r[2]), r != (0, 0, 0)),
)


class Place:
    def __init__(self):
        self.d, self.s = lax.axis_index("dp"), lax.axis_index("sp")
        self.x, self.c = self.d // 2, self.d % 2
        self.z, self.y = self.s // 2, self.s % 2

    def at(self, rel):
        rx, ry, dz = rel
        return (1 - self.x if rx else self.x, self.z + dz, 1 - self.y if ry else self.y)

    def exists(self, dz):
        return None if dz == 0 else ((self.z + dz >= 0) & (self.z + dz <= 3))

    def neighbour(self, direction):
        x, c, z, y = self.x, self.c, self.z, self.y
        return {
            "x": lambda: dev(1 - x, c, z, y),
            "y": lambda: dev(x, c, z, 1 - y),
            "u": lambda: dev(x, c, z + 1, y),
            "d": lambda: dev(x, c, z - 1, y),
            "c": lambda: dev(x, 1 - c, z, y),
        }[direction]()

    def has(self, direction):
        return {"u": lambda: self.z < 3, "d": lambda: self.z > 0}.get(direction, lambda: None)()


def dev(x, c, z, y):
    return (x * 2 + c, z * 2 + y)


def blk(b):
    return (b[0] * 4 + b[1]) * 2 + b[2]


def both(a, b):
    return b if a is None else (a if b is None else (a & b))


def guarded(cond, f):
    if cond is None:
        f()
    else:
        pl.when(cond)(f)


def greet(me):
    barrier = pltpu.get_barrier_semaphore()
    for k in range(1, 4):
        pl.semaphore_signal(
            barrier, inc=1, device_id=((me.d + k) % 4, me.s), device_id_type=MESH
        )
    for k in range(1, 8):
        pl.semaphore_signal(
            barrier, inc=1, device_id=(me.d, (me.s + k) % 8), device_id_type=MESH
        )
    pl.semaphore_wait(barrier, 10)


def links(rel, order):
    nz = {"x": rel[0], "y": rel[1], "z": rel[2]}
    last = max([i for i in range(3) if nz[order[i]]], default=-1)
    out = []
    for i, dim in enumerate(order):
        if i > last:
            out += ["u", "d"] if dim == "z" else [dim]
        elif i == last and dim == "z":
            out += ["u"] if rel[2] < 0 else ["d"]
    parent = None
    if last >= 0:
        parent = order[last] if order[last] != "z" else ("d" if rel[2] < 0 else "u")
    return out, parent


class Gather:
    SEMS = ((5, 16), (5, 16), (5, 5, 16), (5,))

    def __init__(self, me, chunks, p_in, s_in, p_out, s_out, arrived, crossed, sent, local):
        self.chunks = chunks
        self.me, self.ins, self.outs = me, {"p": p_in, "s": s_in}, {"p": p_out, "s": s_out}
        self.arrived, self.crossed, self.sent, self.local = arrived, crossed, sent, local

    def own(self, ch):
        return self.ins[ch[0]].at[pl.ds(ch[1], ch[2]), :]

    def place(self, ch, b, core):
        d, s = b[0] * 2 + core, b[1] * 2 + b[2]
        if ch[0] == "p":
            return self.outs["p"].at[s, pl.ds(d * 288 + ch[1], ch[2]), :]
        return self.outs["s"].at[d, pl.ds(s * 144 + ch[1], ch[2]), :]

    def copy(self, k, rel, direction):
        me, ch = self.me, self.chunks[k]
        b = me.at(rel)
        there = self.place(ch, b, me.c)
        return pltpu.make_async_remote_copy(
            src_ref=self.own(ch) if rel == (0, 0, 0) else there,
            dst_ref=there,
            send_sem=self.sent.at[k, "xyudc".index(direction), blk(b)],
            recv_sem=(self.crossed if direction == "c" else self.arrived).at[k, blk(b)],
            device_id=me.neighbour(direction),
            device_id_type=MESH,
        )

    def ends(self, k, rel):
        return links(rel, self.chunks[k][3])[0] + ["c"]

    def event(self, k, rel):
        me, ch = self.me, self.chunks[k]

        def body():
            if rel == (0, 0, 0):
                pltpu.make_async_copy(
                    self.own(ch), self.place(ch, me.at(rel), me.c), self.local.at[k]
                ).start()
            else:
                self.wait_in(k, rel, me.c, self.arrived)
            for direction in self.ends(k, rel):
                guarded(me.has(direction), lambda: self.copy(k, rel, direction).start())

        guarded(me.exists(rel[2]), body)

    def wait_in(self, k, rel, core, sems):
        b, ch = self.me.at(rel), self.chunks[k]
        pltpu.make_async_copy(self.own(ch), self.place(ch, b, core), sems.at[k, blk(b)]).wait()

    def events(self):
        return [
            functools.partial(self.event, k, rel) for rel in RELS for k in range(len(self.chunks))
        ]

    def finish(self):
        me = self.me
        for k, ch in enumerate(self.chunks):
            pltpu.make_async_copy(
                self.own(ch), self.place(ch, me.at((0, 0, 0)), me.c), self.local.at[k]
            ).wait()
        for rel in RELS:

            def body():
                for k in range(len(self.chunks)):
                    self.wait_in(k, rel, 1 - me.c, self.crossed)
                    for direction in self.ends(k, rel):
                        guarded(
                            me.has(direction), lambda: self.copy(k, rel, direction).wait_send()
                        )

            guarded(me.exists(rel[2]), body)


def slots_of(order):
    base, total, count = {}, 0, 1
    for dim in order:
        base[dim] = total
        total += count * (5 if dim == "z" else 1)
        count *= 4 if dim == "z" else 2
    return base, total


class Scatter:
    def __init__(self, me, chunks, compute, own, buffer, base, ring, out, *sems):
        self.me, self.chunks, self.compute, self.own = me, chunks, compute, own
        self.buffer, self.base, self.ring, self.out = buffer, base, ring, out
        self.crossed, self.cross_sent, self.arrived, self.sent = sems
        self.rels = RELS[::-1]
        self.block = sum(ch[2] for ch in chunks)
        self.slot_row, total = [], base + 16 * self.block
        for ch in chunks:
            self.slot_row.append(total)
            total += slots_of(ch[3])[1] * ch[2]
        self.ring_row = total

    @staticmethod
    def rows(chunks, ring):
        block = sum(ch[2] for ch in chunks)
        return (16 + ring) * block + sum(slots_of(ch[3])[1] * ch[2] for ch in chunks)

    @staticmethod
    def sems(chunks):
        n, most = len(chunks), max(slots_of(ch[3])[1] for ch in chunks)
        return [(16,), (16,), (n, most), (n, 16)]

    def at_row(self, row, n):
        return self.buffer.at[pl.ds(row, n), :]

    def core(self, b, first=0, n=None):
        row = self.base + blk(b) * self.block + first
        return self.at_row(pl.multiple_of(row, 16), self.block if n is None else n)

    def ring_at(self, i):
        return self.at_row(self.ring_row + (i % self.ring) * self.block, self.block)

    def cross_copy(self, i):
        b = self.me.at(self.rels[i])
        return pltpu.make_async_remote_copy(
            src_ref=self.ring_at(i),
            dst_ref=self.core(b),
            send_sem=self.cross_sent.at[blk(b)],
            recv_sem=self.crossed.at[blk(b)],
            device_id=self.me.neighbour("c"),
            device_id_type=MESH,
        )

    def slot(self, k, b, direction, z):
        order = self.chunks[k][3]
        base, _ = slots_of(order)
        dim = "z" if direction in "ud" else direction
        coord = {"x": (b[0], 2), "y": (b[2], 2), "z": (b[1], 4)}
        index = 0
        for d in order[: order.index(dim)]:
            index = index * coord[d][1] + coord[d][0]
        if dim == "z":
            inner = b[1] if direction == "d" else jnp.where(b[1] == z, 4, b[1])
            index = index * 5 + inner
        return base[dim] + index

    def got(self, k, j):
        n = self.chunks[k][2]
        return self.at_row(pl.multiple_of(self.slot_row[k] + j * n, 16), n)

    def send(self, k, i):
        rel, ch = self.rels[i], self.chunks[k]
        b, direction = self.me.at(rel), links(rel, ch[3])[1]
        z = self.me.z + {"u": 1, "d": -1}.get(direction, 0)
        j = self.slot(k, b, {"x": "x", "y": "y", "u": "d", "d": "u"}[direction], z)
        return pltpu.make_async_remote_copy(
            src_ref=self.core(b, ch[1], ch[2]),
            dst_ref=self.got(k, j),
            send_sem=self.sent.at[k, blk(b)],
            recv_sem=self.arrived.at[k, j],
            device_id=self.me.neighbour(direction),
            device_id_type=MESH,
        )

    def add(self, k, b, messages, final):
        ch = self.chunks[k]
        step = 16
        core_row = self.base + blk(b) * self.block + ch[1]

        @pl.loop(0, ch[2] // step)
        def _(t):
            r = pl.ds(pl.multiple_of(ch[1] + t * step, 16), step)
            held = pl.ds(pl.multiple_of(core_row + t * step, 16), step)
            v = self.own[r, :].astype(jnp.float32) + self.buffer[held, :].astype(jnp.float32)
            for cond, j in messages:
                at = pl.ds(pl.multiple_of(self.slot_row[k] + j * ch[2] + t * step, 16), step)
                q = self.buffer[at, :].astype(jnp.float32)
                v = v + (q if cond is None else jnp.where(cond, q, 0.0))
            if final:
                self.out[r, :] = v
            else:
                self.buffer[held, :] = v.astype(jnp.bfloat16)

    def guarded(self, i, body):
        guarded(self.me.exists(self.rels[i][2]), body)

    def free_cross(self, i):
        self.guarded(i, lambda: self.cross_copy(i).wait_send())

    def cross_event(self, i):
        if i >= self.ring:
            self.free_cross(i - self.ring)

        def body():
            self.compute(self.me.at(self.rels[i]), 1 - self.me.c, self.ring_at(i))
            self.cross_copy(i).start()

        self.guarded(i, body)

    def own_event(self, i):
        me, rel = self.me, self.rels[i]

        def body():
            b = me.at(rel)
            self.compute(b, me.c, self.own)
            held = self.core(b)
            pltpu.make_async_copy(held, held, self.crossed.at[blk(b)]).wait()
            for k, ch in enumerate(self.chunks):
                children, parent = links(rel, ch[3])
                messages = []
                for direction in children:
                    cond, j = me.has(direction), self.slot(k, b, direction, me.z)

                    def wait():
                        at = self.got(k, j)
                        pltpu.make_async_copy(at, at, self.arrived.at[k, j]).wait()

                    guarded(cond, wait)
                    messages.append((cond, j))
                self.add(k, b, messages, not parent)
                if parent:
                    self.send(k, i).start()

        self.guarded(i, body)

    def events(self, lag=2):
        n, out = len(self.rels), []
        for i in range(n + lag):
            if i < n:
                out.append(functools.partial(self.cross_event, i))
            if i >= lag:
                out.append(functools.partial(self.own_event, i - lag))
        return out

    def finish(self):
        n = len(self.rels)
        for i in range(n - self.ring, n):
            self.free_cross(i)
        for i in range(n):

            def body():
                for k, ch in enumerate(self.chunks):
                    if links(self.rels[i], ch[3])[1]:
                        self.send(k, i).wait_send()

            self.guarded(i, body)


class Exchange:
    def __init__(self, me, source, target, sent, arrived, local):
        self.me, self.source, self.target = me, source, target
        self.sent, self.arrived, self.local = sent, arrived, local

    def rows(self, ref, s):
        return ref.at[pl.ds(pl.multiple_of(s * 32, 32), 32), :]

    def copy(self, k):
        me = self.me
        other = (me.s + k) % 8
        return pltpu.make_async_remote_copy(
            src_ref=self.rows(self.source, other),
            dst_ref=self.rows(self.target, me.s),
            send_sem=self.sent.at[k],
            recv_sem=self.arrived.at[k],
            device_id=(me.d, other),
            device_id_type=MESH,
        )

    def stay(self):
        return pltpu.make_async_copy(
            self.rows(self.source, self.me.s), self.rows(self.target, self.me.s), self.local
        )

    def start(self):
        self.stay().start()
        for k in range(1, 8):
            self.copy(k).start()

    def finish(self):
        self.stay().wait()
        for k in range(1, 8):
            at = self.rows(self.target, (self.me.s - k + 8) % 8)
            pltpu.make_async_copy(at, at, self.arrived.at[k]).wait()
            self.copy(k).wait_send()


class Spread:
    def __init__(self, me, axis, source, target, sent, arrived, each):
        self.me, self.axis, self.source, self.target = me, axis, source, target
        self.sent, self.arrived, self.each = sent, arrived, each
        self.n = 4 if axis == "dp" else 8
        self.i = me.d if axis == "dp" else me.s

    def copy(self, k):
        other = (self.i + k) % self.n
        return pltpu.make_async_remote_copy(
            src_ref=self.source.at[other] if self.each else self.source,
            dst_ref=self.target.at[self.i],
            send_sem=self.sent.at[k],
            recv_sem=self.arrived.at[k],
            device_id=(other, self.me.s) if self.axis == "dp" else (self.me.d, other),
            device_id_type=MESH,
        )

    def start(self):
        for k in range(1, self.n):
            self.copy(k).start()
        self.target[self.i] = self.source[self.i] if self.each else self.source[...]

    def finish(self):
        for k in range(1, self.n):
            at = self.target.at[(self.i - k + self.n) % self.n]
            pltpu.make_async_copy(at, at, self.arrived.at[k]).wait()
            self.copy(k).wait_send()


def pieces(start, length, width=WIDTH):
    out, done = [], 0
    while done < length:
        row, column = divmod(start + done, width)
        n = min(width - column, length - done)
        out.append((row, column, n, done))
        done += n
    return out


def spread_out(stages, first, last):
    return [(first + (last - first) * i / len(stages), stage) for i, stage in enumerate(stages)]


def interleave(events, stages):
    cuts = sorted((int(share * len(events)), i) for i, (share, _) in enumerate(stages))
    done = 0
    for cut, i in cuts:
        for event in events[done:cut]:
            event()
        done = max(done, cut)
        stages[i][1]()
    for event in events[done:]:
        event()


def dma_sems(*shapes):
    return [pltpu.SemaphoreType.DMA(shape) for shape in shapes]


ANY_SPEC = pl.BlockSpec(memory_space=pl.ANY)
VMEM_SPEC = pl.BlockSpec(memory_space=pltpu.VMEM)
SLABS = (
    jax.ShapeDtypeStruct((8, WIDTH, WIDTH), jnp.bfloat16),
    jax.ShapeDtypeStruct((4, WIDTH, WIDTH), jnp.bfloat16),
)
STREAM = jax.ShapeDtypeStruct((TOKENS, WIDTH), jnp.bfloat16)


def first_gather_kernel(
    p_in, s_in, pack, cond, weight0, weight1, cot, p_out, s_out, mod_out, bias_out, incoming,
    packs, part, parts, whole, wholes, *sems,
):
    me = Place()
    gather = Gather(me, CHUNKS_ONE, p_in, s_in, p_out, s_out, *sems[:4])
    exchange = Exchange(me, cot, incoming, *sems[4:7])
    biases = Spread(me, "dp", pack, packs, *sems[7:9], False)
    terms = Spread(me, "dp", part, parts, *sems[9:11], True)
    columns = Spread(me, "sp", whole, wholes, *sems[11:13], False)
    greet(me)

    def begin():
        biases.start()
        for i, weight in enumerate((weight0, weight1)):
            product = jnp.dot(cond[...], weight[...], preferred_element_type=jnp.float32)
            for q in range(4):
                part[q, i : i + 1, :] = product[q : q + 1, :]
        terms.start()
        exchange.start()

    def middle():
        terms.finish()
        whole[...] = jnp.sum(parts[...], axis=0)
        columns.start()

    def end():
        columns.finish()
        biases.finish()
        exchange.finish()
        for i in range(2):
            mod_out[i] = jnp.zeros((8, WIDTH), jnp.float32)
            for s in range(8):
                for row, column, n, at in pieces(864 * s, 864):
                    mod_out[i, row : row + 1, column : column + n] = wholes[
                        s, i : i + 1, at : at + n
                    ]
            for k in range(4):
                for first, n_all in ((0, WIDTH), (WIDTH, 576)):
                    source = 6 * i + 4 + first // WIDTH
                    for row, column, n, at in pieces(1728 * k + first, n_all):
                        mod_out[i, row : row + 1, column : column + n] += packs[
                            k, source : source + 1, at : at + n
                        ]
                top = 6 * i
                bias_out[i, k // 2 : k // 2 + 1, 576 * (k % 2) : 576 * (k % 2 + 1)] = packs[
                    k, top : top + 1, 0:576
                ]
                for row in (2, 3):
                    bias_out[i, row : row + 1, 288 * k : 288 * (k + 1)] = packs[
                        k, top + row - 1 : top + row, 0:288
                    ]
                bias_out[i, 4 + k : 5 + k, :] = packs[k, top + 3 : top + 4, :]

    events = gather.events()
    own = len(CHUNKS_ONE)
    interleave(events, [(own / len(events), begin), (0.3, middle), (0.8, end)])
    gather.finish()


def first_gather(p, s, pack, cond, weights, cotangent):
    return pl.pallas_call(
        first_gather_kernel,
        out_shape=SLABS
        + (
            jax.ShapeDtypeStruct((2, 8, WIDTH), jnp.float32),
            jax.ShapeDtypeStruct((2, 8, WIDTH), jnp.float32),
            STREAM,
        ),
        in_specs=[ANY_SPEC] * 2 + [VMEM_SPEC] * 4 + [ANY_SPEC],
        out_specs=(ANY_SPEC, ANY_SPEC, VMEM_SPEC, VMEM_SPEC, ANY_SPEC),
        scratch_shapes=[
            pltpu.VMEM((4, 16, WIDTH), jnp.float32),
            pltpu.VMEM((4, 8, 864), jnp.float32),
            pltpu.VMEM((4, 8, 864), jnp.float32),
            pltpu.VMEM((8, 864), jnp.float32),
            pltpu.VMEM((8, 8, 864), jnp.float32),
        ]
        + dma_sems(*Gather.SEMS, (8,), (8,), (), (4,), (4,), (4,), (4,), (8,), (8,)),
        compiler_params=pltpu.CompilerParams(collective_id=0, has_side_effects=True),
        name="first_gather",
    )(p, s, pack, cond, *weights, cotangent)


def unpack_kernel(*refs):
    ins, outs = refs[:6], refs[6:]
    d = lax.axis_index("dp")
    for i in range(2):
        packed, turned, totals = ins[3 * i : 3 * i + 3]
        a_in, a_bias, a_out, o_bias, expand, e_bias, shrink, s_bias, m_bias = outs[
            9 * i : 9 * i + 9
        ]
        a_in[...] = packed[:, 0:432]
        a_out[...] = packed[:, 432:576]
        expand[...] = packed[:, 576:1152]
        shrink[...] = turned[...].T
        for k in range(4):

            @pl.when(d == k)
            def _():
                half = 576 * (k % 2)
                a_bias[...] = totals[k // 2, 0:1, half : half + 576]
                o_bias[...] = totals[2, 0:1, 288 * k : 288 * (k + 1)]
                s_bias[...] = totals[3, 0:1, 288 * k : 288 * (k + 1)]
                e_bias[...] = totals[4 + k, 0:1, :]
                for s in (2 * k, 2 * k + 1):
                    to = 864 * (s % 2)
                    m_bias[:, to : to + 864] = totals[s, 1:2, 0:864]


def unpack(*grads):
    shapes = [(288, 432), (1, 576), (288, 144), (1, 288), (288, 576), (1, 1152), (1152, 144)]
    shapes += [(1, 288), (1, 1728)]
    outs = pl.pallas_call(
        unpack_kernel,
        out_shape=[jax.ShapeDtypeStruct(shape, jnp.float32) for shape in shapes * 2],
        in_specs=[VMEM_SPEC] * 6,
        out_specs=[VMEM_SPEC] * 18,
        compiler_params=pltpu.CompilerParams(vmem_limit_bytes=32 << 20),
        name="unpack",
    )(*grads)
    return [out.reshape(-1) if out.shape[0] == 1 else out for out in outs]


SCALE = HD ** (-0.5)
NEGATIVE = -1e30


def dot(a, b):
    return lax.dot_general(a, b, (((1,), (0,)), ((), ())), preferred_element_type=jnp.float32)


def dot_nt(a, b):
    return lax.dot_general(a, b, (((1,), (1,)), ((), ())), preferred_element_type=jnp.float32)


def dot_tn(a, b):
    return lax.dot_general(a, b, (((0,), (0,)), ((), ())), preferred_element_type=jnp.float32)


def by_rows(body, step=32):
    @pl.loop(0, TOKENS // step)
    def _(i):
        body(pl.ds(pl.multiple_of(i * step, step), step))


def statistics(v):
    centered = v - jnp.mean(v, axis=1, keepdims=True)
    scale = lax.rsqrt(jnp.mean(centered * centered, axis=1, keepdims=True) + EPSILON)
    return centered * scale, scale


def fold(v):
    return jnp.sum(v.reshape(v.shape[0] // 8, 8, v.shape[1]), axis=0)


def gelu_both(h):
    c, a = math.sqrt(2.0 / math.pi), 0.044715
    square = h * h
    t = jnp.tanh(c * h * (1.0 + a * square))
    half = 0.5 * (1.0 + t)
    return h * half, half + 0.5 * h * (1.0 - t * t) * (c * (1.0 + 3.0 * a * square))


WIN_IN, WIN_OUT, WIN_EXP = slice(0, 512), slice(384, 640), slice(512, 1152)


def forward_stages(e, y):
    mod = e.mod
    shift1, scale1, gate1 = [lambda i=i: mod[i : i + 1, :] for i in range(3)]
    shift2, scale2, gate2 = [lambda i=i: mod[i : i + 1, :] for i in range(3, 6)]

    def normalize():
        e.bslab[...] = jnp.zeros(e.bslab.shape, jnp.float32)
        for s in range(8):
            for row, first in ((0, 0), (1, 2 * WIDTH)):
                lo, hi = max(432 * s, first), min(432 * (s + 1), first + WIDTH)
                if lo < hi:
                    e.bslab[s, 0:1, lo - 432 * s : hi - 432 * s] = e.bias[
                        row : row + 1, lo - first : hi - first
                    ]

        def rows(r):
            n, _ = statistics(e.x[r, :].astype(jnp.float32))
            e.normed[r, :] = (n * (1.0 + scale1()) + shift1()).astype(jnp.bfloat16)

        by_rows(rows)

    def project(first):
        @pl.loop(first, first + 4)
        def _(s):
            e.wait_p(s)
            v = dot(e.normed[...], e.pv[s, :, WIN_IN]) + e.bslab[s, 0:1, :]
            for j in range(6):
                e.heads[6 * s + j] = v[:, HD * j : HD * (j + 1)].astype(jnp.bfloat16)

    def attend(first):
        @pl.loop(first, first + 4)
        def _(h):
            probs = attention_probs(e, h)
            e.mh[h] = dot(probs.astype(jnp.bfloat16), e.heads[2 * H + h]).astype(jnp.bfloat16)

    def join():
        for h in range(H):
            e.mixture[:, HD * h : HD * (h + 1)] = e.mh[h]
        for s in range(8):
            v = dot(e.mixture[...], e.pv[s, :, WIN_OUT])
            e.attended[:, 144 * s : 144 * (s + 1)] = v[:, 48:192]

    def middle():
        def rows(r):
            attended = e.attended[r, :] + e.bias[2:3, :]
            e.attended[r, :] = attended
            middle = e.x[r, :].astype(jnp.float32) + gate1() * attended
            e.middle[r, :] = middle
            n, _ = statistics(middle)
            e.normed2[r, :] = (n * (1.0 + scale2()) + shift2()).astype(jnp.bfloat16)

        by_rows(rows)
        e.branch[...] = jnp.zeros(e.branch.shape, jnp.float32)

    def expand(d):
        for half in range(2):
            v = dot(e.normed2[...], e.pv[2 * d + half, :, WIN_EXP])
            e.tmp[:, 576 * half : 576 * (half + 1)] = v[:, 64:640]

        def rows(r):
            value, slope = gelu_both(e.tmp[r, :] + e.bias[pl.ds(4 + d, 1), :])
            e.act[d, r, :] = value.astype(jnp.bfloat16)
            if e.slope is not None:
                e.slope[d, r, :] = slope.astype(jnp.bfloat16)

        by_rows(rows)

    def shrink(d):
        e.wait_s(d)
        e.branch[...] += dot_nt(e.act[d], e.sv[d])

    def mlp(first, count):
        @pl.loop(first, first + count)
        def _(d):
            expand(d)
            shrink(d)

    def close():
        def rows(r):
            branch = e.branch[r, :] + e.bias[3:4, :]
            e.branch[r, :] = branch
            if y is not None:
                y[r, :] = (e.middle[r, :] + gate2() * branch).astype(jnp.bfloat16)

        by_rows(rows)

    part = functools.partial
    return (
        [normalize, part(project, 0), part(project, 4)]
        + [part(attend, h) for h in range(0, H, 4)]
        + [join, middle]
        + [part(mlp, d, 1) for d in range(4)]
        + [close]
    )


def attention_probs(e, h):
    scores = dot_nt(e.heads[h], e.heads[H + h]) * SCALE
    if e.mask is not None:
        scores = scores + e.mask[...]
    exponent = jnp.exp(scores - jnp.max(scores, axis=1, keepdims=True))
    return exponent / jnp.sum(exponent, axis=1, keepdims=True)


def forward_pass(e, y):
    for stage in forward_stages(e, y):
        stage()


def backward_stages(e):
    mod = e.mod
    gate1, scale1 = lambda: mod[2:3, :], lambda: mod[1:2, :]
    gate2, scale2 = lambda: mod[5:6, :], lambda: mod[4:5, :]

    def open_block():
        e.sums[...] = jnp.zeros(e.sums.shape, jnp.float32)
        e.bout[...] = jnp.zeros(e.bout.shape, jnp.bfloat16)
        for s in range(8):
            e.bexp[s, :, 0:128] = jnp.zeros((TOKENS, 128), jnp.bfloat16)
            e.bin[s, :, 384:512] = jnp.zeros((TOKENS, 128), jnp.bfloat16)
        e.wait_kept("branch")

        def rows(r):
            g = e.g[r, :].astype(jnp.float32)
            back = (gate2() * g).astype(jnp.bfloat16)
            e.bb[r, :] = back
            e.sums[5] += fold(g * e.tmp[r, :])
            e.sums[7] += fold(back.astype(jnp.float32))

        by_rows(rows)
        e.bb_t[...] = e.bb[...].T
        e.wait_kept("slope")

    def hidden(d):
        e.weights.wait("shrink", d)
        e.tmp[...] = dot(e.bb[...], e.weights.at(d, WIDTH))
        e.weights.start("expand", d)

        @pl.loop(0, TOKENS // 32)
        def _(i):
            r = pl.ds(pl.multiple_of(i * 32, 32), 32)
            slope = e.slope[pl.ds(pl.multiple_of(d * TOKENS + i * 32, 32), 32), :]
            back = (e.tmp[r, :] * slope.astype(jnp.float32)).astype(jnp.bfloat16)
            for half in range(2):
                e.bexp[2 * d + half, r, 64:640] = back[:, 576 * half : 576 * (half + 1)]
            e.sums[8 + d] += fold(back.astype(jnp.float32))

    def through(name, width, operand, first, following):
        if first == 0:
            e.tmp[...] = jnp.zeros(e.tmp.shape, jnp.float32)

        @pl.loop(0, 4)
        def _(i):
            e.weights.wait(name, first + i)
            e.tmp[...] += dot_nt(operand[first + i], e.weights.at(i, width))
            if first == 0:
                e.weights.start(name, 4 + i)
            elif following is not None:
                e.weights.start(following, i)

    def middle():
        e.wait_kept("middle")
        e.wait_kept("attended")

        def rows(r):
            n, scale = statistics(e.middle[r, :])
            back_normed = e.tmp[r, :]
            e.sums[3] += fold(back_normed)
            e.sums[4] += fold(back_normed * n)
            u = back_normed * (1.0 + scale2())
            inner = jnp.mean(u, axis=1, keepdims=True) + n * jnp.mean(u * n, axis=1, keepdims=True)
            back_middle = e.g[r, :].astype(jnp.float32) + scale * (u - inner)
            e.middle[r, :] = back_middle
            e.sums[2] += fold(back_middle * e.attended[r, :])
            back = (gate1() * back_middle).astype(jnp.bfloat16)
            e.sums[6] += fold(back.astype(jnp.float32))
            for s in range(8):
                e.bout[s, r, 48:192] = back[:, 144 * s : 144 * (s + 1)]

        by_rows(rows)

    def split():
        e.wait_kept("heads")
        for h in range(H):
            e.mh[h] = e.tmp[:, HD * h : HD * (h + 1)].astype(jnp.bfloat16)

    def attend(first):
        @pl.loop(first, first + 4)
        def _(h):
            q, k, v, back = e.heads[h], e.heads[H + h], e.heads[2 * H + h], e.mh[h]
            probs = attention_probs(e, h)
            back_probs = dot_nt(back, v)
            e.heads[2 * H + h] = dot_tn(probs.astype(jnp.bfloat16), back).astype(jnp.bfloat16)
            delta = jnp.sum(probs * back_probs, axis=1, keepdims=True)
            back_scores = (probs * (back_probs - delta)).astype(jnp.bfloat16)
            e.heads[h] = (dot(back_scores, k) * SCALE).astype(jnp.bfloat16)
            e.heads[H + h] = (dot_tn(back_scores, q) * SCALE).astype(jnp.bfloat16)

    def join():
        ones = jnp.ones((8, TOKENS), jnp.bfloat16)

        @pl.loop(0, 8)
        def _(s):
            for j in range(6):
                e.bin[s, :, HD * j : HD * (j + 1)] = e.heads[6 * s + j]
            e.bslab[s] = dot(ones, e.bin[s])

    def close():
        def rows(r):
            n, scale = statistics(e.x[r, :].astype(jnp.float32))
            back_normed = e.tmp[r, :]
            e.sums[0] += fold(back_normed)
            e.sums[1] += fold(back_normed * n)
            u = back_normed * (1.0 + scale1())
            inner = jnp.mean(u, axis=1, keepdims=True) + n * jnp.mean(u * n, axis=1, keepdims=True)
            e.back_x[r, :] = (e.middle[r, :] + scale * (u - inner)).astype(jnp.bfloat16)

        by_rows(rows)

        for s in range(8):
            for row, first_column in ((0, 0), (1, 2 * WIDTH)):
                lo, hi = max(432 * s, first_column), min(432 * (s + 1), first_column + WIDTH)
                if lo < hi:
                    e.bias_grad[row : row + 1, lo - first_column : hi - first_column] = e.bslab[
                        s, 0:1, lo - 432 * s : hi - 432 * s
                    ]
        for row, slot in ((2, 6), (3, 7), (4, 8), (5, 9), (6, 10), (7, 11)):
            e.bias_grad[row : row + 1, :] = jnp.sum(e.sums[slot], axis=0, keepdims=True)
        for slot in range(6):
            e.mod_grad[slot : slot + 1, :] = jnp.sum(e.sums[slot], axis=0, keepdims=True)
        e.mod_grad[6:8, :] = jnp.zeros((2, WIDTH), jnp.float32)

    part = functools.partial
    return (
        [open_block]
        + [part(hidden, d) for d in range(4)]
        + [part(through, "expand", 640, e.bexp, first, "out") for first in (0, 4)]
        + [middle]
        + [part(through, "out", 256, e.bout, first, "in") for first in (0, 4)]
        + [split]
        + [part(attend, h) for h in range(0, H, 4)]
        + [join]
        + [part(through, "in", 512, e.bin, first, None) for first in (0, 4)]
        + [close]
    )


class Weights:
    WINDOWS = {"shrink": slice(0, WIDTH), "expand": WIN_EXP, "out": WIN_OUT, "in": WIN_IN}

    def __init__(self, p, s, buffer, sems):
        self.p, self.s, self.buffer, self.sems = p, s, buffer, sems

    def slot(self, i):
        return pl.ds(pl.multiple_of((i % 4) * WIDTH, WIDTH), WIDTH)

    def copy(self, name, i):
        window = self.WINDOWS[name]
        source = self.s.at[i] if name == "shrink" else self.p.at[i, :, window]
        width = window.stop - window.start
        target = self.buffer.at[self.slot(i), 0:width]
        return pltpu.make_async_copy(source, target, self.sems.at[i % 4])

    def start(self, name, i):
        self.copy(name, i).start()

    def wait(self, name, i):
        self.copy(name, i).wait()

    def at(self, i, width):
        return self.buffer[self.slot(i), 0:width]


class Refs:
    pass


WEIGHT_SCRATCH = (
    ("pv", (8, WIDTH, WIDTH), jnp.bfloat16),
    ("sv", (4, WIDTH, WIDTH), jnp.bfloat16),
)
FORWARD_SCRATCH = (
    ("bslab", (8, 8, 512), jnp.float32),
    ("heads", (3 * H, TOKENS, HD), jnp.bfloat16),
    ("mh", (H, TOKENS, HD), jnp.bfloat16),
    ("attended", (TOKENS, WIDTH), jnp.float32),
    ("middle", (TOKENS, WIDTH), jnp.float32),
    ("branch", (TOKENS, WIDTH), jnp.float32),
    ("tmp", (TOKENS, WIDTH), jnp.float32),
)
OPERANDS = (
    ("normed", (TOKENS, WIDTH), jnp.bfloat16),
    ("mixture", (TOKENS, WIDTH), jnp.bfloat16),
    ("normed2", (TOKENS, WIDTH), jnp.bfloat16),
    ("act", (4, TOKENS, WIDTH), jnp.bfloat16),
)
BACK_OPERANDS = (
    ("bb", (TOKENS, WIDTH), jnp.bfloat16),
    ("bin", (8, TOKENS, 512), jnp.bfloat16),
    ("bout", (8, TOKENS, 256), jnp.bfloat16),
    ("bexp", (8, TOKENS, 640), jnp.bfloat16),
)
SLOPE = (("slope", (4, TOKENS, WIDTH), jnp.bfloat16),)
SUMS = (("sums", (12, 8, WIDTH), jnp.float32),)
def load_weights(e, p_hbm, s_hbm, psem, ssem):
    def p_copy(s):
        return pltpu.make_async_copy(p_hbm.at[s], e.pv.at[s], psem.at[s])

    def s_copy(d):
        return pltpu.make_async_copy(s_hbm.at[d], e.sv.at[d], ssem.at[d])

    @pl.loop(0, 8)
    def _(s):
        p_copy(s).start()

    @pl.loop(0, 4)
    def _(d):
        s_copy(d).start()

    e.wait_p = lambda s: p_copy(s).wait()
    e.wait_s = lambda d: s_copy(d).wait()


def fill_mask(e):
    frames = e.segments.shape[1]
    each = TOKENS // frames

    def clips(axis):
        frame = lax.broadcasted_iota(jnp.int32, (TOKENS, TOKENS), axis) // each
        clip = jnp.zeros((TOKENS, TOKENS), jnp.int32)
        for f in range(frames):
            clip = jnp.where(frame == f, e.segments[0, f], clip)
        return clip

    def spots(axis):
        return lax.broadcasted_iota(jnp.int32, (TOKENS, TOKENS), axis) % each

    same = (clips(0) == clips(1)) & (spots(0) == spots(1))
    e.mask[...] = jnp.where(same, 0.0, NEGATIVE)


SECOND_SCRATCH = WEIGHT_SCRATCH + FORWARD_SCRATCH + OPERANDS + SLOPE + (
    ("y", (TOKENS, WIDTH), jnp.bfloat16),
    ("mask", (TOKENS, TOKENS), jnp.float32),
    ("xt", (TOKENS, WIDTH), jnp.bfloat16),
)
KEPT = ("branch", "slope", "middle", "attended", "heads", "act", "normed", "mixture", "normed2")
SHAPES = {name: (shape, kind) for name, shape, kind in SECOND_SCRATCH}


def second_gather_kernel(
    p_in, s_in, x, mods, biases, segments, p, s, p_out, s_out, passed, y_t, *refs
):
    n = len(KEPT)
    saved, saved_t, refs = refs[:n], refs[n : 2 * n], refs[2 * n :]
    e = Refs()
    for (name, *_), ref in zip(SECOND_SCRATCH, refs):
        setattr(e, name, ref)
    mask, e.mask, e.x, e.segments = e.mask, None, x, segments
    e.mod, e.bias = mods.at[0], biases.at[0]
    sems = refs[len(SECOND_SCRATCH) :]
    me = Place()
    gather = Gather(me, CHUNKS_ONE, p_in, s_in, p_out, s_out, *sems[:4])
    exchange = Exchange(me, e.y, passed, *sems[4:7])
    greet(me)
    events = gather.events()
    own = len(CHUNKS_ONE) / len(events)
    stages = forward_stages(e, e.y)

    def keeps(targets):
        return [
            pltpu.make_async_copy(getattr(e, name), target, sems[9].at[i])
            for i, (name, target) in enumerate(zip(KEPT, targets))
        ]

    def leave():
        exchange.start()
        for keep in keeps(saved):
            keep.start()

    def left():
        exchange.finish()
        for keep in keeps(saved):
            keep.wait()

    take = pltpu.make_async_copy(passed, e.xt, sems[10])

    def turn():
        take.start()
        e.mask = mask
        fill_mask(e)
        take.wait()

    timed = [(own, lambda: load_weights(e, p, s, *sems[7:9]))]
    timed += spread_out(stages, own, 0.6) + [(0.6, leave), (0.9, left), (0.95, turn)]
    interleave(events, timed)
    gather.finish()
    e.x, e.mod, e.bias = e.xt, mods.at[1], biases.at[1]
    load_weights(e, p_out, s_out, *sems[7:9])
    for stage in forward_stages(e, e.y):
        stage()
    last = keeps(saved_t) + [pltpu.make_async_copy(e.y, y_t, sems[10])]
    for keep in last:
        keep.start()
    for keep in last:
        keep.wait()


def second_gather(p_own, s_own, x, mods, biases, segments, p, s):
    kept = tuple(jax.ShapeDtypeStruct(*SHAPES[name]) for name in KEPT)
    smem = pl.BlockSpec(memory_space=pltpu.SMEM)
    results = pl.pallas_call(
        second_gather_kernel,
        out_shape=SLABS + (STREAM, STREAM) + kept + kept,
        in_specs=[ANY_SPEC] * 2 + [VMEM_SPEC] * 3 + [smem] + [ANY_SPEC] * 2,
        out_specs=(ANY_SPEC,) * (4 + 2 * len(KEPT)),
        scratch_shapes=[pltpu.VMEM(shape, kind) for _, shape, kind in SECOND_SCRATCH]
        + dma_sems(*Gather.SEMS, (8,), (8,), (), (8,), (4,), (len(KEPT),), ()),
        compiler_params=pltpu.CompilerParams(
            collective_id=1, has_side_effects=True, vmem_limit_bytes=60 << 20
        ),
        name="second_gather",
    )(p_own, s_own, x, mods, biases, segments, p, s)
    n = 4 + len(KEPT)
    return results[:4], results[4:n], results[n:]


S_RING, P_RING = 5, 3
S_ROWS, P_ROWS = Scatter.rows(S_CHUNKS, S_RING), Scatter.rows(P_CHUNKS, P_RING)
SLOPE_ROW, ACT_ROW = 4 * WIDTH, 4 * WIDTH + 4 * TOKENS
BACKWARD_SCRATCH = (
    ("arena", (P_ROWS, WIDTH), jnp.bfloat16),
    ("arena_s", (S_ROWS, WIDTH), jnp.bfloat16),
    ("own_p", (288, WIDTH), jnp.bfloat16),
    ("own_s", (144, WIDTH), jnp.bfloat16),
    ("bslab", (8, 8, 512), jnp.float32),
    ("heads", (3 * H, TOKENS, HD), jnp.bfloat16),
    ("mh", (H, TOKENS, HD), jnp.bfloat16),
    ("attended", (TOKENS, WIDTH), jnp.float32),
    ("middle", (TOKENS, WIDTH), jnp.float32),
    ("tmp", (TOKENS, WIDTH), jnp.float32),
    ("sums", (12, 8, WIDTH), jnp.float32),
    ("bb", (TOKENS, WIDTH), jnp.bfloat16),
    ("bin", (8, TOKENS, 512), jnp.bfloat16),
    ("bout", (8, TOKENS, 256), jnp.bfloat16),
    ("bexp", (8, TOKENS, 640), jnp.bfloat16),
    ("back_x", (TOKENS, WIDTH), jnp.bfloat16),
    ("bb_t", (WIDTH, TOKENS), jnp.bfloat16),
    ("normed_t", (WIDTH, TOKENS), jnp.bfloat16),
    ("mixture_t", (WIDTH, TOKENS), jnp.bfloat16),
    ("normed2_t", (WIDTH, TOKENS), jnp.bfloat16),
    ("bias_grad", (8, WIDTH), jnp.float32),
    ("mod_grad", (8, WIDTH), jnp.float32),
    ("small", (8, 8, WIDTH), jnp.float32),
    ("small_in", (8, 8, WIDTH), jnp.float32),
    ("row_sum", (8, WIDTH), jnp.float32),
    ("row_in", (4, 8, WIDTH), jnp.float32),
    ("total", (8, WIDTH), jnp.float32),
)
MASK = (("mask", (TOKENS, TOKENS), jnp.float32),)


def backward_kernel(block, names, *refs):
    e = Refs()
    e.mask = None
    for name, ref in zip(names, refs):
        setattr(e, name, ref)
    temporal = block == 1
    sems = refs[len(names) :]
    ready, sems = sems[0], sems[1:]
    e.mod = e.mods.at[block]
    e.slope = e.arena.at[SLOPE_ROW : SLOPE_ROW + 4 * TOKENS, :]
    me = Place()

    places = {"branch": e.tmp, "middle": e.middle, "attended": e.attended, "heads": e.heads}

    def kept_copies(name):
        index = KEPT.index(name)
        source, sem = getattr(e, name + "_kept"), sems[0].at[index]
        if name in ("slope", "act"):
            row = SLOPE_ROW if name == "slope" else ACT_ROW
            rows = [
                e.arena.at[row + d * TOKENS : row + (d + 1) * TOKENS, :] for d in range(4)
            ]
            base = 0 if name == "slope" else 4
            return [
                pltpu.make_async_copy(source.at[d], rows[d], sems[1].at[base + d])
                for d in range(4)
            ]
        return [pltpu.make_async_copy(source, places.get(name, e.back_x), sem)]

    def start_kept(name):
        for copy in kept_copies(name):
            copy.start()

    def wait_kept(name):
        for copy in kept_copies(name):
            copy.wait()

    e.wait_kept = wait_kept
    e.weights = Weights(e.p, e.s, e.arena, sems[2])
    start_kept("branch")
    e.weights.start("shrink", 0)
    start_kept("slope")
    for d in range(1, 4):
        e.weights.start("shrink", d)
    for name in ("act", "middle", "attended", "heads", "normed"):
        start_kept(name)

    def compute_s(b, core, target):
        d, s = b[0] * 2 + core, b[1] * 2 + b[2]
        at = pl.ds(pl.multiple_of(s * 144, 16), 144)
        act = e.arena[pl.ds(pl.multiple_of(ACT_ROW + d * TOKENS, 16), TOKENS), :]
        target[...] = dot(e.bb_t[at, :], act).astype(jnp.bfloat16)

    def compute_p(b, core, target):
        d, s = b[0] * 2 + core, b[1] * 2 + b[2]

        @pl.loop(0, 2)
        def _(i):
            at = pl.ds(pl.multiple_of(d * 288 + i * 144, 16), 144)
            to = pl.ds(pl.multiple_of(i * 144, 16), 144)
            first = dot(e.normed_t[at, :], e.bin[s])
            second = dot(e.mixture_t[at, :], e.bout[s])
            third = dot(e.normed2_t[at, :], e.bexp[s])
            target[to, 0:384] = first[:, 0:384].astype(jnp.bfloat16)
            target[to, 384:512] = (first[:, 384:] + second[:, :128]).astype(jnp.bfloat16)
            target[to, 512:640] = (second[:, 128:] + third[:, :128]).astype(jnp.bfloat16)
            target[to, 640:] = third[:, 128:].astype(jnp.bfloat16)

    across = Scatter(
        me, S_CHUNKS, compute_s, e.own_s, e.arena_s, 0, S_RING, e.s_out, *sems[3:7]
    )
    slabs = Scatter(me, P_CHUNKS, compute_p, e.own_p, e.arena, 0, P_RING, e.p_out, *sems[7:11])
    over_frames = Spread(me, "sp", e.small, e.small_in, *sems[11:13], True)
    over_data = Spread(me, "dp", e.row_sum, e.row_in, *sems[13:15], False)
    over_all = Spread(me, "sp", e.total, e.totals, *sems[15:17], False)
    greet(me)

    def turn(name, target, following):
        def step():
            wait_kept(name)
            target[...] = e.back_x[...].T
            if following:
                start_kept(following)

        return step

    if temporal:
        forth = Exchange(me, e.y_t, e.output, *sems[17:20])
        back = Exchange(me, e.back_x, e.back_spatial, *sems[20:23])
        forth.start()
        fill_mask(e)
    else:
        back = pltpu.make_async_copy(e.back_x, e.input_gradient, sems[17])

    stages = backward_stages(e)
    stages[0]()
    wait_kept("act")
    rest = stages[1:]
    rest[2:2] = [turn("normed", e.normed_t, "mixture")]
    rest[5:5] = [turn("mixture", e.mixture_t, "normed2")]
    rest[8:8] = [turn("normed2", e.normed2_t, None)]
    interleave(across.events(), spread_out(rest, 0.05, 1.0))

    for direction in "xycud":

        def signal():
            pl.semaphore_signal(
                ready, inc=1, device_id=me.neighbour(direction), device_id_type=MESH
            )

        guarded(me.has(direction), signal)

    def begin():
        back.start()
        e.small[...] = jnp.zeros(e.small.shape, jnp.float32)
        for s in range(8):
            e.small[s, 0:1, :] = e.bias_grad[s : s + 1, :]
            for row, column, n, at in pieces(864 * s, 864):
                e.small[s, 1:2, at : at + n] = e.mod_grad[row : row + 1, column : column + n]
        over_frames.start()

    begin()
    pl.semaphore_wait(ready, 3 + jnp.where((me.z > 0) & (me.z < 3), 2, 1))

    def second():
        over_frames.finish()
        e.row_sum[...] = jnp.sum(e.small_in[...], axis=0)
        over_data.start()

    def third():
        over_data.finish()
        e.total[...] = jnp.sum(e.row_in[...], axis=0)
        over_all.start()
        for t in range(9):
            r = slice(32 * t, 32 * (t + 1))
            v = e.cond[r, 0:1] * e.row_in[0, 1:2, 0:864]
            for q in range(1, 4):
                v = v + e.cond[r, q : q + 1] * e.row_in[q, 1:2, 0:864]
            e.weight_grad[r, :] = v

    def fourth():
        over_all.finish()
        if temporal:
            forth.finish()
            back.finish()
        else:
            back.wait()

    interleave(slabs.events(), [(0.3, second), (0.55, third), (0.8, fourth)])
    across.finish()
    slabs.finish()


def backward_call(block, x, mods, cond, segments, p, s, g, kept, y_t=None):
    inputs = [("x", x), ("mods", mods), ("cond", cond), ("g", g), ("p", p), ("s", s)]
    inputs += [(name + "_kept", value) for name, value in zip(KEPT, kept)]
    outs = [
        ("p_out", (288, WIDTH), jnp.float32),
        ("s_out", (144, WIDTH), jnp.float32),
        ("weight_grad", (288, 864), jnp.float32),
        ("totals", (8, 8, WIDTH), jnp.float32),
    ]
    scratch = BACKWARD_SCRATCH
    if block == 1:
        inputs += [("segments", segments), ("y_t", y_t)]
        streams = ["output", "back_spatial"]
        scratch = scratch + MASK
        last = [(8,), (8,), ()] * 2
    else:
        streams = ["input_gradient"]
        last = [()]
    outs += [(name, (TOKENS, WIDTH), jnp.bfloat16) for name in streams]
    names = [name for name, *_ in tuple(inputs) + tuple(outs) + scratch]
    smem = pl.BlockSpec(memory_space=pltpu.SMEM)

    def spec(name):
        if name == "segments":
            return smem
        hbm = name in ("p", "s", "y_t") or name in streams or name.endswith("_kept")
        return ANY_SPEC if hbm else VMEM_SPEC

    sems = [(len(KEPT),), (8,), (4,)] + Scatter.sems(S_CHUNKS) + Scatter.sems(P_CHUNKS)
    sems += [(8,), (8,), (4,), (4,), (8,), (8,)] + last
    return pl.pallas_call(
        functools.partial(backward_kernel, block, names),
        out_shape=[jax.ShapeDtypeStruct(shape, kind) for _, shape, kind in outs],
        in_specs=[spec(name) for name, _ in inputs],
        out_specs=[spec(name) for name, *_ in outs],
        scratch_shapes=[pltpu.VMEM(shape, kind) for _, shape, kind in scratch]
        + [pltpu.SemaphoreType.REGULAR]
        + dma_sems(*sems),
        compiler_params=pltpu.CompilerParams(
            collective_id=3 - block, has_side_effects=True, vmem_limit_bytes=63 << 20
        ),
        name="temporal_backward" if block == 1 else "spatial_backward",
    )(*[value for _, value in inputs])


def sinusoid(timesteps):
    half_width = D // 2
    frequencies = jnp.exp(
        -math.log(10000.0) * jnp.arange(half_width, dtype=jnp.float32) / half_width
    )
    angles = timesteps.astype(jnp.float32)[:, None] * frequencies[None, :]
    return jnp.concatenate([jnp.cos(angles), jnp.sin(angles)], axis=1)


def layer_norm(tensor):
    centered = tensor - jnp.mean(tensor, axis=-1, keepdims=True)
    return centered * lax.rsqrt(jnp.mean(centered * centered, axis=-1, keepdims=True) + EPSILON)


def modulate(tensor, shift_part, scale_part):
    return layer_norm(tensor) * (1.0 + scale_part) + shift_part


def matmul(left_side, right_side):
    return jnp.dot(left_side, right_side, preferred_element_type=jnp.float32)


def back_matmul(gradient, matrix):
    return lax.dot_general(
        gradient,
        matrix,
        (((gradient.ndim - 1,), (1,)), ((), ())),
        preferred_element_type=jnp.float32,
    )


def outer_product(left_side, right_side):
    flat_left = left_side.reshape(-1, left_side.shape[-1])
    flat_right = right_side.reshape(-1, right_side.shape[-1])
    return lax.dot_general(
        flat_left, flat_right, (((0,), (0,)), ((), ())), preferred_element_type=jnp.float32
    )


def column_totals(tensor):
    return jnp.sum(tensor.astype(jnp.float32).reshape(-1, tensor.shape[-1]), axis=0)


def per_sequence(tensor):
    return jnp.sum(tensor, axis=(1, 2))


def over_data(core, biases):
    attend_in, attend_out, expand, shrink = core
    attend_bias, out_bias, expand_bias, shrink_bias, modulate_bias = biases
    gathered = (
        lax.all_gather(attend_in, "dp", axis=0, tiled=True),
        lax.all_gather(attend_out, "dp", axis=0, tiled=True),
        lax.all_gather(expand, "dp", axis=0, tiled=True),
        lax.all_gather(shrink, "dp", axis=0, tiled=True),
        lax.all_gather(attend_bias, "dp", axis=0, tiled=True),
        lax.all_gather(out_bias, "dp", axis=0, tiled=True),
        lax.all_gather(expand_bias, "dp", axis=0, tiled=True),
        lax.all_gather(shrink_bias, "dp", axis=0, tiled=True),
        lax.all_gather(modulate_bias, "dp", axis=0, tiled=True),
    )
    return (gathered[:4], gathered[4:])


def over_frames(core):
    attend_in, attend_out, expand, shrink = core
    gathered = (
        lax.all_gather(attend_in, "sp", axis=1, tiled=True),
        lax.all_gather(attend_out, "sp", axis=1, tiled=True),
        lax.all_gather(expand, "sp", axis=1, tiled=True),
        lax.all_gather(shrink, "sp", axis=1, tiled=True),
    )
    return gathered


def collect(core, biases):
    core_rows, biases_full = over_data(core, biases)
    core_full = over_frames(core_rows)
    return (core_full, biases_full)


def own_rows(condition_all, rows):
    return lax.dynamic_slice_in_dim(condition_all, lax.axis_index("dp") * rows, rows, 1)


def modulation_of(condition_all, modulate_weights):
    rows = modulate_weights[0].shape[0]
    own = own_rows(condition_all, rows)
    partial_terms = jnp.stack([matmul(own, weight) for weight in modulate_weights], axis=1)
    summed = lax.psum_scatter(partial_terms, "dp", scatter_dimension=0, tiled=True)
    full = lax.all_gather(summed, "sp", axis=2, tiled=True)
    return [full[:, slot] for slot in range(len(modulate_weights))]


def sum_over_frames(terms):
    attend_in, attend_out, expand, shrink = terms
    return (
        lax.psum_scatter(
            attend_in.astype(jnp.bfloat16), "sp", scatter_dimension=1, tiled=True
        ).astype(jnp.float32),
        lax.psum_scatter(
            attend_out.astype(jnp.bfloat16), "sp", scatter_dimension=1, tiled=True
        ).astype(jnp.float32),
        lax.psum_scatter(expand.astype(jnp.bfloat16), "sp", scatter_dimension=1, tiled=True).astype(
            jnp.float32
        ),
        lax.psum_scatter(shrink.astype(jnp.bfloat16), "sp", scatter_dimension=1, tiled=True).astype(
            jnp.float32
        ),
    )


def sum_over_data(terms):
    attend_in, attend_out, expand, shrink = terms
    return (
        lax.psum_scatter(
            attend_in.astype(jnp.bfloat16), "dp", scatter_dimension=0, tiled=True
        ).astype(jnp.float32),
        lax.psum_scatter(
            attend_out.astype(jnp.bfloat16), "dp", scatter_dimension=0, tiled=True
        ).astype(jnp.float32),
        lax.psum_scatter(expand.astype(jnp.bfloat16), "dp", scatter_dimension=0, tiled=True).astype(
            jnp.float32
        ),
        lax.psum_scatter(shrink.astype(jnp.bfloat16), "dp", scatter_dimension=0, tiled=True).astype(
            jnp.float32
        ),
    )


def modulate_gradients(condition_all, back_modulations, rows):
    joined = jnp.stack(back_modulations, axis=1)
    columns = lax.psum_scatter(joined, "sp", scatter_dimension=2, tiled=True)
    every = lax.all_gather(columns, "dp", axis=0, tiled=True)
    own = own_rows(condition_all, rows).astype(jnp.float32)
    return [
        jnp.dot(own.T, every[:, slot], precision=HIGHEST_PRECISION)
        for slot in range(len(back_modulations))
    ]


def finish(core_terms, bias_terms):
    matrix_grads = sum_over_data(sum_over_frames(core_terms))
    attend_bias, out_bias, expand_bias, shrink_bias, modulate_bias = bias_terms
    totals = lax.psum(
        (attend_bias, out_bias, expand_bias, shrink_bias, modulate_bias), ("dp", "sp")
    )
    data_index = lax.axis_index("dp")
    data_count = lax.axis_size("dp")
    bias_grads = tuple(
        (
            lax.dynamic_slice_in_dim(
                total_bias,
                data_index * (total_bias.shape[0] // data_count),
                total_bias.shape[0] // data_count,
            )
            for total_bias in totals
        )
    )
    return (matrix_grads, bias_grads)


def frames_to_patches(tensor):
    return lax.all_to_all(tensor, "sp", split_axis=2, concat_axis=1, tiled=True)


def patches_to_frames(tensor):
    return lax.all_to_all(tensor, "sp", split_axis=1, concat_axis=2, tiled=True)


def attention_scores(queries, key_rows, forms, allowed):
    scores = jnp.einsum(forms[0], queries, key_rows, preferred_element_type=jnp.float32) * HD ** (
        -0.5
    )
    if allowed is not None:
        scores = jnp.where(allowed, scores, -1e30)
    return scores


def block_forward(stream, modulation, core, biases, forms, allowed):
    attend_in, attend_out, expand, shrink = core
    attend_bias, out_bias, expand_bias, shrink_bias, modulate_bias = biases
    model_width = stream.shape[-1]
    pieces = [
        modulation[:, None, None, slot * model_width : (slot + 1) * model_width]
        for slot in range(6)
    ]
    normed = modulate(stream, pieces[0], pieces[1]).astype(jnp.bfloat16)
    bias_float = attend_bias.astype(jnp.float32)
    joined_bias = jnp.concatenate(
        [bias_float[:model_width], jnp.zeros((model_width,), jnp.float32), bias_float[model_width:]]
    )
    projected = (matmul(normed, attend_in) + joined_bias).astype(jnp.bfloat16)
    head_shape = projected.shape[:3] + (H, HD)
    queries = projected[..., :model_width].reshape(head_shape)
    key_rows = projected[..., model_width : 2 * model_width].reshape(head_shape)
    values = projected[..., 2 * model_width :].reshape(head_shape)
    scores = attention_scores(queries, key_rows, forms, allowed)
    highest = jnp.max(scores, axis=-1, keepdims=True)
    exponent = jnp.exp(scores - highest)
    denominator = jnp.sum(exponent, axis=-1, keepdims=True)
    softmax_probs = exponent / denominator
    logsum = highest + jnp.log(denominator)
    mixture = (
        jnp.einsum(
            forms[1], softmax_probs.astype(jnp.bfloat16), values, preferred_element_type=jnp.float32
        )
        .astype(jnp.bfloat16)
        .reshape(stream.shape)
    )
    attended = matmul(mixture, attend_out) + out_bias.astype(jnp.float32)
    middle = stream + pieces[2] * attended
    normed_second = modulate(middle, pieces[3], pieces[4]).astype(jnp.bfloat16)
    hidden = matmul(normed_second, expand) + expand_bias.astype(jnp.float32)
    activated = jax.nn.gelu(hidden, approximate=True).astype(jnp.bfloat16)
    branch = matmul(activated, shrink) + shrink_bias.astype(jnp.float32)
    result = middle + pieces[5] * branch
    kept = (
        pieces,
        normed,
        queries,
        key_rows,
        values,
        logsum,
        mixture,
        attended,
        middle,
        normed_second,
        hidden,
        activated,
        branch,
    )
    return (result, kept)


def block_backward(incoming, stream, core, forms, allowed, kept):
    attend_in, attend_out, expand, shrink = core
    (
        pieces,
        normed,
        queries,
        key_rows,
        values,
        logsum,
        mixture,
        attended,
        middle,
        normed_second,
        hidden,
        activated,
        branch,
    ) = kept
    model_width = stream.shape[-1]
    sequences = stream.shape[0]
    back_branch = (pieces[5] * incoming).astype(jnp.bfloat16)
    back_gate_second = per_sequence(incoming * branch)
    shrink_term = outer_product(activated, back_branch)
    shrink_bias_term = column_totals(back_branch)
    back_activated = back_matmul(back_branch, shrink)
    _, gelu_pull = jax.vjp(lambda tensor: jax.nn.gelu(tensor, approximate=True), hidden)
    back_hidden = gelu_pull(back_activated)[0].astype(jnp.bfloat16)
    expand_term = outer_product(normed_second, back_hidden)
    expand_bias_term = column_totals(back_hidden)
    back_normed_second = back_matmul(back_hidden, expand)
    _, second_pull = jax.vjp(modulate, middle, pieces[3], pieces[4])
    back_middle, back_shift_second, back_scale_second = second_pull(back_normed_second)
    back_middle = back_middle + incoming
    back_attended = (pieces[2] * back_middle).astype(jnp.bfloat16)
    back_gate_first = per_sequence(back_middle * attended)
    out_term = outer_product(mixture, back_attended)
    out_bias_term = column_totals(back_attended)
    back_mixture = (
        back_matmul(back_attended, attend_out).astype(jnp.bfloat16).reshape(queries.shape)
    )
    scores = attention_scores(queries, key_rows, forms, allowed)
    softmax_probs = jnp.exp(scores - logsum)
    back_probs = jnp.einsum(forms[0], back_mixture, values, preferred_element_type=jnp.float32)
    back_values = jnp.einsum(
        forms[2],
        softmax_probs.astype(jnp.bfloat16),
        back_mixture,
        preferred_element_type=jnp.float32,
    )
    row_delta = jnp.sum(softmax_probs * back_probs, axis=-1, keepdims=True)
    back_scores = (softmax_probs * (back_probs - row_delta)).astype(jnp.bfloat16)
    score_scale = HD ** (-0.5)
    back_queries = (
        jnp.einsum(forms[1], back_scores, key_rows, preferred_element_type=jnp.float32)
        * score_scale
    )
    back_keys = (
        jnp.einsum(forms[2], back_scores, queries, preferred_element_type=jnp.float32) * score_scale
    )
    flat_shape = stream.shape
    back_projected = jnp.concatenate(
        [
            back_queries.reshape(flat_shape),
            back_keys.reshape(flat_shape),
            back_values.reshape(flat_shape),
        ],
        axis=-1,
    ).astype(jnp.bfloat16)
    attend_in_term = outer_product(normed, back_projected)
    projected_totals = column_totals(back_projected)
    attend_bias_term = jnp.concatenate(
        [projected_totals[:model_width], projected_totals[2 * model_width :]]
    )
    back_normed = back_matmul(back_projected, attend_in)
    _, first_pull = jax.vjp(modulate, stream, pieces[0], pieces[1])
    back_stream, back_shift_first, back_scale_first = first_pull(back_normed)
    back_stream = back_stream + back_middle
    back_modulation = jnp.concatenate(
        [
            back_shift_first.reshape(sequences, model_width),
            back_scale_first.reshape(sequences, model_width),
            back_gate_first,
            back_shift_second.reshape(sequences, model_width),
            back_scale_second.reshape(sequences, model_width),
            back_gate_second,
        ],
        axis=1,
    )
    modulate_bias_term = jnp.sum(back_modulation, axis=0)
    core_terms = (attend_in_term, out_term, expand_term, shrink_term)
    bias_terms = (
        attend_bias_term,
        out_bias_term,
        expand_bias_term,
        shrink_bias_term,
        modulate_bias_term,
    )
    return (back_stream, core_terms, back_modulation, bias_terms)


def shards(
    inputs,
    timesteps,
    segment_ids,
    spatial_attend_in,
    spatial_attend_bias,
    spatial_attend_out,
    spatial_out_bias,
    spatial_expand,
    spatial_expand_bias,
    spatial_shrink,
    spatial_shrink_bias,
    spatial_modulate,
    spatial_modulate_bias,
    temporal_attend_in,
    temporal_attend_bias,
    temporal_attend_out,
    temporal_out_bias,
    temporal_expand,
    temporal_expand_bias,
    temporal_shrink,
    temporal_shrink_bias,
    temporal_modulate,
    temporal_modulate_bias,
    cotangent,
):
    condition_all = jax.nn.silu(sinusoid(timesteps)).astype(jnp.bfloat16)
    allowed = (segment_ids[:, :, None] == segment_ids[:, None, :])[:, None, None, :, :]
    spatial_core = (spatial_attend_in, spatial_attend_out, spatial_expand, spatial_shrink)
    spatial_biases = (
        spatial_attend_bias,
        spatial_out_bias,
        spatial_expand_bias,
        spatial_shrink_bias,
        spatial_modulate_bias,
    )
    temporal_core = (temporal_attend_in, temporal_attend_out, temporal_expand, temporal_shrink)
    temporal_biases = (
        temporal_attend_bias,
        temporal_out_bias,
        temporal_expand_bias,
        temporal_shrink_bias,
        temporal_modulate_bias,
    )
    stream = inputs.astype(jnp.float32)
    modulations = modulation_of(condition_all, (spatial_modulate, temporal_modulate))
    core, biases = collect(spatial_core, spatial_biases)
    modulation = modulations[0] + biases[4].astype(jnp.float32)
    spatial_core = core
    spatial_out, spatial_kept = block_forward(stream, modulation, core, biases, SPATIAL_FORMS, None)
    passed = frames_to_patches(spatial_out.astype(jnp.bfloat16)).astype(jnp.float32)
    core, biases = collect(temporal_core, temporal_biases)
    modulation = modulations[1] + biases[4].astype(jnp.float32)
    temporal_out, temporal_kept = block_forward(
        passed, modulation, core, biases, TEMPORAL_FORMS, allowed
    )
    output = patches_to_frames(temporal_out.astype(jnp.bfloat16))
    incoming = frames_to_patches(cotangent).astype(jnp.float32)
    back_passed, core_terms, back_temporal, bias_terms = block_backward(
        incoming, passed, core, TEMPORAL_FORMS, allowed, temporal_kept
    )
    temporal_grads, temporal_bias_grads = finish(core_terms, bias_terms)
    back_spatial = patches_to_frames(back_passed.astype(jnp.bfloat16)).astype(jnp.float32)
    back_inputs, core_terms, back_spatial_modulation, bias_terms = block_backward(
        back_spatial, stream, spatial_core, SPATIAL_FORMS, None, spatial_kept
    )
    spatial_grads, spatial_bias_grads = finish(core_terms, bias_terms)
    modulate_grads = modulate_gradients(
        condition_all, (back_spatial_modulation, back_temporal), spatial_modulate.shape[0]
    )
    return (
        output,
        back_inputs.astype(jnp.bfloat16),
        spatial_grads[0],
        spatial_bias_grads[0],
        spatial_grads[1],
        spatial_bias_grads[1],
        spatial_grads[2],
        spatial_bias_grads[2],
        spatial_grads[3],
        spatial_bias_grads[3],
        modulate_grads[0],
        spatial_bias_grads[4],
        temporal_grads[0],
        temporal_bias_grads[0],
        temporal_grads[1],
        temporal_bias_grads[1],
        temporal_grads[2],
        temporal_bias_grads[2],
        temporal_grads[3],
        temporal_bias_grads[3],
        modulate_grads[1],
        temporal_bias_grads[4],
    )


def fits(mesh):
    return mesh.shape["dp"] == 4 and mesh.shape["sp"] == 8


def condition_rows(timesteps, rows):
    half = D // 2
    index = lax.axis_index("dp") * rows + jnp.arange(rows, dtype=jnp.int32)
    place = (index % half).astype(jnp.float32)
    frequencies = jnp.exp(-math.log(10000.0) * place / half)
    angles = timesteps.astype(jnp.float32)[:, None] * frequencies[None, :]
    wave = jnp.where((index < half)[None, :], jnp.cos(angles), jnp.sin(angles))
    return jax.nn.silu(wave).astype(jnp.bfloat16)


def fast_shards(
    inputs,
    timesteps,
    segment_ids,
    spatial_attend_in,
    spatial_attend_bias,
    spatial_attend_out,
    spatial_out_bias,
    spatial_expand,
    spatial_expand_bias,
    spatial_shrink,
    spatial_shrink_bias,
    spatial_modulate,
    spatial_modulate_bias,
    temporal_attend_in,
    temporal_attend_bias,
    temporal_attend_out,
    temporal_out_bias,
    temporal_expand,
    temporal_expand_bias,
    temporal_shrink,
    temporal_shrink_bias,
    temporal_modulate,
    temporal_modulate_bias,
    cotangent,
):
    def small(attend, out, expand, shrink, modulate):
        rows = [attend, out, shrink, expand, modulate[:D], modulate[D:]]
        return [jnp.pad(row.astype(jnp.float32)[None], ((0, 0), (0, D - row.shape[0]))) for row in rows]

    pack = jnp.concatenate(
        small(
            spatial_attend_bias,
            spatial_out_bias,
            spatial_expand_bias,
            spatial_shrink_bias,
            spatial_modulate_bias,
        )
        + small(
            temporal_attend_bias,
            temporal_out_bias,
            temporal_expand_bias,
            temporal_shrink_bias,
            temporal_modulate_bias,
        )
        + [jnp.zeros((4, D), jnp.float32)]
    )
    cond = jnp.pad(condition_rows(timesteps, spatial_modulate.shape[0]), ((0, 4), (0, 0)))
    cond_columns = cond.astype(jnp.float32).T
    x = inputs.reshape(TOKENS, WIDTH)
    spatial_p, spatial_s, mods, biases, incoming = first_gather(
        jnp.concatenate([spatial_attend_in, spatial_attend_out, spatial_expand], axis=1),
        spatial_shrink.T,
        pack,
        cond,
        (spatial_modulate, temporal_modulate),
        cotangent.reshape(TOKENS, WIDTH),
    )
    (temporal_p, temporal_s, passed, y_t), kept_s, kept_t = second_gather(
        jnp.concatenate([temporal_attend_in, temporal_attend_out, temporal_expand], axis=1),
        temporal_shrink.T,
        x,
        mods,
        biases,
        segment_ids,
        spatial_p,
        spatial_s,
    )
    packed_t, turned_t, modulate_t, totals_t, output, back_spatial = backward_call(
        1, passed, mods, cond_columns, segment_ids, temporal_p, temporal_s, incoming, kept_t, y_t
    )
    packed_s, turned_s, modulate_s, totals_s, input_gradient = backward_call(
        0, x, mods, cond_columns, segment_ids, spatial_p, spatial_s, back_spatial, kept_s
    )
    outs = unpack(packed_s, turned_s, totals_s, packed_t, turned_t, totals_t)
    return (
        output.reshape(inputs.shape),
        input_gradient.reshape(inputs.shape),
        *outs[:8],
        modulate_s,
        outs[8],
        *outs[9:17],
        modulate_t,
        outs[17],
    )


def solution(mesh):
    placed = (
        P("dp", "sp", None, None),
        P(),
        P("dp", None),
        P("dp", "sp"),
        P("dp"),
        P("dp", "sp"),
        P("dp"),
        P("dp", "sp"),
        P("dp"),
        P("dp", "sp"),
        P("dp"),
        P("dp", "sp"),
        P("dp"),
        P("dp", "sp"),
        P("dp"),
        P("dp", "sp"),
        P("dp"),
        P("dp", "sp"),
        P("dp"),
        P("dp", "sp"),
        P("dp"),
        P("dp", "sp"),
        P("dp"),
        P("dp", "sp", None, None),
    )
    return jax.shard_map(
        fast_shards if fits(mesh) else shards,
        mesh=mesh,
        in_specs=placed,
        out_specs=(
            P("dp", "sp", None, None),
            P("dp", "sp", None, None),
            P("dp", "sp"),
            P("dp"),
            P("dp", "sp"),
            P("dp"),
            P("dp", "sp"),
            P("dp"),
            P("dp", "sp"),
            P("dp"),
            P("dp", "sp"),
            P("dp"),
            P("dp", "sp"),
            P("dp"),
            P("dp", "sp"),
            P("dp"),
            P("dp", "sp"),
            P("dp"),
            P("dp", "sp"),
            P("dp"),
            P("dp", "sp"),
            P("dp"),
        ),
        check_vma=False,
    )
```

```python
import functools
import math

import jax
import jax.numpy as jnp
from jax import lax
from jax.experimental import pallas as pl
from jax.experimental.pallas import tpu as pltpu
from jax.sharding import PartitionSpec as P

D = 1152
H = 16
HD = 72


EPSILON = 1e-06
HIGHEST_PRECISION = lax.Precision.HIGHEST
SPATIAL_FORMS = ("sabhe,sache->sahbc", "sahbc,sache->sabhe", "sahbc,sabhe->sache")
TEMPORAL_FORMS = ("sabhe,scbhe->sbhac", "sbhac,scbhe->sabhe", "sbhac,sabhe->scbhe")


MESH = pl.DeviceIdType.MESH
TOKENS = 256
WIDTH = 1152
CHUNKS_ONE = (
    ("p", 0, 144, "zxy"),
    ("p", 144, 144, "zyx"),
    ("s", 0, 80, "yxz"),
    ("s", 80, 32, "zxy"),
    ("s", 112, 32, "zyx"),
)
S_CHUNKS = (("s", 0, 48, "zxy"), ("s", 48, 64, "zyx"), ("s", 112, 32, "yxz"))
P_CHUNKS = (
    ("p", 0, 112, "zxy"),
    ("p", 112, 112, "zyx"),
    ("p", 224, 32, "xyz"),
    ("p", 256, 32, "yxz"),
)
RELS = sorted(
    [(rx, ry, dz) for rx in (0, 1) for ry in (0, 1) for dz in range(-3, 4)],
    key=lambda r: (r[0] + r[1] + abs(r[2]), r != (0, 0, 0)),
)


class Place:
    def __init__(self):
        self.d, self.s = lax.axis_index("dp"), lax.axis_index("sp")
        self.x, self.c = self.d // 2, self.d % 2
        self.z, self.y = self.s // 2, self.s % 2

    def at(self, rel):
        rx, ry, dz = rel
        return (1 - self.x if rx else self.x, self.z + dz, 1 - self.y if ry else self.y)

    def exists(self, dz):
        return None if dz == 0 else ((self.z + dz >= 0) & (self.z + dz <= 3))

    def neighbour(self, direction):
        x, c, z, y = self.x, self.c, self.z, self.y
        return {
            "x": lambda: dev(1 - x, c, z, y),
            "y": lambda: dev(x, c, z, 1 - y),
            "u": lambda: dev(x, c, z + 1, y),
            "d": lambda: dev(x, c, z - 1, y),
            "c": lambda: dev(x, 1 - c, z, y),
        }[direction]()

    def has(self, direction):
        return {"u": lambda: self.z < 3, "d": lambda: self.z > 0}.get(direction, lambda: None)()


def dev(x, c, z, y):
    return (x * 2 + c, z * 2 + y)


def blk(b):
    return (b[0] * 4 + b[1]) * 2 + b[2]


def both(a, b):
    return b if a is None else (a if b is None else (a & b))


def guarded(cond, f):
    if cond is None:
        f()
    else:
        pl.when(cond)(f)


def greet(me):
    barrier = pltpu.get_barrier_semaphore()
    for k in range(1, 4):
        pl.semaphore_signal(
            barrier, inc=1, device_id=((me.d + k) % 4, me.s), device_id_type=MESH
        )
    for k in range(1, 8):
        pl.semaphore_signal(
            barrier, inc=1, device_id=(me.d, (me.s + k) % 8), device_id_type=MESH
        )
    pl.semaphore_wait(barrier, 10)


def links(rel, order):
    nz = {"x": rel[0], "y": rel[1], "z": rel[2]}
    last = max([i for i in range(3) if nz[order[i]]], default=-1)
    out = []
    for i, dim in enumerate(order):
        if i > last:
            out += ["u", "d"] if dim == "z" else [dim]
        elif i == last and dim == "z":
            out += ["u"] if rel[2] < 0 else ["d"]
    parent = None
    if last >= 0:
        parent = order[last] if order[last] != "z" else ("d" if rel[2] < 0 else "u")
    return out, parent


class Gather:
    SEMS = ((7, 16), (7, 16), (7, 5, 16), (7,))

    def __init__(self, me, chunks, p_in, s_in, p_out, s_out, arrived, crossed, sent, local):
        self.chunks = chunks
        self.me, self.ins, self.outs = me, {"p": p_in, "s": s_in}, {"p": p_out, "s": s_out}
        self.arrived, self.crossed, self.sent, self.local = arrived, crossed, sent, local

    def own(self, ch):
        return self.ins[ch[0]].at[pl.ds(ch[1], ch[2]), :]

    def place(self, ch, b, core):
        d, s = b[0] * 2 + core, b[1] * 2 + b[2]
        if ch[0] == "p":
            return self.outs["p"].at[s, pl.ds(d * 288 + ch[1], ch[2]), :]
        return self.outs["s"].at[d, pl.ds(s * 144 + ch[1], ch[2]), :]

    def copy(self, k, rel, direction):
        me, ch = self.me, self.chunks[k]
        b = me.at(rel)
        there = self.place(ch, b, me.c)
        return pltpu.make_async_remote_copy(
            src_ref=self.own(ch) if rel == (0, 0, 0) else there,
            dst_ref=there,
            send_sem=self.sent.at[k, "xyudc".index(direction), blk(b)],
            recv_sem=(self.crossed if direction == "c" else self.arrived).at[k, blk(b)],
            device_id=me.neighbour(direction),
            device_id_type=MESH,
        )

    def ends(self, k, rel):
        return links(rel, self.chunks[k][3])[0] + ["c"]

    def event(self, k, rel):
        me, ch = self.me, self.chunks[k]

        def body():
            if rel == (0, 0, 0):
                pltpu.make_async_copy(
                    self.own(ch), self.place(ch, me.at(rel), me.c), self.local.at[k]
                ).start()
            else:
                self.wait_in(k, rel, me.c, self.arrived)
            for direction in self.ends(k, rel):
                guarded(me.has(direction), lambda: self.copy(k, rel, direction).start())

        guarded(me.exists(rel[2]), body)

    def wait_in(self, k, rel, core, sems):
        b, ch = self.me.at(rel), self.chunks[k]
        pltpu.make_async_copy(self.own(ch), self.place(ch, b, core), sems.at[k, blk(b)]).wait()

    def events(self):
        return [
            functools.partial(self.event, k, rel) for rel in RELS for k in range(len(self.chunks))
        ]

    def level(self, hops, which):
        return [
            functools.partial(self.event, k, rel)
            for rel in RELS
            if rel[0] + rel[1] + abs(rel[2]) == hops
            for k, ch in enumerate(self.chunks)
            if ch[0] == which
        ]

    def complete(self, which):
        me, ks = self.me, [k for k, ch in enumerate(self.chunks) if ch[0] in which]
        for k in ks:
            ch = self.chunks[k]
            pltpu.make_async_copy(
                self.own(ch), self.place(ch, me.at((0, 0, 0)), me.c), self.local.at[k]
            ).wait()
        for rel in RELS:

            def body():
                for k in ks:
                    self.wait_in(k, rel, 1 - me.c, self.crossed)

            guarded(me.exists(rel[2]), body)

    def sent_all(self):
        me = self.me
        for rel in RELS:

            def body():
                for k in range(len(self.chunks)):
                    for direction in self.ends(k, rel):
                        guarded(
                            me.has(direction), lambda: self.copy(k, rel, direction).wait_send()
                        )

            guarded(me.exists(rel[2]), body)

    def finish(self):
        self.complete("ps")
        self.sent_all()


def slots_of(order):
    base, total, count = {}, 0, 1
    for dim in order:
        base[dim] = total
        total += count * (5 if dim == "z" else 1)
        count *= 4 if dim == "z" else 2
    return base, total


class Scatter:
    def __init__(self, me, chunks, compute, own, buffer, base, ring, out, *sems):
        self.me, self.chunks, self.compute, self.own = me, chunks, compute, own
        self.buffer, self.base, self.ring, self.out = buffer, base, ring, out
        self.crossed, self.cross_sent, self.arrived, self.sent = sems
        self.rels = RELS[::-1]
        self.block = sum(ch[2] for ch in chunks)
        self.slot_row, total = [], base + 16 * self.block
        for ch in chunks:
            self.slot_row.append(total)
            total += slots_of(ch[3])[1] * ch[2]
        self.ring_row = total

    @staticmethod
    def rows(chunks, ring):
        block = sum(ch[2] for ch in chunks)
        return (16 + ring) * block + sum(slots_of(ch[3])[1] * ch[2] for ch in chunks)

    @staticmethod
    def sems(chunks):
        n, most = len(chunks), max(slots_of(ch[3])[1] for ch in chunks)
        return [(16,), (16,), (n, most), (n, 16)]

    def at_row(self, row, n):
        return self.buffer.at[pl.ds(row, n), :]

    def core(self, b, first=0, n=None):
        row = self.base + blk(b) * self.block + first
        return self.at_row(pl.multiple_of(row, 16), self.block if n is None else n)

    def ring_at(self, i):
        return self.at_row(self.ring_row + (i % self.ring) * self.block, self.block)

    def cross_copy(self, i):
        b = self.me.at(self.rels[i])
        return pltpu.make_async_remote_copy(
            src_ref=self.ring_at(i),
            dst_ref=self.core(b),
            send_sem=self.cross_sent.at[blk(b)],
            recv_sem=self.crossed.at[blk(b)],
            device_id=self.me.neighbour("c"),
            device_id_type=MESH,
        )

    def slot(self, k, b, direction, z):
        order = self.chunks[k][3]
        base, _ = slots_of(order)
        dim = "z" if direction in "ud" else direction
        coord = {"x": (b[0], 2), "y": (b[2], 2), "z": (b[1], 4)}
        index = 0
        for d in order[: order.index(dim)]:
            index = index * coord[d][1] + coord[d][0]
        if dim == "z":
            inner = b[1] if direction == "d" else jnp.where(b[1] == z, 4, b[1])
            index = index * 5 + inner
        return base[dim] + index

    def got(self, k, j):
        n = self.chunks[k][2]
        return self.at_row(pl.multiple_of(self.slot_row[k] + j * n, 16), n)

    def send(self, k, i):
        rel, ch = self.rels[i], self.chunks[k]
        b, direction = self.me.at(rel), links(rel, ch[3])[1]
        z = self.me.z + {"u": 1, "d": -1}.get(direction, 0)
        j = self.slot(k, b, {"x": "x", "y": "y", "u": "d", "d": "u"}[direction], z)
        return pltpu.make_async_remote_copy(
            src_ref=self.core(b, ch[1], ch[2]),
            dst_ref=self.got(k, j),
            send_sem=self.sent.at[k, blk(b)],
            recv_sem=self.arrived.at[k, j],
            device_id=self.me.neighbour(direction),
            device_id_type=MESH,
        )

    def add(self, k, b, messages, final):
        ch = self.chunks[k]
        step = 16
        core_row = self.base + blk(b) * self.block + ch[1]

        @pl.loop(0, ch[2] // step)
        def _(t):
            r = pl.ds(pl.multiple_of(ch[1] + t * step, 16), step)
            held = pl.ds(pl.multiple_of(core_row + t * step, 16), step)
            v = self.own[r, :].astype(jnp.float32) + self.buffer[held, :].astype(jnp.float32)
            for cond, j in messages:
                at = pl.ds(pl.multiple_of(self.slot_row[k] + j * ch[2] + t * step, 16), step)
                q = self.buffer[at, :].astype(jnp.float32)
                v = v + (q if cond is None else jnp.where(cond, q, 0.0))
            if final:
                self.out[r, :] = v
            else:
                self.buffer[held, :] = v.astype(jnp.bfloat16)

    def guarded(self, i, body):
        guarded(self.me.exists(self.rels[i][2]), body)

    def free_cross(self, i):
        self.guarded(i, lambda: self.cross_copy(i).wait_send())

    def cross_event(self, i):
        if i >= self.ring:
            self.free_cross(i - self.ring)

        def body():
            self.compute(self.me.at(self.rels[i]), 1 - self.me.c, self.ring_at(i))
            self.cross_copy(i).start()

        self.guarded(i, body)

    def own_event(self, i):
        me, rel = self.me, self.rels[i]

        def body():
            b = me.at(rel)
            self.compute(b, me.c, self.own)
            held = self.core(b)
            pltpu.make_async_copy(held, held, self.crossed.at[blk(b)]).wait()
            for k, ch in enumerate(self.chunks):
                children, parent = links(rel, ch[3])
                messages = []
                for direction in children:
                    cond, j = me.has(direction), self.slot(k, b, direction, me.z)

                    def wait():
                        at = self.got(k, j)
                        pltpu.make_async_copy(at, at, self.arrived.at[k, j]).wait()

                    guarded(cond, wait)
                    messages.append((cond, j))
                self.add(k, b, messages, not parent)
                if parent:
                    self.send(k, i).start()

        self.guarded(i, body)

    def events(self, lag=2):
        n, out = len(self.rels), []
        for i in range(n + lag):
            if i < n:
                out.append(functools.partial(self.cross_event, i))
            if i >= lag:
                out.append(functools.partial(self.own_event, i - lag))
        return out

    def finish(self):
        n = len(self.rels)
        for i in range(n - self.ring, n):
            self.free_cross(i)
        for i in range(n):

            def body():
                for k, ch in enumerate(self.chunks):
                    if links(self.rels[i], ch[3])[1]:
                        self.send(k, i).wait_send()

            self.guarded(i, body)


class Exchange:
    def __init__(self, me, source, target, sent, arrived, local):
        self.me, self.source, self.target = me, source, target
        self.sent, self.arrived, self.local = sent, arrived, local

    def rows(self, ref, s):
        return ref.at[pl.ds(pl.multiple_of(s * 32, 32), 32), :]

    def copy(self, k):
        me = self.me
        other = (me.s + k) % 8
        return pltpu.make_async_remote_copy(
            src_ref=self.rows(self.source, other),
            dst_ref=self.rows(self.target, me.s),
            send_sem=self.sent.at[k],
            recv_sem=self.arrived.at[k],
            device_id=(me.d, other),
            device_id_type=MESH,
        )

    def stay(self):
        return pltpu.make_async_copy(
            self.rows(self.source, self.me.s), self.rows(self.target, self.me.s), self.local
        )

    def start(self):
        self.stay().start()
        for k in range(1, 8):
            self.copy(k).start()

    def finish(self):
        self.stay().wait()
        for k in range(1, 8):
            at = self.rows(self.target, (self.me.s - k + 8) % 8)
            pltpu.make_async_copy(at, at, self.arrived.at[k]).wait()
            self.copy(k).wait_send()


class Spread:
    def __init__(self, me, axis, source, target, sent, arrived, each):
        self.me, self.axis, self.source, self.target = me, axis, source, target
        self.sent, self.arrived, self.each = sent, arrived, each
        self.n = 4 if axis == "dp" else 8
        self.i = me.d if axis == "dp" else me.s

    def copy(self, k):
        other = (self.i + k) % self.n
        return pltpu.make_async_remote_copy(
            src_ref=self.source.at[other] if self.each else self.source,
            dst_ref=self.target.at[self.i],
            send_sem=self.sent.at[k],
            recv_sem=self.arrived.at[k],
            device_id=(other, self.me.s) if self.axis == "dp" else (self.me.d, other),
            device_id_type=MESH,
        )

    def start(self):
        for k in range(1, self.n):
            self.copy(k).start()
        self.target[self.i] = self.source[self.i] if self.each else self.source[...]

    def finish(self):
        for k in range(1, self.n):
            at = self.target.at[(self.i - k + self.n) % self.n]
            pltpu.make_async_copy(at, at, self.arrived.at[k]).wait()
            self.copy(k).wait_send()


def pieces(start, length, width=WIDTH):
    out, done = [], 0
    while done < length:
        row, column = divmod(start + done, width)
        n = min(width - column, length - done)
        out.append((row, column, n, done))
        done += n
    return out


def spread_out(stages, first, last):
    return [(first + (last - first) * i / len(stages), stage) for i, stage in enumerate(stages)]


def interleave(events, stages):
    cuts = sorted((int(share * len(events)), i) for i, (share, _) in enumerate(stages))
    done = 0
    for cut, i in cuts:
        for event in events[done:cut]:
            event()
        done = max(done, cut)
        stages[i][1]()
    for event in events[done:]:
        event()


def dma_sems(*shapes):
    return [pltpu.SemaphoreType.DMA(shape) for shape in shapes]


ANY_SPEC = pl.BlockSpec(memory_space=pl.ANY)
VMEM_SPEC = pl.BlockSpec(memory_space=pltpu.VMEM)
SLABS = (
    jax.ShapeDtypeStruct((8, WIDTH, WIDTH), jnp.bfloat16),
    jax.ShapeDtypeStruct((4, WIDTH, WIDTH), jnp.bfloat16),
)
STREAM = jax.ShapeDtypeStruct((TOKENS, WIDTH), jnp.bfloat16)


def first_gather_kernel(
    p_in, s_in, pack, cond, weight0, weight1, cot, p_out, s_out, mod_out, bias_out, incoming,
    packs, part, parts, whole, wholes, *sems,
):
    me = Place()
    gather = Gather(me, CHUNKS_ONE, p_in, s_in, p_out, s_out, *sems[:4])
    exchange = Exchange(me, cot, incoming, *sems[4:7])
    biases = Spread(me, "dp", pack, packs, *sems[7:9], False)
    terms = Spread(me, "dp", part, parts, *sems[9:11], True)
    columns = Spread(me, "sp", whole, wholes, *sems[11:13], False)
    greet(me)

    def begin():
        biases.start()
        for i, weight in enumerate((weight0, weight1)):
            product = jnp.dot(cond[...], weight[...], preferred_element_type=jnp.float32)
            for q in range(4):
                part[q, i : i + 1, :] = product[q : q + 1, :]
        terms.start()
        exchange.start()

    def middle():
        terms.finish()
        whole[...] = jnp.sum(parts[...], axis=0)
        columns.start()

    def end():
        columns.finish()
        biases.finish()
        exchange.finish()
        for i in range(2):
            mod_out[i] = jnp.zeros((8, WIDTH), jnp.float32)
            for s in range(8):
                for row, column, n, at in pieces(864 * s, 864):
                    mod_out[i, row : row + 1, column : column + n] = wholes[
                        s, i : i + 1, at : at + n
                    ]
            for k in range(4):
                for first, n_all in ((0, WIDTH), (WIDTH, 576)):
                    source = 6 * i + 4 + first // WIDTH
                    for row, column, n, at in pieces(1728 * k + first, n_all):
                        mod_out[i, row : row + 1, column : column + n] += packs[
                            k, source : source + 1, at : at + n
                        ]
                top = 6 * i
                bias_out[i, k // 2 : k // 2 + 1, 576 * (k % 2) : 576 * (k % 2 + 1)] = packs[
                    k, top : top + 1, 0:576
                ]
                for row in (2, 3):
                    bias_out[i, row : row + 1, 288 * k : 288 * (k + 1)] = packs[
                        k, top + row - 1 : top + row, 0:288
                    ]
                bias_out[i, 4 + k : 5 + k, :] = packs[k, top + 3 : top + 4, :]

    events = gather.events()
    own = len(CHUNKS_ONE)
    interleave(events, [(own / len(events), begin), (0.3, middle), (0.8, end)])
    gather.finish()


def first_gather(p, s, pack, cond, weights, cotangent):
    return pl.pallas_call(
        first_gather_kernel,
        out_shape=SLABS
        + (
            jax.ShapeDtypeStruct((2, 8, WIDTH), jnp.float32),
            jax.ShapeDtypeStruct((2, 8, WIDTH), jnp.float32),
            STREAM,
        ),
        in_specs=[VMEM_SPEC] * 6 + [ANY_SPEC],
        out_specs=(ANY_SPEC, ANY_SPEC, VMEM_SPEC, VMEM_SPEC, ANY_SPEC),
        scratch_shapes=[
            pltpu.VMEM((4, 16, WIDTH), jnp.float32),
            pltpu.VMEM((4, 8, 864), jnp.float32),
            pltpu.VMEM((4, 8, 864), jnp.float32),
            pltpu.VMEM((8, 864), jnp.float32),
            pltpu.VMEM((8, 8, 864), jnp.float32),
        ]
        + dma_sems(*Gather.SEMS, (8,), (8,), (), (4,), (4,), (4,), (4,), (8,), (8,)),
        compiler_params=pltpu.CompilerParams(collective_id=0, has_side_effects=True),
        name="first_gather",
    )(p, s, pack, cond, *weights, cotangent)


UNPACKED = ((288, 432), (576,), (144, 288), (288,), (288, 576), (1152,), (144, 1152), (288,), (1728,))


def unpack_kernel(*refs):
    ins, passing, outs = refs[:6], refs[6:10], refs[10:28]
    passed, scratch, sem = refs[28:32], refs[32:38], refs[44]
    through = refs[38:44]
    d = lax.axis_index("dp")

    def copy(i, source, target):
        c = pltpu.make_async_copy(source, target, sem.at[i])
        c.start()
        return c

    loads = [copy(i, ins[3 * i], scratch[3 * i]) for i in range(2)]
    routes = list(zip(passing, passed)) + [(ins[3 * i + 1], outs[9 * i + 6]) for i in range(2)]
    halfway = [copy(2 + i, source, through[i]) for i, (source, _) in enumerate(routes)]
    waits = []
    for i in range(2):
        totals = ins[3 * i + 2]
        a_in, a_bias, a_out, o_bias, expand, e_bias, _, s_bias, m_bias = outs[9 * i : 9 * i + 9]
        for k in range(4):

            @pl.when(d == k)
            def _():
                half = 576 * (k % 2)
                a_bias[...] = totals[k // 2, 0, half : half + 576]
                o_bias[...] = totals[2, 0, 288 * k : 288 * (k + 1)]
                s_bias[...] = totals[3, 0, 288 * k : 288 * (k + 1)]
                e_bias[...] = totals[4 + k, 0, :]
                m_bias[...] = jnp.concatenate(
                    [totals[2 * k, 1, 0:864], totals[2 * k + 1, 1, 0:864]]
                )

        packed, turned, wide = scratch[3 * i : 3 * i + 3]
        loads[i].wait()
        turned[...] = packed[:, 432:576].T
        wide[...] = packed[:, 576:1152]
        waits.append(copy(8 + i, turned, a_out))
        waits.append(copy(10 + i, wide, expand))
        a_in[...] = packed[:, 0:432]
    for i, (_, target) in enumerate(routes):
        halfway[i].wait()
        waits.append(copy(12 + i, through[i], target))
    for wait in waits:
        wait.wait()


def unpack(grads, passing):
    rows = jax.ShapeDtypeStruct
    hbm = (2, 4, 6)
    outs = pl.pallas_call(
        unpack_kernel,
        out_shape=[rows(shape, jnp.float32) for shape in UNPACKED * 2]
        + [rows(a.shape, a.dtype) for a in passing],
        in_specs=[ANY_SPEC, ANY_SPEC, VMEM_SPEC] * 2 + [ANY_SPEC] * 4,
        out_specs=[ANY_SPEC if i in hbm else VMEM_SPEC for i in range(9)] * 2 + [ANY_SPEC] * 4,
        scratch_shapes=[
            pltpu.VMEM((288, WIDTH), jnp.float32),
            pltpu.VMEM((144, 288), jnp.float32),
            pltpu.VMEM((288, 576), jnp.float32),
        ]
        * 2
        + [pltpu.VMEM(a.shape, a.dtype) for a in passing]
        + [pltpu.VMEM((144, WIDTH), jnp.float32)] * 2
        + dma_sems((18,)),
        compiler_params=pltpu.CompilerParams(vmem_limit_bytes=63 << 20),
        name="unpack",
    )(*grads, *passing)
    outs = list(outs)
    for i in range(2):
        for j in (2, 6):
            outs[9 * i + j] = outs[9 * i + j].T
    return outs[:18], outs[18:]


SCALE = HD ** (-0.5)
NEGATIVE = -1e30


def dot(a, b):
    return lax.dot_general(a, b, (((1,), (0,)), ((), ())), preferred_element_type=jnp.float32)


def dot_nt(a, b):
    return lax.dot_general(a, b, (((1,), (1,)), ((), ())), preferred_element_type=jnp.float32)


def dot_tn(a, b):
    return lax.dot_general(a, b, (((0,), (0,)), ((), ())), preferred_element_type=jnp.float32)


def by_rows(body, step=32):
    @pl.loop(0, TOKENS // step)
    def _(i):
        body(pl.ds(pl.multiple_of(i * step, step), step))


def statistics(v):
    centered = v - jnp.mean(v, axis=1, keepdims=True)
    scale = lax.rsqrt(jnp.mean(centered * centered, axis=1, keepdims=True) + EPSILON)
    return centered * scale, scale


def fold(v):
    return jnp.sum(v.reshape(v.shape[0] // 8, 8, v.shape[1]), axis=0)


def gelu_both(h):
    c, a = math.sqrt(2.0 / math.pi), 0.044715
    square = h * h
    t = jnp.tanh(c * h * (1.0 + a * square))
    half = 0.5 * (1.0 + t)
    return h * half, half + 0.5 * h * (1.0 - t * t) * (c * (1.0 + 3.0 * a * square))


WIN_IN, WIN_OUT, WIN_EXP = slice(0, 512), slice(384, 640), slice(512, 1152)


def forward_stages(e, y, shrink_last=False):
    mod = e.mod
    shift1, scale1, gate1 = [lambda i=i: mod[i : i + 1, :] for i in range(3)]
    shift2, scale2, gate2 = [lambda i=i: mod[i : i + 1, :] for i in range(3, 6)]

    def normalize():
        e.bslab[...] = jnp.zeros(e.bslab.shape, jnp.float32)
        for s in range(8):
            for row, first in ((0, 0), (1, 2 * WIDTH)):
                lo, hi = max(432 * s, first), min(432 * (s + 1), first + WIDTH)
                if lo < hi:
                    e.bslab[s, 0:1, lo - 432 * s : hi - 432 * s] = e.bias[
                        row : row + 1, lo - first : hi - first
                    ]

        def rows(r):
            n, _ = statistics(e.x[r, :].astype(jnp.float32))
            e.normed[r, :] = (n * (1.0 + scale1()) + shift1()).astype(jnp.bfloat16)

        by_rows(rows)

    def project(first):
        @pl.loop(first, first + 4)
        def _(s):
            e.wait_p(s)
            v = dot(e.normed[...], e.pv[s, :, WIN_IN]) + e.bslab[s, 0:1, :]
            for j in range(6):
                e.heads[6 * s + j] = v[:, HD * j : HD * (j + 1)].astype(jnp.bfloat16)

    def attend(first):
        @pl.loop(first, first + 4)
        def _(h):
            probs = attention_probs(e, h)
            e.mh[h] = dot(probs.astype(jnp.bfloat16), e.heads[2 * H + h]).astype(jnp.bfloat16)

    def join():
        for h in range(H):
            e.mixture[:, HD * h : HD * (h + 1)] = e.mh[h]
        for s in range(8):
            v = dot(e.mixture[...], e.pv[s, :, WIN_OUT])
            e.attended[:, 144 * s : 144 * (s + 1)] = v[:, 48:192]

    def middle():
        def rows(r):
            attended = e.attended[r, :] + e.bias[2:3, :]
            e.attended[r, :] = attended
            middle = e.x[r, :].astype(jnp.float32) + gate1() * attended
            e.middle[r, :] = middle
            n, _ = statistics(middle)
            e.normed2[r, :] = (n * (1.0 + scale2()) + shift2()).astype(jnp.bfloat16)

        by_rows(rows)
        e.branch[...] = jnp.zeros(e.branch.shape, jnp.float32)

    def expand(d):
        for half in range(2):
            v = dot(e.normed2[...], e.pv[2 * d + half, :, WIN_EXP])
            e.tmp[:, 576 * half : 576 * (half + 1)] = v[:, 64:640]

        def rows(r):
            value, slope = gelu_both(e.tmp[r, :] + e.bias[4 + d : 5 + d, :])
            e.act[d, r, :] = value.astype(jnp.bfloat16)
            if e.slope is not None:
                e.slope[d, r, :] = slope.astype(jnp.bfloat16)

        by_rows(rows)

    def shrink(d):
        e.wait_s(d)
        e.branch[...] += dot_nt(e.act[d], e.sv[d])

    def mlp(d):
        expand(d)
        shrink(d)

    def close():
        def rows(r):
            branch = e.branch[r, :] + e.bias[3:4, :]
            e.branch[r, :] = branch
            if y is not None:
                y[r, :] = (e.middle[r, :] + gate2() * branch).astype(jnp.bfloat16)

        by_rows(rows)

    part = functools.partial
    return (
        [normalize, part(project, 0), part(project, 4)]
        + [part(attend, h) for h in range(0, H, 4)]
        + [join, middle]
        + (
            [part(expand, d) for d in range(4)] + [part(shrink, d) for d in range(4)]
            if shrink_last
            else [part(mlp, d) for d in range(4)]
        )
        + [close]
    )


def attention_probs(e, h):
    scores = dot_nt(e.heads[h], e.heads[H + h]) * SCALE
    if e.mask is not None:
        scores = scores + e.mask[...]
    exponent = jnp.exp(scores - jnp.max(scores, axis=1, keepdims=True))
    return exponent / jnp.sum(exponent, axis=1, keepdims=True)


def forward_pass(e, y):
    for stage in forward_stages(e, y):
        stage()


def backward_stages(e):
    mod = e.mod
    gate1, scale1 = lambda: mod[2:3, :], lambda: mod[1:2, :]
    gate2, scale2 = lambda: mod[5:6, :], lambda: mod[4:5, :]

    def open_block():
        e.sums[...] = jnp.zeros(e.sums.shape, jnp.float32)
        e.bout[...] = jnp.zeros(e.bout.shape, jnp.bfloat16)
        for s in range(8):
            e.bexp[s, :, 0:128] = jnp.zeros((TOKENS, 128), jnp.bfloat16)
            e.bin[s, :, 384:512] = jnp.zeros((TOKENS, 128), jnp.bfloat16)
        e.wait_kept("branch")

        def rows(r):
            g = e.g[r, :].astype(jnp.float32)
            back = (gate2() * g).astype(jnp.bfloat16)
            e.bb[r, :] = back
            e.sums[5] += fold(g * e.tmp[r, :])
            e.sums[7] += fold(back.astype(jnp.float32))

        by_rows(rows)
        e.bb_t[...] = e.bb[...].T
        e.wait_kept("slope")

    def hidden(d):
        e.weights.wait("shrink", d)
        e.tmp[...] = dot(e.bb[...], e.weights.at(d, WIDTH))
        e.weights.start("expand", d)

        @pl.loop(0, TOKENS // 32)
        def _(i):
            r = pl.ds(pl.multiple_of(i * 32, 32), 32)
            slope = e.slope[pl.ds(pl.multiple_of(d * TOKENS + i * 32, 32), 32), :]
            back = (e.tmp[r, :] * slope.astype(jnp.float32)).astype(jnp.bfloat16)
            for half in range(2):
                e.bexp[2 * d + half, r, 64:640] = back[:, 576 * half : 576 * (half + 1)]
            e.sums[8 + d] += fold(back.astype(jnp.float32))

    def through(name, width, operand, first, following):
        if first == 0:
            e.tmp[...] = jnp.zeros(e.tmp.shape, jnp.float32)

        @pl.loop(0, 4)
        def _(i):
            e.weights.wait(name, first + i)
            e.tmp[...] += dot_nt(operand[first + i], e.weights.at(i, width))
            if first == 0:
                e.weights.start(name, 4 + i)
            elif following is not None:
                e.weights.start(following, i)

    def middle():
        e.wait_kept("middle")
        e.wait_kept("attended")

        def rows(r):
            n, scale = statistics(e.middle[r, :])
            back_normed = e.tmp[r, :]
            e.sums[3] += fold(back_normed)
            e.sums[4] += fold(back_normed * n)
            u = back_normed * (1.0 + scale2())
            inner = jnp.mean(u, axis=1, keepdims=True) + n * jnp.mean(u * n, axis=1, keepdims=True)
            back_middle = e.g[r, :].astype(jnp.float32) + scale * (u - inner)
            e.middle[r, :] = back_middle
            e.sums[2] += fold(back_middle * e.attended[r, :])
            back = (gate1() * back_middle).astype(jnp.bfloat16)
            e.sums[6] += fold(back.astype(jnp.float32))
            for s in range(8):
                e.bout[s, r, 48:192] = back[:, 144 * s : 144 * (s + 1)]

        by_rows(rows)

    def split():
        e.wait_kept("heads")
        for h in range(H):
            e.mh[h] = e.tmp[:, HD * h : HD * (h + 1)].astype(jnp.bfloat16)

    def attend(first):
        @pl.loop(first, first + 4)
        def _(h):
            q, k, v, back = e.heads[h], e.heads[H + h], e.heads[2 * H + h], e.mh[h]
            probs = attention_probs(e, h)
            back_probs = dot_nt(back, v)
            e.heads[2 * H + h] = dot_tn(probs.astype(jnp.bfloat16), back).astype(jnp.bfloat16)
            delta = jnp.sum(probs * back_probs, axis=1, keepdims=True)
            back_scores = (probs * (back_probs - delta)).astype(jnp.bfloat16)
            e.heads[h] = (dot(back_scores, k) * SCALE).astype(jnp.bfloat16)
            e.heads[H + h] = (dot_tn(back_scores, q) * SCALE).astype(jnp.bfloat16)

    def join():
        ones = jnp.ones((8, TOKENS), jnp.bfloat16)

        @pl.loop(0, 8)
        def _(s):
            for j in range(6):
                e.bin[s, :, HD * j : HD * (j + 1)] = e.heads[6 * s + j]
            e.bslab[s] = dot(ones, e.bin[s])

    def close():
        def rows(r):
            n, scale = statistics(e.x[r, :].astype(jnp.float32))
            back_normed = e.tmp[r, :]
            e.sums[0] += fold(back_normed)
            e.sums[1] += fold(back_normed * n)
            u = back_normed * (1.0 + scale1())
            inner = jnp.mean(u, axis=1, keepdims=True) + n * jnp.mean(u * n, axis=1, keepdims=True)
            e.back_x[r, :] = (e.middle[r, :] + scale * (u - inner)).astype(jnp.bfloat16)

        by_rows(rows)

        for s in range(8):
            for row, first_column in ((0, 0), (1, 2 * WIDTH)):
                lo, hi = max(432 * s, first_column), min(432 * (s + 1), first_column + WIDTH)
                if lo < hi:
                    e.bias_grad[row : row + 1, lo - first_column : hi - first_column] = e.bslab[
                        s, 0:1, lo - 432 * s : hi - 432 * s
                    ]
        for row, slot in ((2, 6), (3, 7), (4, 8), (5, 9), (6, 10), (7, 11)):
            e.bias_grad[row : row + 1, :] = jnp.sum(e.sums[slot], axis=0, keepdims=True)
        for slot in range(6):
            e.mod_grad[slot : slot + 1, :] = jnp.sum(e.sums[slot], axis=0, keepdims=True)
        e.mod_grad[6:8, :] = jnp.zeros((2, WIDTH), jnp.float32)

    part = functools.partial
    return (
        [open_block]
        + [part(hidden, d) for d in range(4)]
        + [part(through, "expand", 640, e.bexp, first, "out") for first in (0, 4)]
        + [middle]
        + [part(through, "out", 256, e.bout, first, "in") for first in (0, 4)]
        + [split]
        + [part(attend, h) for h in range(0, H, 4)]
        + [join]
        + [part(through, "in", 512, e.bin, first, None) for first in (0, 4)]
        + [close]
    )


class Weights:
    WINDOWS = {"shrink": slice(0, WIDTH), "expand": WIN_EXP, "out": WIN_OUT, "in": WIN_IN}

    def __init__(self, p, s, buffer, sems):
        self.p, self.s, self.buffer, self.sems = p, s, buffer, sems

    def slot(self, i):
        return pl.ds(pl.multiple_of((i % 4) * WIDTH, WIDTH), WIDTH)

    def copy(self, name, i):
        window = self.WINDOWS[name]
        source = self.s.at[i] if name == "shrink" else self.p.at[i, :, window]
        width = window.stop - window.start
        target = self.buffer.at[self.slot(i), 0:width]
        return pltpu.make_async_copy(source, target, self.sems.at[i % 4])

    def start(self, name, i):
        self.copy(name, i).start()

    def wait(self, name, i):
        self.copy(name, i).wait()

    def at(self, i, width):
        return self.buffer[self.slot(i), 0:width]


class Refs:
    pass


WEIGHT_SCRATCH = (
    ("pv", (8, WIDTH, WIDTH), jnp.bfloat16),
    ("sv", (4, WIDTH, WIDTH), jnp.bfloat16),
)
FORWARD_SCRATCH = (
    ("bslab", (8, 8, 512), jnp.float32),
    ("heads", (3 * H, TOKENS, HD), jnp.bfloat16),
    ("mh", (H, TOKENS, HD), jnp.bfloat16),
    ("attended", (TOKENS, WIDTH), jnp.float32),
    ("middle", (TOKENS, WIDTH), jnp.float32),
    ("branch", (TOKENS, WIDTH), jnp.float32),
    ("tmp", (TOKENS, WIDTH), jnp.float32),
)
OPERANDS = (
    ("normed", (TOKENS, WIDTH), jnp.bfloat16),
    ("mixture", (TOKENS, WIDTH), jnp.bfloat16),
    ("normed2", (TOKENS, WIDTH), jnp.bfloat16),
    ("act", (4, TOKENS, WIDTH), jnp.bfloat16),
)
BACK_OPERANDS = (
    ("bb", (TOKENS, WIDTH), jnp.bfloat16),
    ("bin", (8, TOKENS, 512), jnp.bfloat16),
    ("bout", (8, TOKENS, 256), jnp.bfloat16),
    ("bexp", (8, TOKENS, 640), jnp.bfloat16),
)
SLOPE = (("slope", (4, TOKENS, WIDTH), jnp.bfloat16),)
SUMS = (("sums", (12, 8, WIDTH), jnp.float32),)
def weight_loads(e, p_hbm, s_hbm, psem, ssem):
    def p_copy(s):
        return pltpu.make_async_copy(p_hbm.at[s], e.pv.at[s], psem.at[s])

    def s_copy(d):
        return pltpu.make_async_copy(s_hbm.at[d], e.sv.at[d], ssem.at[d])

    def start_p():
        @pl.loop(0, 8)
        def _(s):
            p_copy(s).start()

    def start_s():
        @pl.loop(0, 4)
        def _(d):
            s_copy(d).start()

    e.wait_p = lambda s: p_copy(s).wait()
    e.wait_s = lambda d: s_copy(d).wait()
    return start_p, start_s


def fill_mask(e):
    frames = e.segments.shape[1]
    each = TOKENS // frames

    def clips(axis):
        frame = lax.broadcasted_iota(jnp.int32, (TOKENS, TOKENS), axis) // each
        clip = jnp.zeros((TOKENS, TOKENS), jnp.int32)
        for f in range(frames):
            clip = jnp.where(frame == f, e.segments[0, f], clip)
        return clip

    def spots(axis):
        return lax.broadcasted_iota(jnp.int32, (TOKENS, TOKENS), axis) % each

    same = (clips(0) == clips(1)) & (spots(0) == spots(1))
    e.mask[...] = jnp.where(same, 0.0, NEGATIVE)


SECOND_SCRATCH = WEIGHT_SCRATCH + FORWARD_SCRATCH + OPERANDS + SLOPE + (
    ("y", (TOKENS, WIDTH), jnp.bfloat16),
    ("mask", (TOKENS, TOKENS), jnp.float32),
    ("xt", (TOKENS, WIDTH), jnp.bfloat16),
)
KEPT = ("branch", "slope", "middle", "attended", "heads", "act", "normed", "mixture", "normed2")
SHAPES = {name: (shape, kind) for name, shape, kind in SECOND_SCRATCH}


def second_gather_kernel(
    p_in, s_in, x, mods, biases, segments, p, s, p_out, s_out, passed, y_t, *refs
):
    n = len(KEPT)
    saved, saved_t, refs = refs[:n], refs[n : 2 * n], refs[2 * n :]
    e = Refs()
    for (name, *_), ref in zip(SECOND_SCRATCH, refs):
        setattr(e, name, ref)
    mask, e.mask, e.x, e.segments = e.mask, None, x, segments
    e.mod, e.bias = mods.at[0], biases.at[0]
    sems = refs[len(SECOND_SCRATCH) :]
    me = Place()
    gather = Gather(me, P_CHUNKS + S_CHUNKS, p_in, s_in, p_out, s_out, *sems[:4])
    exchange = Exchange(me, e.y, passed, *sems[4:7])
    greet(me)
    stages = forward_stages(e, e.y)

    def keeps(targets):
        return [
            pltpu.make_async_copy(getattr(e, name), target, sems[9].at[i])
            for i, (name, target) in enumerate(zip(KEPT, targets))
        ]

    def leave():
        exchange.start()
        for keep in keeps(saved):
            keep.start()

    def left():
        exchange.finish()
        for keep in keeps(saved):
            keep.wait()

    take = pltpu.make_async_copy(passed, e.xt, sems[10])

    def turn():
        take.start()
        e.mask = mask
        fill_mask(e)
        take.wait()

    def load():
        for start in weight_loads(e, p, s, *sems[7:9]):
            start()

    lag, levels = 4, 6
    early, late = [], []
    for hops in range(levels + lag):
        if hops < levels:
            early += gather.level(hops, "p")
        if hops >= lag:
            (early if hops < levels else late).extend(gather.level(hops - lag, "s"))
    own = len(P_CHUNKS) / len(early)
    timed = [(own, load)] + spread_out(stages, own, 0.55)
    interleave(early, timed + [(0.55, leave), (0.9, left), (0.95, turn)])
    gather.complete("p")
    e.x, e.mod, e.bias = e.xt, mods.at[1], biases.at[1]
    start_p, start_s = weight_loads(e, p_out, s_out, *sems[7:9])
    start_p()
    stages = forward_stages(e, e.y, shrink_last=True)
    interleave(late, spread_out(stages[:-5], 0.0, 1.0))
    gather.complete("s")
    start_s()
    for stage in stages[-5:]:
        stage()
    gather.sent_all()
    last = keeps(saved_t) + [pltpu.make_async_copy(e.y, y_t, sems[10])]
    for keep in last:
        keep.start()
    for keep in last:
        keep.wait()


def second_gather(p_own, s_own, x, mods, biases, segments, p, s):
    kept = tuple(jax.ShapeDtypeStruct(*SHAPES[name]) for name in KEPT)
    smem = pl.BlockSpec(memory_space=pltpu.SMEM)
    results = pl.pallas_call(
        second_gather_kernel,
        out_shape=SLABS + (STREAM, STREAM) + kept + kept,
        in_specs=[VMEM_SPEC] * 5 + [smem] + [ANY_SPEC] * 2,
        out_specs=(ANY_SPEC,) * (4 + 2 * len(KEPT)),
        scratch_shapes=[pltpu.VMEM(shape, kind) for _, shape, kind in SECOND_SCRATCH]
        + dma_sems(*Gather.SEMS, (8,), (8,), (), (8,), (4,), (len(KEPT),), ()),
        compiler_params=pltpu.CompilerParams(
            collective_id=1, has_side_effects=True, vmem_limit_bytes=60 << 20
        ),
        name="second_gather",
    )(p_own, s_own, x, mods, biases, segments, p, s)
    n = 4 + len(KEPT)
    return results[:4], results[4:n], results[n:]


S_RING, P_RING = 5, 3
S_ROWS, P_ROWS = Scatter.rows(S_CHUNKS, S_RING), Scatter.rows(P_CHUNKS, P_RING)
SLOPE_ROW, ACT_ROW = 4 * WIDTH, 4 * WIDTH + 4 * TOKENS
BACKWARD_SCRATCH = (
    ("arena", (P_ROWS, WIDTH), jnp.bfloat16),
    ("arena_s", (S_ROWS, WIDTH), jnp.bfloat16),
    ("own_p", (288, WIDTH), jnp.bfloat16),
    ("own_s", (144, WIDTH), jnp.bfloat16),
    ("bslab", (8, 8, 512), jnp.float32),
    ("heads", (3 * H, TOKENS, HD), jnp.bfloat16),
    ("mh", (H, TOKENS, HD), jnp.bfloat16),
    ("attended", (TOKENS, WIDTH), jnp.float32),
    ("middle", (TOKENS, WIDTH), jnp.float32),
    ("tmp", (TOKENS, WIDTH), jnp.float32),
    ("sums", (12, 8, WIDTH), jnp.float32),
    ("bb", (TOKENS, WIDTH), jnp.bfloat16),
    ("bin", (8, TOKENS, 512), jnp.bfloat16),
    ("bout", (8, TOKENS, 256), jnp.bfloat16),
    ("bexp", (8, TOKENS, 640), jnp.bfloat16),
    ("back_x", (TOKENS, WIDTH), jnp.bfloat16),
    ("bb_t", (WIDTH, TOKENS), jnp.bfloat16),
    ("normed_t", (WIDTH, TOKENS), jnp.bfloat16),
    ("mixture_t", (WIDTH, TOKENS), jnp.bfloat16),
    ("normed2_t", (WIDTH, TOKENS), jnp.bfloat16),
    ("bias_grad", (8, WIDTH), jnp.float32),
    ("mod_grad", (8, WIDTH), jnp.float32),
    ("small", (8, 8, WIDTH), jnp.float32),
    ("small_in", (8, 8, WIDTH), jnp.float32),
    ("row_sum", (8, WIDTH), jnp.float32),
    ("row_in", (4, 8, WIDTH), jnp.float32),
    ("total", (8, WIDTH), jnp.float32),
)
MASK = (("mask", (TOKENS, TOKENS), jnp.float32),)


def backward_kernel(block, names, *refs):
    e = Refs()
    e.mask = None
    for name, ref in zip(names, refs):
        setattr(e, name, ref)
    temporal = block == 1
    sems = refs[len(names) :]
    ready, sems = sems[0], sems[1:]
    e.mod = e.mods.at[block]
    e.slope = e.arena.at[SLOPE_ROW : SLOPE_ROW + 4 * TOKENS, :]
    me = Place()

    places = {"branch": e.tmp, "middle": e.middle, "attended": e.attended, "heads": e.heads}

    def kept_copies(name):
        index = KEPT.index(name)
        source, sem = getattr(e, name + "_kept"), sems[0].at[index]
        if name in ("slope", "act"):
            row = SLOPE_ROW if name == "slope" else ACT_ROW
            rows = [
                e.arena.at[row + d * TOKENS : row + (d + 1) * TOKENS, :] for d in range(4)
            ]
            base = 0 if name == "slope" else 4
            return [
                pltpu.make_async_copy(source.at[d], rows[d], sems[1].at[base + d])
                for d in range(4)
            ]
        return [pltpu.make_async_copy(source, places.get(name, e.back_x), sem)]

    def start_kept(name):
        for copy in kept_copies(name):
            copy.start()

    def wait_kept(name):
        for copy in kept_copies(name):
            copy.wait()

    e.wait_kept = wait_kept
    e.weights = Weights(e.p, e.s, e.arena, sems[2])
    start_kept("branch")
    e.weights.start("shrink", 0)
    start_kept("slope")
    for d in range(1, 4):
        e.weights.start("shrink", d)
    for name in ("act", "middle", "attended", "heads", "normed"):
        start_kept(name)

    def compute_s(b, core, target):
        d, s = b[0] * 2 + core, b[1] * 2 + b[2]
        at = pl.ds(pl.multiple_of(s * 144, 16), 144)
        act = e.arena[pl.ds(pl.multiple_of(ACT_ROW + d * TOKENS, 16), TOKENS), :]
        target[...] = dot(e.bb_t[at, :], act).astype(jnp.bfloat16)

    def compute_p(b, core, target):
        d, s = b[0] * 2 + core, b[1] * 2 + b[2]

        @pl.loop(0, 2)
        def _(i):
            at = pl.ds(pl.multiple_of(d * 288 + i * 144, 16), 144)
            to = pl.ds(pl.multiple_of(i * 144, 16), 144)
            first = dot(e.normed_t[at, :], e.bin[s])
            second = dot(e.mixture_t[at, :], e.bout[s])
            third = dot(e.normed2_t[at, :], e.bexp[s])
            target[to, 0:384] = first[:, 0:384].astype(jnp.bfloat16)
            target[to, 384:512] = (first[:, 384:] + second[:, :128]).astype(jnp.bfloat16)
            target[to, 512:640] = (second[:, 128:] + third[:, :128]).astype(jnp.bfloat16)
            target[to, 640:] = third[:, 128:].astype(jnp.bfloat16)

    across = Scatter(
        me, S_CHUNKS, compute_s, e.own_s, e.arena_s, 0, S_RING, e.s_out, *sems[3:7]
    )
    slabs = Scatter(me, P_CHUNKS, compute_p, e.own_p, e.arena, 0, P_RING, e.p_out, *sems[7:11])
    over_frames = Spread(me, "sp", e.small, e.small_in, *sems[11:13], True)
    over_data = Spread(me, "dp", e.row_sum, e.row_in, *sems[13:15], False)
    over_all = Spread(me, "sp", e.total, e.totals, *sems[15:17], False)
    greet(me)

    def turn(name, target, following):
        def step():
            wait_kept(name)
            target[...] = e.back_x[...].T
            if following:
                start_kept(following)

        return step

    if temporal:
        forth = Exchange(me, e.y_t, e.output, *sems[17:20])
        back = Exchange(me, e.back_x, e.back_spatial, *sems[20:23])
        forth.start()
        fill_mask(e)
    else:
        back = pltpu.make_async_copy(e.back_x, e.input_gradient, sems[17])

    stages = backward_stages(e)
    stages[0]()
    wait_kept("act")
    rest = stages[1:]
    rest[2:2] = [turn("normed", e.normed_t, "mixture")]
    rest[5:5] = [turn("mixture", e.mixture_t, "normed2")]
    rest[8:8] = [turn("normed2", e.normed2_t, None)]
    interleave(across.events(), spread_out(rest, 0.05, 1.0))

    for direction in "xycud":

        def signal():
            pl.semaphore_signal(
                ready, inc=1, device_id=me.neighbour(direction), device_id_type=MESH
            )

        guarded(me.has(direction), signal)

    def begin():
        back.start()
        e.small[...] = jnp.zeros(e.small.shape, jnp.float32)
        for s in range(8):
            e.small[s, 0:1, :] = e.bias_grad[s : s + 1, :]
            for row, column, n, at in pieces(864 * s, 864):
                e.small[s, 1:2, at : at + n] = e.mod_grad[row : row + 1, column : column + n]
        over_frames.start()

    begin()
    pl.semaphore_wait(ready, 3 + jnp.where((me.z > 0) & (me.z < 3), 2, 1))

    def second():
        over_frames.finish()
        e.row_sum[...] = jnp.sum(e.small_in[...], axis=0)
        over_data.start()

    def third():
        over_data.finish()
        e.total[...] = jnp.sum(e.row_in[...], axis=0)
        over_all.start()
        for t in range(9):
            r = slice(32 * t, 32 * (t + 1))
            v = e.cond[r, 0:1] * e.row_in[0, 1:2, 0:864]
            for q in range(1, 4):
                v = v + e.cond[r, q : q + 1] * e.row_in[q, 1:2, 0:864]
            e.weight_grad[r, :] = v

    def fourth():
        over_all.finish()
        if temporal:
            forth.finish()
            back.finish()
        else:
            back.wait()

    interleave(slabs.events(), [(0.3, second), (0.55, third), (0.8, fourth)])
    across.finish()
    slabs.finish()


def backward_call(block, x, mods, cond, segments, p, s, g, kept, y_t=None):
    inputs = [("x", x), ("mods", mods), ("cond", cond), ("g", g), ("p", p), ("s", s)]
    inputs += [(name + "_kept", value) for name, value in zip(KEPT, kept)]
    outs = [
        ("p_out", (288, WIDTH), jnp.float32),
        ("s_out", (144, WIDTH), jnp.float32),
        ("weight_grad", (288, 864), jnp.float32),
        ("totals", (8, 8, WIDTH), jnp.float32),
    ]
    scratch = BACKWARD_SCRATCH
    if block == 1:
        inputs += [("segments", segments), ("y_t", y_t)]
        streams = ["output", "back_spatial"]
        scratch = scratch + MASK
        last = [(8,), (8,), ()] * 2
    else:
        streams = ["input_gradient"]
        last = [()]
    outs += [(name, (TOKENS, WIDTH), jnp.bfloat16) for name in streams]
    names = [name for name, *_ in tuple(inputs) + tuple(outs) + scratch]
    smem = pl.BlockSpec(memory_space=pltpu.SMEM)

    def spec(name):
        if name == "segments":
            return smem
        hbm = name in ("p", "s", "y_t") or name in streams or name.endswith("_kept")
        return ANY_SPEC if hbm else VMEM_SPEC

    sems = [(len(KEPT),), (8,), (4,)] + Scatter.sems(S_CHUNKS) + Scatter.sems(P_CHUNKS)
    sems += [(8,), (8,), (4,), (4,), (8,), (8,)] + last
    return pl.pallas_call(
        functools.partial(backward_kernel, block, names),
        out_shape=[jax.ShapeDtypeStruct(shape, kind) for _, shape, kind in outs],
        in_specs=[spec(name) for name, _ in inputs],
        out_specs=[spec(name) for name, *_ in outs],
        scratch_shapes=[pltpu.VMEM(shape, kind) for _, shape, kind in scratch]
        + [pltpu.SemaphoreType.REGULAR]
        + dma_sems(*sems),
        compiler_params=pltpu.CompilerParams(
            collective_id=3 - block, has_side_effects=True, vmem_limit_bytes=63 << 20
        ),
        name="temporal_backward" if block == 1 else "spatial_backward",
    )(*[value for _, value in inputs])


def sinusoid(timesteps):
    half_width = D // 2
    frequencies = jnp.exp(
        -math.log(10000.0) * jnp.arange(half_width, dtype=jnp.float32) / half_width
    )
    angles = timesteps.astype(jnp.float32)[:, None] * frequencies[None, :]
    return jnp.concatenate([jnp.cos(angles), jnp.sin(angles)], axis=1)


def layer_norm(tensor):
    centered = tensor - jnp.mean(tensor, axis=-1, keepdims=True)
    return centered * lax.rsqrt(jnp.mean(centered * centered, axis=-1, keepdims=True) + EPSILON)


def modulate(tensor, shift_part, scale_part):
    return layer_norm(tensor) * (1.0 + scale_part) + shift_part


def matmul(left_side, right_side):
    return jnp.dot(left_side, right_side, preferred_element_type=jnp.float32)


def back_matmul(gradient, matrix):
    return lax.dot_general(
        gradient,
        matrix,
        (((gradient.ndim - 1,), (1,)), ((), ())),
        preferred_element_type=jnp.float32,
    )


def outer_product(left_side, right_side):
    flat_left = left_side.reshape(-1, left_side.shape[-1])
    flat_right = right_side.reshape(-1, right_side.shape[-1])
    return lax.dot_general(
        flat_left, flat_right, (((0,), (0,)), ((), ())), preferred_element_type=jnp.float32
    )


def column_totals(tensor):
    return jnp.sum(tensor.astype(jnp.float32).reshape(-1, tensor.shape[-1]), axis=0)


def per_sequence(tensor):
    return jnp.sum(tensor, axis=(1, 2))


def over_data(core, biases):
    attend_in, attend_out, expand, shrink = core
    attend_bias, out_bias, expand_bias, shrink_bias, modulate_bias = biases
    gathered = (
        lax.all_gather(attend_in, "dp", axis=0, tiled=True),
        lax.all_gather(attend_out, "dp", axis=0, tiled=True),
        lax.all_gather(expand, "dp", axis=0, tiled=True),
        lax.all_gather(shrink, "dp", axis=0, tiled=True),
        lax.all_gather(attend_bias, "dp", axis=0, tiled=True),
        lax.all_gather(out_bias, "dp", axis=0, tiled=True),
        lax.all_gather(expand_bias, "dp", axis=0, tiled=True),
        lax.all_gather(shrink_bias, "dp", axis=0, tiled=True),
        lax.all_gather(modulate_bias, "dp", axis=0, tiled=True),
    )
    return (gathered[:4], gathered[4:])


def over_frames(core):
    attend_in, attend_out, expand, shrink = core
    gathered = (
        lax.all_gather(attend_in, "sp", axis=1, tiled=True),
        lax.all_gather(attend_out, "sp", axis=1, tiled=True),
        lax.all_gather(expand, "sp", axis=1, tiled=True),
        lax.all_gather(shrink, "sp", axis=1, tiled=True),
    )
    return gathered


def collect(core, biases):
    core_rows, biases_full = over_data(core, biases)
    core_full = over_frames(core_rows)
    return (core_full, biases_full)


def own_rows(condition_all, rows):
    return lax.dynamic_slice_in_dim(condition_all, lax.axis_index("dp") * rows, rows, 1)


def modulation_of(condition_all, modulate_weights):
    rows = modulate_weights[0].shape[0]
    own = own_rows(condition_all, rows)
    partial_terms = jnp.stack([matmul(own, weight) for weight in modulate_weights], axis=1)
    summed = lax.psum_scatter(partial_terms, "dp", scatter_dimension=0, tiled=True)
    full = lax.all_gather(summed, "sp", axis=2, tiled=True)
    return [full[:, slot] for slot in range(len(modulate_weights))]


def sum_over_frames(terms):
    attend_in, attend_out, expand, shrink = terms
    return (
        lax.psum_scatter(
            attend_in.astype(jnp.bfloat16), "sp", scatter_dimension=1, tiled=True
        ).astype(jnp.float32),
        lax.psum_scatter(
            attend_out.astype(jnp.bfloat16), "sp", scatter_dimension=1, tiled=True
        ).astype(jnp.float32),
        lax.psum_scatter(expand.astype(jnp.bfloat16), "sp", scatter_dimension=1, tiled=True).astype(
            jnp.float32
        ),
        lax.psum_scatter(shrink.astype(jnp.bfloat16), "sp", scatter_dimension=1, tiled=True).astype(
            jnp.float32
        ),
    )


def sum_over_data(terms):
    attend_in, attend_out, expand, shrink = terms
    return (
        lax.psum_scatter(
            attend_in.astype(jnp.bfloat16), "dp", scatter_dimension=0, tiled=True
        ).astype(jnp.float32),
        lax.psum_scatter(
            attend_out.astype(jnp.bfloat16), "dp", scatter_dimension=0, tiled=True
        ).astype(jnp.float32),
        lax.psum_scatter(expand.astype(jnp.bfloat16), "dp", scatter_dimension=0, tiled=True).astype(
            jnp.float32
        ),
        lax.psum_scatter(shrink.astype(jnp.bfloat16), "dp", scatter_dimension=0, tiled=True).astype(
            jnp.float32
        ),
    )


def modulate_gradients(condition_all, back_modulations, rows):
    joined = jnp.stack(back_modulations, axis=1)
    columns = lax.psum_scatter(joined, "sp", scatter_dimension=2, tiled=True)
    every = lax.all_gather(columns, "dp", axis=0, tiled=True)
    own = own_rows(condition_all, rows).astype(jnp.float32)
    return [
        jnp.dot(own.T, every[:, slot], precision=HIGHEST_PRECISION)
        for slot in range(len(back_modulations))
    ]


def finish(core_terms, bias_terms):
    matrix_grads = sum_over_data(sum_over_frames(core_terms))
    attend_bias, out_bias, expand_bias, shrink_bias, modulate_bias = bias_terms
    totals = lax.psum(
        (attend_bias, out_bias, expand_bias, shrink_bias, modulate_bias), ("dp", "sp")
    )
    data_index = lax.axis_index("dp")
    data_count = lax.axis_size("dp")
    bias_grads = tuple(
        (
            lax.dynamic_slice_in_dim(
                total_bias,
                data_index * (total_bias.shape[0] // data_count),
                total_bias.shape[0] // data_count,
            )
            for total_bias in totals
        )
    )
    return (matrix_grads, bias_grads)


def frames_to_patches(tensor):
    return lax.all_to_all(tensor, "sp", split_axis=2, concat_axis=1, tiled=True)


def patches_to_frames(tensor):
    return lax.all_to_all(tensor, "sp", split_axis=1, concat_axis=2, tiled=True)


def attention_scores(queries, key_rows, forms, allowed):
    scores = jnp.einsum(forms[0], queries, key_rows, preferred_element_type=jnp.float32) * HD ** (
        -0.5
    )
    if allowed is not None:
        scores = jnp.where(allowed, scores, -1e30)
    return scores


def block_forward(stream, modulation, core, biases, forms, allowed):
    attend_in, attend_out, expand, shrink = core
    attend_bias, out_bias, expand_bias, shrink_bias, modulate_bias = biases
    model_width = stream.shape[-1]
    pieces = [
        modulation[:, None, None, slot * model_width : (slot + 1) * model_width]
        for slot in range(6)
    ]
    normed = modulate(stream, pieces[0], pieces[1]).astype(jnp.bfloat16)
    bias_float = attend_bias.astype(jnp.float32)
    joined_bias = jnp.concatenate(
        [bias_float[:model_width], jnp.zeros((model_width,), jnp.float32), bias_float[model_width:]]
    )
    projected = (matmul(normed, attend_in) + joined_bias).astype(jnp.bfloat16)
    head_shape = projected.shape[:3] + (H, HD)
    queries = projected[..., :model_width].reshape(head_shape)
    key_rows = projected[..., model_width : 2 * model_width].reshape(head_shape)
    values = projected[..., 2 * model_width :].reshape(head_shape)
    scores = attention_scores(queries, key_rows, forms, allowed)
    highest = jnp.max(scores, axis=-1, keepdims=True)
    exponent = jnp.exp(scores - highest)
    denominator = jnp.sum(exponent, axis=-1, keepdims=True)
    softmax_probs = exponent / denominator
    logsum = highest + jnp.log(denominator)
    mixture = (
        jnp.einsum(
            forms[1], softmax_probs.astype(jnp.bfloat16), values, preferred_element_type=jnp.float32
        )
        .astype(jnp.bfloat16)
        .reshape(stream.shape)
    )
    attended = matmul(mixture, attend_out) + out_bias.astype(jnp.float32)
    middle = stream + pieces[2] * attended
    normed_second = modulate(middle, pieces[3], pieces[4]).astype(jnp.bfloat16)
    hidden = matmul(normed_second, expand) + expand_bias.astype(jnp.float32)
    activated = jax.nn.gelu(hidden, approximate=True).astype(jnp.bfloat16)
    branch = matmul(activated, shrink) + shrink_bias.astype(jnp.float32)
    result = middle + pieces[5] * branch
    kept = (
        pieces,
        normed,
        queries,
        key_rows,
        values,
        logsum,
        mixture,
        attended,
        middle,
        normed_second,
        hidden,
        activated,
        branch,
    )
    return (result, kept)


def block_backward(incoming, stream, core, forms, allowed, kept):
    attend_in, attend_out, expand, shrink = core
    (
        pieces,
        normed,
        queries,
        key_rows,
        values,
        logsum,
        mixture,
        attended,
        middle,
        normed_second,
        hidden,
        activated,
        branch,
    ) = kept
    model_width = stream.shape[-1]
    sequences = stream.shape[0]
    back_branch = (pieces[5] * incoming).astype(jnp.bfloat16)
    back_gate_second = per_sequence(incoming * branch)
    shrink_term = outer_product(activated, back_branch)
    shrink_bias_term = column_totals(back_branch)
    back_activated = back_matmul(back_branch, shrink)
    _, gelu_pull = jax.vjp(lambda tensor: jax.nn.gelu(tensor, approximate=True), hidden)
    back_hidden = gelu_pull(back_activated)[0].astype(jnp.bfloat16)
    expand_term = outer_product(normed_second, back_hidden)
    expand_bias_term = column_totals(back_hidden)
    back_normed_second = back_matmul(back_hidden, expand)
    _, second_pull = jax.vjp(modulate, middle, pieces[3], pieces[4])
    back_middle, back_shift_second, back_scale_second = second_pull(back_normed_second)
    back_middle = back_middle + incoming
    back_attended = (pieces[2] * back_middle).astype(jnp.bfloat16)
    back_gate_first = per_sequence(back_middle * attended)
    out_term = outer_product(mixture, back_attended)
    out_bias_term = column_totals(back_attended)
    back_mixture = (
        back_matmul(back_attended, attend_out).astype(jnp.bfloat16).reshape(queries.shape)
    )
    scores = attention_scores(queries, key_rows, forms, allowed)
    softmax_probs = jnp.exp(scores - logsum)
    back_probs = jnp.einsum(forms[0], back_mixture, values, preferred_element_type=jnp.float32)
    back_values = jnp.einsum(
        forms[2],
        softmax_probs.astype(jnp.bfloat16),
        back_mixture,
        preferred_element_type=jnp.float32,
    )
    row_delta = jnp.sum(softmax_probs * back_probs, axis=-1, keepdims=True)
    back_scores = (softmax_probs * (back_probs - row_delta)).astype(jnp.bfloat16)
    score_scale = HD ** (-0.5)
    back_queries = (
        jnp.einsum(forms[1], back_scores, key_rows, preferred_element_type=jnp.float32)
        * score_scale
    )
    back_keys = (
        jnp.einsum(forms[2], back_scores, queries, preferred_element_type=jnp.float32) * score_scale
    )
    flat_shape = stream.shape
    back_projected = jnp.concatenate(
        [
            back_queries.reshape(flat_shape),
            back_keys.reshape(flat_shape),
            back_values.reshape(flat_shape),
        ],
        axis=-1,
    ).astype(jnp.bfloat16)
    attend_in_term = outer_product(normed, back_projected)
    projected_totals = column_totals(back_projected)
    attend_bias_term = jnp.concatenate(
        [projected_totals[:model_width], projected_totals[2 * model_width :]]
    )
    back_normed = back_matmul(back_projected, attend_in)
    _, first_pull = jax.vjp(modulate, stream, pieces[0], pieces[1])
    back_stream, back_shift_first, back_scale_first = first_pull(back_normed)
    back_stream = back_stream + back_middle
    back_modulation = jnp.concatenate(
        [
            back_shift_first.reshape(sequences, model_width),
            back_scale_first.reshape(sequences, model_width),
            back_gate_first,
            back_shift_second.reshape(sequences, model_width),
            back_scale_second.reshape(sequences, model_width),
            back_gate_second,
        ],
        axis=1,
    )
    modulate_bias_term = jnp.sum(back_modulation, axis=0)
    core_terms = (attend_in_term, out_term, expand_term, shrink_term)
    bias_terms = (
        attend_bias_term,
        out_bias_term,
        expand_bias_term,
        shrink_bias_term,
        modulate_bias_term,
    )
    return (back_stream, core_terms, back_modulation, bias_terms)


def shards(
    inputs,
    timesteps,
    segment_ids,
    spatial_attend_in,
    spatial_attend_bias,
    spatial_attend_out,
    spatial_out_bias,
    spatial_expand,
    spatial_expand_bias,
    spatial_shrink,
    spatial_shrink_bias,
    spatial_modulate,
    spatial_modulate_bias,
    temporal_attend_in,
    temporal_attend_bias,
    temporal_attend_out,
    temporal_out_bias,
    temporal_expand,
    temporal_expand_bias,
    temporal_shrink,
    temporal_shrink_bias,
    temporal_modulate,
    temporal_modulate_bias,
    cotangent,
):
    condition_all = jax.nn.silu(sinusoid(timesteps)).astype(jnp.bfloat16)
    allowed = (segment_ids[:, :, None] == segment_ids[:, None, :])[:, None, None, :, :]
    spatial_core = (spatial_attend_in, spatial_attend_out, spatial_expand, spatial_shrink)
    spatial_biases = (
        spatial_attend_bias,
        spatial_out_bias,
        spatial_expand_bias,
        spatial_shrink_bias,
        spatial_modulate_bias,
    )
    temporal_core = (temporal_attend_in, temporal_attend_out, temporal_expand, temporal_shrink)
    temporal_biases = (
        temporal_attend_bias,
        temporal_out_bias,
        temporal_expand_bias,
        temporal_shrink_bias,
        temporal_modulate_bias,
    )
    stream = inputs.astype(jnp.float32)
    modulations = modulation_of(condition_all, (spatial_modulate, temporal_modulate))
    core, biases = collect(spatial_core, spatial_biases)
    modulation = modulations[0] + biases[4].astype(jnp.float32)
    spatial_core = core
    spatial_out, spatial_kept = block_forward(stream, modulation, core, biases, SPATIAL_FORMS, None)
    passed = frames_to_patches(spatial_out.astype(jnp.bfloat16)).astype(jnp.float32)
    core, biases = collect(temporal_core, temporal_biases)
    modulation = modulations[1] + biases[4].astype(jnp.float32)
    temporal_out, temporal_kept = block_forward(
        passed, modulation, core, biases, TEMPORAL_FORMS, allowed
    )
    output = patches_to_frames(temporal_out.astype(jnp.bfloat16))
    incoming = frames_to_patches(cotangent).astype(jnp.float32)
    back_passed, core_terms, back_temporal, bias_terms = block_backward(
        incoming, passed, core, TEMPORAL_FORMS, allowed, temporal_kept
    )
    temporal_grads, temporal_bias_grads = finish(core_terms, bias_terms)
    back_spatial = patches_to_frames(back_passed.astype(jnp.bfloat16)).astype(jnp.float32)
    back_inputs, core_terms, back_spatial_modulation, bias_terms = block_backward(
        back_spatial, stream, spatial_core, SPATIAL_FORMS, None, spatial_kept
    )
    spatial_grads, spatial_bias_grads = finish(core_terms, bias_terms)
    modulate_grads = modulate_gradients(
        condition_all, (back_spatial_modulation, back_temporal), spatial_modulate.shape[0]
    )
    return (
        output,
        back_inputs.astype(jnp.bfloat16),
        spatial_grads[0],
        spatial_bias_grads[0],
        spatial_grads[1],
        spatial_bias_grads[1],
        spatial_grads[2],
        spatial_bias_grads[2],
        spatial_grads[3],
        spatial_bias_grads[3],
        modulate_grads[0],
        spatial_bias_grads[4],
        temporal_grads[0],
        temporal_bias_grads[0],
        temporal_grads[1],
        temporal_bias_grads[1],
        temporal_grads[2],
        temporal_bias_grads[2],
        temporal_grads[3],
        temporal_bias_grads[3],
        modulate_grads[1],
        temporal_bias_grads[4],
    )


def fits(mesh):
    return mesh.shape["dp"] == 4 and mesh.shape["sp"] == 8


def condition_rows(timesteps, rows):
    half = D // 2
    index = lax.axis_index("dp") * rows + jnp.arange(rows, dtype=jnp.int32)
    place = (index % half).astype(jnp.float32)
    frequencies = jnp.exp(-math.log(10000.0) * place / half)
    angles = timesteps.astype(jnp.float32)[:, None] * frequencies[None, :]
    wave = jnp.where((index < half)[None, :], jnp.cos(angles), jnp.sin(angles))
    return jax.nn.silu(wave).astype(jnp.bfloat16)


def fast_shards(
    inputs,
    timesteps,
    segment_ids,
    spatial_attend_in,
    spatial_attend_bias,
    spatial_attend_out,
    spatial_out_bias,
    spatial_expand,
    spatial_expand_bias,
    spatial_shrink,
    spatial_shrink_bias,
    spatial_modulate,
    spatial_modulate_bias,
    temporal_attend_in,
    temporal_attend_bias,
    temporal_attend_out,
    temporal_out_bias,
    temporal_expand,
    temporal_expand_bias,
    temporal_shrink,
    temporal_shrink_bias,
    temporal_modulate,
    temporal_modulate_bias,
    cotangent,
):
    def small(attend, out, expand, shrink, modulate):
        rows = [attend, out, shrink, expand, modulate[:D], modulate[D:]]
        return [jnp.pad(row.astype(jnp.float32)[None], ((0, 0), (0, D - row.shape[0]))) for row in rows]

    pack = jnp.concatenate(
        small(
            spatial_attend_bias,
            spatial_out_bias,
            spatial_expand_bias,
            spatial_shrink_bias,
            spatial_modulate_bias,
        )
        + small(
            temporal_attend_bias,
            temporal_out_bias,
            temporal_expand_bias,
            temporal_shrink_bias,
            temporal_modulate_bias,
        )
        + [jnp.zeros((4, D), jnp.float32)]
    )
    cond = jnp.pad(condition_rows(timesteps, spatial_modulate.shape[0]), ((0, 4), (0, 0)))
    cond_columns = cond.astype(jnp.float32).T
    x = inputs.reshape(TOKENS, WIDTH)
    spatial_p, spatial_s, mods, biases, incoming = first_gather(
        jnp.concatenate([spatial_attend_in, spatial_attend_out, spatial_expand], axis=1),
        spatial_shrink.T,
        pack,
        cond,
        (spatial_modulate, temporal_modulate),
        cotangent.reshape(TOKENS, WIDTH),
    )
    (temporal_p, temporal_s, passed, y_t), kept_s, kept_t = second_gather(
        jnp.concatenate([temporal_attend_in, temporal_attend_out, temporal_expand], axis=1),
        temporal_shrink.T,
        x,
        mods,
        biases,
        segment_ids,
        spatial_p,
        spatial_s,
    )
    packed_t, turned_t, modulate_t, totals_t, output, back_spatial = backward_call(
        1, passed, mods, cond_columns, segment_ids, temporal_p, temporal_s, incoming, kept_t, y_t
    )
    packed_s, turned_s, modulate_s, totals_s, input_gradient = backward_call(
        0, x, mods, cond_columns, segment_ids, spatial_p, spatial_s, back_spatial, kept_s
    )
    outs, (output, input_gradient, modulate_s, modulate_t) = unpack(
        (packed_s, turned_s, totals_s, packed_t, turned_t, totals_t),
        (output, input_gradient, modulate_s, modulate_t),
    )
    return (
        output.reshape(inputs.shape),
        input_gradient.reshape(inputs.shape),
        *outs[:8],
        modulate_s,
        outs[8],
        *outs[9:17],
        modulate_t,
        outs[17],
    )


def solution(mesh):
    placed = (
        P("dp", "sp", None, None),
        P(),
        P("dp", None),
        P("dp", "sp"),
        P("dp"),
        P("dp", "sp"),
        P("dp"),
        P("dp", "sp"),
        P("dp"),
        P("dp", "sp"),
        P("dp"),
        P("dp", "sp"),
        P("dp"),
        P("dp", "sp"),
        P("dp"),
        P("dp", "sp"),
        P("dp"),
        P("dp", "sp"),
        P("dp"),
        P("dp", "sp"),
        P("dp"),
        P("dp", "sp"),
        P("dp"),
        P("dp", "sp", None, None),
    )
    return jax.shard_map(
        fast_shards if fits(mesh) else shards,
        mesh=mesh,
        in_specs=placed,
        out_specs=(
            P("dp", "sp", None, None),
            P("dp", "sp", None, None),
            P("dp", "sp"),
            P("dp"),
            P("dp", "sp"),
            P("dp"),
            P("dp", "sp"),
            P("dp"),
            P("dp", "sp"),
            P("dp"),
            P("dp", "sp"),
            P("dp"),
            P("dp", "sp"),
            P("dp"),
            P("dp", "sp"),
            P("dp"),
            P("dp", "sp"),
            P("dp"),
            P("dp", "sp"),
            P("dp"),
            P("dp", "sp"),
            P("dp"),
        ),
        check_vma=False,
    )
```

```python
import functools
import math

import jax
import jax.numpy as jnp
from jax import lax
from jax.experimental import pallas as pl
from jax.experimental.pallas import tpu as pltpu
from jax.sharding import PartitionSpec as P

D = 1152
H = 16
HD = 72


EPSILON = 1e-06
HIGHEST_PRECISION = lax.Precision.HIGHEST
SPATIAL_FORMS = ("sabhe,sache->sahbc", "sahbc,sache->sabhe", "sahbc,sabhe->sache")
TEMPORAL_FORMS = ("sabhe,scbhe->sbhac", "sbhac,scbhe->sabhe", "sbhac,sabhe->scbhe")


MESH = pl.DeviceIdType.MESH
TOKENS = 256
WIDTH = 1152
CHUNKS_ONE = (
    ("p", 0, 144, "zxy"),
    ("p", 144, 144, "zyx"),
    ("s", 0, 80, "yxz"),
    ("s", 80, 32, "zxy"),
    ("s", 112, 32, "zyx"),
)
S_CHUNKS = (("s", 0, 48, "zxy"), ("s", 48, 64, "zyx"), ("s", 112, 32, "yxz"))
P_CHUNKS = (
    ("p", 0, 112, "zxy"),
    ("p", 112, 112, "zyx"),
    ("p", 224, 32, "xyz"),
    ("p", 256, 32, "yxz"),
)
RELS = sorted(
    [(rx, ry, dz) for rx in (0, 1) for ry in (0, 1) for dz in range(-3, 4)],
    key=lambda r: (r[0] + r[1] + abs(r[2]), r != (0, 0, 0)),
)


class Place:
    def __init__(self):
        self.d, self.s = lax.axis_index("dp"), lax.axis_index("sp")
        self.x, self.c = self.d // 2, self.d % 2
        self.z, self.y = self.s // 2, self.s % 2

    def at(self, rel):
        rx, ry, dz = rel
        return (1 - self.x if rx else self.x, self.z + dz, 1 - self.y if ry else self.y)

    def exists(self, dz):
        return None if dz == 0 else ((self.z + dz >= 0) & (self.z + dz <= 3))

    def neighbour(self, direction):
        x, c, z, y = self.x, self.c, self.z, self.y
        return {
            "x": lambda: dev(1 - x, c, z, y),
            "y": lambda: dev(x, c, z, 1 - y),
            "u": lambda: dev(x, c, z + 1, y),
            "d": lambda: dev(x, c, z - 1, y),
            "c": lambda: dev(x, 1 - c, z, y),
        }[direction]()

    def has(self, direction):
        return {"u": lambda: self.z < 3, "d": lambda: self.z > 0}.get(direction, lambda: None)()


def dev(x, c, z, y):
    return (x * 2 + c, z * 2 + y)


def blk(b):
    return (b[0] * 4 + b[1]) * 2 + b[2]


def both(a, b):
    return b if a is None else (a if b is None else (a & b))


def guarded(cond, f):
    if cond is None:
        f()
    else:
        pl.when(cond)(f)


def greet(me):
    barrier = pltpu.get_barrier_semaphore()
    for k in range(1, 4):
        pl.semaphore_signal(
            barrier, inc=1, device_id=((me.d + k) % 4, me.s), device_id_type=MESH
        )
    for k in range(1, 8):
        pl.semaphore_signal(
            barrier, inc=1, device_id=(me.d, (me.s + k) % 8), device_id_type=MESH
        )
    pl.semaphore_wait(barrier, 10)


def links(rel, order):
    nz = {"x": rel[0], "y": rel[1], "z": rel[2]}
    last = max([i for i in range(3) if nz[order[i]]], default=-1)
    out = []
    for i, dim in enumerate(order):
        if i > last:
            out += ["u", "d"] if dim == "z" else [dim]
        elif i == last and dim == "z":
            out += ["u"] if rel[2] < 0 else ["d"]
    parent = None
    if last >= 0:
        parent = order[last] if order[last] != "z" else ("d" if rel[2] < 0 else "u")
    return out, parent


class Gather:
    SEMS = ((7, 16), (7, 16), (7, 5, 16), (7,))

    def __init__(self, me, chunks, p_in, s_in, p_out, s_out, arrived, crossed, sent, local):
        self.chunks = chunks
        self.me, self.ins, self.outs = me, {"p": p_in, "s": s_in}, {"p": p_out, "s": s_out}
        self.arrived, self.crossed, self.sent, self.local = arrived, crossed, sent, local

    def own(self, ch):
        return self.ins[ch[0]].at[pl.ds(ch[1], ch[2]), :]

    def place(self, ch, b, core):
        d, s = b[0] * 2 + core, b[1] * 2 + b[2]
        if ch[0] == "p":
            return self.outs["p"].at[s, pl.ds(d * 288 + ch[1], ch[2]), :]
        return self.outs["s"].at[d, pl.ds(s * 144 + ch[1], ch[2]), :]

    def copy(self, k, rel, direction):
        me, ch = self.me, self.chunks[k]
        b = me.at(rel)
        there = self.place(ch, b, me.c)
        return pltpu.make_async_remote_copy(
            src_ref=self.own(ch) if rel == (0, 0, 0) else there,
            dst_ref=there,
            send_sem=self.sent.at[k, "xyudc".index(direction), blk(b)],
            recv_sem=(self.crossed if direction == "c" else self.arrived).at[k, blk(b)],
            device_id=me.neighbour(direction),
            device_id_type=MESH,
        )

    def ends(self, k, rel):
        return links(rel, self.chunks[k][3])[0] + ["c"]

    def event(self, k, rel):
        me, ch = self.me, self.chunks[k]

        def body():
            if rel == (0, 0, 0):
                pltpu.make_async_copy(
                    self.own(ch), self.place(ch, me.at(rel), me.c), self.local.at[k]
                ).start()
            else:
                self.wait_in(k, rel, me.c, self.arrived)
            for direction in self.ends(k, rel):
                guarded(me.has(direction), lambda: self.copy(k, rel, direction).start())

        guarded(me.exists(rel[2]), body)

    def wait_in(self, k, rel, core, sems):
        b, ch = self.me.at(rel), self.chunks[k]
        pltpu.make_async_copy(self.own(ch), self.place(ch, b, core), sems.at[k, blk(b)]).wait()

    def events(self):
        return [
            functools.partial(self.event, k, rel) for rel in RELS for k in range(len(self.chunks))
        ]

    def level(self, hops, which):
        return [
            functools.partial(self.event, k, rel)
            for rel in RELS
            if rel[0] + rel[1] + abs(rel[2]) == hops
            for k, ch in enumerate(self.chunks)
            if ch[0] == which
        ]

    def complete(self, which):
        me, ks = self.me, [k for k, ch in enumerate(self.chunks) if ch[0] in which]
        for k in ks:
            ch = self.chunks[k]
            pltpu.make_async_copy(
                self.own(ch), self.place(ch, me.at((0, 0, 0)), me.c), self.local.at[k]
            ).wait()
        for rel in RELS:

            def body():
                for k in ks:
                    self.wait_in(k, rel, 1 - me.c, self.crossed)

            guarded(me.exists(rel[2]), body)

    def sent_all(self):
        me = self.me
        for rel in RELS:

            def body():
                for k in range(len(self.chunks)):
                    for direction in self.ends(k, rel):
                        guarded(
                            me.has(direction), lambda: self.copy(k, rel, direction).wait_send()
                        )

            guarded(me.exists(rel[2]), body)

    def finish(self):
        self.complete("ps")
        self.sent_all()


def slots_of(order):
    base, total, count = {}, 0, 1
    for dim in order:
        base[dim] = total
        total += count * (5 if dim == "z" else 1)
        count *= 4 if dim == "z" else 2
    return base, total


class Scatter:
    def __init__(self, me, chunks, compute, own, buffer, base, ring, out, *sems):
        self.me, self.chunks, self.compute, self.own = me, chunks, compute, own
        self.buffer, self.base, self.ring, self.out = buffer, base, ring, out
        self.crossed, self.cross_sent, self.arrived, self.sent = sems
        self.rels = RELS[::-1]
        self.block = sum(ch[2] for ch in chunks)
        self.slot_row, total = [], base + 16 * self.block
        for ch in chunks:
            self.slot_row.append(total)
            total += slots_of(ch[3])[1] * ch[2]
        self.ring_row = total

    @staticmethod
    def rows(chunks, ring):
        block = sum(ch[2] for ch in chunks)
        return (16 + ring) * block + sum(slots_of(ch[3])[1] * ch[2] for ch in chunks)

    @staticmethod
    def sems(chunks):
        n, most = len(chunks), max(slots_of(ch[3])[1] for ch in chunks)
        return [(16,), (16,), (n, most), (n, 16)]

    def at_row(self, row, n):
        return self.buffer.at[pl.ds(row, n), :]

    def core(self, b, first=0, n=None):
        row = self.base + blk(b) * self.block + first
        return self.at_row(pl.multiple_of(row, 16), self.block if n is None else n)

    def ring_at(self, i):
        return self.at_row(self.ring_row + (i % self.ring) * self.block, self.block)

    def cross_copy(self, i):
        b = self.me.at(self.rels[i])
        return pltpu.make_async_remote_copy(
            src_ref=self.ring_at(i),
            dst_ref=self.core(b),
            send_sem=self.cross_sent.at[blk(b)],
            recv_sem=self.crossed.at[blk(b)],
            device_id=self.me.neighbour("c"),
            device_id_type=MESH,
        )

    def slot(self, k, b, direction, z):
        order = self.chunks[k][3]
        base, _ = slots_of(order)
        dim = "z" if direction in "ud" else direction
        coord = {"x": (b[0], 2), "y": (b[2], 2), "z": (b[1], 4)}
        index = 0
        for d in order[: order.index(dim)]:
            index = index * coord[d][1] + coord[d][0]
        if dim == "z":
            inner = b[1] if direction == "d" else jnp.where(b[1] == z, 4, b[1])
            index = index * 5 + inner
        return base[dim] + index

    def got(self, k, j):
        n = self.chunks[k][2]
        return self.at_row(pl.multiple_of(self.slot_row[k] + j * n, 16), n)

    def send(self, k, i):
        rel, ch = self.rels[i], self.chunks[k]
        b, direction = self.me.at(rel), links(rel, ch[3])[1]
        z = self.me.z + {"u": 1, "d": -1}.get(direction, 0)
        j = self.slot(k, b, {"x": "x", "y": "y", "u": "d", "d": "u"}[direction], z)
        return pltpu.make_async_remote_copy(
            src_ref=self.core(b, ch[1], ch[2]),
            dst_ref=self.got(k, j),
            send_sem=self.sent.at[k, blk(b)],
            recv_sem=self.arrived.at[k, j],
            device_id=self.me.neighbour(direction),
            device_id_type=MESH,
        )

    def add(self, k, b, messages, final):
        ch = self.chunks[k]
        step = 16
        core_row = self.base + blk(b) * self.block + ch[1]

        @pl.loop(0, ch[2] // step)
        def _(t):
            r = pl.ds(pl.multiple_of(ch[1] + t * step, 16), step)
            held = pl.ds(pl.multiple_of(core_row + t * step, 16), step)
            v = self.own[r, :].astype(jnp.float32) + self.buffer[held, :].astype(jnp.float32)
            for cond, j in messages:
                at = pl.ds(pl.multiple_of(self.slot_row[k] + j * ch[2] + t * step, 16), step)
                q = self.buffer[at, :].astype(jnp.float32)
                v = v + (q if cond is None else jnp.where(cond, q, 0.0))
            if final:
                self.out[r, :] = v
            else:
                self.buffer[held, :] = v.astype(jnp.bfloat16)

    def guarded(self, i, body):
        guarded(self.me.exists(self.rels[i][2]), body)

    def free_cross(self, i):
        self.guarded(i, lambda: self.cross_copy(i).wait_send())

    def cross_event(self, i):
        if i >= self.ring:
            self.free_cross(i - self.ring)

        def body():
            self.compute(self.me.at(self.rels[i]), 1 - self.me.c, self.ring_at(i))
            self.cross_copy(i).start()

        self.guarded(i, body)

    def own_event(self, i):
        me, rel = self.me, self.rels[i]

        def body():
            b = me.at(rel)
            self.compute(b, me.c, self.own)
            held = self.core(b)
            pltpu.make_async_copy(held, held, self.crossed.at[blk(b)]).wait()
            for k, ch in enumerate(self.chunks):
                children, parent = links(rel, ch[3])
                messages = []
                for direction in children:
                    cond, j = me.has(direction), self.slot(k, b, direction, me.z)

                    def wait():
                        at = self.got(k, j)
                        pltpu.make_async_copy(at, at, self.arrived.at[k, j]).wait()

                    guarded(cond, wait)
                    messages.append((cond, j))
                self.add(k, b, messages, not parent)
                if parent:
                    self.send(k, i).start()

        self.guarded(i, body)

    def events(self, lag=2):
        n, out = len(self.rels), []
        for i in range(n + lag):
            if i < n:
                out.append(functools.partial(self.cross_event, i))
            if i >= lag:
                out.append(functools.partial(self.own_event, i - lag))
        return out

    def finish(self):
        n = len(self.rels)
        for i in range(n - self.ring, n):
            self.free_cross(i)
        for i in range(n):

            def body():
                for k, ch in enumerate(self.chunks):
                    if links(self.rels[i], ch[3])[1]:
                        self.send(k, i).wait_send()

            self.guarded(i, body)


class Exchange:
    def __init__(self, me, source, target, sent, arrived, local):
        self.me, self.source, self.target = me, source, target
        self.sent, self.arrived, self.local = sent, arrived, local

    def rows(self, ref, s):
        return ref.at[pl.ds(pl.multiple_of(s * 32, 32), 32), :]

    def copy(self, k):
        me = self.me
        other = (me.s + k) % 8
        return pltpu.make_async_remote_copy(
            src_ref=self.rows(self.source, other),
            dst_ref=self.rows(self.target, me.s),
            send_sem=self.sent.at[k],
            recv_sem=self.arrived.at[k],
            device_id=(me.d, other),
            device_id_type=MESH,
        )

    def stay(self):
        return pltpu.make_async_copy(
            self.rows(self.source, self.me.s), self.rows(self.target, self.me.s), self.local
        )

    def start(self):
        self.stay().start()
        for k in range(1, 8):
            self.copy(k).start()

    def finish(self):
        self.stay().wait()
        for k in range(1, 8):
            at = self.rows(self.target, (self.me.s - k + 8) % 8)
            pltpu.make_async_copy(at, at, self.arrived.at[k]).wait()
            self.copy(k).wait_send()


class Spread:
    def __init__(self, me, axis, source, target, sent, arrived, each):
        self.me, self.axis, self.source, self.target = me, axis, source, target
        self.sent, self.arrived, self.each = sent, arrived, each
        self.n = 4 if axis == "dp" else 8
        self.i = me.d if axis == "dp" else me.s

    def copy(self, k):
        other = (self.i + k) % self.n
        return pltpu.make_async_remote_copy(
            src_ref=self.source.at[other] if self.each else self.source,
            dst_ref=self.target.at[self.i],
            send_sem=self.sent.at[k],
            recv_sem=self.arrived.at[k],
            device_id=(other, self.me.s) if self.axis == "dp" else (self.me.d, other),
            device_id_type=MESH,
        )

    def start(self):
        for k in range(1, self.n):
            self.copy(k).start()
        self.target[self.i] = self.source[self.i] if self.each else self.source[...]

    def finish(self):
        for k in range(1, self.n):
            at = self.target.at[(self.i - k + self.n) % self.n]
            pltpu.make_async_copy(at, at, self.arrived.at[k]).wait()
            self.copy(k).wait_send()


def pieces(start, length, width=WIDTH):
    out, done = [], 0
    while done < length:
        row, column = divmod(start + done, width)
        n = min(width - column, length - done)
        out.append((row, column, n, done))
        done += n
    return out


def spread_out(stages, first, last):
    return [(first + (last - first) * i / len(stages), stage) for i, stage in enumerate(stages)]


def interleave(events, stages):
    cuts = sorted((int(share * len(events)), i) for i, (share, _) in enumerate(stages))
    done = 0
    for cut, i in cuts:
        for event in events[done:cut]:
            event()
        done = max(done, cut)
        stages[i][1]()
    for event in events[done:]:
        event()


def dma_sems(*shapes):
    return [pltpu.SemaphoreType.DMA(shape) for shape in shapes]


ANY_SPEC = pl.BlockSpec(memory_space=pl.ANY)
VMEM_SPEC = pl.BlockSpec(memory_space=pltpu.VMEM)
SLABS = (
    jax.ShapeDtypeStruct((8, WIDTH, WIDTH), jnp.bfloat16),
    jax.ShapeDtypeStruct((4, WIDTH, WIDTH), jnp.bfloat16),
)
STREAM = jax.ShapeDtypeStruct((TOKENS, WIDTH), jnp.bfloat16)


def first_gather_kernel(
    p_in, s_in, pack, cond, weight0, weight1, cot, p_out, s_out, mod_out, bias_out, incoming,
    packs, part, parts, whole, wholes, *sems,
):
    me = Place()
    gather = Gather(me, CHUNKS_ONE, p_in, s_in, p_out, s_out, *sems[:4])
    exchange = Exchange(me, cot, incoming, *sems[4:7])
    biases = Spread(me, "dp", pack, packs, *sems[7:9], False)
    terms = Spread(me, "dp", part, parts, *sems[9:11], True)
    columns = Spread(me, "sp", whole, wholes, *sems[11:13], False)
    greet(me)

    def begin():
        biases.start()
        for i, weight in enumerate((weight0, weight1)):
            product = jnp.dot(cond[...], weight[...], preferred_element_type=jnp.float32)
            for q in range(4):
                part[q, i : i + 1, :] = product[q : q + 1, :]
        terms.start()
        exchange.start()

    def middle():
        terms.finish()
        whole[...] = jnp.sum(parts[...], axis=0)
        columns.start()

    def end():
        columns.finish()
        biases.finish()
        exchange.finish()
        for i in range(2):
            mod_out[i] = jnp.zeros((8, WIDTH), jnp.float32)
            for s in range(8):
                for row, column, n, at in pieces(864 * s, 864):
                    mod_out[i, row : row + 1, column : column + n] = wholes[
                        s, i : i + 1, at : at + n
                    ]
            for k in range(4):
                for first, n_all in ((0, WIDTH), (WIDTH, 576)):
                    source = 6 * i + 4 + first // WIDTH
                    for row, column, n, at in pieces(1728 * k + first, n_all):
                        mod_out[i, row : row + 1, column : column + n] += packs[
                            k, source : source + 1, at : at + n
                        ]
                top = 6 * i
                bias_out[i, k // 2 : k // 2 + 1, 576 * (k % 2) : 576 * (k % 2 + 1)] = packs[
                    k, top : top + 1, 0:576
                ]
                for row in (2, 3):
                    bias_out[i, row : row + 1, 288 * k : 288 * (k + 1)] = packs[
                        k, top + row - 1 : top + row, 0:288
                    ]
                bias_out[i, 4 + k : 5 + k, :] = packs[k, top + 3 : top + 4, :]

    events = gather.events()
    own = len(CHUNKS_ONE)
    interleave(events, [(own / len(events), begin), (0.3, middle), (0.8, end)])
    gather.finish()


def first_gather(p, s, pack, cond, weights, cotangent):
    return pl.pallas_call(
        first_gather_kernel,
        out_shape=SLABS
        + (
            jax.ShapeDtypeStruct((2, 8, WIDTH), jnp.float32),
            jax.ShapeDtypeStruct((2, 8, WIDTH), jnp.float32),
            STREAM,
        ),
        in_specs=[VMEM_SPEC] * 6 + [ANY_SPEC],
        out_specs=(ANY_SPEC, ANY_SPEC, VMEM_SPEC, VMEM_SPEC, ANY_SPEC),
        scratch_shapes=[
            pltpu.VMEM((4, 16, WIDTH), jnp.float32),
            pltpu.VMEM((4, 8, 864), jnp.float32),
            pltpu.VMEM((4, 8, 864), jnp.float32),
            pltpu.VMEM((8, 864), jnp.float32),
            pltpu.VMEM((8, 8, 864), jnp.float32),
        ]
        + dma_sems(*Gather.SEMS, (8,), (8,), (), (4,), (4,), (4,), (4,), (8,), (8,)),
        compiler_params=pltpu.CompilerParams(collective_id=0, has_side_effects=True),
        name="first_gather",
    )(p, s, pack, cond, *weights, cotangent)


UNPACKED = ((288, 432), (576,), (144, 288), (288,), (288, 576), (1152,), (144, 1152), (288,), (1728,))


def unpack_kernel(*refs):
    ins, passing, outs = refs[:6], refs[6:10], refs[10:28]
    passed, scratch, sem = refs[28:32], refs[32:38], refs[44]
    through = refs[38:44]
    d = lax.axis_index("dp")

    def copy(i, source, target):
        c = pltpu.make_async_copy(source, target, sem.at[i])
        c.start()
        return c

    loads = [copy(i, ins[3 * i], scratch[3 * i]) for i in range(2)]
    routes = list(zip(passing, passed)) + [(ins[3 * i + 1], outs[9 * i + 6]) for i in range(2)]
    halfway = [copy(2 + i, source, through[i]) for i, (source, _) in enumerate(routes)]
    waits = []
    for i in range(2):
        totals = ins[3 * i + 2]
        a_in, a_bias, a_out, o_bias, expand, e_bias, _, s_bias, m_bias = outs[9 * i : 9 * i + 9]
        for k in range(4):

            @pl.when(d == k)
            def _():
                half = 576 * (k % 2)
                a_bias[...] = totals[k // 2, 0, half : half + 576]
                o_bias[...] = totals[2, 0, 288 * k : 288 * (k + 1)]
                s_bias[...] = totals[3, 0, 288 * k : 288 * (k + 1)]
                e_bias[...] = totals[4 + k, 0, :]
                m_bias[...] = jnp.concatenate(
                    [totals[2 * k, 1, 0:864], totals[2 * k + 1, 1, 0:864]]
                )

        packed, turned, wide = scratch[3 * i : 3 * i + 3]
        loads[i].wait()
        turned[...] = packed[:, 432:576].T
        wide[...] = packed[:, 576:1152]
        waits.append(copy(8 + i, turned, a_out))
        waits.append(copy(10 + i, wide, expand))
        a_in[...] = packed[:, 0:432]
    for i, (_, target) in enumerate(routes):
        halfway[i].wait()
        waits.append(copy(12 + i, through[i], target))
    for wait in waits:
        wait.wait()


def unpack(grads, passing):
    rows = jax.ShapeDtypeStruct
    hbm = (2, 4, 6)
    outs = pl.pallas_call(
        unpack_kernel,
        out_shape=[rows(shape, jnp.float32) for shape in UNPACKED * 2]
        + [rows(a.shape, a.dtype) for a in passing],
        in_specs=[ANY_SPEC, ANY_SPEC, VMEM_SPEC] * 2 + [ANY_SPEC] * 4,
        out_specs=[ANY_SPEC if i in hbm else VMEM_SPEC for i in range(9)] * 2 + [ANY_SPEC] * 4,
        scratch_shapes=[
            pltpu.VMEM((288, WIDTH), jnp.float32),
            pltpu.VMEM((144, 288), jnp.float32),
            pltpu.VMEM((288, 576), jnp.float32),
        ]
        * 2
        + [pltpu.VMEM(a.shape, a.dtype) for a in passing]
        + [pltpu.VMEM((144, WIDTH), jnp.float32)] * 2
        + dma_sems((18,)),
        compiler_params=pltpu.CompilerParams(vmem_limit_bytes=63 << 20),
        name="unpack",
    )(*grads, *passing)
    outs = list(outs)
    for i in range(2):
        for j in (2, 6):
            outs[9 * i + j] = outs[9 * i + j].T
    return outs[:18], outs[18:]


SCALE = HD ** (-0.5)
NEGATIVE = -1e30


def dot(a, b):
    return lax.dot_general(a, b, (((1,), (0,)), ((), ())), preferred_element_type=jnp.float32)


def dot_nt(a, b):
    return lax.dot_general(a, b, (((1,), (1,)), ((), ())), preferred_element_type=jnp.float32)


def dot_tn(a, b):
    return lax.dot_general(a, b, (((0,), (0,)), ((), ())), preferred_element_type=jnp.float32)


def by_rows(body, step=32):
    @pl.loop(0, TOKENS // step)
    def _(i):
        body(pl.ds(pl.multiple_of(i * step, step), step))


def statistics(v):
    centered = v - jnp.mean(v, axis=1, keepdims=True)
    scale = lax.rsqrt(jnp.mean(centered * centered, axis=1, keepdims=True) + EPSILON)
    return centered * scale, scale


def fold(v):
    return jnp.sum(v.reshape(v.shape[0] // 8, 8, v.shape[1]), axis=0)


def gelu_both(h):
    c, a = math.sqrt(2.0 / math.pi), 0.044715
    square = h * h
    t = jnp.tanh(c * h * (1.0 + a * square))
    half = 0.5 * (1.0 + t)
    return h * half, half + 0.5 * h * (1.0 - t * t) * (c * (1.0 + 3.0 * a * square))


WIN_IN, WIN_OUT, WIN_EXP = slice(0, 512), slice(384, 640), slice(512, 1152)


def forward_stages(e, y, shrink_last=False):
    mod = e.mod
    shift1, scale1, gate1 = [lambda i=i: mod[i : i + 1, :] for i in range(3)]
    shift2, scale2, gate2 = [lambda i=i: mod[i : i + 1, :] for i in range(3, 6)]

    def normalize():
        e.bslab[...] = jnp.zeros(e.bslab.shape, jnp.float32)
        for s in range(8):
            for row, first in ((0, 0), (1, 2 * WIDTH)):
                lo, hi = max(432 * s, first), min(432 * (s + 1), first + WIDTH)
                if lo < hi:
                    e.bslab[s, 0:1, lo - 432 * s : hi - 432 * s] = e.bias[
                        row : row + 1, lo - first : hi - first
                    ]

        def rows(r):
            n, _ = statistics(e.x[r, :].astype(jnp.float32))
            e.normed[r, :] = (n * (1.0 + scale1()) + shift1()).astype(jnp.bfloat16)

        by_rows(rows)

    def project(first):
        @pl.loop(first, first + 4)
        def _(s):
            e.wait_p(s)
            v = dot(e.normed[...], e.pv[s, :, WIN_IN]) + e.bslab[s, 0:1, :]
            for j in range(6):
                e.heads[6 * s + j] = v[:, HD * j : HD * (j + 1)].astype(jnp.bfloat16)

    def attend(first):
        @pl.loop(first, first + 4)
        def _(h):
            probs = attention_probs(e, h)
            e.mh[h] = dot(probs.astype(jnp.bfloat16), e.heads[2 * H + h]).astype(jnp.bfloat16)

    def join():
        for h in range(H):
            e.mixture[:, HD * h : HD * (h + 1)] = e.mh[h]
        for s in range(8):
            v = dot(e.mixture[...], e.pv[s, :, WIN_OUT])
            e.attended[:, 144 * s : 144 * (s + 1)] = v[:, 48:192]

    def middle():
        def rows(r):
            attended = e.attended[r, :] + e.bias[2:3, :]
            e.attended[r, :] = attended
            middle = e.x[r, :].astype(jnp.float32) + gate1() * attended
            e.middle[r, :] = middle
            n, _ = statistics(middle)
            e.normed2[r, :] = (n * (1.0 + scale2()) + shift2()).astype(jnp.bfloat16)

        by_rows(rows)
        e.branch[...] = jnp.zeros(e.branch.shape, jnp.float32)

    def expand(d):
        for half in range(2):
            v = dot(e.normed2[...], e.pv[2 * d + half, :, WIN_EXP])
            e.tmp[:, 576 * half : 576 * (half + 1)] = v[:, 64:640]

        def rows(r):
            value, slope = gelu_both(e.tmp[r, :] + e.bias[4 + d : 5 + d, :])
            e.act[d, r, :] = value.astype(jnp.bfloat16)
            if e.slope is not None:
                e.slope[d, r, :] = slope.astype(jnp.bfloat16)

        by_rows(rows)

    def shrink(d):
        e.wait_s(d)
        e.branch[...] += dot_nt(e.act[d], e.sv[d])

    def mlp(d):
        expand(d)
        shrink(d)

    def close():
        def rows(r):
            branch = e.branch[r, :] + e.bias[3:4, :]
            e.branch[r, :] = branch
            if y is not None:
                y[r, :] = (e.middle[r, :] + gate2() * branch).astype(jnp.bfloat16)

        by_rows(rows)

    part = functools.partial
    return (
        [normalize, part(project, 0), part(project, 4)]
        + [part(attend, h) for h in range(0, H, 4)]
        + [join, middle]
        + (
            [part(expand, d) for d in range(4)] + [part(shrink, d) for d in range(4)]
            if shrink_last
            else [part(mlp, d) for d in range(4)]
        )
        + [close]
    )


def attention_probs(e, h):
    scores = dot_nt(e.heads[h], e.heads[H + h]) * SCALE
    if e.mask is not None:
        scores = scores + e.mask[...]
    exponent = jnp.exp(scores - jnp.max(scores, axis=1, keepdims=True))
    return exponent / jnp.sum(exponent, axis=1, keepdims=True)


def forward_pass(e, y):
    for stage in forward_stages(e, y):
        stage()


def backward_stages(e):
    mod = e.mod
    gate1, scale1 = lambda: mod[2:3, :], lambda: mod[1:2, :]
    gate2, scale2 = lambda: mod[5:6, :], lambda: mod[4:5, :]

    def open_block():
        e.sums[...] = jnp.zeros(e.sums.shape, jnp.float32)
        e.bout[...] = jnp.zeros(e.bout.shape, jnp.bfloat16)
        for s in range(8):
            e.bexp[s, :, 0:128] = jnp.zeros((TOKENS, 128), jnp.bfloat16)
            e.bin[s, :, 384:512] = jnp.zeros((TOKENS, 128), jnp.bfloat16)
        e.wait_kept("branch")

        def rows(r):
            g = e.g[r, :].astype(jnp.float32)
            back = (gate2() * g).astype(jnp.bfloat16)
            e.bb[r, :] = back
            e.sums[5] += fold(g * e.tmp[r, :])
            e.sums[7] += fold(back.astype(jnp.float32))

        by_rows(rows)
        e.bb_t[...] = e.bb[...].T
        e.wait_kept("slope")

    def hidden(d):
        e.weights.wait("shrink", d)
        e.tmp[...] = dot(e.bb[...], e.weights.at(d, WIDTH))
        e.weights.start("expand", d)

        @pl.loop(0, TOKENS // 32)
        def _(i):
            r = pl.ds(pl.multiple_of(i * 32, 32), 32)
            slope = e.slope[pl.ds(pl.multiple_of(d * TOKENS + i * 32, 32), 32), :]
            back = (e.tmp[r, :] * slope.astype(jnp.float32)).astype(jnp.bfloat16)
            for half in range(2):
                e.bexp[2 * d + half, r, 64:640] = back[:, 576 * half : 576 * (half + 1)]
            e.sums[8 + d] += fold(back.astype(jnp.float32))

    def through(name, width, operand, first, following):
        if first == 0:
            e.tmp[...] = jnp.zeros(e.tmp.shape, jnp.float32)

        @pl.loop(0, 4)
        def _(i):
            e.weights.wait(name, first + i)
            e.tmp[...] += dot_nt(operand[first + i], e.weights.at(i, width))
            if first == 0:
                e.weights.start(name, 4 + i)
            elif following is not None:
                e.weights.start(following, i)

    def middle():
        e.wait_kept("middle")
        e.wait_kept("attended")

        def rows(r):
            n, scale = statistics(e.middle[r, :])
            back_normed = e.tmp[r, :]
            e.sums[3] += fold(back_normed)
            e.sums[4] += fold(back_normed * n)
            u = back_normed * (1.0 + scale2())
            inner = jnp.mean(u, axis=1, keepdims=True) + n * jnp.mean(u * n, axis=1, keepdims=True)
            back_middle = e.g[r, :].astype(jnp.float32) + scale * (u - inner)
            e.middle[r, :] = back_middle
            e.sums[2] += fold(back_middle * e.attended[r, :])
            back = (gate1() * back_middle).astype(jnp.bfloat16)
            e.sums[6] += fold(back.astype(jnp.float32))
            for s in range(8):
                e.bout[s, r, 48:192] = back[:, 144 * s : 144 * (s + 1)]

        by_rows(rows)

    def split():
        e.wait_kept("heads")
        for h in range(H):
            e.mh[h] = e.tmp[:, HD * h : HD * (h + 1)].astype(jnp.bfloat16)

    def attend(first):
        @pl.loop(first, first + 4)
        def _(h):
            q, k, v, back = e.heads[h], e.heads[H + h], e.heads[2 * H + h], e.mh[h]
            probs = attention_probs(e, h)
            back_probs = dot_nt(back, v)
            e.heads[2 * H + h] = dot_tn(probs.astype(jnp.bfloat16), back).astype(jnp.bfloat16)
            delta = jnp.sum(probs * back_probs, axis=1, keepdims=True)
            back_scores = (probs * (back_probs - delta)).astype(jnp.bfloat16)
            e.heads[h] = (dot(back_scores, k) * SCALE).astype(jnp.bfloat16)
            e.heads[H + h] = (dot_tn(back_scores, q) * SCALE).astype(jnp.bfloat16)

    def join():
        ones = jnp.ones((8, TOKENS), jnp.bfloat16)

        @pl.loop(0, 8)
        def _(s):
            for j in range(6):
                e.bin[s, :, HD * j : HD * (j + 1)] = e.heads[6 * s + j]
            e.bslab[s] = dot(ones, e.bin[s])

    def close():
        def rows(r):
            n, scale = statistics(e.x[r, :].astype(jnp.float32))
            back_normed = e.tmp[r, :]
            e.sums[0] += fold(back_normed)
            e.sums[1] += fold(back_normed * n)
            u = back_normed * (1.0 + scale1())
            inner = jnp.mean(u, axis=1, keepdims=True) + n * jnp.mean(u * n, axis=1, keepdims=True)
            e.back_x[r, :] = (e.middle[r, :] + scale * (u - inner)).astype(jnp.bfloat16)

        by_rows(rows)

        for s in range(8):
            for row, first_column in ((0, 0), (1, 2 * WIDTH)):
                lo, hi = max(432 * s, first_column), min(432 * (s + 1), first_column + WIDTH)
                if lo < hi:
                    e.bias_grad[row : row + 1, lo - first_column : hi - first_column] = e.bslab[
                        s, 0:1, lo - 432 * s : hi - 432 * s
                    ]
        for row, slot in ((2, 6), (3, 7), (4, 8), (5, 9), (6, 10), (7, 11)):
            e.bias_grad[row : row + 1, :] = jnp.sum(e.sums[slot], axis=0, keepdims=True)
        for slot in range(6):
            e.mod_grad[slot : slot + 1, :] = jnp.sum(e.sums[slot], axis=0, keepdims=True)
        e.mod_grad[6:8, :] = jnp.zeros((2, WIDTH), jnp.float32)

    part = functools.partial
    return (
        [open_block]
        + [part(hidden, d) for d in range(4)]
        + [part(through, "expand", 640, e.bexp, first, "out") for first in (0, 4)]
        + [middle]
        + [part(through, "out", 256, e.bout, first, "in") for first in (0, 4)]
        + [split]
        + [part(attend, h) for h in range(0, H, 4)]
        + [join]
        + [part(through, "in", 512, e.bin, first, None) for first in (0, 4)]
        + [close]
    )


class Weights:
    WINDOWS = {"shrink": slice(0, WIDTH), "expand": WIN_EXP, "out": WIN_OUT, "in": WIN_IN}

    def __init__(self, p, s, buffer, sems):
        self.p, self.s, self.buffer, self.sems = p, s, buffer, sems

    def slot(self, i):
        return pl.ds(pl.multiple_of((i % 4) * WIDTH, WIDTH), WIDTH)

    def copy(self, name, i):
        window = self.WINDOWS[name]
        source = self.s.at[i] if name == "shrink" else self.p.at[i, :, window]
        width = window.stop - window.start
        target = self.buffer.at[self.slot(i), 0:width]
        return pltpu.make_async_copy(source, target, self.sems.at[i % 4])

    def start(self, name, i):
        self.copy(name, i).start()

    def wait(self, name, i):
        self.copy(name, i).wait()

    def at(self, i, width):
        return self.buffer[self.slot(i), 0:width]


class Refs:
    pass


WEIGHT_SCRATCH = (
    ("pv", (8, WIDTH, WIDTH), jnp.bfloat16),
    ("sv", (4, WIDTH, WIDTH), jnp.bfloat16),
)
FORWARD_SCRATCH = (
    ("bslab", (8, 8, 512), jnp.float32),
    ("heads", (3 * H, TOKENS, HD), jnp.bfloat16),
    ("mh", (H, TOKENS, HD), jnp.bfloat16),
    ("attended", (TOKENS, WIDTH), jnp.float32),
    ("middle", (TOKENS, WIDTH), jnp.float32),
    ("branch", (TOKENS, WIDTH), jnp.float32),
    ("tmp", (TOKENS, WIDTH), jnp.float32),
)
OPERANDS = (
    ("normed", (TOKENS, WIDTH), jnp.bfloat16),
    ("mixture", (TOKENS, WIDTH), jnp.bfloat16),
    ("normed2", (TOKENS, WIDTH), jnp.bfloat16),
    ("act", (4, TOKENS, WIDTH), jnp.bfloat16),
)
BACK_OPERANDS = (
    ("bb", (TOKENS, WIDTH), jnp.bfloat16),
    ("bin", (8, TOKENS, 512), jnp.bfloat16),
    ("bout", (8, TOKENS, 256), jnp.bfloat16),
    ("bexp", (8, TOKENS, 640), jnp.bfloat16),
)
SLOPE = (("slope", (4, TOKENS, WIDTH), jnp.bfloat16),)
SUMS = (("sums", (12, 8, WIDTH), jnp.float32),)
def weight_loads(e, p_hbm, s_hbm, psem, ssem):
    def p_copy(s):
        return pltpu.make_async_copy(p_hbm.at[s], e.pv.at[s], psem.at[s])

    def s_copy(d):
        return pltpu.make_async_copy(s_hbm.at[d], e.sv.at[d], ssem.at[d])

    def start_p():
        @pl.loop(0, 8)
        def _(s):
            p_copy(s).start()

    def start_s():
        @pl.loop(0, 4)
        def _(d):
            s_copy(d).start()

    e.wait_p = lambda s: p_copy(s).wait()
    e.wait_s = lambda d: s_copy(d).wait()
    return start_p, start_s


def fill_mask(e):
    frames = e.segments.shape[1]
    each = TOKENS // frames

    def clips(axis):
        frame = lax.broadcasted_iota(jnp.int32, (TOKENS, TOKENS), axis) // each
        clip = jnp.zeros((TOKENS, TOKENS), jnp.int32)
        for f in range(frames):
            clip = jnp.where(frame == f, e.segments[0, f], clip)
        return clip

    def spots(axis):
        return lax.broadcasted_iota(jnp.int32, (TOKENS, TOKENS), axis) % each

    same = (clips(0) == clips(1)) & (spots(0) == spots(1))
    e.mask[...] = jnp.where(same, 0.0, NEGATIVE)


SECOND_SCRATCH = WEIGHT_SCRATCH + FORWARD_SCRATCH + OPERANDS + SLOPE + (
    ("y", (TOKENS, WIDTH), jnp.bfloat16),
    ("mask", (TOKENS, TOKENS), jnp.float32),
    ("xt", (TOKENS, WIDTH), jnp.bfloat16),
)
KEPT = ("branch", "slope", "middle", "attended", "heads", "act", "normed", "mixture", "normed2")
SHAPES = {name: (shape, kind) for name, shape, kind in SECOND_SCRATCH}


def second_gather_kernel(
    p_in, s_in, x, mods, biases, segments, p, s, p_out, s_out, passed, y_t, *refs
):
    n = len(KEPT)
    saved, saved_t, refs = refs[:n], refs[n : 2 * n], refs[2 * n :]
    e = Refs()
    for (name, *_), ref in zip(SECOND_SCRATCH, refs):
        setattr(e, name, ref)
    mask, e.mask, e.x, e.segments = e.mask, None, x, segments
    e.mod, e.bias = mods.at[0], biases.at[0]
    sems = refs[len(SECOND_SCRATCH) :]
    me = Place()
    gather = Gather(me, P_CHUNKS + S_CHUNKS, p_in, s_in, p_out, s_out, *sems[:4])
    exchange = Exchange(me, e.y, passed, *sems[4:7])
    greet(me)
    stages = forward_stages(e, e.y)

    def keeps(targets):
        return [
            pltpu.make_async_copy(getattr(e, name), target, sems[9].at[i])
            for i, (name, target) in enumerate(zip(KEPT, targets))
        ]

    def leave():
        exchange.start()
        for keep in keeps(saved):
            keep.start()

    def left():
        exchange.finish()
        for keep in keeps(saved):
            keep.wait()

    take = pltpu.make_async_copy(passed, e.xt, sems[10])

    def turn():
        take.start()
        e.mask = mask
        fill_mask(e)
        take.wait()

    def load():
        for start in weight_loads(e, p, s, *sems[7:9]):
            start()

    lag, levels = 4, 6
    early, late = [], []
    for hops in range(levels + lag):
        if hops < levels:
            early += gather.level(hops, "p")
        if hops >= lag:
            (early if hops < levels else late).extend(gather.level(hops - lag, "s"))
    own = len(P_CHUNKS) / len(early)
    timed = [(own, load)] + spread_out(stages, own, 0.4)
    interleave(early, timed + [(0.4, leave), (0.7, left), (0.75, turn)])
    gather.complete("p")
    e.x, e.mod, e.bias = e.xt, mods.at[1], biases.at[1]
    start_p, start_s = weight_loads(e, p_out, s_out, *sems[7:9])
    start_p()
    stages = forward_stages(e, e.y, shrink_last=True)
    interleave(late, spread_out(stages[:-5], 0.0, 1.0))
    gather.complete("s")
    start_s()
    for stage in stages[-5:]:
        stage()
    gather.sent_all()
    last = keeps(saved_t) + [pltpu.make_async_copy(e.y, y_t, sems[10])]
    for keep in last:
        keep.start()
    for keep in last:
        keep.wait()


def second_gather(p_own, s_own, x, mods, biases, segments, p, s):
    kept = tuple(jax.ShapeDtypeStruct(*SHAPES[name]) for name in KEPT)
    smem = pl.BlockSpec(memory_space=pltpu.SMEM)
    results = pl.pallas_call(
        second_gather_kernel,
        out_shape=SLABS + (STREAM, STREAM) + kept + kept,
        in_specs=[VMEM_SPEC] * 5 + [smem] + [ANY_SPEC] * 2,
        out_specs=(ANY_SPEC,) * (4 + 2 * len(KEPT)),
        scratch_shapes=[pltpu.VMEM(shape, kind) for _, shape, kind in SECOND_SCRATCH]
        + dma_sems(*Gather.SEMS, (8,), (8,), (), (8,), (4,), (len(KEPT),), ()),
        compiler_params=pltpu.CompilerParams(
            collective_id=1, has_side_effects=True, vmem_limit_bytes=60 << 20
        ),
        name="second_gather",
    )(p_own, s_own, x, mods, biases, segments, p, s)
    n = 4 + len(KEPT)
    return results[:4], results[4:n], results[n:]


S_RING, P_RING = 5, 3
S_ROWS, P_ROWS = Scatter.rows(S_CHUNKS, S_RING), Scatter.rows(P_CHUNKS, P_RING)
SLOPE_ROW, ACT_ROW = 4 * WIDTH, 4 * WIDTH + 4 * TOKENS
BACKWARD_SCRATCH = (
    ("arena", (P_ROWS, WIDTH), jnp.bfloat16),
    ("arena_s", (S_ROWS, WIDTH), jnp.bfloat16),
    ("own_p", (288, WIDTH), jnp.bfloat16),
    ("own_s", (144, WIDTH), jnp.bfloat16),
    ("bslab", (8, 8, 512), jnp.float32),
    ("heads", (3 * H, TOKENS, HD), jnp.bfloat16),
    ("mh", (H, TOKENS, HD), jnp.bfloat16),
    ("attended", (TOKENS, WIDTH), jnp.float32),
    ("middle", (TOKENS, WIDTH), jnp.float32),
    ("tmp", (TOKENS, WIDTH), jnp.float32),
    ("sums", (12, 8, WIDTH), jnp.float32),
    ("bb", (TOKENS, WIDTH), jnp.bfloat16),
    ("bin", (8, TOKENS, 512), jnp.bfloat16),
    ("bout", (8, TOKENS, 256), jnp.bfloat16),
    ("bexp", (8, TOKENS, 640), jnp.bfloat16),
    ("back_x", (TOKENS, WIDTH), jnp.bfloat16),
    ("bb_t", (WIDTH, TOKENS), jnp.bfloat16),
    ("normed_t", (WIDTH, TOKENS), jnp.bfloat16),
    ("mixture_t", (WIDTH, TOKENS), jnp.bfloat16),
    ("normed2_t", (WIDTH, TOKENS), jnp.bfloat16),
    ("bias_grad", (8, WIDTH), jnp.float32),
    ("mod_grad", (8, WIDTH), jnp.float32),
    ("small", (8, 8, WIDTH), jnp.float32),
    ("small_in", (8, 8, WIDTH), jnp.float32),
    ("row_sum", (8, WIDTH), jnp.float32),
    ("row_in", (4, 8, WIDTH), jnp.float32),
    ("total", (8, WIDTH), jnp.float32),
)
MASK = (("mask", (TOKENS, TOKENS), jnp.float32),)


def backward_kernel(block, names, *refs):
    e = Refs()
    e.mask = None
    for name, ref in zip(names, refs):
        setattr(e, name, ref)
    temporal = block == 1
    sems = refs[len(names) :]
    ready, sems = sems[0], sems[1:]
    e.mod = e.mods.at[block]
    e.slope = e.arena.at[SLOPE_ROW : SLOPE_ROW + 4 * TOKENS, :]
    me = Place()

    places = {"branch": e.tmp, "middle": e.middle, "attended": e.attended, "heads": e.heads}

    def kept_copies(name):
        index = KEPT.index(name)
        source, sem = getattr(e, name + "_kept"), sems[0].at[index]
        if name in ("slope", "act"):
            row = SLOPE_ROW if name == "slope" else ACT_ROW
            rows = [
                e.arena.at[row + d * TOKENS : row + (d + 1) * TOKENS, :] for d in range(4)
            ]
            base = 0 if name == "slope" else 4
            return [
                pltpu.make_async_copy(source.at[d], rows[d], sems[1].at[base + d])
                for d in range(4)
            ]
        return [pltpu.make_async_copy(source, places.get(name, e.back_x), sem)]

    def start_kept(name):
        for copy in kept_copies(name):
            copy.start()

    def wait_kept(name):
        for copy in kept_copies(name):
            copy.wait()

    e.wait_kept = wait_kept
    e.weights = Weights(e.p, e.s, e.arena, sems[2])
    start_kept("branch")
    e.weights.start("shrink", 0)
    start_kept("slope")
    for d in range(1, 4):
        e.weights.start("shrink", d)
    for name in ("act", "middle", "attended", "heads", "normed"):
        start_kept(name)

    def compute_s(b, core, target):
        d, s = b[0] * 2 + core, b[1] * 2 + b[2]
        at = pl.ds(pl.multiple_of(s * 144, 16), 144)
        act = e.arena[pl.ds(pl.multiple_of(ACT_ROW + d * TOKENS, 16), TOKENS), :]
        target[...] = dot(e.bb_t[at, :], act).astype(jnp.bfloat16)

    def compute_p(b, core, target):
        d, s = b[0] * 2 + core, b[1] * 2 + b[2]

        @pl.loop(0, 2)
        def _(i):
            at = pl.ds(pl.multiple_of(d * 288 + i * 144, 16), 144)
            to = pl.ds(pl.multiple_of(i * 144, 16), 144)
            first = dot(e.normed_t[at, :], e.bin[s])
            second = dot(e.mixture_t[at, :], e.bout[s])
            third = dot(e.normed2_t[at, :], e.bexp[s])
            target[to, 0:384] = first[:, 0:384].astype(jnp.bfloat16)
            target[to, 384:512] = (first[:, 384:] + second[:, :128]).astype(jnp.bfloat16)
            target[to, 512:640] = (second[:, 128:] + third[:, :128]).astype(jnp.bfloat16)
            target[to, 640:] = third[:, 128:].astype(jnp.bfloat16)

    across = Scatter(
        me, S_CHUNKS, compute_s, e.own_s, e.arena_s, 0, S_RING, e.s_out, *sems[3:7]
    )
    slabs = Scatter(me, P_CHUNKS, compute_p, e.own_p, e.arena, 0, P_RING, e.p_out, *sems[7:11])
    over_frames = Spread(me, "sp", e.small, e.small_in, *sems[11:13], True)
    over_data = Spread(me, "dp", e.row_sum, e.row_in, *sems[13:15], False)
    over_all = Spread(me, "sp", e.total, e.totals, *sems[15:17], False)
    greet(me)

    def turn(name, target, following):
        def step():
            wait_kept(name)
            target[...] = e.back_x[...].T
            if following:
                start_kept(following)

        return step

    if temporal:
        forth = Exchange(me, e.y_t, e.output, *sems[17:20])
        back = Exchange(me, e.back_x, e.back_spatial, *sems[20:23])
        forth.start()
        fill_mask(e)
    else:
        back = pltpu.make_async_copy(e.back_x, e.input_gradient, sems[17])

    stages = backward_stages(e)
    stages[0]()
    wait_kept("act")
    rest = stages[1:]
    rest[2:2] = [turn("normed", e.normed_t, "mixture")]
    rest[5:5] = [turn("mixture", e.mixture_t, "normed2")]
    rest[8:8] = [turn("normed2", e.normed2_t, None)]
    interleave(across.events(), spread_out(rest, 0.15, 1.05))

    for direction in "xycud":

        def signal():
            pl.semaphore_signal(
                ready, inc=1, device_id=me.neighbour(direction), device_id_type=MESH
            )

        guarded(me.has(direction), signal)

    def begin():
        back.start()
        e.small[...] = jnp.zeros(e.small.shape, jnp.float32)
        for s in range(8):
            e.small[s, 0:1, :] = e.bias_grad[s : s + 1, :]
            for row, column, n, at in pieces(864 * s, 864):
                e.small[s, 1:2, at : at + n] = e.mod_grad[row : row + 1, column : column + n]
        over_frames.start()

    begin()
    pl.semaphore_wait(ready, 3 + jnp.where((me.z > 0) & (me.z < 3), 2, 1))

    def second():
        over_frames.finish()
        e.row_sum[...] = jnp.sum(e.small_in[...], axis=0)
        over_data.start()

    def third():
        over_data.finish()
        e.total[...] = jnp.sum(e.row_in[...], axis=0)
        over_all.start()
        for t in range(9):
            r = slice(32 * t, 32 * (t + 1))
            v = e.cond[r, 0:1] * e.row_in[0, 1:2, 0:864]
            for q in range(1, 4):
                v = v + e.cond[r, q : q + 1] * e.row_in[q, 1:2, 0:864]
            e.weight_grad[r, :] = v

    def fourth():
        over_all.finish()
        if temporal:
            forth.finish()
            back.finish()
        else:
            back.wait()

    interleave(slabs.events(), [(0.3, second), (0.55, third), (0.8, fourth)])
    across.finish()
    slabs.finish()


def backward_call(block, x, mods, cond, segments, p, s, g, kept, y_t=None):
    inputs = [("x", x), ("mods", mods), ("cond", cond), ("g", g), ("p", p), ("s", s)]
    inputs += [(name + "_kept", value) for name, value in zip(KEPT, kept)]
    outs = [
        ("p_out", (288, WIDTH), jnp.float32),
        ("s_out", (144, WIDTH), jnp.float32),
        ("weight_grad", (288, 864), jnp.float32),
        ("totals", (8, 8, WIDTH), jnp.float32),
    ]
    scratch = BACKWARD_SCRATCH
    if block == 1:
        inputs += [("segments", segments), ("y_t", y_t)]
        streams = ["output", "back_spatial"]
        scratch = scratch + MASK
        last = [(8,), (8,), ()] * 2
    else:
        streams = ["input_gradient"]
        last = [()]
    outs += [(name, (TOKENS, WIDTH), jnp.bfloat16) for name in streams]
    names = [name for name, *_ in tuple(inputs) + tuple(outs) + scratch]
    smem = pl.BlockSpec(memory_space=pltpu.SMEM)

    def spec(name):
        if name == "segments":
            return smem
        hbm = name in ("p", "s", "y_t") or name in streams or name.endswith("_kept")
        return ANY_SPEC if hbm else VMEM_SPEC

    sems = [(len(KEPT),), (8,), (4,)] + Scatter.sems(S_CHUNKS) + Scatter.sems(P_CHUNKS)
    sems += [(8,), (8,), (4,), (4,), (8,), (8,)] + last
    return pl.pallas_call(
        functools.partial(backward_kernel, block, names),
        out_shape=[jax.ShapeDtypeStruct(shape, kind) for _, shape, kind in outs],
        in_specs=[spec(name) for name, _ in inputs],
        out_specs=[spec(name) for name, *_ in outs],
        scratch_shapes=[pltpu.VMEM(shape, kind) for _, shape, kind in scratch]
        + [pltpu.SemaphoreType.REGULAR]
        + dma_sems(*sems),
        compiler_params=pltpu.CompilerParams(
            collective_id=3 - block, has_side_effects=True, vmem_limit_bytes=63 << 20
        ),
        name="temporal_backward" if block == 1 else "spatial_backward",
    )(*[value for _, value in inputs])


def sinusoid(timesteps):
    half_width = D // 2
    frequencies = jnp.exp(
        -math.log(10000.0) * jnp.arange(half_width, dtype=jnp.float32) / half_width
    )
    angles = timesteps.astype(jnp.float32)[:, None] * frequencies[None, :]
    return jnp.concatenate([jnp.cos(angles), jnp.sin(angles)], axis=1)


def layer_norm(tensor):
    centered = tensor - jnp.mean(tensor, axis=-1, keepdims=True)
    return centered * lax.rsqrt(jnp.mean(centered * centered, axis=-1, keepdims=True) + EPSILON)


def modulate(tensor, shift_part, scale_part):
    return layer_norm(tensor) * (1.0 + scale_part) + shift_part


def matmul(left_side, right_side):
    return jnp.dot(left_side, right_side, preferred_element_type=jnp.float32)


def back_matmul(gradient, matrix):
    return lax.dot_general(
        gradient,
        matrix,
        (((gradient.ndim - 1,), (1,)), ((), ())),
        preferred_element_type=jnp.float32,
    )


def outer_product(left_side, right_side):
    flat_left = left_side.reshape(-1, left_side.shape[-1])
    flat_right = right_side.reshape(-1, right_side.shape[-1])
    return lax.dot_general(
        flat_left, flat_right, (((0,), (0,)), ((), ())), preferred_element_type=jnp.float32
    )


def column_totals(tensor):
    return jnp.sum(tensor.astype(jnp.float32).reshape(-1, tensor.shape[-1]), axis=0)


def per_sequence(tensor):
    return jnp.sum(tensor, axis=(1, 2))


def over_data(core, biases):
    attend_in, attend_out, expand, shrink = core
    attend_bias, out_bias, expand_bias, shrink_bias, modulate_bias = biases
    gathered = (
        lax.all_gather(attend_in, "dp", axis=0, tiled=True),
        lax.all_gather(attend_out, "dp", axis=0, tiled=True),
        lax.all_gather(expand, "dp", axis=0, tiled=True),
        lax.all_gather(shrink, "dp", axis=0, tiled=True),
        lax.all_gather(attend_bias, "dp", axis=0, tiled=True),
        lax.all_gather(out_bias, "dp", axis=0, tiled=True),
        lax.all_gather(expand_bias, "dp", axis=0, tiled=True),
        lax.all_gather(shrink_bias, "dp", axis=0, tiled=True),
        lax.all_gather(modulate_bias, "dp", axis=0, tiled=True),
    )
    return (gathered[:4], gathered[4:])


def over_frames(core):
    attend_in, attend_out, expand, shrink = core
    gathered = (
        lax.all_gather(attend_in, "sp", axis=1, tiled=True),
        lax.all_gather(attend_out, "sp", axis=1, tiled=True),
        lax.all_gather(expand, "sp", axis=1, tiled=True),
        lax.all_gather(shrink, "sp", axis=1, tiled=True),
    )
    return gathered


def collect(core, biases):
    core_rows, biases_full = over_data(core, biases)
    core_full = over_frames(core_rows)
    return (core_full, biases_full)


def own_rows(condition_all, rows):
    return lax.dynamic_slice_in_dim(condition_all, lax.axis_index("dp") * rows, rows, 1)


def modulation_of(condition_all, modulate_weights):
    rows = modulate_weights[0].shape[0]
    own = own_rows(condition_all, rows)
    partial_terms = jnp.stack([matmul(own, weight) for weight in modulate_weights], axis=1)
    summed = lax.psum_scatter(partial_terms, "dp", scatter_dimension=0, tiled=True)
    full = lax.all_gather(summed, "sp", axis=2, tiled=True)
    return [full[:, slot] for slot in range(len(modulate_weights))]


def sum_over_frames(terms):
    attend_in, attend_out, expand, shrink = terms
    return (
        lax.psum_scatter(
            attend_in.astype(jnp.bfloat16), "sp", scatter_dimension=1, tiled=True
        ).astype(jnp.float32),
        lax.psum_scatter(
            attend_out.astype(jnp.bfloat16), "sp", scatter_dimension=1, tiled=True
        ).astype(jnp.float32),
        lax.psum_scatter(expand.astype(jnp.bfloat16), "sp", scatter_dimension=1, tiled=True).astype(
            jnp.float32
        ),
        lax.psum_scatter(shrink.astype(jnp.bfloat16), "sp", scatter_dimension=1, tiled=True).astype(
            jnp.float32
        ),
    )


def sum_over_data(terms):
    attend_in, attend_out, expand, shrink = terms
    return (
        lax.psum_scatter(
            attend_in.astype(jnp.bfloat16), "dp", scatter_dimension=0, tiled=True
        ).astype(jnp.float32),
        lax.psum_scatter(
            attend_out.astype(jnp.bfloat16), "dp", scatter_dimension=0, tiled=True
        ).astype(jnp.float32),
        lax.psum_scatter(expand.astype(jnp.bfloat16), "dp", scatter_dimension=0, tiled=True).astype(
            jnp.float32
        ),
        lax.psum_scatter(shrink.astype(jnp.bfloat16), "dp", scatter_dimension=0, tiled=True).astype(
            jnp.float32
        ),
    )


def modulate_gradients(condition_all, back_modulations, rows):
    joined = jnp.stack(back_modulations, axis=1)
    columns = lax.psum_scatter(joined, "sp", scatter_dimension=2, tiled=True)
    every = lax.all_gather(columns, "dp", axis=0, tiled=True)
    own = own_rows(condition_all, rows).astype(jnp.float32)
    return [
        jnp.dot(own.T, every[:, slot], precision=HIGHEST_PRECISION)
        for slot in range(len(back_modulations))
    ]


def finish(core_terms, bias_terms):
    matrix_grads = sum_over_data(sum_over_frames(core_terms))
    attend_bias, out_bias, expand_bias, shrink_bias, modulate_bias = bias_terms
    totals = lax.psum(
        (attend_bias, out_bias, expand_bias, shrink_bias, modulate_bias), ("dp", "sp")
    )
    data_index = lax.axis_index("dp")
    data_count = lax.axis_size("dp")
    bias_grads = tuple(
        (
            lax.dynamic_slice_in_dim(
                total_bias,
                data_index * (total_bias.shape[0] // data_count),
                total_bias.shape[0] // data_count,
            )
            for total_bias in totals
        )
    )
    return (matrix_grads, bias_grads)


def frames_to_patches(tensor):
    return lax.all_to_all(tensor, "sp", split_axis=2, concat_axis=1, tiled=True)


def patches_to_frames(tensor):
    return lax.all_to_all(tensor, "sp", split_axis=1, concat_axis=2, tiled=True)


def attention_scores(queries, key_rows, forms, allowed):
    scores = jnp.einsum(forms[0], queries, key_rows, preferred_element_type=jnp.float32) * HD ** (
        -0.5
    )
    if allowed is not None:
        scores = jnp.where(allowed, scores, -1e30)
    return scores


def block_forward(stream, modulation, core, biases, forms, allowed):
    attend_in, attend_out, expand, shrink = core
    attend_bias, out_bias, expand_bias, shrink_bias, modulate_bias = biases
    model_width = stream.shape[-1]
    pieces = [
        modulation[:, None, None, slot * model_width : (slot + 1) * model_width]
        for slot in range(6)
    ]
    normed = modulate(stream, pieces[0], pieces[1]).astype(jnp.bfloat16)
    bias_float = attend_bias.astype(jnp.float32)
    joined_bias = jnp.concatenate(
        [bias_float[:model_width], jnp.zeros((model_width,), jnp.float32), bias_float[model_width:]]
    )
    projected = (matmul(normed, attend_in) + joined_bias).astype(jnp.bfloat16)
    head_shape = projected.shape[:3] + (H, HD)
    queries = projected[..., :model_width].reshape(head_shape)
    key_rows = projected[..., model_width : 2 * model_width].reshape(head_shape)
    values = projected[..., 2 * model_width :].reshape(head_shape)
    scores = attention_scores(queries, key_rows, forms, allowed)
    highest = jnp.max(scores, axis=-1, keepdims=True)
    exponent = jnp.exp(scores - highest)
    denominator = jnp.sum(exponent, axis=-1, keepdims=True)
    softmax_probs = exponent / denominator
    logsum = highest + jnp.log(denominator)
    mixture = (
        jnp.einsum(
            forms[1], softmax_probs.astype(jnp.bfloat16), values, preferred_element_type=jnp.float32
        )
        .astype(jnp.bfloat16)
        .reshape(stream.shape)
    )
    attended = matmul(mixture, attend_out) + out_bias.astype(jnp.float32)
    middle = stream + pieces[2] * attended
    normed_second = modulate(middle, pieces[3], pieces[4]).astype(jnp.bfloat16)
    hidden = matmul(normed_second, expand) + expand_bias.astype(jnp.float32)
    activated = jax.nn.gelu(hidden, approximate=True).astype(jnp.bfloat16)
    branch = matmul(activated, shrink) + shrink_bias.astype(jnp.float32)
    result = middle + pieces[5] * branch
    kept = (
        pieces,
        normed,
        queries,
        key_rows,
        values,
        logsum,
        mixture,
        attended,
        middle,
        normed_second,
        hidden,
        activated,
        branch,
    )
    return (result, kept)


def block_backward(incoming, stream, core, forms, allowed, kept):
    attend_in, attend_out, expand, shrink = core
    (
        pieces,
        normed,
        queries,
        key_rows,
        values,
        logsum,
        mixture,
        attended,
        middle,
        normed_second,
        hidden,
        activated,
        branch,
    ) = kept
    model_width = stream.shape[-1]
    sequences = stream.shape[0]
    back_branch = (pieces[5] * incoming).astype(jnp.bfloat16)
    back_gate_second = per_sequence(incoming * branch)
    shrink_term = outer_product(activated, back_branch)
    shrink_bias_term = column_totals(back_branch)
    back_activated = back_matmul(back_branch, shrink)
    _, gelu_pull = jax.vjp(lambda tensor: jax.nn.gelu(tensor, approximate=True), hidden)
    back_hidden = gelu_pull(back_activated)[0].astype(jnp.bfloat16)
    expand_term = outer_product(normed_second, back_hidden)
    expand_bias_term = column_totals(back_hidden)
    back_normed_second = back_matmul(back_hidden, expand)
    _, second_pull = jax.vjp(modulate, middle, pieces[3], pieces[4])
    back_middle, back_shift_second, back_scale_second = second_pull(back_normed_second)
    back_middle = back_middle + incoming
    back_attended = (pieces[2] * back_middle).astype(jnp.bfloat16)
    back_gate_first = per_sequence(back_middle * attended)
    out_term = outer_product(mixture, back_attended)
    out_bias_term = column_totals(back_attended)
    back_mixture = (
        back_matmul(back_attended, attend_out).astype(jnp.bfloat16).reshape(queries.shape)
    )
    scores = attention_scores(queries, key_rows, forms, allowed)
    softmax_probs = jnp.exp(scores - logsum)
    back_probs = jnp.einsum(forms[0], back_mixture, values, preferred_element_type=jnp.float32)
    back_values = jnp.einsum(
        forms[2],
        softmax_probs.astype(jnp.bfloat16),
        back_mixture,
        preferred_element_type=jnp.float32,
    )
    row_delta = jnp.sum(softmax_probs * back_probs, axis=-1, keepdims=True)
    back_scores = (softmax_probs * (back_probs - row_delta)).astype(jnp.bfloat16)
    score_scale = HD ** (-0.5)
    back_queries = (
        jnp.einsum(forms[1], back_scores, key_rows, preferred_element_type=jnp.float32)
        * score_scale
    )
    back_keys = (
        jnp.einsum(forms[2], back_scores, queries, preferred_element_type=jnp.float32) * score_scale
    )
    flat_shape = stream.shape
    back_projected = jnp.concatenate(
        [
            back_queries.reshape(flat_shape),
            back_keys.reshape(flat_shape),
            back_values.reshape(flat_shape),
        ],
        axis=-1,
    ).astype(jnp.bfloat16)
    attend_in_term = outer_product(normed, back_projected)
    projected_totals = column_totals(back_projected)
    attend_bias_term = jnp.concatenate(
        [projected_totals[:model_width], projected_totals[2 * model_width :]]
    )
    back_normed = back_matmul(back_projected, attend_in)
    _, first_pull = jax.vjp(modulate, stream, pieces[0], pieces[1])
    back_stream, back_shift_first, back_scale_first = first_pull(back_normed)
    back_stream = back_stream + back_middle
    back_modulation = jnp.concatenate(
        [
            back_shift_first.reshape(sequences, model_width),
            back_scale_first.reshape(sequences, model_width),
            back_gate_first,
            back_shift_second.reshape(sequences, model_width),
            back_scale_second.reshape(sequences, model_width),
            back_gate_second,
        ],
        axis=1,
    )
    modulate_bias_term = jnp.sum(back_modulation, axis=0)
    core_terms = (attend_in_term, out_term, expand_term, shrink_term)
    bias_terms = (
        attend_bias_term,
        out_bias_term,
        expand_bias_term,
        shrink_bias_term,
        modulate_bias_term,
    )
    return (back_stream, core_terms, back_modulation, bias_terms)


def shards(
    inputs,
    timesteps,
    segment_ids,
    spatial_attend_in,
    spatial_attend_bias,
    spatial_attend_out,
    spatial_out_bias,
    spatial_expand,
    spatial_expand_bias,
    spatial_shrink,
    spatial_shrink_bias,
    spatial_modulate,
    spatial_modulate_bias,
    temporal_attend_in,
    temporal_attend_bias,
    temporal_attend_out,
    temporal_out_bias,
    temporal_expand,
    temporal_expand_bias,
    temporal_shrink,
    temporal_shrink_bias,
    temporal_modulate,
    temporal_modulate_bias,
    cotangent,
):
    condition_all = jax.nn.silu(sinusoid(timesteps)).astype(jnp.bfloat16)
    allowed = (segment_ids[:, :, None] == segment_ids[:, None, :])[:, None, None, :, :]
    spatial_core = (spatial_attend_in, spatial_attend_out, spatial_expand, spatial_shrink)
    spatial_biases = (
        spatial_attend_bias,
        spatial_out_bias,
        spatial_expand_bias,
        spatial_shrink_bias,
        spatial_modulate_bias,
    )
    temporal_core = (temporal_attend_in, temporal_attend_out, temporal_expand, temporal_shrink)
    temporal_biases = (
        temporal_attend_bias,
        temporal_out_bias,
        temporal_expand_bias,
        temporal_shrink_bias,
        temporal_modulate_bias,
    )
    stream = inputs.astype(jnp.float32)
    modulations = modulation_of(condition_all, (spatial_modulate, temporal_modulate))
    core, biases = collect(spatial_core, spatial_biases)
    modulation = modulations[0] + biases[4].astype(jnp.float32)
    spatial_core = core
    spatial_out, spatial_kept = block_forward(stream, modulation, core, biases, SPATIAL_FORMS, None)
    passed = frames_to_patches(spatial_out.astype(jnp.bfloat16)).astype(jnp.float32)
    core, biases = collect(temporal_core, temporal_biases)
    modulation = modulations[1] + biases[4].astype(jnp.float32)
    temporal_out, temporal_kept = block_forward(
        passed, modulation, core, biases, TEMPORAL_FORMS, allowed
    )
    output = patches_to_frames(temporal_out.astype(jnp.bfloat16))
    incoming = frames_to_patches(cotangent).astype(jnp.float32)
    back_passed, core_terms, back_temporal, bias_terms = block_backward(
        incoming, passed, core, TEMPORAL_FORMS, allowed, temporal_kept
    )
    temporal_grads, temporal_bias_grads = finish(core_terms, bias_terms)
    back_spatial = patches_to_frames(back_passed.astype(jnp.bfloat16)).astype(jnp.float32)
    back_inputs, core_terms, back_spatial_modulation, bias_terms = block_backward(
        back_spatial, stream, spatial_core, SPATIAL_FORMS, None, spatial_kept
    )
    spatial_grads, spatial_bias_grads = finish(core_terms, bias_terms)
    modulate_grads = modulate_gradients(
        condition_all, (back_spatial_modulation, back_temporal), spatial_modulate.shape[0]
    )
    return (
        output,
        back_inputs.astype(jnp.bfloat16),
        spatial_grads[0],
        spatial_bias_grads[0],
        spatial_grads[1],
        spatial_bias_grads[1],
        spatial_grads[2],
        spatial_bias_grads[2],
        spatial_grads[3],
        spatial_bias_grads[3],
        modulate_grads[0],
        spatial_bias_grads[4],
        temporal_grads[0],
        temporal_bias_grads[0],
        temporal_grads[1],
        temporal_bias_grads[1],
        temporal_grads[2],
        temporal_bias_grads[2],
        temporal_grads[3],
        temporal_bias_grads[3],
        modulate_grads[1],
        temporal_bias_grads[4],
    )


def fits(mesh):
    return mesh.shape["dp"] == 4 and mesh.shape["sp"] == 8


def condition_rows(timesteps, rows):
    half = D // 2
    index = lax.axis_index("dp") * rows + jnp.arange(rows, dtype=jnp.int32)
    place = (index % half).astype(jnp.float32)
    frequencies = jnp.exp(-math.log(10000.0) * place / half)
    angles = timesteps.astype(jnp.float32)[:, None] * frequencies[None, :]
    wave = jnp.where((index < half)[None, :], jnp.cos(angles), jnp.sin(angles))
    return jax.nn.silu(wave).astype(jnp.bfloat16)


def fast_shards(
    inputs,
    timesteps,
    segment_ids,
    spatial_attend_in,
    spatial_attend_bias,
    spatial_attend_out,
    spatial_out_bias,
    spatial_expand,
    spatial_expand_bias,
    spatial_shrink,
    spatial_shrink_bias,
    spatial_modulate,
    spatial_modulate_bias,
    temporal_attend_in,
    temporal_attend_bias,
    temporal_attend_out,
    temporal_out_bias,
    temporal_expand,
    temporal_expand_bias,
    temporal_shrink,
    temporal_shrink_bias,
    temporal_modulate,
    temporal_modulate_bias,
    cotangent,
):
    def small(attend, out, expand, shrink, modulate):
        rows = [attend, out, shrink, expand, modulate[:D], modulate[D:]]
        return [jnp.pad(row.astype(jnp.float32)[None], ((0, 0), (0, D - row.shape[0]))) for row in rows]

    pack = jnp.concatenate(
        small(
            spatial_attend_bias,
            spatial_out_bias,
            spatial_expand_bias,
            spatial_shrink_bias,
            spatial_modulate_bias,
        )
        + small(
            temporal_attend_bias,
            temporal_out_bias,
            temporal_expand_bias,
            temporal_shrink_bias,
            temporal_modulate_bias,
        )
        + [jnp.zeros((4, D), jnp.float32)]
    )
    cond = jnp.pad(condition_rows(timesteps, spatial_modulate.shape[0]), ((0, 4), (0, 0)))
    cond_columns = cond.astype(jnp.float32).T
    x = inputs.reshape(TOKENS, WIDTH)
    spatial_p, spatial_s, mods, biases, incoming = first_gather(
        jnp.concatenate([spatial_attend_in, spatial_attend_out, spatial_expand], axis=1),
        spatial_shrink.T,
        pack,
        cond,
        (spatial_modulate, temporal_modulate),
        cotangent.reshape(TOKENS, WIDTH),
    )
    (temporal_p, temporal_s, passed, y_t), kept_s, kept_t = second_gather(
        jnp.concatenate([temporal_attend_in, temporal_attend_out, temporal_expand], axis=1),
        temporal_shrink.T,
        x,
        mods,
        biases,
        segment_ids,
        spatial_p,
        spatial_s,
    )
    packed_t, turned_t, modulate_t, totals_t, output, back_spatial = backward_call(
        1, passed, mods, cond_columns, segment_ids, temporal_p, temporal_s, incoming, kept_t, y_t
    )
    packed_s, turned_s, modulate_s, totals_s, input_gradient = backward_call(
        0, x, mods, cond_columns, segment_ids, spatial_p, spatial_s, back_spatial, kept_s
    )
    outs, (output, input_gradient, modulate_s, modulate_t) = unpack(
        (packed_s, turned_s, totals_s, packed_t, turned_t, totals_t),
        (output, input_gradient, modulate_s, modulate_t),
    )
    return (
        output.reshape(inputs.shape),
        input_gradient.reshape(inputs.shape),
        *outs[:8],
        modulate_s,
        outs[8],
        *outs[9:17],
        modulate_t,
        outs[17],
    )


def solution(mesh):
    placed = (
        P("dp", "sp", None, None),
        P(),
        P("dp", None),
        P("dp", "sp"),
        P("dp"),
        P("dp", "sp"),
        P("dp"),
        P("dp", "sp"),
        P("dp"),
        P("dp", "sp"),
        P("dp"),
        P("dp", "sp"),
        P("dp"),
        P("dp", "sp"),
        P("dp"),
        P("dp", "sp"),
        P("dp"),
        P("dp", "sp"),
        P("dp"),
        P("dp", "sp"),
        P("dp"),
        P("dp", "sp"),
        P("dp"),
        P("dp", "sp", None, None),
    )
    return jax.shard_map(
        fast_shards if fits(mesh) else shards,
        mesh=mesh,
        in_specs=placed,
        out_specs=(
            P("dp", "sp", None, None),
            P("dp", "sp", None, None),
            P("dp", "sp"),
            P("dp"),
            P("dp", "sp"),
            P("dp"),
            P("dp", "sp"),
            P("dp"),
            P("dp", "sp"),
            P("dp"),
            P("dp", "sp"),
            P("dp"),
            P("dp", "sp"),
            P("dp"),
            P("dp", "sp"),
            P("dp"),
            P("dp", "sp"),
            P("dp"),
            P("dp", "sp"),
            P("dp"),
            P("dp", "sp"),
            P("dp"),
        ),
        check_vma=False,
    )
```
